32 devices in a mesh: dp: 16 (over z, y, x), head: 2 (over core).
Axes of the slice: x: 2, y: 2, z: 4, core: 2. Of those that a mesh axis runs over, the one named last changes fastest.
Arguments:
- tokens: bfloat16 [32768, 768], P(('dp', 'head')), may hold values from -6 to 6
- lengths: int32 [16, 4], P('dp'), may hold values from 1 to 1024, 2048 in all within a row
- norm_gains: float32 [2, 768], replicated, may hold values from 0.5 to 1.5
- joined_weight: float32 [2, 1152, 768], P('head', 'dp'), may hold values from -0.21875 to 0.21875
- mixer_weight: float32 [2, 768, 384], P('head', 'dp'), may hold values from -0.875 to 0.875
- expand_weight: float32 [2, 1152, 768], P('head', 'dp'), may hold values from -0.21875 to 0.21875
- shrink_weight: float32 [2, 768, 576], P('head', 'dp'), may hold values from -0.1875 to 0.1875
- joined_momentum: float32 [2, 1152, 768], P('head', 'dp'), may hold values from -320 to 320
- mixer_momentum: float32 [2, 768, 384], P('head', 'dp'), may hold values from -320 to 320
- expand_momentum: float32 [2, 1152, 768], P('head', 'dp'), may hold values from -320 to 320
- shrink_momentum: float32 [2, 768, 576], P('head', 'dp'), may hold values from -320 to 320
- gain_momentum: float32 [2, 768], replicated, may hold values from -320 to 320
- cotangent: bfloat16 [32768, 768], P('dp'), may hold values from -6 to 6
Outputs:
- layer_output: bfloat16 [32768, 768], P(('dp', 'head'))
- input_gradient: float32 [32768, 768], P(('dp', 'head'))
- momentum_joined: float32 [2, 1152, 768], P('head', 'dp')
- momentum_mixer: float32 [2, 768, 384], P('head', 'dp')
- momentum_expand: float32 [2, 1152, 768], P('head', 'dp')
- momentum_shrink: float32 [2, 768, 576], P('head', 'dp')
- updated_joined: float32 [2, 1152, 768], P('head', 'dp')
- updated_mixer: float32 [2, 768, 384], P('head', 'dp')
- updated_expand: float32 [2, 1152, 768], P('head', 'dp')
- updated_shrink: float32 [2, 768, 576], P('head', 'dp')
- momentum_gains: float32 [2, 768], replicated
- updated_gains: float32 [2, 768], replicated
The draws below stay inside these ranges and needn't reach their ends.
Inputs may be any that keep to these rules, and one draw needn't show every extreme that they name: Each row of lengths sums to 2048, and its largest entry is 1024.
All inputs are finite; a program needn't handle non-finite values.
Results may differ from the reference program's by a relative error of at most 0.015.
Values may be sent and summed in bfloat16 or wider, within the bound.
No kernel may reach another device: no remote copies, remote signals or barrier semaphores. Data moves between devices by JAX's collectives and lax.ppermute only.
A program may use at most 256 MiB of HBM per device.

```python
import math
import jax
import jax.numpy as jnp
import numpy as np
from jax import lax

D = 768
FF = 1152
HEADS = 12
HEAD_DIM = 64
TOK_DEV = 2048
DOCS = 4
NS_ITERS = 3
LONGEST = 1024
TOKENS = 32768
N_DP = 16
N_HEAD = 2


def block_scale(rng, shape, shards, low, top_value):
    def one(dim, parts):
        steps = jax.random.uniform(jax.random.fold_in(jax.random.fold_in(rng, 6), dim), (parts,), jnp.float32, low / len(shards), top_value / len(shards))
        return jnp.repeat(jnp.exp(steps), shape[dim] // parts).reshape((-1,) + (1,) * (len(shape) - dim - 1))

    gain = one(*shards[0])
    for cut in shards[1:]:
        gain = gain * one(*cut)
    return gain


def split_up(number_of, total, most, lean):
    loads = [(1 << 20) // math.isqrt(rank ** lean) + 1 for rank in range(2, number_of + 1)]
    surplus, holding = total - most - (number_of - 1), [1] * (number_of - 1)
    while surplus > 0:
        free = [i for i in range(number_of - 1) if holding[i] < most]
        whole, remaining = sum([loads[i] for i in free]), surplus
        for i in free:
            addition = min(most - holding[i], max(1, remaining * loads[i] // whole), surplus)
            holding[i] = holding[i] + addition
            surplus = surplus - addition
    return np.array([most] + holding)


def uneven_parts(own_key, amount, total, limit, slope):
    if amount == 2:
        one = jax.random.randint(own_key, (), max(1, total - limit), min(limit, total - 1) + 1)
        return jnp.stack([one, total - one])
    tallies = jnp.asarray(split_up(amount, total, limit, slope), jnp.int32)
    pairs = (amount - 1) // 2
    source_of, receiver = tallies[1:1 + 2 * pairs:2], tallies[2:2 + 2 * pairs:2]
    slack = jnp.minimum(source_of - 1, limit - receiver)
    passed = jax.random.randint(jax.random.fold_in(own_key, 1), (pairs,), 0, 1 << 20) % (slack + 1)
    tallies = tallies.at[1:1 + 2 * pairs:2].set(source_of - passed).at[2:2 + 2 * pairs:2].set(receiver + passed)
    return tallies[jax.random.permutation(jax.random.fold_in(own_key, 2), amount)]


def bell_draw(own_key, dims, deviation, most, cuts=(), kind=jnp.bfloat16):
    values = jax.random.normal(own_key, dims, jnp.float32) * deviation
    if len(cuts) > 0:
        values = block_scale(own_key, dims, cuts, -0.22, 0.18) * values
    return jnp.clip(values, min=-most, max=most).astype(kind)


def setup_inputs(seed: int = 0) -> dict:
    splits = jax.random.split(jax.random.key(seed), 14)
    tokens = bell_draw(splits[0], (TOKENS, D), 1.0, 6.0, ((0, 32),))
    lengths = jax.vmap(lambda own: uneven_parts(own, DOCS, TOK_DEV, LONGEST, 1))(jax.random.split(splits[1], N_DP)).reshape((N_DP, DOCS)).astype(jnp.int32)
    norm_gains = jnp.clip(1.0 + 0.1 * jax.random.normal(splits[2], (2, D), jnp.float32), 0.5, 1.5)
    joined_weight = bell_draw(splits[3], (N_HEAD, 3 * D // N_HEAD, D), D ** -0.5, 0.21875, ((0, 2), (1, 16)), jnp.float32)
    mixer_weight = bell_draw(splits[4], (N_HEAD, D, D // N_HEAD), (D // 16) ** -0.5, 0.875, ((0, 2), (1, 16)), jnp.float32)
    expand_weight = bell_draw(splits[5], (N_HEAD, 2 * FF // N_HEAD, D), D ** -0.5, 0.21875, ((0, 2), (1, 16)), jnp.float32)
    shrink_weight = bell_draw(splits[6], (N_HEAD, D, FF // N_HEAD), FF ** -0.5, 0.1875, ((0, 2), (1, 16)), jnp.float32)
    joined_momentum = bell_draw(splits[7], (N_HEAD, 3 * D // N_HEAD, D), (0.3 * (TOK_DEV * N_DP) ** 0.5), 320.0, ((0, 2), (1, 16)), jnp.float32)
    mixer_momentum = bell_draw(splits[8], (N_HEAD, D, D // N_HEAD), (0.3 * (TOK_DEV * N_DP) ** 0.5), 320.0, ((0, 2), (1, 16)), jnp.float32)
    expand_momentum = bell_draw(splits[9], (N_HEAD, 2 * FF // N_HEAD, D), (0.3 * (TOK_DEV * N_DP) ** 0.5), 320.0, ((0, 2), (1, 16)), jnp.float32)
    shrink_momentum = bell_draw(splits[10], (N_HEAD, D, FF // N_HEAD), (0.3 * (TOK_DEV * N_DP) ** 0.5), 320.0, ((0, 2), (1, 16)), jnp.float32)
    gain_momentum = bell_draw(splits[11], (2, D), (0.3 * (TOK_DEV * N_DP) ** 0.5), 320.0, (), jnp.float32)
    cotangent = bell_draw(splits[12], (TOKENS, D), 1.0, 6.0, ((0, 16),))
    return {"tokens": tokens, "lengths": lengths, "norm_gains": norm_gains, "joined_weight": joined_weight, "mixer_weight": mixer_weight, "expand_weight": expand_weight, "shrink_weight": shrink_weight, "joined_momentum": joined_momentum, "mixer_momentum": mixer_momentum, "expand_momentum": expand_momentum, "shrink_momentum": shrink_momentum, "gain_momentum": gain_momentum, "cotangent": cotangent}


theta_base = 160000.0
norm_epsilon = 1e-05
ns_first = 3.4445
ns_second = -4.775
ns_third = 2.0315
muon_rate = 1.0
gain_rate = 0.3
masked_score = -1e+30
highest = lax.Precision.HIGHEST

@jax.custom_vjp
def low(v):
    return lax.optimization_barrier(v.astype(jnp.bfloat16)).astype(jnp.float32)

@jax.custom_vjp
def low_back(v):
    return v

def low_keep(v):
    return (low(v), None)

def low_pass(kept, grad):
    return (grad,)

def back_keep(v):
    return (v, None)

def back_low(kept, grad):
    return (low(grad),)
low.defvjp(low_keep, low_pass)
low_back.defvjp(back_keep, back_low)

def doc_tables(length_row, row_count):
    doc_ends = jnp.cumsum(length_row).astype(jnp.int32)
    starts = (doc_ends - length_row).astype(jnp.int32)
    places = jnp.arange(row_count, dtype=jnp.int32)
    segment = lax.optimization_barrier(jnp.sum((places[:, None] >= doc_ends[None, :]).astype(jnp.int32), axis=1)).astype(jnp.int32)
    labels = jnp.arange(length_row.shape[0], dtype=jnp.int32)
    doc_first = lax.optimization_barrier(jnp.sum(jnp.where(segment[:, None] == labels[None, :], starts[None, :], 0), axis=1)).astype(jnp.int32)
    position = (places - doc_first).astype(jnp.float32)
    half_dim = HEAD_DIM // 2
    frequency = jnp.exp(jnp.arange(half_dim, dtype=jnp.float32) * (-2.0 * math.log(theta_base) / HEAD_DIM))
    angles = position[:, None] * frequency[None, :]
    cosine = jnp.concatenate([jnp.cos(angles), jnp.cos(angles)], axis=1)
    sine_wave = jnp.concatenate([jnp.sin(angles), jnp.sin(angles)], axis=1)
    return (segment, cosine, sine_wave)

def rotate_pairs(values, cosine, sine_wave):
    half_dim = values.shape[-1] // 2
    turned = jnp.concatenate([-values[..., half_dim:], values[..., :half_dim]], axis=-1)
    return values * cosine[:, None, :] + turned * sine_wave[:, None, :]

def layer_norm(values, gain_row):
    centred = values - lax.optimization_barrier(jnp.mean(values, axis=-1, keepdims=True))
    inverse = lax.rsqrt(lax.optimization_barrier(jnp.mean(centred * centred, axis=-1, keepdims=True)) + norm_epsilon)
    return centred * inverse * gain_row

def forward(residual, norm_gains, joined_weight, mixer_weight, expand_weight, shrink_weight, segment, cosine, sine_wave):
    joined_low = low(joined_weight)
    mixer_low = low(mixer_weight)
    expand_low = low(expand_weight)
    shrink_low = low(shrink_weight)
    group_heads = HEADS // N_HEAD
    group_width = group_heads * HEAD_DIM
    hidden_width = FF // N_HEAD

    def one_row(row_values, row_segment, row_cosine, row_sine):
        row_count = row_values.shape[0]
        normed = low(layer_norm(row_values, norm_gains[0]))
        joined = low_back(jnp.einsum('td,gcd->gtc', normed, joined_low, precision=highest))

        def heads_of(offset):
            picked = joined[:, :, offset:offset + group_width].reshape(N_HEAD, row_count, group_heads, HEAD_DIM)
            return jnp.transpose(picked, (1, 0, 2, 3)).reshape(row_count, HEADS, HEAD_DIM)
        queries = low(rotate_pairs(heads_of(0), row_cosine, row_sine))
        keys_rot = low(rotate_pairs(heads_of(group_width), row_cosine, row_sine))
        values_low = low(heads_of(2 * group_width))
        scores = low_back(jnp.einsum('qhd,khd->hqk', queries, keys_rot, precision=highest) * 0.125)
        same_doc = row_segment[:, None] == row_segment[None, :]
        scores = jnp.where(same_doc[None], scores, masked_score)
        softmax_low = low(jax.nn.softmax(scores, axis=-1))
        attended = low_back(low(jnp.einsum('hqk,khd->qhd', softmax_low, values_low, precision=highest)))
        grouped = attended.reshape(row_count, N_HEAD, group_width)
        middle = row_values + low_back(jnp.einsum('tgc,gdc->td', grouped, mixer_low, precision=highest))
        second = low(layer_norm(middle, norm_gains[1]))
        expanded = low_back(jnp.einsum('td,gcd->gtc', second, expand_low, precision=highest))
        hidden = low(jax.nn.gelu(expanded[:, :, :hidden_width], approximate=False) * expanded[:, :, hidden_width:])
        return middle + jnp.einsum('gtf,gdf->td', hidden, shrink_low, precision=highest)

    def scan_step(carry, inputs):
        return (carry, jax.checkpoint(one_row)(inputs[0], inputs[1], inputs[2], inputs[3]))
    return lax.scan(scan_step, jnp.zeros((), jnp.float32), (residual, segment, cosine, sine_wave))[1]

def orthogonalize(momentum):
    norm_value = jnp.sqrt(jnp.sum(momentum * momentum)) + 1e-07
    matrix = momentum / norm_value
    for iteration in range(NS_ITERS):
        gram_matrix = jnp.dot(matrix.T, matrix, precision=highest)
        once_applied = jnp.dot(matrix, gram_matrix, precision=highest)
        twice_applied = jnp.dot(once_applied, gram_matrix, precision=highest)
        matrix = ns_first * matrix + ns_second * once_applied + ns_third * twice_applied
    return matrix

def muon_update(weight, momentum, gradient):
    momentum_new = 0.5 * momentum + gradient
    direction = jax.vmap(orthogonalize)(momentum_new)
    shape_scale = math.sqrt(weight.shape[1] / weight.shape[2])
    return (momentum_new, weight - muon_rate * shape_scale * direction)

def reference(tokens, lengths, norm_gains, joined_weight, mixer_weight, expand_weight, shrink_weight, joined_momentum, mixer_momentum, expand_momentum, shrink_momentum, gain_momentum, cotangent):
    segment, cosine, sine_wave = jax.vmap(lambda length_row: doc_tables(length_row, TOK_DEV))(lengths)
    residual = tokens.astype(jnp.float32).reshape(N_DP, TOK_DEV, D)

    def wrapped(residual_in, gains_in, joined_in, mixer_in, expand_in, shrink_in):
        return forward(residual_in, gains_in, joined_in, mixer_in, expand_in, shrink_in, segment, cosine, sine_wave)
    primal, pullback = jax.vjp(wrapped, residual, norm_gains, joined_weight, mixer_weight, expand_weight, shrink_weight)
    gradients = pullback(cotangent.astype(jnp.float32).reshape(N_DP, TOK_DEV, D))
    layer_output = primal.reshape(TOKENS, D).astype(jnp.bfloat16)
    input_gradient = gradients[0].reshape(TOKENS, D)
    momentum_joined, updated_joined = muon_update(joined_weight, joined_momentum, gradients[2])
    momentum_mixer, updated_mixer = muon_update(mixer_weight, mixer_momentum, gradients[3])
    momentum_expand, updated_expand = muon_update(expand_weight, expand_momentum, gradients[4])
    momentum_shrink, updated_shrink = muon_update(shrink_weight, shrink_momentum, gradients[5])
    momentum_gains = 0.5 * gain_momentum + gradients[1]
    updated_gains = norm_gains - gain_rate * momentum_gains * lax.rsqrt(lax.optimization_barrier(jnp.mean(momentum_gains * momentum_gains, axis=-1, keepdims=True)) + 1e-06)
    return (layer_output, input_gradient, momentum_joined, momentum_mixer, momentum_expand, momentum_shrink, updated_joined, updated_mixer, updated_expand, updated_shrink, momentum_gains, updated_gains)
```

```python
import functools
import math

import jax
import jax.numpy as jnp
from jax import lax
from jax.experimental import pallas as pl
from jax.experimental.pallas import tpu as pltpu
from jax.sharding import PartitionSpec as P

HEAD_DIM = 64
NS_ITERS = 3

theta_base = 160000.0
norm_epsilon = 1e-05
ns_first = 3.4445
ns_second = -4.775
ns_third = 2.0315
muon_rate = 1.0
gain_rate = 0.3

bf16 = jnp.bfloat16
f32 = jnp.float32
LOG2E = math.log2(math.e)
QUERY_SCALE = 0.125 * LOG2E
SAFE_SCORE = 60.0
DEPTH = 128
TILE_Q = 256
TILE_K = 256
FWD_SKEW = 6
BWD_SKEW = 2

NN = (((1,), (0,)), ((), ()))
NT = (((1,), (1,)), ((), ()))
TN = (((0,), (0,)), ((), ()))
TT = (((0,), (1,)), ((), ()))


def dot(left, right, dims):
    return lax.dot_general(left, right, dims, preferred_element_type=f32)


def key_bounds(length_row, row_count):
    ends = jnp.cumsum(length_row)
    starts = ends - length_row
    first = jnp.arange(row_count // TILE_Q, dtype=jnp.int32) * TILE_Q
    labels = jnp.arange(length_row.shape[0], dtype=jnp.int32)

    def pick(places, table):
        segment = jnp.sum((places[:, None] >= ends[None, :]).astype(jnp.int32), axis=1)
        return jnp.sum(jnp.where(segment[:, None] == labels[None, :], table[None, :], 0), axis=1)

    low = pick(first, starts) // TILE_K
    high = (pick(first + TILE_Q - 1, ends) + TILE_K - 1) // TILE_K
    return low.astype(jnp.int32), high.astype(jnp.int32)


def doc_tables(length_row, row_count):
    ends = jnp.cumsum(length_row)
    starts = ends - length_row
    count = length_row.shape[0]
    places = jnp.arange(row_count, dtype=jnp.int32)[None, :]
    member = (places >= starts[:, None]) & (places < ends[:, None])
    rest = jnp.zeros((16 - count, row_count), f32)
    key_rows = jnp.concatenate([member.astype(f32), rest], axis=0).astype(bf16)
    query_rows = jnp.concatenate([jnp.where(member, 0.0, -1e30), rest], axis=0).astype(bf16)
    doc_first = jnp.sum(jnp.where(member, starts[:, None], 0), axis=0, keepdims=True)
    position = (places - doc_first).astype(f32)
    half_dim = HEAD_DIM // 2
    frequency = jnp.exp(
        jnp.arange(half_dim, dtype=f32) * (-2.0 * math.log(theta_base) / HEAD_DIM)
    )
    angles = frequency[:, None] * position
    return key_rows, query_rows, jnp.cos(angles), jnp.sin(angles)


def rotate(values, cosine, sine):
    half = HEAD_DIM // 2
    heads = values.reshape(-1, HEAD_DIM, values.shape[1])
    low, high = heads[:, :half], heads[:, half:]
    turned = jnp.concatenate([low * cosine - high * sine, high * cosine + low * sine], axis=1)
    return turned.reshape(values.shape)


def unrotate(values, cosine, sine):
    return rotate(values, cosine, -sine)


def rows16(parts):
    rest = jnp.zeros((16 - len(parts), parts[0].shape[1]), f32)
    return jnp.concatenate([part.astype(f32) for part in parts] + [rest], axis=0).astype(bf16)


def split3(value):
    first = value.astype(bf16)
    left = value - first.astype(f32)
    second = left.astype(bf16)
    third = (left - second.astype(f32)).astype(bf16)
    return [first, second, third]


def three_ones(count):
    return jnp.concatenate([jnp.ones((3, count), f32), jnp.zeros((13, count), f32)], axis=0).astype(
        bf16
    )


def forward_kernel(
    low, high, queries, keys, values, key_rows, query_rows, out, logsum, keys_in, values_in, queries_in, safe
):
    heads = queries.shape[0] // HEAD_DIM
    rows = keys.shape[1]
    step = pl.program_id(0)

    @pl.when(step == 0)
    def _():
        worst = jnp.zeros((1, 1), f32)
        ones = rows16([jnp.ones((1, rows), f32)])
        for h in range(heads):
            band = slice(h * HEAD_DIM, (h + 1) * HEAD_DIM)
            key = keys[band, :]
            pad = jnp.zeros((DEPTH - HEAD_DIM - 16, rows), bf16)
            keys_in[h] = jnp.concatenate([key, key_rows[...], pad], axis=0).T
            values_in[h, :HEAD_DIM, :] = values[band, :]
            values_in[h, HEAD_DIM:, :] = ones
            query_full = queries[band, :].astype(f32)
            key_full = key.astype(f32)
            query_top = jnp.max(
                jnp.sum(query_full * query_full, axis=0, keepdims=True), axis=1, keepdims=True
            )
            key_top = jnp.max(
                jnp.sum(key_full * key_full, axis=0, keepdims=True), axis=1, keepdims=True
            )
            worst = jnp.maximum(worst, query_top * key_top)
        safe[0] = jnp.where(worst[0, 0] <= SAFE_SCORE * SAFE_SCORE, 1, 0)

    first = pl.multiple_of(step * TILE_Q, TILE_Q)
    for h in range(heads):
        queries_in[h, :HEAD_DIM, :] = queries[h * HEAD_DIM : (h + 1) * HEAD_DIM, pl.ds(first, TILE_Q)]
        queries_in[h, HEAD_DIM : HEAD_DIM + 16, :] = query_rows[...]
        queries_in[h, HEAD_DIM + 16 :, :] = jnp.zeros((DEPTH - HEAD_DIM - 16, TILE_Q), bf16)

    def finish(peaks, totals):
        for h in range(heads):
            weight = totals[h][HEAD_DIM : HEAD_DIM + 1, :]
            out[h * HEAD_DIM : (h + 1) * HEAD_DIM, :] = (totals[h][:HEAD_DIM, :] / weight).astype(bf16)
            level = jnp.log2(weight)
            logsum[h : h + 1, :] = level if peaks is None else peaks[h] + level

    empty = tuple(jnp.zeros((HEAD_DIM + 16, TILE_Q), f32) for _ in range(heads))

    @pl.when(safe[0] == 1)
    def _():
        def block(j, totals):
            span = pl.ds(pl.multiple_of(j * TILE_K, TILE_K), TILE_K)
            result = [None] * heads
            waiting = {}
            for t in range(heads + FWD_SKEW):
                if t < heads:
                    waiting[t] = dot(keys_in[t, span, :], queries_in[t], NN)
                h = t - FWD_SKEW
                if h >= 0:
                    raised = jnp.exp2(waiting.pop(h)).astype(bf16)
                    result[h] = totals[h] + dot(values_in[h, :, span], raised, NN)
            return tuple(result)

        finish(None, lax.fori_loop(low[step], high[step], block, empty))

    @pl.when(safe[0] == 0)
    def _():
        def block(j, carry):
            peaks, totals = carry
            span = pl.ds(pl.multiple_of(j * TILE_K, TILE_K), TILE_K)
            new_peaks = []
            new_totals = []
            for h in range(heads):
                scores = dot(keys_in[h, span, :], queries_in[h], NN)
                peak = jnp.maximum(peaks[h], jnp.max(scores, axis=0, keepdims=True))
                raised = jnp.exp2(scores - peak).astype(bf16)
                new_totals.append(
                    totals[h] * jnp.exp2(peaks[h] - peak) + dot(values_in[h, :, span], raised, NN)
                )
                new_peaks.append(peak)
            return tuple(new_peaks), tuple(new_totals)

        lowest = tuple(jnp.full((1, TILE_Q), -3e38, f32) for _ in range(heads))
        finish(*lax.fori_loop(low[step], high[step], block, (lowest, empty)))


def attention_forward(low, high, queries, keys, values, key_rows, query_rows):
    width, rows = queries.shape
    heads = width // HEAD_DIM

    def full(count):
        return pl.BlockSpec((count, rows), lambda i, low, high: (0, 0))

    def tile(count):
        return pl.BlockSpec((count, TILE_Q), lambda i, low, high: (0, i))

    return pl.pallas_call(
        forward_kernel,
        out_shape=(
            jax.ShapeDtypeStruct((width, rows), bf16),
            jax.ShapeDtypeStruct((heads, rows), f32),
        ),
        grid_spec=pltpu.PrefetchScalarGridSpec(
            num_scalar_prefetch=2,
            grid=(rows // TILE_Q,),
            in_specs=[full(width), full(width), full(width), full(16), tile(16)],
            out_specs=[tile(width), tile(heads)],
            scratch_shapes=[
                pltpu.VMEM((heads, rows, DEPTH), bf16),
                pltpu.VMEM((heads, HEAD_DIM + 16, rows), bf16),
                pltpu.VMEM((heads, DEPTH, TILE_Q), bf16),
                pltpu.SMEM((1,), jnp.int32),
            ],
        ),
        compiler_params=pltpu.CompilerParams(
            dimension_semantics=("arbitrary",), vmem_limit_bytes=40 << 20
        ),
        name="attention_forward",
    )(low, high, queries, keys, values, key_rows, query_rows)


def backward_kernel(
    low, high, queries, keys, values, grads, outs, logsum, key_rows, query_rows,
    query_grad, key_grad, value_grad, *scratch
):
    heads = queries.shape[0] // HEAD_DIM
    rows = keys.shape[1]
    keys_in, values_in, queries_in, grads_in = scratch[:4]
    key_sum = scratch[4 : 4 + heads]
    value_sum = scratch[4 + heads : 4 + 2 * heads]
    query_sum = scratch[4 + 2 * heads : 4 + 3 * heads]
    step = pl.program_id(0)

    @pl.when(step == 0)
    def _():
        ones = three_ones(rows)
        for h in range(heads):
            band = slice(h * HEAD_DIM, (h + 1) * HEAD_DIM)
            pad = jnp.zeros((DEPTH - HEAD_DIM - 32, rows), bf16)
            keys_in[h] = jnp.concatenate([keys[band, :], key_rows[...], ones, pad], axis=0).T
            pad = jnp.zeros((DEPTH - HEAD_DIM - 16, rows), bf16)
            values_in[h] = jnp.concatenate([values[band, :], ones, pad], axis=0).T
            key_sum[h][...] = jnp.zeros((HEAD_DIM, rows), f32)
            value_sum[h][...] = jnp.zeros((HEAD_DIM, rows), f32)

    for h in range(heads):
        band = slice(h * HEAD_DIM, (h + 1) * HEAD_DIM)
        queries_in[h, :HEAD_DIM, :] = queries[band, :]
        queries_in[h, HEAD_DIM : HEAD_DIM + 16, :] = query_rows[...]
        queries_in[h, HEAD_DIM + 16 : HEAD_DIM + 32, :] = rows16(split3(-logsum[h : h + 1, :]))
        queries_in[h, HEAD_DIM + 32 :, :] = jnp.zeros((DEPTH - HEAD_DIM - 32, TILE_Q), bf16)
        inner = jnp.sum(grads[band, :].astype(f32) * outs[band, :].astype(f32), axis=0, keepdims=True)
        grads_in[h, :HEAD_DIM, :] = grads[band, :]
        grads_in[h, HEAD_DIM : HEAD_DIM + 16, :] = rows16(split3(-inner))
        grads_in[h, HEAD_DIM + 16 :, :] = jnp.zeros((DEPTH - HEAD_DIM - 16, TILE_Q), bf16)
        query_sum[h][...] = jnp.zeros((HEAD_DIM, TILE_Q), f32)

    def block(j, carry):
        span = pl.ds(pl.multiple_of(j * TILE_K, TILE_K), TILE_K)
        waiting = {}
        for t in range(heads + BWD_SKEW):
            if t < heads:
                waiting[t] = (
                    dot(keys_in[t, span, :], queries_in[t], NN),
                    dot(values_in[t, span, :], grads_in[t], NN),
                )
            h = t - BWD_SKEW
            if h < 0:
                continue
            band = slice(h * HEAD_DIM, (h + 1) * HEAD_DIM)
            scores, weight_grad = waiting.pop(h)
            softmax = jnp.exp2(scores)
            score_grad = (softmax * weight_grad).astype(bf16)
            value_sum[h][:, span] += dot(grads[band, :], softmax.astype(bf16), NT)
            key_sum[h][:, span] += dot(queries[band, :], score_grad, NT)
            query_sum[h][...] += dot(keys[band, span], score_grad, NN)
        return carry

    lax.fori_loop(low[step], high[step], block, 0)
    for h in range(heads):
        query_grad[h * HEAD_DIM : (h + 1) * HEAD_DIM, :] = query_sum[h][...] * 0.125

    @pl.when(step == pl.num_programs(0) - 1)
    def _():
        for h in range(heads):
            band = slice(h * HEAD_DIM, (h + 1) * HEAD_DIM)
            key_grad[band, :] = key_sum[h][...] * (1.0 / LOG2E)
            value_grad[band, :] = value_sum[h][...]


def attention_backward(low, high, queries, keys, values, grads, outs, logsum, key_rows, query_rows):
    width, rows = queries.shape
    heads = width // HEAD_DIM

    def full(count):
        return pl.BlockSpec((count, rows), lambda i, low, high: (0, 0))

    def tile(count):
        return pl.BlockSpec((count, TILE_Q), lambda i, low, high: (0, i))

    result = jax.ShapeDtypeStruct((width, rows), f32)
    return pl.pallas_call(
        backward_kernel,
        out_shape=(result, result, result),
        grid_spec=pltpu.PrefetchScalarGridSpec(
            num_scalar_prefetch=2,
            grid=(rows // TILE_Q,),
            in_specs=[
                tile(width), full(width), full(width), tile(width), tile(width), tile(heads),
                full(16), tile(16),
            ],
            out_specs=[tile(width), full(width), full(width)],
            scratch_shapes=[
                pltpu.VMEM((heads, rows, DEPTH), bf16),
                pltpu.VMEM((heads, rows, DEPTH), bf16),
                pltpu.VMEM((heads, DEPTH, TILE_Q), bf16),
                pltpu.VMEM((heads, DEPTH, TILE_Q), bf16),
            ]
            + [pltpu.VMEM((HEAD_DIM, rows), f32)] * (2 * heads)
            + [pltpu.VMEM((HEAD_DIM, TILE_Q), f32)] * heads,
        ),
        compiler_params=pltpu.CompilerParams(
            dimension_semantics=("arbitrary",), vmem_limit_bytes=52 << 20
        ),
        name="attention_backward",
    )(low, high, queries, keys, values, grads, outs, logsum, key_rows, query_rows)


def swap(value, axis, bit):
    count = lax.axis_size(axis)
    return lax.ppermute(value, axis, [(i, i ^ bit) for i in range(count)])


def bit_orders(count):
    bits = count.bit_length() - 1
    return [[(start + k) % bits for k in range(bits)] for start in range(min(3, bits))]


def column_parts(columns, parts):
    unit = 128
    whole = columns // unit
    cuts = [0]
    for k in range(parts):
        cuts.append(columns if k == parts - 1 else unit * (whole * (k + 1) // parts))
    return list(zip(cuts[:-1], cuts[1:]))


def reduce_rows(value):
    count = lax.axis_size("dp")
    place = lax.axis_index("dp")
    orders = bit_orders(count)
    bits = count.bit_length() - 1
    rows = value.shape[0] // count
    pieces = []
    for (start, stop), order in zip(column_parts(value.shape[1], len(orders)), orders):
        held = value[:, start:stop].reshape((2,) * bits + (rows, stop - start))
        for bit in order:
            axis = bits - 1 - bit
            side = (place >> bit) & 1
            kept = lax.dynamic_slice_in_dim(held, side, 1, axis)
            sent = lax.dynamic_slice_in_dim(held, 1 - side, 1, axis)
            got = swap(sent.astype(bf16), "dp", 1 << bit)
            held = kept.astype(f32) + got.astype(f32)
            if bit != order[-1]:
                held = held.astype(bf16)
        pieces.append(held.reshape(rows, stop - start))
    return jnp.concatenate(pieces, axis=1)


def gather_rows(value, ordered):
    count = lax.axis_size("dp")
    place = lax.axis_index("dp")
    orders = bit_orders(count)
    bits = count.bit_length() - 1
    pieces = []
    for (start, stop), order in zip(column_parts(value.shape[1], len(orders)), orders):
        held = value[:, start:stop][(None,) * bits]
        for bit in reversed(order):
            axis = bits - 1 - bit
            held = jnp.concatenate([held, swap(held, "dp", 1 << bit)], axis=axis)
        held = held.reshape(count, value.shape[0], stop - start)
        if ordered:
            held = jnp.concatenate(
                [lax.dynamic_slice_in_dim(held, place ^ k, 1, 0) for k in range(count)], axis=0
            )
        pieces.append(held.reshape(count * value.shape[0], stop - start))
    return jnp.concatenate(pieces, axis=1)


def total_everywhere(value):
    value = value + swap(value, "head", 1)
    for bit in range(lax.axis_size("dp").bit_length() - 1):
        value = value + swap(value, "dp", 1 << bit)
    return value


def halves(own, other, head):
    first = jnp.where(head == 0, own, other)
    second = jnp.where(head == 0, other, own)
    return jnp.concatenate([first, second], axis=0)


def layer_norm(values, gain_row):
    centred = values - jnp.mean(values, axis=-1, keepdims=True)
    inverse = lax.rsqrt(jnp.mean(centred * centred, axis=-1, keepdims=True) + norm_epsilon)
    normal = centred * inverse
    return normal * gain_row, normal, inverse


def norm_back(upstream, gain_row, normal, inverse):
    scaled = upstream * gain_row
    inner_mean = jnp.mean(scaled * normal, axis=-1, keepdims=True)
    return inverse * (scaled - jnp.mean(scaled, axis=-1, keepdims=True) - normal * inner_mean)


def gated(active_in, linear_in):
    return jax.nn.gelu(active_in, approximate=False) * linear_in


def newton_schulz(own, gathered):
    gram = dot(gathered, gathered, TN)
    norm_value = jnp.sqrt(jnp.trace(gram)) + 1e-07
    rows = own / norm_value
    gram = gram / (norm_value * norm_value)
    for iteration in range(NS_ITERS):
        low_gram = gram.astype(bf16)
        change = (ns_second * gram + ns_third * dot(low_gram, low_gram, NN)).astype(bf16)
        rows = ns_first * rows + dot(rows.astype(bf16), change, NN)
        if iteration + 1 < NS_ITERS:
            once = ns_first * gram + dot(low_gram, change, NN)
            gram = ns_first * once + dot(once.astype(bf16), change, NN)
    return rows


def shards(
    tokens,
    lengths,
    norm_gains,
    joined_weight,
    mixer_weight,
    expand_weight,
    shrink_weight,
    joined_momentum,
    mixer_momentum,
    expand_momentum,
    shrink_momentum,
    gain_momentum,
    cotangent,
):
    row_count = cotangent.shape[0]
    local_rows = tokens.shape[0]
    head = lax.axis_index("head")
    mixer_width = mixer_weight.shape[2]

    joined_low = gather_rows(joined_weight[0].astype(bf16), True)
    both_low = gather_rows(
        jnp.concatenate([mixer_weight[0], shrink_weight[0]], axis=1).astype(bf16), True
    )
    mixer_low, shrink_low = both_low[:, :mixer_width], both_low[:, mixer_width:]
    expand_low = gather_rows(expand_weight[0].astype(bf16), True)
    mixer_other = swap(mixer_low, "head", 1)

    key_rows, query_rows, cosine, sine = doc_tables(lengths[0], row_count)
    low, high = key_bounds(lengths[0], row_count)
    residual = halves(tokens, swap(tokens, "head", 1), head).astype(f32)
    first_normed, first_normal, first_inverse = layer_norm(residual, norm_gains[0])
    first_low = first_normed.astype(bf16)

    joined = dot(joined_low, first_low, NT)
    width = joined.shape[0] // 3
    queries = (rotate(joined[:width], cosine, sine) * QUERY_SCALE).astype(bf16)
    keys = rotate(joined[width : 2 * width], cosine, sine).astype(bf16)
    values = joined[2 * width :].astype(bf16)
    attended, logsum = attention_forward(low, high, queries, keys, values, key_rows, query_rows)
    attended_other = swap(attended, "head", 1)

    middle = residual + dot(attended, mixer_low, TT) + dot(attended_other, mixer_other, TT)
    second_normed, second_normal, second_inverse = layer_norm(middle, norm_gains[1])
    second_low = second_normed.astype(bf16)

    expanded = dot(second_low, expand_low, NT)
    hidden_width = expanded.shape[1] // 2
    activated, linear_part = expanded[:, :hidden_width], expanded[:, hidden_width:]
    hidden = gated(activated, linear_part).astype(bf16)

    def own_half(value):
        return lax.dynamic_slice_in_dim(value, head * local_rows, local_rows, 0)

    def other_half(value):
        return lax.dynamic_slice_in_dim(value, (1 - head) * local_rows, local_rows, 0)

    fed_own = dot(own_half(hidden), shrink_low, NT)
    fed_other = swap(dot(other_half(hidden), shrink_low, NT).astype(bf16), "head", 1)
    layer_output = (own_half(middle) + fed_own + fed_other.astype(f32)).astype(bf16)

    hidden_grad = dot(cotangent, shrink_low, NN)
    shrink_grad = dot(cotangent, hidden, TN)
    unused, gate_pull = jax.vjp(gated, activated, linear_part)
    active_grad, linear_grad = gate_pull(hidden_grad)
    expand_back = jnp.concatenate([active_grad, linear_grad], axis=1).astype(bf16)
    expand_grad = dot(expand_back, second_low, TN)
    second_part = dot(expand_back, expand_low, NN)
    second_back = second_part + swap(second_part.astype(bf16), "head", 1).astype(f32)
    middle_grad = cotangent.astype(f32) + norm_back(
        second_back, norm_gains[1], second_normal, second_inverse
    )
    second_gain_grad = jnp.sum(own_half(second_back * second_normal), axis=0)
    middle_low = middle_grad.astype(bf16)

    attended_grad = dot(mixer_low, middle_low, TT).astype(bf16)
    mixer_grad = lax.dot_general(middle_low, attended, (((0,), (1,)), ((), ())), preferred_element_type=f32)
    query_grad, key_grad, value_grad = attention_backward(
        low, high, queries, keys, values, attended_grad, attended, logsum, key_rows, query_rows
    )
    joined_back = jnp.concatenate(
        [unrotate(query_grad, cosine, sine), unrotate(key_grad, cosine, sine), value_grad], axis=0
    ).astype(bf16)
    joined_grad = dot(joined_back, first_low, NN)

    def first_part(start):
        columns = lax.dynamic_slice_in_dim(joined_back, start, local_rows, 1)
        return dot(columns, joined_low, TN)

    first_other = swap(first_part((1 - head) * local_rows).astype(bf16), "head", 1)
    first_back = first_part(head * local_rows) + first_other.astype(f32)
    own_normal = own_half(first_normal)
    input_gradient = own_half(middle_grad) + norm_back(
        first_back, norm_gains[0], own_normal, own_half(first_inverse)
    )
    first_gain_grad = jnp.sum(first_back * own_normal, axis=0)

    both_summed = reduce_rows(jnp.concatenate([mixer_grad, shrink_grad], axis=1).astype(bf16))
    expand_summed = reduce_rows(expand_grad.astype(bf16))
    joined_summed = reduce_rows(joined_grad.astype(bf16))
    mixer_next = 0.5 * mixer_momentum[0] + both_summed[:, :mixer_width]
    shrink_next = 0.5 * shrink_momentum[0] + both_summed[:, mixer_width:]
    expand_next = 0.5 * expand_momentum[0] + expand_summed
    joined_next = 0.5 * joined_momentum[0] + joined_summed
    both_full = gather_rows(jnp.concatenate([mixer_next, shrink_next], axis=1).astype(bf16), False)
    expand_full = gather_rows(expand_next.astype(bf16), False)
    joined_full = gather_rows(joined_next.astype(bf16), False)
    dp_count = lax.axis_size("dp")
    updated = []
    for weight, own, gathered in (
        (joined_weight, joined_next, joined_full),
        (mixer_weight, mixer_next, both_full[:, :mixer_width]),
        (expand_weight, expand_next, expand_full),
        (shrink_weight, shrink_next, both_full[:, mixer_width:]),
    ):
        shape_scale = math.sqrt(own.shape[0] * dp_count / own.shape[1])
        updated.append((weight[0] - muon_rate * shape_scale * newton_schulz(own, gathered))[None])

    gain_totals = total_everywhere(jnp.stack([first_gain_grad, second_gain_grad]))
    momentum_gains = 0.5 * gain_momentum + gain_totals
    updated_gains = norm_gains - gain_rate * momentum_gains * lax.rsqrt(
        jnp.mean(momentum_gains * momentum_gains, axis=-1, keepdims=True) + 1e-06
    )
    return (
        layer_output,
        input_gradient,
        joined_next[None],
        mixer_next[None],
        expand_next[None],
        shrink_next[None],
        updated[0],
        updated[1],
        updated[2],
        updated[3],
        momentum_gains,
        updated_gains,
    )


def solution(mesh):
    rows = P(("dp", "head"), None)
    weight = P("head", "dp", None)
    return jax.shard_map(
        shards,
        mesh=mesh,
        in_specs=(rows, P("dp", None), P()) + (weight,) * 8 + (P(), P("dp", None)),
        out_specs=(rows, rows) + (weight,) * 8 + (P(), P()),
        check_vma=False,
    )
```

```python
import functools
import math

import jax
import jax.numpy as jnp
from jax import lax
from jax.experimental import pallas as pl
from jax.experimental.pallas import tpu as pltpu
from jax.sharding import PartitionSpec as P

HEAD_DIM = 64
NS_ITERS = 3

theta_base = 160000.0
norm_epsilon = 1e-05
ns_first = 3.4445
ns_second = -4.775
ns_third = 2.0315
muon_rate = 1.0
gain_rate = 0.3

bf16 = jnp.bfloat16
f32 = jnp.float32
LOG2E = math.log2(math.e)
QUERY_SCALE = 0.125 * LOG2E
SAFE_SCORE = 60.0
DEPTH = 128
TILE_Q = 256
TILE_K = 256
FWD_SKEW = 3
BWD_SKEW = 2

NN = (((1,), (0,)), ((), ()))
NT = (((1,), (1,)), ((), ()))
TN = (((0,), (0,)), ((), ()))
TT = (((0,), (1,)), ((), ()))
TT_LEFT = TT
GROUPS = 2


def dot(left, right, dims):
    return lax.dot_general(left, right, dims, preferred_element_type=f32)


def key_bounds(length_row, row_count):
    ends = jnp.cumsum(length_row)
    starts = ends - length_row
    first = jnp.arange(row_count // TILE_Q, dtype=jnp.int32) * TILE_Q
    labels = jnp.arange(length_row.shape[0], dtype=jnp.int32)

    def pick(places, table):
        segment = jnp.sum((places[:, None] >= ends[None, :]).astype(jnp.int32), axis=1)
        return jnp.sum(jnp.where(segment[:, None] == labels[None, :], table[None, :], 0), axis=1)

    low = pick(first, starts) // TILE_K
    high = (pick(first + TILE_Q - 1, ends) + TILE_K - 1) // TILE_K
    return low.astype(jnp.int32), high.astype(jnp.int32)


def doc_tables(length_row, row_count):
    ends = jnp.cumsum(length_row)
    starts = ends - length_row
    count = length_row.shape[0]
    places = jnp.arange(row_count, dtype=jnp.int32)[None, :]
    member = (places >= starts[:, None]) & (places < ends[:, None])
    rest = jnp.zeros((16 - count, row_count), f32)
    key_rows = jnp.concatenate([member.astype(f32), rest], axis=0).astype(bf16)
    query_rows = jnp.concatenate([jnp.where(member, 0.0, -1e30), rest], axis=0).astype(bf16)
    doc_first = jnp.sum(jnp.where(member, starts[:, None], 0), axis=0, keepdims=True)
    position = (places - doc_first).astype(f32)
    half_dim = HEAD_DIM // 2
    frequency = jnp.exp(
        jnp.arange(half_dim, dtype=f32) * (-2.0 * math.log(theta_base) / HEAD_DIM)
    )
    angles = frequency[:, None] * position
    return key_rows, query_rows, jnp.cos(angles), jnp.sin(angles)


def rotate(values, cosine, sine):
    half = HEAD_DIM // 2
    heads = values.reshape(-1, HEAD_DIM, values.shape[1])
    low, high = heads[:, :half], heads[:, half:]
    turned = jnp.concatenate([low * cosine - high * sine, high * cosine + low * sine], axis=1)
    return turned.reshape(values.shape)


def unrotate(values, cosine, sine):
    return rotate(values, cosine, -sine)


def rows16(parts):
    rest = jnp.zeros((16 - len(parts), parts[0].shape[1]), f32)
    return jnp.concatenate([part.astype(f32) for part in parts] + [rest], axis=0).astype(bf16)


def split3(value):
    first = value.astype(bf16)
    left = value - first.astype(f32)
    second = left.astype(bf16)
    third = (left - second.astype(f32)).astype(bf16)
    return [first, second, third]


def three_ones(count):
    return jnp.concatenate([jnp.ones((3, count), f32), jnp.zeros((13, count), f32)], axis=0).astype(
        bf16
    )


def forward_kernel(
    low, high, queries, keys, values, key_rows, query_rows, out, logsum, keys_in, values_in, queries_in, safe
):
    heads = queries.shape[0] // HEAD_DIM
    rows = keys.shape[1]
    step = pl.program_id(0)

    @pl.when(step == 0)
    def _():
        worst = jnp.zeros((1, 1), f32)
        ones = rows16([jnp.ones((1, rows), f32)])
        for h in range(heads):
            band = slice(h * HEAD_DIM, (h + 1) * HEAD_DIM)
            key = keys[band, :]
            pad = jnp.zeros((DEPTH - HEAD_DIM - 16, rows), bf16)
            keys_in[h] = jnp.concatenate([key, key_rows[...], pad], axis=0).T
            values_in[h, :HEAD_DIM, :] = values[band, :]
            values_in[h, HEAD_DIM:, :] = ones
            query_full = queries[band, :].astype(f32)
            key_full = key.astype(f32)
            query_top = jnp.max(
                jnp.sum(query_full * query_full, axis=0, keepdims=True), axis=1, keepdims=True
            )
            key_top = jnp.max(
                jnp.sum(key_full * key_full, axis=0, keepdims=True), axis=1, keepdims=True
            )
            worst = jnp.maximum(worst, query_top * key_top)
        safe[0] = jnp.where(worst[0, 0] <= SAFE_SCORE * SAFE_SCORE, 1, 0)

    first = pl.multiple_of(step * TILE_Q, TILE_Q)
    for h in range(heads):
        queries_in[h, :HEAD_DIM, :] = queries[h * HEAD_DIM : (h + 1) * HEAD_DIM, pl.ds(first, TILE_Q)]
        queries_in[h, HEAD_DIM : HEAD_DIM + 16, :] = query_rows[...]
        queries_in[h, HEAD_DIM + 16 :, :] = jnp.zeros((DEPTH - HEAD_DIM - 16, TILE_Q), bf16)

    def finish(peaks, totals):
        for h in range(heads):
            weight = totals[h][HEAD_DIM : HEAD_DIM + 1, :]
            out[h * HEAD_DIM : (h + 1) * HEAD_DIM, :] = (totals[h][:HEAD_DIM, :] / weight).astype(bf16)
            level = jnp.log2(weight)
            logsum[h : h + 1, :] = level if peaks is None else peaks[h] + level

    empty = tuple(jnp.zeros((HEAD_DIM + 16, TILE_Q), f32) for _ in range(heads))

    @pl.when(safe[0] == 1)
    def _():
        def block(j, totals):
            span = pl.ds(pl.multiple_of(j * TILE_K, TILE_K), TILE_K)
            result = [None] * heads
            waiting = {}
            for t in range(heads + FWD_SKEW):
                if t < heads:
                    waiting[t] = dot(keys_in[t, span, :], queries_in[t], NN)
                h = t - FWD_SKEW
                if h >= 0:
                    raised = jnp.exp2(waiting.pop(h)).astype(bf16)
                    result[h] = totals[h] + dot(values_in[h, :, span], raised, NN)
            return tuple(result)

        finish(None, lax.fori_loop(low[step], high[step], block, empty))

    @pl.when(safe[0] == 0)
    def _():
        def block(j, carry):
            peaks, totals = carry
            span = pl.ds(pl.multiple_of(j * TILE_K, TILE_K), TILE_K)
            new_peaks = []
            new_totals = []
            for h in range(heads):
                scores = dot(keys_in[h, span, :], queries_in[h], NN)
                peak = jnp.maximum(peaks[h], jnp.max(scores, axis=0, keepdims=True))
                raised = jnp.exp2(scores - peak).astype(bf16)
                new_totals.append(
                    totals[h] * jnp.exp2(peaks[h] - peak) + dot(values_in[h, :, span], raised, NN)
                )
                new_peaks.append(peak)
            return tuple(new_peaks), tuple(new_totals)

        lowest = tuple(jnp.full((1, TILE_Q), -3e38, f32) for _ in range(heads))
        finish(*lax.fori_loop(low[step], high[step], block, (lowest, empty)))


def attention_forward(low, high, queries, keys, values, key_rows, query_rows):
    width, rows = queries.shape
    heads = width // HEAD_DIM

    def full(count):
        return pl.BlockSpec((count, rows), lambda i, low, high: (0, 0))

    def tile(count):
        return pl.BlockSpec((count, TILE_Q), lambda i, low, high: (0, i))

    return pl.pallas_call(
        forward_kernel,
        out_shape=(
            jax.ShapeDtypeStruct((width, rows), bf16),
            jax.ShapeDtypeStruct((heads, rows), f32),
        ),
        grid_spec=pltpu.PrefetchScalarGridSpec(
            num_scalar_prefetch=2,
            grid=(rows // TILE_Q,),
            in_specs=[full(width), full(width), full(width), full(16), tile(16)],
            out_specs=[tile(width), tile(heads)],
            scratch_shapes=[
                pltpu.VMEM((heads, rows, DEPTH), bf16),
                pltpu.VMEM((heads, HEAD_DIM + 16, rows), bf16),
                pltpu.VMEM((heads, DEPTH, TILE_Q), bf16),
                pltpu.SMEM((1,), jnp.int32),
            ],
        ),
        compiler_params=pltpu.CompilerParams(
            dimension_semantics=("arbitrary",), vmem_limit_bytes=40 << 20
        ),
        name="attention_forward",
    )(low, high, queries, keys, values, key_rows, query_rows)


def backward_kernel(
    low, high, queries, keys, values, grads, outs, logsum, key_rows, query_rows,
    query_grad, key_grad, value_grad, *scratch
):
    heads = queries.shape[0] // HEAD_DIM
    rows = keys.shape[1]
    keys_in, values_in, queries_in, grads_in = scratch[:4]
    key_sum = scratch[4 : 4 + heads]
    value_sum = scratch[4 + heads : 4 + 2 * heads]
    query_sum = scratch[4 + 2 * heads : 4 + 3 * heads]
    step = pl.program_id(0)

    @pl.when(step == 0)
    def _():
        ones = three_ones(rows)
        for h in range(heads):
            band = slice(h * HEAD_DIM, (h + 1) * HEAD_DIM)
            pad = jnp.zeros((DEPTH - HEAD_DIM - 32, rows), bf16)
            keys_in[h] = jnp.concatenate([keys[band, :], key_rows[...], ones, pad], axis=0).T
            pad = jnp.zeros((DEPTH - HEAD_DIM - 16, rows), bf16)
            values_in[h] = jnp.concatenate([values[band, :], ones, pad], axis=0).T
            key_sum[h][...] = jnp.zeros((HEAD_DIM, rows), f32)
            value_sum[h][...] = jnp.zeros((HEAD_DIM, rows), f32)

    for h in range(heads):
        band = slice(h * HEAD_DIM, (h + 1) * HEAD_DIM)
        queries_in[h, :HEAD_DIM, :] = queries[band, :]
        queries_in[h, HEAD_DIM : HEAD_DIM + 16, :] = query_rows[...]
        queries_in[h, HEAD_DIM + 16 : HEAD_DIM + 32, :] = rows16(split3(-logsum[h : h + 1, :]))
        queries_in[h, HEAD_DIM + 32 :, :] = jnp.zeros((DEPTH - HEAD_DIM - 32, TILE_Q), bf16)
        inner = jnp.sum(grads[band, :].astype(f32) * outs[band, :].astype(f32), axis=0, keepdims=True)
        grads_in[h, :HEAD_DIM, :] = grads[band, :]
        grads_in[h, HEAD_DIM : HEAD_DIM + 16, :] = rows16(split3(-inner))
        grads_in[h, HEAD_DIM + 16 :, :] = jnp.zeros((DEPTH - HEAD_DIM - 16, TILE_Q), bf16)
        query_sum[h][...] = jnp.zeros((HEAD_DIM, TILE_Q), f32)

    def block(j, carry):
        span = pl.ds(pl.multiple_of(j * TILE_K, TILE_K), TILE_K)
        waiting = {}
        for t in range(heads + BWD_SKEW):
            if t < heads:
                waiting[t] = (
                    dot(keys_in[t, span, :], queries_in[t], NN),
                    dot(values_in[t, span, :], grads_in[t], NN),
                )
            h = t - BWD_SKEW
            if h < 0:
                continue
            band = slice(h * HEAD_DIM, (h + 1) * HEAD_DIM)
            scores, weight_grad = waiting.pop(h)
            softmax = jnp.exp2(scores)
            score_grad = (softmax * weight_grad).astype(bf16)
            value_sum[h][:, span] += dot(grads[band, :], softmax.astype(bf16), NT)
            key_sum[h][:, span] += dot(queries[band, :], score_grad, NT)
            query_sum[h][...] += dot(keys[band, span], score_grad, NN)
        return carry

    lax.fori_loop(low[step], high[step], block, 0)
    for h in range(heads):
        query_grad[h * HEAD_DIM : (h + 1) * HEAD_DIM, :] = query_sum[h][...] * 0.125

    @pl.when(step == pl.num_programs(0) - 1)
    def _():
        for h in range(heads):
            band = slice(h * HEAD_DIM, (h + 1) * HEAD_DIM)
            key_grad[band, :] = key_sum[h][...] * (1.0 / LOG2E)
            value_grad[band, :] = value_sum[h][...]


def attention_backward(low, high, queries, keys, values, grads, outs, logsum, key_rows, query_rows):
    width, rows = queries.shape
    heads = width // HEAD_DIM

    def full(count):
        return pl.BlockSpec((count, rows), lambda i, low, high: (0, 0))

    def tile(count):
        return pl.BlockSpec((count, TILE_Q), lambda i, low, high: (0, i))

    result = jax.ShapeDtypeStruct((width, rows), f32)
    return pl.pallas_call(
        backward_kernel,
        out_shape=(result, result, result),
        grid_spec=pltpu.PrefetchScalarGridSpec(
            num_scalar_prefetch=2,
            grid=(rows // TILE_Q,),
            in_specs=[
                tile(width), full(width), full(width), tile(width), tile(width), tile(heads),
                full(16), tile(16),
            ],
            out_specs=[tile(width), full(width), full(width)],
            scratch_shapes=[
                pltpu.VMEM((heads, rows, DEPTH), bf16),
                pltpu.VMEM((heads, rows, DEPTH), bf16),
                pltpu.VMEM((heads, DEPTH, TILE_Q), bf16),
                pltpu.VMEM((heads, DEPTH, TILE_Q), bf16),
            ]
            + [pltpu.VMEM((HEAD_DIM, rows), f32)] * (2 * heads)
            + [pltpu.VMEM((HEAD_DIM, TILE_Q), f32)] * heads,
        ),
        compiler_params=pltpu.CompilerParams(
            dimension_semantics=("arbitrary",), vmem_limit_bytes=52 << 20
        ),
        name="attention_backward",
    )(low, high, queries, keys, values, grads, outs, logsum, key_rows, query_rows)


def swap(value, axis, bit):
    count = lax.axis_size(axis)
    return lax.ppermute(value, axis, [(i, i ^ bit) for i in range(count)])


def bit_orders():
    bits = lax.axis_size("dp").bit_length() - 1
    return [[(start + k) % (bits - 1) for k in range(bits - 1)] + [bits - 1] for start in range(3)]


def steps_count():
    return lax.axis_size("dp").bit_length() - 1


def reduce_start(value):
    bits = steps_count()
    rows = value.shape[0] >> bits
    return value.reshape((2,) * bits + (rows, value.shape[1]))


def reduce_step(held, step, which):
    bits = steps_count()
    bit = bit_orders()[which][step]
    axis = bits - 1 - bit
    side = (lax.axis_index("dp") >> bit) & 1
    kept = lax.dynamic_slice_in_dim(held, side, 1, axis)
    sent = lax.dynamic_slice_in_dim(held, 1 - side, 1, axis)
    total = kept.astype(f32) + swap(sent, "dp", 1 << bit).astype(f32)
    if step + 1 == bits:
        return total.reshape(held.shape[-2:])
    return total.astype(bf16)


def gather_start(value):
    return value[(None,) * steps_count()]


def gather_step(held, step, which):
    bits = steps_count()
    bit = bit_orders()[which][bits - 1 - step]
    return jnp.concatenate([held, swap(held, "dp", 1 << bit)], axis=bits - 1 - bit)


def gather_rows(held):
    return held.reshape(-1, held.shape[-1])


def ordered_rows(held):
    count = lax.axis_size("dp")
    place = lax.axis_index("dp")
    held = held.reshape((count,) + held.shape[-2:])
    held = jnp.concatenate(
        [lax.dynamic_slice_in_dim(held, place ^ k, 1, 0) for k in range(count)], axis=0
    )
    return gather_rows(held)


def thirds(value):
    unit = value.shape[1] // 3 // 128 * 128
    return [value[:, :unit], value[:, unit : 2 * unit], value[:, 2 * unit :]]


def halves_of(value):
    unit = value.shape[1] // 256 * 128
    return [value[:, :unit], value[:, unit:]]


def stepped(step, states, index):
    return [step(state, index, which) for which, state in enumerate(states)]


def tie(*values):
    return lax.optimization_barrier(values)


def total_everywhere(value):
    value = value + swap(value, "head", 1)
    for bit in range(lax.axis_size("dp").bit_length() - 1):
        value = value + swap(value, "dp", 1 << bit)
    return value


def halves(own, other, head):
    first = jnp.where(head == 0, own, other)
    second = jnp.where(head == 0, other, own)
    return jnp.concatenate([first, second], axis=0)


def layer_norm(values, gain_row):
    centred = values - jnp.mean(values, axis=-1, keepdims=True)
    inverse = lax.rsqrt(jnp.mean(centred * centred, axis=-1, keepdims=True) + norm_epsilon)
    normal = centred * inverse
    return normal * gain_row, normal, inverse


def norm_back(upstream, gain_row, normal, inverse):
    scaled = upstream * gain_row
    inner_mean = jnp.mean(scaled * normal, axis=-1, keepdims=True)
    return inverse * (scaled - jnp.mean(scaled, axis=-1, keepdims=True) - normal * inner_mean)


def gated(active_in, linear_in):
    return jax.nn.gelu(active_in, approximate=False) * linear_in


def newton_schulz(own, gathered):
    gram = dot(gathered, gathered, TN)
    norm_value = jnp.sqrt(jnp.trace(gram)) + 1e-07
    rows = own / norm_value
    gram = gram / (norm_value * norm_value)
    for iteration in range(NS_ITERS):
        low_gram = gram.astype(bf16)
        change = (ns_second * gram + ns_third * dot(low_gram, low_gram, NN)).astype(bf16)
        rows = ns_first * rows + dot(rows.astype(bf16), change, NN)
        if iteration + 1 < NS_ITERS:
            once = ns_first * gram + dot(low_gram, change, NN)
            gram = ns_first * once + dot(once.astype(bf16), change, NN)
    return rows


def shards(
    tokens,
    lengths,
    norm_gains,
    joined_weight,
    mixer_weight,
    expand_weight,
    shrink_weight,
    joined_momentum,
    mixer_momentum,
    expand_momentum,
    shrink_momentum,
    gain_momentum,
    cotangent,
):
    row_count = cotangent.shape[0]
    local_rows = tokens.shape[0]
    head = lax.axis_index("head")
    mixer_width = mixer_weight.shape[2]
    bits = steps_count()

    def own_half(value):
        return lax.dynamic_slice_in_dim(value, head * local_rows, local_rows, 0)

    def other_half(value):
        return lax.dynamic_slice_in_dim(value, (1 - head) * local_rows, local_rows, 0)

    states = [gather_start(part) for part in thirds(joined_weight[0].astype(bf16))]
    for index in range(bits):
        states = stepped(gather_step, states, index)
    joined_low = jnp.concatenate([ordered_rows(state) for state in states], axis=1)

    key_rows, query_rows, cosine, sine = doc_tables(lengths[0], row_count)
    low, high = key_bounds(lengths[0], row_count)
    residual = halves(tokens, swap(tokens, "head", 1), head).astype(f32)
    first_normed, first_normal, first_inverse = layer_norm(residual, norm_gains[0])
    first_low = first_normed.astype(bf16)

    joined_low, expand_now, mixer_now, shrink_now = tie(
        joined_low, expand_weight[0], mixer_weight[0], shrink_weight[0]
    )
    states = [gather_start(part) for part in halves_of(expand_now.astype(bf16))] + [
        gather_start(jnp.concatenate([mixer_now, shrink_now], axis=1).astype(bf16))
    ]
    width = joined_low.shape[0] // 3
    band = width // GROUPS
    bands = [slice(g * band, (g + 1) * band) for g in range(GROUPS)]
    index = 0
    projected = []
    for g in range(GROUPS):
        moved = stepped(gather_step, states, index) if index < bits else states
        weight = jnp.concatenate(
            [joined_low[k * width + g * band : k * width + (g + 1) * band] for k in range(3)], axis=0
        )
        joined = dot(weight, first_low, NT)
        queries = (rotate(joined[:band], cosine, sine) * QUERY_SCALE).astype(bf16)
        keys = rotate(joined[band : 2 * band], cosine, sine).astype(bf16)
        values = joined[2 * band :].astype(bf16)
        states, (queries, keys, values), first_low = tie(moved, (queries, keys, values), first_low)
        projected.append((queries, keys, values))
        index += 1
    attended, attended_other, logsums = [], [], []
    for g in range(GROUPS):
        last = g + 1 == GROUPS
        moved = states
        while index < bits:
            moved = stepped(gather_step, moved, index)
            index += 1
            if not last:
                break
        out, logsum = attention_forward(low, high, *projected[g], key_rows, query_rows)
        states, out, projected = tie(moved, out, projected)
        attended.append(out)
        attended_other.append(swap(out, "head", 1))
        logsums.append(logsum)
    expand_low = jnp.concatenate([ordered_rows(state) for state in states[:2]], axis=1)
    both_low = ordered_rows(states[2])
    mixer_low, shrink_low = both_low[:, :mixer_width], both_low[:, mixer_width:]
    mixer_other = swap(mixer_low, "head", 1)

    middle = residual
    for g in range(GROUPS):
        middle = middle + dot(attended[g], mixer_low[:, bands[g]], TT)
        middle = middle + dot(attended_other[g], mixer_other[:, bands[g]], TT)
    second_normed, second_normal, second_inverse = layer_norm(middle, norm_gains[1])
    second_low = second_normed.astype(bf16)

    expanded = dot(second_low, expand_low, NT)
    hidden_width = expanded.shape[1] // 2
    activated, linear_part = expanded[:, :hidden_width], expanded[:, hidden_width:]
    hidden = gated(activated, linear_part).astype(bf16)

    hidden_grad = dot(cotangent, shrink_low, NN)
    unused, gate_pull = jax.vjp(gated, activated, linear_part)
    active_grad, linear_grad = gate_pull(hidden_grad)
    expand_back = jnp.concatenate([active_grad, linear_grad], axis=1).astype(bf16)
    second_part = dot(expand_back, expand_low, NN)
    second_other = swap(second_part.astype(bf16), "head", 1)
    shrink_grad = dot(cotangent, hidden, TN).astype(bf16)
    expand_grad = dot(expand_back, second_low, TN).astype(bf16)
    fed_own = dot(own_half(hidden), shrink_low, NT)
    fed_other = dot(other_half(hidden), shrink_low, NT).astype(bf16)
    second_other, shrink_grad, expand_grad, fed_own, fed_other = tie(
        second_other, shrink_grad, expand_grad, fed_own, fed_other
    )
    fed_other = swap(fed_other, "head", 1)
    layer_output = (own_half(middle) + fed_own + fed_other.astype(f32)).astype(bf16)

    moved = stepped(reduce_step, [reduce_start(x) for x in halves_of(expand_grad) + [shrink_grad]], 0)
    second_back = second_part + second_other.astype(f32)
    middle_grad = cotangent.astype(f32) + norm_back(
        second_back, norm_gains[1], second_normal, second_inverse
    )
    second_gain_grad = jnp.sum(own_half(second_back * second_normal), axis=0)
    middle_low = middle_grad.astype(bf16)
    attended_grad = [dot(mixer_low[:, bands[g]], middle_low, TT).astype(bf16) for g in range(GROUPS)]
    mixer_grad = jnp.concatenate(
        [lax.dot_general(middle_low, attended[g], TT_LEFT, preferred_element_type=f32) for g in range(GROUPS)],
        axis=1,
    ).astype(bf16)
    states, attended_grad, mixer_grad = tie(moved, attended_grad, mixer_grad)
    mixer_state = reduce_start(mixer_grad)
    grads = []
    for g in range(GROUPS):
        moved = stepped(reduce_step, states, 1 + g)
        mixer_moved = reduce_step(mixer_state, g, 2)
        part = attention_backward(
            low, high, *projected[g], attended_grad[g], attended[g], logsums[g], key_rows, query_rows
        )
        states, mixer_state, part, attended_grad = tie(moved, mixer_moved, part, attended_grad)
        grads.append(part)
    back_parts = [
        jnp.concatenate([unrotate(part[0], cosine, sine) for part in grads], axis=0),
        jnp.concatenate([unrotate(part[1], cosine, sine) for part in grads], axis=0),
        jnp.concatenate([part[2] for part in grads], axis=0),
    ]
    joined_back = jnp.concatenate(back_parts, axis=0).astype(bf16)
    step = 1 + GROUPS
    while step < bits:
        states = stepped(reduce_step, states, step)
        step += 1
    mixer_step = GROUPS
    while mixer_step + 1 < bits:
        mixer_state = reduce_step(mixer_state, mixer_step, 2)
        mixer_step += 1
    joined_grad = dot(joined_back, first_low, NN).astype(bf16)

    def first_part(start):
        columns = lax.dynamic_slice_in_dim(joined_back, start, local_rows, 1)
        return dot(columns, joined_low, TN)

    states, mixer_state, joined_grad, joined_back = tie(states, mixer_state, joined_grad, joined_back)
    expand_next = 0.5 * expand_momentum[0] + jnp.concatenate(states[:2], axis=1)
    shrink_next = 0.5 * shrink_momentum[0] + states[2]
    gathers = [gather_start(part) for part in halves_of(expand_next.astype(bf16))]
    gathers.append(gather_start(shrink_next.astype(bf16)))
    states = [reduce_start(part) for part in thirds(joined_grad)]
    first_other = swap(first_part((1 - head) * local_rows).astype(bf16), "head", 1)
    first_mine = first_part(head * local_rows)

    moved = stepped(reduce_step, states, 0)
    mixer_moved = reduce_step(mixer_state, mixer_step, 2)
    states, mixer_moved, first_other, first_mine = tie(moved, mixer_moved, first_other, first_mine)
    mixer_next = 0.5 * mixer_momentum[0] + mixer_moved
    mixer_gather = gather_start(mixer_next.astype(bf16))

    first_back = first_mine + first_other.astype(f32)
    own_normal = own_half(first_normal)
    input_gradient = own_half(middle_grad) + norm_back(
        first_back, norm_gains[0], own_normal, own_half(first_inverse)
    )
    first_gain_grad = jnp.sum(first_back * own_normal, axis=0)
    gain_totals = total_everywhere(jnp.stack([first_gain_grad, second_gain_grad]))

    for index in range(bits):
        if index + 1 < bits:
            states = stepped(reduce_step, states, index + 1)
        if index + 2 == bits:
            joined_next = 0.5 * joined_momentum[0] + jnp.concatenate(states, axis=1)
            states = [gather_start(part) for part in thirds(joined_next.astype(bf16))]
        if index + 1 == bits:
            states = stepped(gather_step, states, 0)
        gathers = stepped(gather_step, gathers, index)
        mixer_gather = gather_step(mixer_gather, index, 2)
        states, gathers, mixer_gather = tie(states, gathers, mixer_gather)
    for index in range(1, bits):
        states = stepped(gather_step, states, index)
    joined_full = jnp.concatenate([gather_rows(state) for state in states], axis=1)
    expand_full = jnp.concatenate([gather_rows(state) for state in gathers[:2]], axis=1)
    shrink_full = gather_rows(gathers[2])
    mixer_full = gather_rows(mixer_gather)
    dp_count = lax.axis_size("dp")
    updated = []
    for weight, own, gathered in (
        (joined_weight, joined_next, joined_full),
        (mixer_weight, mixer_next, mixer_full),
        (expand_weight, expand_next, expand_full),
        (shrink_weight, shrink_next, shrink_full),
    ):
        shape_scale = math.sqrt(own.shape[0] * dp_count / own.shape[1])
        updated.append((weight[0] - muon_rate * shape_scale * newton_schulz(own, gathered))[None])

    momentum_gains = 0.5 * gain_momentum + gain_totals
    updated_gains = norm_gains - gain_rate * momentum_gains * lax.rsqrt(
        jnp.mean(momentum_gains * momentum_gains, axis=-1, keepdims=True) + 1e-06
    )
    return (
        layer_output,
        input_gradient,
        joined_next[None],
        mixer_next[None],
        expand_next[None],
        shrink_next[None],
        updated[0],
        updated[1],
        updated[2],
        updated[3],
        momentum_gains,
        updated_gains,
    )


def solution(mesh):
    rows = P(("dp", "head"), None)
    weight = P("head", "dp", None)
    return jax.shard_map(
        shards,
        mesh=mesh,
        in_specs=(rows, P("dp", None), P()) + (weight,) * 8 + (P(), P("dp", None)),
        out_specs=(rows, rows) + (weight,) * 8 + (P(), P()),
        check_vma=False,
    )
```

```python
import functools
import math

import jax
import jax.numpy as jnp
from jax import lax
from jax.experimental import pallas as pl
from jax.experimental.pallas import tpu as pltpu
from jax.sharding import PartitionSpec as P

HEAD_DIM = 64
NS_ITERS = 3

theta_base = 160000.0
norm_epsilon = 1e-05
ns_first = 3.4445
ns_second = -4.775
ns_third = 2.0315
muon_rate = 1.0
gain_rate = 0.3

bf16 = jnp.bfloat16
f32 = jnp.float32
LOG2E = math.log2(math.e)
QUERY_SCALE = 0.125 * LOG2E
SAFE_SCORE = 60.0
DEPTH = 128
TILE_Q = 256
TILE_K = 256
FWD_SKEW = 6
BWD_SKEW = 2

NN = (((1,), (0,)), ((), ()))
NT = (((1,), (1,)), ((), ()))
TN = (((0,), (0,)), ((), ()))
TT = (((0,), (1,)), ((), ()))
QUARTERS = 4


def dot(left, right, dims):
    return lax.dot_general(left, right, dims, preferred_element_type=f32)


def key_bounds(length_row, row_count):
    ends = jnp.cumsum(length_row)
    starts = ends - length_row
    first = jnp.arange(row_count // TILE_Q, dtype=jnp.int32) * TILE_Q
    labels = jnp.arange(length_row.shape[0], dtype=jnp.int32)

    def pick(places, table):
        segment = jnp.sum((places[:, None] >= ends[None, :]).astype(jnp.int32), axis=1)
        return jnp.sum(jnp.where(segment[:, None] == labels[None, :], table[None, :], 0), axis=1)

    low = pick(first, starts) // TILE_K
    high = (pick(first + TILE_Q - 1, ends) + TILE_K - 1) // TILE_K
    return low.astype(jnp.int32), high.astype(jnp.int32)


def doc_tables(length_row, row_count):
    ends = jnp.cumsum(length_row)
    starts = ends - length_row
    count = length_row.shape[0]
    places = jnp.arange(row_count, dtype=jnp.int32)[None, :]
    member = (places >= starts[:, None]) & (places < ends[:, None])
    rest = jnp.zeros((16 - count, row_count), f32)
    key_rows = jnp.concatenate([member.astype(f32), rest], axis=0).astype(bf16)
    query_rows = jnp.concatenate([jnp.where(member, 0.0, -1e30), rest], axis=0).astype(bf16)
    doc_first = jnp.sum(jnp.where(member, starts[:, None], 0), axis=0, keepdims=True)
    position = (places - doc_first).astype(f32)
    half_dim = HEAD_DIM // 2
    frequency = jnp.exp(
        jnp.arange(half_dim, dtype=f32) * (-2.0 * math.log(theta_base) / HEAD_DIM)
    )
    angles = frequency[:, None] * position
    return key_rows, query_rows, jnp.cos(angles), jnp.sin(angles)


def rotate(values, cosine, sine):
    half = HEAD_DIM // 2
    heads = values.reshape(-1, HEAD_DIM, values.shape[1])
    low, high = heads[:, :half], heads[:, half:]
    turned = jnp.concatenate([low * cosine - high * sine, high * cosine + low * sine], axis=1)
    return turned.reshape(values.shape)


def unrotate(values, cosine, sine):
    return rotate(values, cosine, -sine)


def rows16(parts):
    rest = jnp.zeros((16 - len(parts), parts[0].shape[1]), f32)
    return jnp.concatenate([part.astype(f32) for part in parts] + [rest], axis=0).astype(bf16)


def split3(value):
    first = value.astype(bf16)
    left = value - first.astype(f32)
    second = left.astype(bf16)
    third = (left - second.astype(f32)).astype(bf16)
    return [first, second, third]


def three_ones(count):
    return jnp.concatenate([jnp.ones((3, count), f32), jnp.zeros((13, count), f32)], axis=0).astype(
        bf16
    )


def forward_kernel(
    low, high, queries, keys, values, key_rows, query_rows, out, logsum, keys_in, values_in, queries_in, safe
):
    heads = queries.shape[0] // HEAD_DIM
    rows = keys.shape[1]
    step = pl.program_id(0)

    @pl.when(step == 0)
    def _():
        worst = jnp.zeros((1, 1), f32)
        ones = rows16([jnp.ones((1, rows), f32)])
        for h in range(heads):
            band = slice(h * HEAD_DIM, (h + 1) * HEAD_DIM)
            key = keys[band, :]
            pad = jnp.zeros((DEPTH - HEAD_DIM - 16, rows), bf16)
            keys_in[h] = jnp.concatenate([key, key_rows[...], pad], axis=0).T
            values_in[h, :HEAD_DIM, :] = values[band, :]
            values_in[h, HEAD_DIM:, :] = ones
            query_full = queries[band, :].astype(f32)
            key_full = key.astype(f32)
            query_top = jnp.max(
                jnp.sum(query_full * query_full, axis=0, keepdims=True), axis=1, keepdims=True
            )
            key_top = jnp.max(
                jnp.sum(key_full * key_full, axis=0, keepdims=True), axis=1, keepdims=True
            )
            worst = jnp.maximum(worst, query_top * key_top)
        safe[0] = jnp.where(worst[0, 0] <= SAFE_SCORE * SAFE_SCORE, 1, 0)

    first = pl.multiple_of(step * TILE_Q, TILE_Q)
    for h in range(heads):
        queries_in[h, :HEAD_DIM, :] = queries[h * HEAD_DIM : (h + 1) * HEAD_DIM, pl.ds(first, TILE_Q)]
        queries_in[h, HEAD_DIM : HEAD_DIM + 16, :] = query_rows[...]
        queries_in[h, HEAD_DIM + 16 :, :] = jnp.zeros((DEPTH - HEAD_DIM - 16, TILE_Q), bf16)

    def finish(peaks, totals):
        for h in range(heads):
            weight = totals[h][HEAD_DIM : HEAD_DIM + 1, :]
            out[h * HEAD_DIM : (h + 1) * HEAD_DIM, :] = (totals[h][:HEAD_DIM, :] / weight).astype(bf16)
            level = jnp.log2(weight)
            logsum[h : h + 1, :] = level if peaks is None else peaks[h] + level

    empty = tuple(jnp.zeros((HEAD_DIM + 16, TILE_Q), f32) for _ in range(heads))

    @pl.when(safe[0] == 1)
    def _():
        def block(j, totals):
            span = pl.ds(pl.multiple_of(j * TILE_K, TILE_K), TILE_K)
            result = [None] * heads
            waiting = {}
            for t in range(heads + FWD_SKEW):
                if t < heads:
                    waiting[t] = dot(keys_in[t, span, :], queries_in[t], NN)
                h = t - FWD_SKEW
                if h >= 0:
                    raised = jnp.exp2(waiting.pop(h)).astype(bf16)
                    result[h] = totals[h] + dot(values_in[h, :, span], raised, NN)
            return tuple(result)

        finish(None, lax.fori_loop(low[step], high[step], block, empty))

    @pl.when(safe[0] == 0)
    def _():
        def block(j, carry):
            peaks, totals = carry
            span = pl.ds(pl.multiple_of(j * TILE_K, TILE_K), TILE_K)
            new_peaks = []
            new_totals = []
            for h in range(heads):
                scores = dot(keys_in[h, span, :], queries_in[h], NN)
                peak = jnp.maximum(peaks[h], jnp.max(scores, axis=0, keepdims=True))
                raised = jnp.exp2(scores - peak).astype(bf16)
                new_totals.append(
                    totals[h] * jnp.exp2(peaks[h] - peak) + dot(values_in[h, :, span], raised, NN)
                )
                new_peaks.append(peak)
            return tuple(new_peaks), tuple(new_totals)

        lowest = tuple(jnp.full((1, TILE_Q), -3e38, f32) for _ in range(heads))
        finish(*lax.fori_loop(low[step], high[step], block, (lowest, empty)))


def attention_forward(low, high, queries, keys, values, key_rows, query_rows):
    width, rows = queries.shape
    heads = width // HEAD_DIM

    def full(count):
        return pl.BlockSpec((count, rows), lambda i, low, high: (0, 0))

    def tile(count):
        return pl.BlockSpec((count, TILE_Q), lambda i, low, high: (0, i))

    return pl.pallas_call(
        forward_kernel,
        out_shape=(
            jax.ShapeDtypeStruct((width, rows), bf16),
            jax.ShapeDtypeStruct((heads, rows), f32),
        ),
        grid_spec=pltpu.PrefetchScalarGridSpec(
            num_scalar_prefetch=2,
            grid=(rows // TILE_Q,),
            in_specs=[full(width), full(width), full(width), full(16), tile(16)],
            out_specs=[tile(width), tile(heads)],
            scratch_shapes=[
                pltpu.VMEM((heads, rows, DEPTH), bf16),
                pltpu.VMEM((heads, HEAD_DIM + 16, rows), bf16),
                pltpu.VMEM((heads, DEPTH, TILE_Q), bf16),
                pltpu.SMEM((1,), jnp.int32),
            ],
        ),
        compiler_params=pltpu.CompilerParams(
            dimension_semantics=("arbitrary",), vmem_limit_bytes=40 << 20
        ),
        name="attention_forward",
    )(low, high, queries, keys, values, key_rows, query_rows)


def backward_kernel(
    low, high, queries, keys, values, grads, outs, logsum, key_rows, query_rows,
    query_grad, key_grad, value_grad, *scratch
):
    heads = queries.shape[0] // HEAD_DIM
    rows = keys.shape[1]
    keys_in, values_in, queries_in, grads_in = scratch[:4]
    key_sum = scratch[4 : 4 + heads]
    value_sum = scratch[4 + heads : 4 + 2 * heads]
    query_sum = scratch[4 + 2 * heads : 4 + 3 * heads]
    step = pl.program_id(0)

    @pl.when(step == 0)
    def _():
        ones = three_ones(rows)
        for h in range(heads):
            band = slice(h * HEAD_DIM, (h + 1) * HEAD_DIM)
            pad = jnp.zeros((DEPTH - HEAD_DIM - 32, rows), bf16)
            keys_in[h] = jnp.concatenate([keys[band, :], key_rows[...], ones, pad], axis=0).T
            pad = jnp.zeros((DEPTH - HEAD_DIM - 16, rows), bf16)
            values_in[h] = jnp.concatenate([values[band, :], ones, pad], axis=0).T
            key_sum[h][...] = jnp.zeros((HEAD_DIM, rows), f32)
            value_sum[h][...] = jnp.zeros((HEAD_DIM, rows), f32)

    for h in range(heads):
        band = slice(h * HEAD_DIM, (h + 1) * HEAD_DIM)
        queries_in[h, :HEAD_DIM, :] = queries[band, :]
        queries_in[h, HEAD_DIM : HEAD_DIM + 16, :] = query_rows[...]
        queries_in[h, HEAD_DIM + 16 : HEAD_DIM + 32, :] = rows16(split3(-logsum[h : h + 1, :]))
        queries_in[h, HEAD_DIM + 32 :, :] = jnp.zeros((DEPTH - HEAD_DIM - 32, TILE_Q), bf16)
        inner = jnp.sum(grads[band, :].astype(f32) * outs[band, :].astype(f32), axis=0, keepdims=True)
        grads_in[h, :HEAD_DIM, :] = grads[band, :]
        grads_in[h, HEAD_DIM : HEAD_DIM + 16, :] = rows16(split3(-inner))
        grads_in[h, HEAD_DIM + 16 :, :] = jnp.zeros((DEPTH - HEAD_DIM - 16, TILE_Q), bf16)
        query_sum[h][...] = jnp.zeros((HEAD_DIM, TILE_Q), f32)

    def block(j, carry):
        span = pl.ds(pl.multiple_of(j * TILE_K, TILE_K), TILE_K)
        waiting = {}
        for t in range(heads + BWD_SKEW):
            if t < heads:
                waiting[t] = (
                    dot(keys_in[t, span, :], queries_in[t], NN),
                    dot(values_in[t, span, :], grads_in[t], NN),
                )
            h = t - BWD_SKEW
            if h < 0:
                continue
            band = slice(h * HEAD_DIM, (h + 1) * HEAD_DIM)
            scores, weight_grad = waiting.pop(h)
            softmax = jnp.exp2(scores)
            score_grad = (softmax * weight_grad).astype(bf16)
            value_sum[h][:, span] += dot(grads[band, :], softmax.astype(bf16), NT)
            key_sum[h][:, span] += dot(queries[band, :], score_grad, NT)
            query_sum[h][...] += dot(keys[band, span], score_grad, NN)
        return carry

    lax.fori_loop(low[step], high[step], block, 0)
    for h in range(heads):
        query_grad[h * HEAD_DIM : (h + 1) * HEAD_DIM, :] = query_sum[h][...] * 0.125

    @pl.when(step == pl.num_programs(0) - 1)
    def _():
        for h in range(heads):
            band = slice(h * HEAD_DIM, (h + 1) * HEAD_DIM)
            key_grad[band, :] = key_sum[h][...] * (1.0 / LOG2E)
            value_grad[band, :] = value_sum[h][...]


def attention_backward(low, high, queries, keys, values, grads, outs, logsum, key_rows, query_rows):
    width, rows = queries.shape
    heads = width // HEAD_DIM

    def full(count):
        return pl.BlockSpec((count, rows), lambda i, low, high: (0, 0))

    def tile(count):
        return pl.BlockSpec((count, TILE_Q), lambda i, low, high: (0, i))

    result = jax.ShapeDtypeStruct((width, rows), f32)
    return pl.pallas_call(
        backward_kernel,
        out_shape=(result, result, result),
        grid_spec=pltpu.PrefetchScalarGridSpec(
            num_scalar_prefetch=2,
            grid=(rows // TILE_Q,),
            in_specs=[
                tile(width), full(width), full(width), tile(width), tile(width), tile(heads),
                full(16), tile(16),
            ],
            out_specs=[tile(width), full(width), full(width)],
            scratch_shapes=[
                pltpu.VMEM((heads, rows, DEPTH), bf16),
                pltpu.VMEM((heads, rows, DEPTH), bf16),
                pltpu.VMEM((heads, DEPTH, TILE_Q), bf16),
                pltpu.VMEM((heads, DEPTH, TILE_Q), bf16),
            ]
            + [pltpu.VMEM((HEAD_DIM, rows), f32)] * (2 * heads)
            + [pltpu.VMEM((HEAD_DIM, TILE_Q), f32)] * heads,
        ),
        compiler_params=pltpu.CompilerParams(
            dimension_semantics=("arbitrary",), vmem_limit_bytes=52 << 20
        ),
        name="attention_backward",
    )(low, high, queries, keys, values, grads, outs, logsum, key_rows, query_rows)


def swap(value, axis, bit):
    count = lax.axis_size(axis)
    return lax.ppermute(value, axis, [(i, i ^ bit) for i in range(count)])


def bit_orders():
    bits = lax.axis_size("dp").bit_length() - 1
    return [[(start + k) % (bits - 1) for k in range(bits - 1)] + [bits - 1] for start in range(3)]


def steps_count():
    return lax.axis_size("dp").bit_length() - 1


def reduce_start(value):
    bits = steps_count()
    rows = value.shape[0] >> bits
    return value.reshape((2,) * bits + (rows, value.shape[1]))


def reduce_step(held, step, which):
    bits = steps_count()
    bit = bit_orders()[which][step]
    axis = bits - 1 - bit
    side = (lax.axis_index("dp") >> bit) & 1
    kept = lax.dynamic_slice_in_dim(held, side, 1, axis)
    sent = lax.dynamic_slice_in_dim(held, 1 - side, 1, axis)
    total = kept.astype(f32) + swap(sent, "dp", 1 << bit).astype(f32)
    if step + 1 == bits:
        return total.reshape(held.shape[-2:])
    return total.astype(bf16)


def gather_start(value):
    return value[(None,) * steps_count()]


def gather_step(held, step, which):
    bits = steps_count()
    bit = bit_orders()[which][bits - 1 - step]
    return jnp.concatenate([held, swap(held, "dp", 1 << bit)], axis=bits - 1 - bit)


def ordered_step(held, step, which):
    bits = steps_count()
    bit = bit_orders()[which][bits - 1 - step]
    got = swap(held, "dp", 1 << bit)
    low_side = ((lax.axis_index("dp") >> bit) & 1) == 0
    return jnp.concatenate(
        [jnp.where(low_side, held, got), jnp.where(low_side, got, held)], axis=bits - 1 - bit
    )


def gather_rows(held):
    return held.reshape(-1, held.shape[-1])


def thirds(value):
    unit = value.shape[1] // 3 // 128 * 128
    return [value[:, :unit], value[:, unit : 2 * unit], value[:, 2 * unit :]]


def halves_of(value):
    unit = value.shape[1] // 256 * 128
    return [value[:, :unit], value[:, unit:]]


def quarter(step, states, part, first=0):
    bits = steps_count()
    for index in range(bits * part // QUARTERS, bits * (part + 1) // QUARTERS):
        states = [step(state, index, first + which) for which, state in enumerate(states)]
    return states


def tie(*values):
    return lax.optimization_barrier(values)


def total_step(value, part):
    if part == 0:
        return value + swap(value, "head", 1)
    bits = steps_count()
    for bit in range(bits * (part - 1) // QUARTERS, bits * part // QUARTERS):
        value = value + swap(value, "dp", 1 << bit)
    return value


def halves(own, other, head):
    first = jnp.where(head == 0, own, other)
    second = jnp.where(head == 0, other, own)
    return jnp.concatenate([first, second], axis=0)


def layer_norm(values, gain_row):
    centred = values - jnp.mean(values, axis=-1, keepdims=True)
    inverse = lax.rsqrt(jnp.mean(centred * centred, axis=-1, keepdims=True) + norm_epsilon)
    normal = centred * inverse
    return normal * gain_row, normal, inverse


def norm_back(upstream, gain_row, normal, inverse):
    scaled = upstream * gain_row
    inner_mean = jnp.mean(scaled * normal, axis=-1, keepdims=True)
    return inverse * (scaled - jnp.mean(scaled, axis=-1, keepdims=True) - normal * inner_mean)


def gated(active_in, linear_in):
    return jax.nn.gelu(active_in, approximate=False) * linear_in


def schulz_start(own, gathered):
    gram = dot(gathered, gathered, TN)
    norm_value = jnp.sqrt(jnp.trace(gram)) + 1e-07
    return own / norm_value, gram / (norm_value * norm_value)


def schulz_step(state, last=False):
    rows, gram = state
    low_gram = gram.astype(bf16)
    change = (ns_second * gram + ns_third * dot(low_gram, low_gram, NN)).astype(bf16)
    rows = ns_first * rows + dot(rows.astype(bf16), change, NN)
    if last:
        return rows
    once = ns_first * gram + dot(low_gram, change, NN)
    return rows, ns_first * once + dot(once.astype(bf16), change, NN)


def schulz_rest(state):
    for iteration in range(NS_ITERS):
        state = schulz_step(state, iteration + 1 == NS_ITERS)
    return state


def shards(
    tokens,
    lengths,
    norm_gains,
    joined_weight,
    mixer_weight,
    expand_weight,
    shrink_weight,
    joined_momentum,
    mixer_momentum,
    expand_momentum,
    shrink_momentum,
    gain_momentum,
    cotangent,
):
    row_count = cotangent.shape[0]
    local_rows = tokens.shape[0]
    head = lax.axis_index("head")
    mixer_width = mixer_weight.shape[2]

    def own_half(value):
        return lax.dynamic_slice_in_dim(value, head * local_rows, local_rows, 0)

    def other_half(value):
        return lax.dynamic_slice_in_dim(value, (1 - head) * local_rows, local_rows, 0)

    joined_parts = [gather_start(part) for part in thirds(joined_weight[0].astype(bf16))]
    joined_parts = quarter(ordered_step, joined_parts, 0)
    others = [gather_start(part) for part in halves_of(expand_weight[0].astype(bf16))] + [
        gather_start(jnp.concatenate([mixer_weight[0], shrink_weight[0]], axis=1).astype(bf16))
    ]
    key_rows, query_rows, cosine, sine = doc_tables(lengths[0], row_count)
    low, high = key_bounds(lengths[0], row_count)
    residual = halves(tokens, swap(tokens, "head", 1), head).astype(f32)
    first_normed, first_normal, first_inverse = layer_norm(residual, norm_gains[0])
    first_low = first_normed.astype(bf16)

    joined_parts, others = tie(joined_parts, others)
    joined_parts = quarter(ordered_step, joined_parts, 1)
    others = quarter(ordered_step, others, 0)
    joined_parts, others = tie(joined_parts, others)
    joined_parts = quarter(ordered_step, joined_parts, 2)
    moved = quarter(ordered_step, others, 1)
    joined_parts, first_low = tie(joined_parts, first_low)
    joined_parts = quarter(ordered_step, joined_parts, 3)
    joined_parts, others = tie(joined_parts, moved)

    moved = quarter(ordered_step, others, 2)
    joined_low = jnp.concatenate([gather_rows(part) for part in joined_parts], axis=1)
    joined = dot(joined_low, first_low, NT)
    width = joined.shape[0] // 3
    queries = (rotate(joined[:width], cosine, sine) * QUERY_SCALE).astype(bf16)
    keys = rotate(joined[width : 2 * width], cosine, sine).astype(bf16)
    values = joined[2 * width :].astype(bf16)
    others, queries, keys, values, low = tie(moved, queries, keys, values, low)
    moved = quarter(ordered_step, others, 3)
    attended, logsum = attention_forward(low, high, queries, keys, values, key_rows, query_rows)
    others, attended, logsum = tie(moved, attended, logsum)
    attended_other = swap(attended, "head", 1)
    expand_low = jnp.concatenate([gather_rows(part) for part in others[:2]], axis=1)
    both_low = gather_rows(others[2])
    mixer_low, shrink_low = both_low[:, :mixer_width], both_low[:, mixer_width:]
    mixer_other = swap(mixer_low, "head", 1)

    middle = residual + dot(attended, mixer_low, TT) + dot(attended_other, mixer_other, TT)
    second_normed, second_normal, second_inverse = layer_norm(middle, norm_gains[1])
    second_low = second_normed.astype(bf16)

    expanded = dot(second_low, expand_low, NT)
    hidden_width = expanded.shape[1] // 2
    activated, linear_part = expanded[:, :hidden_width], expanded[:, hidden_width:]
    hidden = gated(activated, linear_part).astype(bf16)

    hidden_grad = dot(cotangent, shrink_low, NN)
    unused, gate_pull = jax.vjp(gated, activated, linear_part)
    active_grad, linear_grad = gate_pull(hidden_grad)
    expand_back = jnp.concatenate([active_grad, linear_grad], axis=1).astype(bf16)
    second_part = dot(expand_back, expand_low, NN)
    second_other = swap(second_part.astype(bf16), "head", 1)
    shrink_grad = dot(cotangent, hidden, TN).astype(bf16)
    expand_grad = dot(expand_back, second_low, TN).astype(bf16)

    sums, second_other = tie(
        [reduce_start(part) for part in halves_of(expand_grad) + [shrink_grad]], second_other
    )
    moved = quarter(reduce_step, sums, 0)
    second_back = second_part + second_other.astype(f32)
    middle_grad = cotangent.astype(f32) + norm_back(
        second_back, norm_gains[1], second_normal, second_inverse
    )
    middle_low = middle_grad.astype(bf16)
    attended_grad = dot(mixer_low, middle_low, TT).astype(bf16)

    sums, attended_grad, middle_low = tie(moved, attended_grad, middle_low)
    moved = quarter(reduce_step, sums, 1)
    mixer_grad = lax.dot_general(
        middle_low, attended, (((0,), (1,)), ((), ())), preferred_element_type=f32
    ).astype(bf16)
    second_gain_grad = jnp.sum(own_half(second_back * second_normal), axis=0)

    sums, mixer_grad, second_gain_grad, shrink_now = tie(
        moved, mixer_grad, second_gain_grad, shrink_low
    )
    moved = quarter(reduce_step, sums, 2)
    mixer_moved = quarter(reduce_step, [reduce_start(mixer_grad)], 0, 2)
    fed_own = dot(own_half(hidden), shrink_now, NT)
    fed_other = dot(other_half(hidden), shrink_now, NT).astype(bf16)

    sums, mixer_sum, fed_other, low = tie(moved, mixer_moved, fed_other, low)
    moved = quarter(reduce_step, sums, 3)
    mixer_moved = quarter(reduce_step, mixer_sum, 1, 2)
    fed_other = swap(fed_other, "head", 1)
    query_grad, key_grad, value_grad = attention_backward(
        low, high, queries, keys, values, attended_grad, attended, logsum, key_rows, query_rows
    )
    sums, mixer_sum, query_grad, key_grad, value_grad = tie(
        moved, mixer_moved, query_grad, key_grad, value_grad
    )
    expand_next = 0.5 * expand_momentum[0] + jnp.concatenate(sums[:2], axis=1)
    shrink_next = 0.5 * shrink_momentum[0] + sums[2]
    gathers = [gather_start(part) for part in halves_of(expand_next.astype(bf16))]
    gathers.append(gather_start(shrink_next.astype(bf16)))

    moved = quarter(gather_step, gathers, 0)
    mixer_moved = quarter(reduce_step, mixer_sum, 2, 2)
    joined_back = jnp.concatenate(
        [unrotate(query_grad, cosine, sine), unrotate(key_grad, cosine, sine), value_grad], axis=0
    ).astype(bf16)
    joined_grad = dot(joined_back, first_low, NN).astype(bf16)

    def first_part(start, weight):
        columns = lax.dynamic_slice_in_dim(joined_back, start, local_rows, 1)
        return dot(columns, weight, TN)

    gathers, mixer_sum, joined_grad, joined_now = tie(moved, mixer_moved, joined_grad, joined_low)
    sums = quarter(reduce_step, [reduce_start(part) for part in thirds(joined_grad)], 0)
    moved = quarter(gather_step, gathers, 1)
    mixer_moved = quarter(reduce_step, mixer_sum, 3, 2)
    first_other = swap(
        first_part((1 - head) * local_rows, joined_now).astype(bf16), "head", 1
    )
    first_mine = first_part(head * local_rows, joined_now)
    layer_output = (own_half(middle) + fed_own + fed_other.astype(f32)).astype(bf16)

    sums, gathers, mixer_sum, first_other, first_mine = tie(
        sums, moved, mixer_moved, first_other, first_mine
    )
    mixer_next = 0.5 * mixer_momentum[0] + mixer_sum[0]
    moved = quarter(reduce_step, sums, 1)
    gathers_moved = quarter(gather_step, gathers, 2)
    first_back = first_mine + first_other.astype(f32)
    own_normal = own_half(first_normal)
    first_gain_grad = jnp.sum(first_back * own_normal, axis=0)

    sums, gathers, first_gain_grad, first_gain = tie(
        moved, gathers_moved, first_gain_grad, norm_gains[0]
    )
    moved = quarter(reduce_step, sums, 2)
    gathers_moved = quarter(gather_step, gathers, 3)
    input_gradient = own_half(middle_grad) + norm_back(
        first_back, first_gain, own_normal, own_half(first_inverse)
    )

    sums, gathers, input_gradient = tie(moved, gathers_moved, input_gradient)
    mixer_gather = [gather_start(mixer_next.astype(bf16))]
    gain_totals = jnp.stack([first_gain_grad, second_gain_grad])
    expand_full = jnp.concatenate([gather_rows(state) for state in gathers[:2]], axis=1)
    shrink_full = gather_rows(gathers[2])

    moved = quarter(reduce_step, sums, 3)
    mixer_moved = quarter(gather_step, mixer_gather, 0, 2)
    gain_moved = total_step(gain_totals, 0)
    shrink_state = schulz_step(schulz_start(shrink_next, shrink_full))
    sums, mixer_gather, gain_totals, shrink_state, expand_full = tie(
        moved, mixer_moved, gain_moved, shrink_state, expand_full
    )
    joined_next = 0.5 * joined_momentum[0] + jnp.concatenate(sums, axis=1)
    joined_gather = [gather_start(part) for part in thirds(joined_next.astype(bf16))]

    moved = quarter(gather_step, joined_gather, 0)
    mixer_moved = quarter(gather_step, mixer_gather, 1, 2)
    gain_moved = total_step(gain_totals, 1)
    shrink_rows = schulz_step(schulz_step(shrink_state), True)
    expand_state = schulz_start(expand_next, expand_full)
    joined_gather, mixer_gather, gain_totals, shrink_rows, expand_state = tie(
        moved, mixer_moved, gain_moved, shrink_rows, expand_state
    )

    moved = quarter(gather_step, joined_gather, 1)
    mixer_moved = quarter(gather_step, mixer_gather, 2, 2)
    gain_moved = total_step(gain_totals, 2)
    expand_state = schulz_step(expand_state)
    joined_gather, mixer_gather, gain_totals, expand_state = tie(
        moved, mixer_moved, gain_moved, expand_state
    )

    moved = quarter(gather_step, joined_gather, 2)
    mixer_moved = quarter(gather_step, mixer_gather, 3, 2)
    gain_moved = total_step(gain_totals, 3)
    expand_rows = schulz_step(schulz_step(expand_state), True)
    joined_gather, mixer_gather, gain_totals, expand_rows = tie(
        moved, mixer_moved, gain_moved, expand_rows
    )

    moved = quarter(gather_step, joined_gather, 3)
    gain_totals = total_step(gain_totals, 4)
    mixer_rows = schulz_rest(schulz_start(mixer_next, gather_rows(mixer_gather[0])))
    joined_gather, mixer_rows = tie(moved, mixer_rows)
    joined_full = jnp.concatenate([gather_rows(state) for state in joined_gather], axis=1)
    joined_rows = schulz_rest(schulz_start(joined_next, joined_full))

    dp_count = lax.axis_size("dp")
    updated = []
    for weight, rows in (
        (joined_weight, joined_rows),
        (mixer_weight, mixer_rows),
        (expand_weight, expand_rows),
        (shrink_weight, shrink_rows),
    ):
        shape_scale = math.sqrt(rows.shape[0] * dp_count / rows.shape[1])
        updated.append((weight[0] - muon_rate * shape_scale * rows)[None])

    momentum_gains = 0.5 * gain_momentum + gain_totals
    updated_gains = norm_gains - gain_rate * momentum_gains * lax.rsqrt(
        jnp.mean(momentum_gains * momentum_gains, axis=-1, keepdims=True) + 1e-06
    )
    return (
        layer_output,
        input_gradient,
        joined_next[None],
        mixer_next[None],
        expand_next[None],
        shrink_next[None],
        updated[0],
        updated[1],
        updated[2],
        updated[3],
        momentum_gains,
        updated_gains,
    )


def solution(mesh):
    rows = P(("dp", "head"), None)
    weight = P("head", "dp", None)
    return jax.shard_map(
        shards,
        mesh=mesh,
        in_specs=(rows, P("dp", None), P()) + (weight,) * 8 + (P(), P("dp", None)),
        out_specs=(rows, rows) + (weight,) * 8 + (P(), P()),
        check_vma=False,
    )
```

```python
import functools
import math

import jax
import jax.numpy as jnp
from jax import lax
from jax.experimental import pallas as pl
from jax.experimental.pallas import tpu as pltpu
from jax.sharding import PartitionSpec as P

HEAD_DIM = 64
NS_ITERS = 3

theta_base = 160000.0
norm_epsilon = 1e-05
ns_first = 3.4445
ns_second = -4.775
ns_third = 2.0315
muon_rate = 1.0
gain_rate = 0.3

bf16 = jnp.bfloat16
f32 = jnp.float32
LOG2E = math.log2(math.e)
QUERY_SCALE = 0.125 * LOG2E
SAFE_SCORE = 60.0
DEPTH = 128
TILE_Q = 256
TILE_K = 256
FWD_SKEW = 6
BWD_SKEW = 2

NN = (((1,), (0,)), ((), ()))
NT = (((1,), (1,)), ((), ()))
TN = (((0,), (0,)), ((), ()))
TT = (((0,), (1,)), ((), ()))
QUARTERS = 4
FEED_ROWS = 256
FEED_CHUNKS = 3
ERF_TOP = (
    -2.72614225801306e-10, 2.77068142495902e-08, -2.10102402082508e-06, -5.69250639462346e-05,
    -7.34990630326855e-04, -2.95459980854025e-03, -1.60960333262415e-02,
)
ERF_BOTTOM = (
    -1.45660718464996e-05, -2.13374055278905e-04, -1.68282697438203e-03, -7.37332916720468e-03,
    -1.42647390514189e-02,
)


def dot(left, right, dims):
    return lax.dot_general(left, right, dims, preferred_element_type=f32)


def key_bounds(length_row, row_count):
    ends = jnp.cumsum(length_row)
    starts = ends - length_row
    first = jnp.arange(row_count // TILE_Q, dtype=jnp.int32) * TILE_Q
    labels = jnp.arange(length_row.shape[0], dtype=jnp.int32)

    def pick(places, table):
        segment = jnp.sum((places[:, None] >= ends[None, :]).astype(jnp.int32), axis=1)
        return jnp.sum(jnp.where(segment[:, None] == labels[None, :], table[None, :], 0), axis=1)

    low = pick(first, starts) // TILE_K
    high = (pick(first + TILE_Q - 1, ends) + TILE_K - 1) // TILE_K
    return low.astype(jnp.int32), high.astype(jnp.int32)


def doc_tables(length_row, row_count):
    ends = jnp.cumsum(length_row)
    starts = ends - length_row
    count = length_row.shape[0]
    places = jnp.arange(row_count, dtype=jnp.int32)[None, :]
    member = (places >= starts[:, None]) & (places < ends[:, None])
    rest = jnp.zeros((16 - count, row_count), f32)
    key_rows = jnp.concatenate([member.astype(f32), rest], axis=0).astype(bf16)
    query_rows = jnp.concatenate([jnp.where(member, 0.0, -1e30), rest], axis=0).astype(bf16)
    doc_first = jnp.sum(jnp.where(member, starts[:, None], 0), axis=0, keepdims=True)
    position = (places - doc_first).astype(f32)
    half_dim = HEAD_DIM // 2
    frequency = jnp.exp(
        jnp.arange(half_dim, dtype=f32) * (-2.0 * math.log(theta_base) / HEAD_DIM)
    )
    angles = frequency[:, None] * position
    return key_rows, query_rows, jnp.cos(angles), jnp.sin(angles)


def rotate(values, cosine, sine):
    half = HEAD_DIM // 2
    heads = values.reshape(-1, HEAD_DIM, values.shape[1])
    low, high = heads[:, :half], heads[:, half:]
    turned = jnp.concatenate([low * cosine - high * sine, high * cosine + low * sine], axis=1)
    return turned.reshape(values.shape)


def rows16(parts):
    rest = jnp.zeros((16 - len(parts), parts[0].shape[1]), f32)
    return jnp.concatenate([part.astype(f32) for part in parts] + [rest], axis=0).astype(bf16)


def split3(value):
    first = value.astype(bf16)
    left = value - first.astype(f32)
    second = left.astype(bf16)
    third = (left - second.astype(f32)).astype(bf16)
    return [first, second, third]


def three_ones(count):
    return jnp.concatenate([jnp.ones((3, count), f32), jnp.zeros((13, count), f32)], axis=0).astype(
        bf16
    )


def forward_kernel(
    low, high, queries, keys, values, key_rows, query_rows, out, logsum, keys_in, values_in, queries_in, safe
):
    heads = queries.shape[0] // HEAD_DIM
    rows = keys.shape[1]
    step = pl.program_id(0)

    @pl.when(step == 0)
    def _():
        worst = jnp.zeros((1, 1), f32)
        ones = rows16([jnp.ones((1, rows), f32)])
        for h in range(heads):
            band = slice(h * HEAD_DIM, (h + 1) * HEAD_DIM)
            key = keys[band, :]
            pad = jnp.zeros((DEPTH - HEAD_DIM - 16, rows), bf16)
            keys_in[h] = jnp.concatenate([key, key_rows[...], pad], axis=0).T
            values_in[h, :HEAD_DIM, :] = values[band, :]
            values_in[h, HEAD_DIM:, :] = ones
            query_full = queries[band, :].astype(f32)
            key_full = key.astype(f32)
            query_top = jnp.max(
                jnp.sum(query_full * query_full, axis=0, keepdims=True), axis=1, keepdims=True
            )
            key_top = jnp.max(
                jnp.sum(key_full * key_full, axis=0, keepdims=True), axis=1, keepdims=True
            )
            worst = jnp.maximum(worst, query_top * key_top)
        safe[0] = jnp.where(worst[0, 0] <= SAFE_SCORE * SAFE_SCORE, 1, 0)

    first = pl.multiple_of(step * TILE_Q, TILE_Q)
    for h in range(heads):
        queries_in[h, :HEAD_DIM, :] = queries[h * HEAD_DIM : (h + 1) * HEAD_DIM, pl.ds(first, TILE_Q)]
        queries_in[h, HEAD_DIM : HEAD_DIM + 16, :] = query_rows[...]
        queries_in[h, HEAD_DIM + 16 :, :] = jnp.zeros((DEPTH - HEAD_DIM - 16, TILE_Q), bf16)

    def finish(peaks, totals):
        for h in range(heads):
            weight = totals[h][HEAD_DIM : HEAD_DIM + 1, :]
            out[h * HEAD_DIM : (h + 1) * HEAD_DIM, :] = (totals[h][:HEAD_DIM, :] / weight).astype(bf16)
            level = jnp.log2(weight)
            logsum[h : h + 1, :] = level if peaks is None else peaks[h] + level

    empty = tuple(jnp.zeros((HEAD_DIM + 16, TILE_Q), f32) for _ in range(heads))

    @pl.when(safe[0] == 1)
    def _():
        def block(j, totals):
            span = pl.ds(pl.multiple_of(j * TILE_K, TILE_K), TILE_K)
            result = [None] * heads
            waiting = {}
            for t in range(heads + FWD_SKEW):
                if t < heads:
                    waiting[t] = dot(keys_in[t, span, :], queries_in[t], NN)
                h = t - FWD_SKEW
                if h >= 0:
                    raised = jnp.exp2(waiting.pop(h)).astype(bf16)
                    result[h] = totals[h] + dot(values_in[h, :, span], raised, NN)
            return tuple(result)

        finish(None, lax.fori_loop(low[step], high[step], block, empty))

    @pl.when(safe[0] == 0)
    def _():
        def block(j, carry):
            peaks, totals = carry
            span = pl.ds(pl.multiple_of(j * TILE_K, TILE_K), TILE_K)
            new_peaks = []
            new_totals = []
            for h in range(heads):
                scores = dot(keys_in[h, span, :], queries_in[h], NN)
                peak = jnp.maximum(peaks[h], jnp.max(scores, axis=0, keepdims=True))
                raised = jnp.exp2(scores - peak).astype(bf16)
                new_totals.append(
                    totals[h] * jnp.exp2(peaks[h] - peak) + dot(values_in[h, :, span], raised, NN)
                )
                new_peaks.append(peak)
            return tuple(new_peaks), tuple(new_totals)

        lowest = tuple(jnp.full((1, TILE_Q), -3e38, f32) for _ in range(heads))
        finish(*lax.fori_loop(low[step], high[step], block, (lowest, empty)))


def attention_forward(low, high, queries, keys, values, key_rows, query_rows):
    width, rows = queries.shape
    heads = width // HEAD_DIM

    def full(count):
        return pl.BlockSpec((count, rows), lambda i, low, high: (0, 0))

    def tile(count):
        return pl.BlockSpec((count, TILE_Q), lambda i, low, high: (0, i))

    return pl.pallas_call(
        forward_kernel,
        out_shape=(
            jax.ShapeDtypeStruct((width, rows), bf16),
            jax.ShapeDtypeStruct((heads, rows), f32),
        ),
        grid_spec=pltpu.PrefetchScalarGridSpec(
            num_scalar_prefetch=2,
            grid=(rows // TILE_Q,),
            in_specs=[full(width), full(width), full(width), full(16), tile(16)],
            out_specs=[tile(width), tile(heads)],
            scratch_shapes=[
                pltpu.VMEM((heads, rows, DEPTH), bf16),
                pltpu.VMEM((heads, HEAD_DIM + 16, rows), bf16),
                pltpu.VMEM((heads, DEPTH, TILE_Q), bf16),
                pltpu.SMEM((1,), jnp.int32),
            ],
        ),
        compiler_params=pltpu.CompilerParams(
            dimension_semantics=("arbitrary",), vmem_limit_bytes=40 << 20
        ),
        name="attention_forward",
    )(low, high, queries, keys, values, key_rows, query_rows)


def backward_kernel(
    low, high, queries, keys, values, grads, outs, logsum, key_rows, query_rows, cosine, sine,
    joined_back, *scratch
):
    heads = queries.shape[0] // HEAD_DIM
    rows = keys.shape[1]
    keys_in, values_in, queries_in, grads_in = scratch[:4]
    key_sum = scratch[4 : 4 + heads]
    value_sum = scratch[4 + heads : 4 + 2 * heads]
    query_sum = scratch[4 + 2 * heads : 4 + 3 * heads]
    step = pl.program_id(0)

    @pl.when(step == 0)
    def _():
        ones = three_ones(rows)
        for h in range(heads):
            band = slice(h * HEAD_DIM, (h + 1) * HEAD_DIM)
            pad = jnp.zeros((DEPTH - HEAD_DIM - 32, rows), bf16)
            keys_in[h] = jnp.concatenate([keys[band, :], key_rows[...], ones, pad], axis=0).T
            pad = jnp.zeros((DEPTH - HEAD_DIM - 16, rows), bf16)
            values_in[h] = jnp.concatenate([values[band, :], ones, pad], axis=0).T
            key_sum[h][...] = jnp.zeros((HEAD_DIM, rows), f32)
            value_sum[h][...] = jnp.zeros((HEAD_DIM, rows), f32)

    for h in range(heads):
        band = slice(h * HEAD_DIM, (h + 1) * HEAD_DIM)
        queries_in[h, :HEAD_DIM, :] = queries[band, :]
        queries_in[h, HEAD_DIM : HEAD_DIM + 16, :] = query_rows[...]
        queries_in[h, HEAD_DIM + 16 : HEAD_DIM + 32, :] = rows16(split3(-logsum[h : h + 1, :]))
        queries_in[h, HEAD_DIM + 32 :, :] = jnp.zeros((DEPTH - HEAD_DIM - 32, TILE_Q), bf16)
        inner = jnp.sum(grads[band, :].astype(f32) * outs[band, :].astype(f32), axis=0, keepdims=True)
        grads_in[h, :HEAD_DIM, :] = grads[band, :]
        grads_in[h, HEAD_DIM : HEAD_DIM + 16, :] = rows16(split3(-inner))
        grads_in[h, HEAD_DIM + 16 :, :] = jnp.zeros((DEPTH - HEAD_DIM - 16, TILE_Q), bf16)
        query_sum[h][...] = jnp.zeros((HEAD_DIM, TILE_Q), f32)

    def block(j, carry):
        span = pl.ds(pl.multiple_of(j * TILE_K, TILE_K), TILE_K)
        waiting = {}
        for t in range(heads + BWD_SKEW):
            if t < heads:
                waiting[t] = (
                    dot(keys_in[t, span, :], queries_in[t], NN),
                    dot(values_in[t, span, :], grads_in[t], NN),
                )
            h = t - BWD_SKEW
            if h < 0:
                continue
            band = slice(h * HEAD_DIM, (h + 1) * HEAD_DIM)
            scores, weight_grad = waiting.pop(h)
            softmax = jnp.exp2(scores)
            score_grad = (softmax * weight_grad).astype(bf16)
            value_sum[h][:, span] += dot(grads[band, :], softmax.astype(bf16), NT)
            key_sum[h][:, span] += dot(queries[band, :], score_grad, NT)
            query_sum[h][...] += dot(keys[band, span], score_grad, NN)
        return carry

    lax.fori_loop(low[step], high[step], block, 0)

    def store(offset, columns, value):
        half = HEAD_DIM // 2
        upper, lower = value[:half], value[half:]
        cos, sin = cosine[:, columns], sine[:, columns]
        joined_back[offset : offset + half, columns] = (upper * cos + lower * sin).astype(bf16)
        joined_back[offset + half : offset + HEAD_DIM, columns] = (lower * cos - upper * sin).astype(bf16)

    width = heads * HEAD_DIM
    columns = pl.ds(pl.multiple_of(step * TILE_Q, TILE_Q), TILE_Q)
    for h in range(heads):
        store(h * HEAD_DIM, columns, query_sum[h][...] * 0.125)

    @pl.when(step == pl.num_programs(0) - 1)
    def _():
        for h in range(heads):
            first = width + h * HEAD_DIM
            store(first, slice(0, rows), key_sum[h][...] * (1.0 / LOG2E))
            first += width
            joined_back[first : first + HEAD_DIM, :] = value_sum[h][...].astype(bf16)


def attention_backward(
    low, high, queries, keys, values, grads, outs, logsum, key_rows, query_rows, cosine, sine
):
    width, rows = queries.shape
    heads = width // HEAD_DIM

    def full(count):
        return pl.BlockSpec((count, rows), lambda i, low, high: (0, 0))

    def tile(count):
        return pl.BlockSpec((count, TILE_Q), lambda i, low, high: (0, i))

    return pl.pallas_call(
        backward_kernel,
        out_shape=jax.ShapeDtypeStruct((3 * width, rows), bf16),
        grid_spec=pltpu.PrefetchScalarGridSpec(
            num_scalar_prefetch=2,
            grid=(rows // TILE_Q,),
            in_specs=[
                tile(width), full(width), full(width), tile(width), tile(width), tile(heads),
                full(16), tile(16), full(HEAD_DIM // 2), full(HEAD_DIM // 2),
            ],
            out_specs=full(3 * width),
            scratch_shapes=[
                pltpu.VMEM((heads, rows, DEPTH), bf16),
                pltpu.VMEM((heads, rows, DEPTH), bf16),
                pltpu.VMEM((heads, DEPTH, TILE_Q), bf16),
                pltpu.VMEM((heads, DEPTH, TILE_Q), bf16),
            ]
            + [pltpu.VMEM((HEAD_DIM, rows), f32)] * (2 * heads)
            + [pltpu.VMEM((HEAD_DIM, TILE_Q), f32)] * heads,
        ),
        compiler_params=pltpu.CompilerParams(
            dimension_semantics=("arbitrary",), vmem_limit_bytes=52 << 20
        ),
        name="attention_backward",
    )(low, high, queries, keys, values, grads, outs, logsum, key_rows, query_rows, cosine, sine)


def layer_norm(values, gain_row):
    centred = values - jnp.mean(values, axis=-1, keepdims=True)
    inverse = lax.rsqrt(jnp.mean(centred * centred, axis=-1, keepdims=True) + norm_epsilon)
    normal = centred * inverse
    return normal * gain_row, normal, inverse


def norm_back(upstream, gain_row, normal, inverse):
    scaled = upstream * gain_row
    inner_mean = jnp.mean(scaled * normal, axis=-1, keepdims=True)
    return inverse * (scaled - jnp.mean(scaled, axis=-1, keepdims=True) - normal * inner_mean)


def horner(square, factors):
    total = factors[0] * square + factors[1]
    for factor in factors[2:]:
        total = total * square + factor
    return total


def error_function(value):
    value = jnp.clip(value, -4.0, 4.0)
    square = value * value
    return value * horner(square, ERF_TOP) / horner(square, ERF_BOTTOM)


def feed_kernel(
    rows, attended, attended_other, upstream, gain, mixer, mixer_other, expand, shrink,
    middle, hidden, second_part, shrink_grad, expand_grad, shrink_sum, expand_sum
):
    step = pl.program_id(0)
    units = shrink.shape[0]
    chunk = units // FEED_CHUNKS

    @pl.when(step == 0)
    def _():
        shrink_sum[...] = jnp.zeros(shrink_sum.shape, f32)
        expand_sum[...] = jnp.zeros(expand_sum.shape, f32)

    total = rows[...].astype(f32) + dot(attended[...].T, mixer[...], NT)
    total = total + dot(attended_other[...].T, mixer_other[...], NT)
    middle[...] = total
    normed = layer_norm(total, gain[...])[0].astype(bf16)
    above = upstream[...]

    def project(c):
        first = slice(c * chunk, (c + 1) * chunk)
        second = slice(units + c * chunk, units + (c + 1) * chunk)
        return (
            dot(expand[first, :], normed, NT),
            dot(expand[second, :], normed, NT),
            dot(shrink[first, :], above, NT),
        )

    waiting = project(0)
    back = jnp.zeros(total.shape, f32)
    for c in range(FEED_CHUNKS):
        active, linear, grad = waiting
        if c + 1 < FEED_CHUNKS:
            waiting = project(c + 1)
        first = slice(c * chunk, (c + 1) * chunk)
        second = slice(units + c * chunk, units + (c + 1) * chunk)
        area = 0.5 * error_function(active * math.sqrt(0.5)) + 0.5
        gate = active * area
        density = jnp.exp(-0.5 * active * active) * (1.0 / math.sqrt(2.0 * math.pi))
        unit = (gate * linear).astype(bf16)
        active_back = (grad * linear * (area + active * density)).astype(bf16)
        linear_back = (grad * gate).astype(bf16)
        hidden[first, :] = unit
        shrink_sum[first, :] += dot(unit, above, NN)
        expand_sum[first, :] += dot(active_back, normed, NN)
        expand_sum[second, :] += dot(linear_back, normed, NN)
        back = back + dot(active_back, expand[first, :], TN) + dot(linear_back, expand[second, :], TN)
    second_part[...] = back.astype(bf16)

    @pl.when(step == pl.num_programs(0) - 1)
    def _():
        shrink_grad[...] = shrink_sum[...].astype(bf16)
        expand_grad[...] = expand_sum[...].astype(bf16)


def feed_forward(rows, attended, attended_other, upstream, gain, mixer, mixer_other, expand, shrink):
    count, width = rows.shape
    mixed, units = attended.shape[0], shrink.shape[0]

    def full(*shape):
        return pl.BlockSpec(shape, lambda i: (0, 0))

    def down(columns):
        return pl.BlockSpec((FEED_ROWS, columns), lambda i: (i, 0))

    def along(lines):
        return pl.BlockSpec((lines, FEED_ROWS), lambda i: (0, i))

    return pl.pallas_call(
        feed_kernel,
        grid=(count // FEED_ROWS,),
        in_specs=[
            down(width), along(mixed), along(mixed), down(width), full(1, width),
            full(width, mixed), full(width, mixed), full(2 * units, width), full(units, width),
        ],
        out_specs=[
            down(width), along(units), down(width), full(units, width), full(2 * units, width),
        ],
        out_shape=(
            jax.ShapeDtypeStruct((count, width), f32),
            jax.ShapeDtypeStruct((units, count), bf16),
            jax.ShapeDtypeStruct((count, width), bf16),
            jax.ShapeDtypeStruct((units, width), bf16),
            jax.ShapeDtypeStruct((2 * units, width), bf16),
        ),
        scratch_shapes=[pltpu.VMEM((units, width), f32), pltpu.VMEM((2 * units, width), f32)],
        compiler_params=pltpu.CompilerParams(
            dimension_semantics=("arbitrary",), vmem_limit_bytes=48 << 20
        ),
        name="feed_forward",
    )(rows, attended, attended_other, upstream, gain, mixer, mixer_other, expand, shrink)


def norm_kernel(
    middle, own, other, upstream, gain, mixer, attended,
    middle_grad, attended_grad, mixer_grad, gain_grad, mixer_turned, mixer_sum
):
    step = pl.program_id(0)

    @pl.when(step == 0)
    def _():
        mixer_turned[...] = mixer[...].T
        mixer_sum[...] = jnp.zeros(mixer_sum.shape, f32)
        gain_grad[...] = jnp.zeros(gain_grad.shape, f32)

    unused, normal, inverse = layer_norm(middle[...], gain[...])
    back = own[...].astype(f32) + other[...].astype(f32)
    grad = upstream[...].astype(f32) + norm_back(back, gain[...], normal, inverse)
    middle_grad[...] = grad
    grad_low = grad.astype(bf16)
    attended_grad[...] = dot(mixer_turned[...], grad_low, NT).astype(bf16)
    mixer_sum[...] += dot(attended[...], grad_low, NN)
    gain_grad[...] += jnp.sum(back * normal, axis=0, keepdims=True)

    @pl.when(step == pl.num_programs(0) - 1)
    def _():
        mixer_grad[...] = mixer_sum[...].T.astype(bf16)


def norm_backward(middle, own, other, upstream, gain, mixer, attended):
    count, width = middle.shape
    mixed = attended.shape[0]

    def full(*shape):
        return pl.BlockSpec(shape, lambda i: (0, 0))

    def down(columns):
        return pl.BlockSpec((FEED_ROWS, columns), lambda i: (i, 0))

    def along(lines):
        return pl.BlockSpec((lines, FEED_ROWS), lambda i: (0, i))

    return pl.pallas_call(
        norm_kernel,
        grid=(count // FEED_ROWS,),
        in_specs=[
            down(width), down(width), down(width), down(width), full(1, width),
            full(width, mixed), along(mixed),
        ],
        out_specs=[down(width), along(mixed), full(width, mixed), full(1, width)],
        out_shape=(
            jax.ShapeDtypeStruct((count, width), f32),
            jax.ShapeDtypeStruct((mixed, count), bf16),
            jax.ShapeDtypeStruct((width, mixed), bf16),
            jax.ShapeDtypeStruct((1, width), f32),
        ),
        scratch_shapes=[pltpu.VMEM((mixed, width), bf16), pltpu.VMEM((mixed, width), f32)],
        compiler_params=pltpu.CompilerParams(
            dimension_semantics=("arbitrary",), vmem_limit_bytes=40 << 20
        ),
        name="norm_backward",
    )(middle, own, other, upstream, gain, mixer, attended)


def swap(value, axis, bit):
    count = lax.axis_size(axis)
    return lax.ppermute(value, axis, [(i, i ^ bit) for i in range(count)])


def bit_orders():
    bits = lax.axis_size("dp").bit_length() - 1
    return [[(start + k) % (bits - 1) for k in range(bits - 1)] + [bits - 1] for start in range(3)]


def steps_count():
    return lax.axis_size("dp").bit_length() - 1


def reduce_start(value):
    bits = steps_count()
    rows = value.shape[0] >> bits
    return value.reshape((2,) * bits + (rows, value.shape[1]))


def reduce_step(held, step, which):
    bits = steps_count()
    bit = bit_orders()[which][step]
    axis = bits - 1 - bit
    side = (lax.axis_index("dp") >> bit) & 1
    kept = lax.dynamic_slice_in_dim(held, side, 1, axis)
    sent = lax.dynamic_slice_in_dim(held, 1 - side, 1, axis)
    total = kept.astype(f32) + swap(sent, "dp", 1 << bit).astype(f32)
    if step + 1 == bits:
        return total.reshape(held.shape[-2:])
    return total.astype(bf16)


def gather_start(value):
    return value[(None,) * steps_count()]


def gather_step(held, step, which):
    bits = steps_count()
    bit = bit_orders()[which][bits - 1 - step]
    return jnp.concatenate([held, swap(held, "dp", 1 << bit)], axis=bits - 1 - bit)


def ordered_step(held, step, which):
    bits = steps_count()
    bit = bit_orders()[which][bits - 1 - step]
    got = swap(held, "dp", 1 << bit)
    low_side = ((lax.axis_index("dp") >> bit) & 1) == 0
    return jnp.concatenate(
        [jnp.where(low_side, held, got), jnp.where(low_side, got, held)], axis=bits - 1 - bit
    )


def gather_rows(held):
    return held.reshape(-1, held.shape[-1])


def thirds(value):
    unit = value.shape[1] // 3 // 128 * 128
    return [value[:, :unit], value[:, unit : 2 * unit], value[:, 2 * unit :]]


def halves_of(value):
    unit = value.shape[1] // 256 * 128
    return [value[:, :unit], value[:, unit:]]


def quarter(step, states, part, first=0):
    bits = steps_count()
    for index in range(bits * part // QUARTERS, bits * (part + 1) // QUARTERS):
        states = [step(state, index, first + which) for which, state in enumerate(states)]
    return states


def tie(*values):
    return lax.optimization_barrier(values)


def total_step(value, part):
    if part == 0:
        return value + swap(value, "head", 1)
    bits = steps_count()
    for bit in range(bits * (part - 1) // QUARTERS, bits * part // QUARTERS):
        value = value + swap(value, "dp", 1 << bit)
    return value


def halves(own, other, head):
    first = jnp.where(head == 0, own, other)
    second = jnp.where(head == 0, other, own)
    return jnp.concatenate([first, second], axis=0)


def schulz_start(own, gathered):
    gram = dot(gathered, gathered, TN)
    norm_value = jnp.sqrt(jnp.trace(gram)) + 1e-07
    return own / norm_value, gram / (norm_value * norm_value)


def schulz_step(state, last=False):
    rows, gram = state
    low_gram = gram.astype(bf16)
    change = (ns_second * gram + ns_third * dot(low_gram, low_gram, NN)).astype(bf16)
    rows = ns_first * rows + dot(rows.astype(bf16), change, NN)
    if last:
        return rows
    once = ns_first * gram + dot(low_gram, change, NN)
    return rows, ns_first * once + dot(once.astype(bf16), change, NN)


def schulz_rest(state):
    for iteration in range(NS_ITERS):
        state = schulz_step(state, iteration + 1 == NS_ITERS)
    return state


def shards(
    tokens,
    lengths,
    norm_gains,
    joined_weight,
    mixer_weight,
    expand_weight,
    shrink_weight,
    joined_momentum,
    mixer_momentum,
    expand_momentum,
    shrink_momentum,
    gain_momentum,
    cotangent,
):
    row_count = cotangent.shape[0]
    local_rows = tokens.shape[0]
    head = lax.axis_index("head")
    mixer_width = mixer_weight.shape[2]

    def own_half(value):
        return lax.dynamic_slice_in_dim(value, head * local_rows, local_rows, 0)

    joined_parts = [gather_start(part) for part in thirds(joined_weight[0].astype(bf16))]
    joined_parts = quarter(ordered_step, joined_parts, 0)
    others = [gather_start(part) for part in halves_of(expand_weight[0].astype(bf16))] + [
        gather_start(jnp.concatenate([mixer_weight[0], shrink_weight[0]], axis=1).astype(bf16))
    ]
    key_rows, query_rows, cosine, sine = doc_tables(lengths[0], row_count)
    low, high = key_bounds(lengths[0], row_count)
    rows_low = halves(tokens, swap(tokens, "head", 1), head)
    first_normed, first_normal, first_inverse = layer_norm(rows_low.astype(f32), norm_gains[0])
    first_low = first_normed.astype(bf16)

    joined_parts, others = tie(joined_parts, others)
    joined_parts = quarter(ordered_step, joined_parts, 1)
    others = quarter(ordered_step, others, 0)
    joined_parts, others = tie(joined_parts, others)
    joined_parts = quarter(ordered_step, joined_parts, 2)
    moved = quarter(ordered_step, others, 1)
    joined_parts, first_low = tie(joined_parts, first_low)
    joined_parts = quarter(ordered_step, joined_parts, 3)
    joined_parts, others = tie(joined_parts, moved)

    moved = quarter(ordered_step, others, 2)
    joined_low = jnp.concatenate([gather_rows(part) for part in joined_parts], axis=1)
    joined = dot(joined_low, first_low, NT)
    width = joined.shape[0] // 3
    queries = (rotate(joined[:width], cosine, sine) * QUERY_SCALE).astype(bf16)
    keys = rotate(joined[width : 2 * width], cosine, sine).astype(bf16)
    values = joined[2 * width :].astype(bf16)
    others, queries, keys, values, low = tie(moved, queries, keys, values, low)
    moved = quarter(ordered_step, others, 3)
    attended, logsum = attention_forward(low, high, queries, keys, values, key_rows, query_rows)
    others, attended, logsum = tie(moved, attended, logsum)
    attended_other = swap(attended, "head", 1)
    expand_low = jnp.concatenate([gather_rows(part) for part in others[:2]], axis=1)
    both_low = gather_rows(others[2])
    mixer_low, shrink_turned = both_low[:, :mixer_width], both_low[:, mixer_width:].T
    mixer_other = swap(mixer_low, "head", 1)

    second_gain = norm_gains[1:2]
    middle, hidden, second_part, shrink_grad, expand_grad = feed_forward(
        rows_low, attended, attended_other, cotangent, second_gain,
        mixer_low, mixer_other, expand_low, shrink_turned,
    )
    second_other = swap(second_part, "head", 1)

    sums, second_other = tie(
        [reduce_start(part) for part in halves_of(expand_grad) + [shrink_grad.T]], second_other
    )
    moved = quarter(reduce_step, sums, 0)
    middle_grad, attended_grad, mixer_grad, second_gain_grad = norm_backward(
        middle, second_part, second_other, cotangent, second_gain, mixer_low, attended
    )
    second_gain_grad = 0.5 * second_gain_grad[0]

    sums, attended_grad, shrink_now = tie(moved, attended_grad, shrink_turned)
    moved = quarter(reduce_step, sums, 1)

    def fed(columns, weight):
        return dot(lax.dynamic_slice_in_dim(hidden, columns, local_rows, 1), weight, TN)

    fed_other = fed((1 - head) * local_rows, shrink_now).astype(bf16)
    sums, mixer_grad, fed_other, shrink_now = tie(moved, mixer_grad, fed_other, shrink_now)
    moved = quarter(reduce_step, sums, 2)
    mixer_moved = quarter(reduce_step, [reduce_start(mixer_grad)], 0, 2)
    fed_own = fed(head * local_rows, shrink_now)

    sums, mixer_sum, fed_own, low = tie(moved, mixer_moved, fed_own, low)
    moved = quarter(reduce_step, sums, 3)
    mixer_moved = quarter(reduce_step, mixer_sum, 1, 2)
    fed_other = swap(fed_other, "head", 1)
    joined_back = attention_backward(
        low, high, queries, keys, values, attended_grad, attended, logsum, key_rows, query_rows,
        cosine, sine,
    )
    sums, mixer_sum, joined_back = tie(moved, mixer_moved, joined_back)
    expand_next = 0.5 * expand_momentum[0] + jnp.concatenate(sums[:2], axis=1)
    shrink_next = 0.5 * shrink_momentum[0] + sums[2]
    gathers = [gather_start(part) for part in halves_of(expand_next.astype(bf16))]
    gathers.append(gather_start(shrink_next.astype(bf16)))

    moved = quarter(gather_step, gathers, 0)
    mixer_moved = quarter(reduce_step, mixer_sum, 2, 2)
    joined_grad = dot(joined_back, first_low, NN).astype(bf16)

    def first_part(start, weight):
        columns = lax.dynamic_slice_in_dim(joined_back, start, local_rows, 1)
        return dot(columns, weight, TN)

    gathers, mixer_sum, joined_grad, joined_now = tie(moved, mixer_moved, joined_grad, joined_low)
    sums = quarter(reduce_step, [reduce_start(part) for part in thirds(joined_grad)], 0)
    moved = quarter(gather_step, gathers, 1)
    mixer_moved = quarter(reduce_step, mixer_sum, 3, 2)
    first_other = swap(
        first_part((1 - head) * local_rows, joined_now).astype(bf16), "head", 1
    )
    first_mine = first_part(head * local_rows, joined_now)
    layer_output = (own_half(middle) + fed_own + fed_other.astype(f32)).astype(bf16)

    sums, gathers, mixer_sum, first_other, first_mine = tie(
        sums, moved, mixer_moved, first_other, first_mine
    )
    mixer_next = 0.5 * mixer_momentum[0] + mixer_sum[0]
    moved = quarter(reduce_step, sums, 1)
    gathers_moved = quarter(gather_step, gathers, 2)
    first_back = first_mine + first_other.astype(f32)
    own_normal = own_half(first_normal)
    first_gain_grad = jnp.sum(first_back * own_normal, axis=0)

    sums, gathers, first_gain_grad, first_gain = tie(
        moved, gathers_moved, first_gain_grad, norm_gains[0]
    )
    moved = quarter(reduce_step, sums, 2)
    gathers_moved = quarter(gather_step, gathers, 3)
    input_gradient = own_half(middle_grad) + norm_back(
        first_back, first_gain, own_normal, own_half(first_inverse)
    )

    sums, gathers, input_gradient = tie(moved, gathers_moved, input_gradient)
    mixer_gather = [gather_start(mixer_next.astype(bf16))]
    gain_totals = jnp.stack([first_gain_grad, second_gain_grad])
    expand_full = jnp.concatenate([gather_rows(state) for state in gathers[:2]], axis=1)
    shrink_full = gather_rows(gathers[2])

    moved = quarter(reduce_step, sums, 3)
    mixer_moved = quarter(gather_step, mixer_gather, 0, 2)
    gain_moved = total_step(gain_totals, 0)
    shrink_state = schulz_step(schulz_start(shrink_next, shrink_full))
    sums, mixer_gather, gain_totals, shrink_state, expand_full = tie(
        moved, mixer_moved, gain_moved, shrink_state, expand_full
    )
    joined_next = 0.5 * joined_momentum[0] + jnp.concatenate(sums, axis=1)
    joined_gather = [gather_start(part) for part in thirds(joined_next.astype(bf16))]

    moved = quarter(gather_step, joined_gather, 0)
    mixer_moved = quarter(gather_step, mixer_gather, 1, 2)
    gain_moved = total_step(gain_totals, 1)
    shrink_rows = schulz_step(schulz_step(shrink_state), True)
    expand_state = schulz_start(expand_next, expand_full)
    joined_gather, mixer_gather, gain_totals, shrink_rows, expand_state = tie(
        moved, mixer_moved, gain_moved, shrink_rows, expand_state
    )

    moved = quarter(gather_step, joined_gather, 1)
    mixer_moved = quarter(gather_step, mixer_gather, 2, 2)
    gain_moved = total_step(gain_totals, 2)
    expand_state = schulz_step(expand_state)
    joined_gather, mixer_gather, gain_totals, expand_state = tie(
        moved, mixer_moved, gain_moved, expand_state
    )

    moved = quarter(gather_step, joined_gather, 2)
    mixer_moved = quarter(gather_step, mixer_gather, 3, 2)
    gain_moved = total_step(gain_totals, 3)
    expand_rows = schulz_step(schulz_step(expand_state), True)
    joined_gather, mixer_gather, gain_totals, expand_rows = tie(
        moved, mixer_moved, gain_moved, expand_rows
    )

    moved = quarter(gather_step, joined_gather, 3)
    gain_totals = total_step(gain_totals, 4)
    mixer_rows = schulz_rest(schulz_start(mixer_next, gather_rows(mixer_gather[0])))
    joined_gather, mixer_rows = tie(moved, mixer_rows)
    joined_full = jnp.concatenate([gather_rows(state) for state in joined_gather], axis=1)
    joined_rows = schulz_rest(schulz_start(joined_next, joined_full))

    dp_count = lax.axis_size("dp")
    updated = []
    for weight, rows in (
        (joined_weight, joined_rows),
        (mixer_weight, mixer_rows),
        (expand_weight, expand_rows),
        (shrink_weight, shrink_rows),
    ):
        shape_scale = math.sqrt(rows.shape[0] * dp_count / rows.shape[1])
        updated.append((weight[0] - muon_rate * shape_scale * rows)[None])

    momentum_gains = 0.5 * gain_momentum + gain_totals
    updated_gains = norm_gains - gain_rate * momentum_gains * lax.rsqrt(
        jnp.mean(momentum_gains * momentum_gains, axis=-1, keepdims=True) + 1e-06
    )
    return (
        layer_output,
        input_gradient,
        joined_next[None],
        mixer_next[None],
        expand_next[None],
        shrink_next[None],
        updated[0],
        updated[1],
        updated[2],
        updated[3],
        momentum_gains,
        updated_gains,
    )


def solution(mesh):
    rows = P(("dp", "head"), None)
    weight = P("head", "dp", None)
    return jax.shard_map(
        shards,
        mesh=mesh,
        in_specs=(rows, P("dp", None), P()) + (weight,) * 8 + (P(), P("dp", None)),
        out_specs=(rows, rows) + (weight,) * 8 + (P(), P()),
        check_vma=False,
    )
```

```python
import functools
import math

import jax
import jax.numpy as jnp
from jax import lax
from jax.experimental import pallas as pl
from jax.experimental.pallas import tpu as pltpu
from jax.sharding import PartitionSpec as P

HEAD_DIM = 64
NS_ITERS = 3

theta_base = 160000.0
norm_epsilon = 1e-05
ns_first = 3.4445
ns_second = -4.775
ns_third = 2.0315
muon_rate = 1.0
gain_rate = 0.3

bf16 = jnp.bfloat16
f32 = jnp.float32
LOG2E = math.log2(math.e)
QUERY_SCALE = 0.125 * LOG2E
SAFE_SCORE = 60.0
DEPTH = 128
TILE_Q = 256
TILE_K = 256
FWD_SKEW = 6
BWD_SKEW = 2

NN = (((1,), (0,)), ((), ()))
NT = (((1,), (1,)), ((), ()))
TN = (((0,), (0,)), ((), ()))
TT = (((0,), (1,)), ((), ()))
QUARTERS = 4
FEED_ROWS = 256
FEED_CHUNKS = 3
ERF_TOP = (
    -2.72614225801306e-10, 2.77068142495902e-08, -2.10102402082508e-06, -5.69250639462346e-05,
    -7.34990630326855e-04, -2.95459980854025e-03, -1.60960333262415e-02,
)
ERF_BOTTOM = (
    -1.45660718464996e-05, -2.13374055278905e-04, -1.68282697438203e-03, -7.37332916720468e-03,
    -1.42647390514189e-02,
)


def dot(left, right, dims):
    return lax.dot_general(left, right, dims, preferred_element_type=f32)


def key_bounds(length_row, row_count):
    ends = jnp.cumsum(length_row)
    starts = ends - length_row
    first = jnp.arange(row_count // TILE_Q, dtype=jnp.int32) * TILE_Q
    labels = jnp.arange(length_row.shape[0], dtype=jnp.int32)

    def pick(places, table):
        segment = jnp.sum((places[:, None] >= ends[None, :]).astype(jnp.int32), axis=1)
        return jnp.sum(jnp.where(segment[:, None] == labels[None, :], table[None, :], 0), axis=1)

    low = pick(first, starts) // TILE_K
    high = (pick(first + TILE_Q - 1, ends) + TILE_K - 1) // TILE_K
    return low.astype(jnp.int32), high.astype(jnp.int32)


def doc_tables(length_row, row_count):
    ends = jnp.cumsum(length_row)
    starts = ends - length_row
    count = length_row.shape[0]
    places = jnp.arange(row_count, dtype=jnp.int32)[None, :]
    member = (places >= starts[:, None]) & (places < ends[:, None])
    rest = jnp.zeros((16 - count, row_count), f32)
    key_rows = jnp.concatenate([member.astype(f32), rest], axis=0).astype(bf16)
    query_rows = jnp.concatenate([jnp.where(member, 0.0, -1e30), rest], axis=0).astype(bf16)
    doc_first = jnp.sum(jnp.where(member, starts[:, None], 0), axis=0, keepdims=True)
    position = (places - doc_first).astype(f32)
    half_dim = HEAD_DIM // 2
    frequency = jnp.exp(
        jnp.arange(half_dim, dtype=f32) * (-2.0 * math.log(theta_base) / HEAD_DIM)
    )
    angles = frequency[:, None] * position
    return key_rows, query_rows, jnp.cos(angles), jnp.sin(angles)


def rotate(values, cosine, sine):
    half = HEAD_DIM // 2
    heads = values.reshape(-1, HEAD_DIM, values.shape[1])
    low, high = heads[:, :half], heads[:, half:]
    turned = jnp.concatenate([low * cosine - high * sine, high * cosine + low * sine], axis=1)
    return turned.reshape(values.shape)


def rows16(parts):
    rest = jnp.zeros((16 - len(parts), parts[0].shape[1]), f32)
    return jnp.concatenate([part.astype(f32) for part in parts] + [rest], axis=0).astype(bf16)


def split3(value):
    first = value.astype(bf16)
    left = value - first.astype(f32)
    second = left.astype(bf16)
    third = (left - second.astype(f32)).astype(bf16)
    return [first, second, third]


def three_ones(count):
    return jnp.concatenate([jnp.ones((3, count), f32), jnp.zeros((13, count), f32)], axis=0).astype(
        bf16
    )


def forward_kernel(
    low, high, queries, keys, values, key_rows, query_rows, out, logsum, keys_in, values_in, queries_in, safe
):
    heads = queries.shape[0] // HEAD_DIM
    rows = keys.shape[1]
    step = pl.program_id(0)

    @pl.when(step == 0)
    def _():
        worst = jnp.zeros((1, 1), f32)
        ones = rows16([jnp.ones((1, rows), f32)])
        for h in range(heads):
            band = slice(h * HEAD_DIM, (h + 1) * HEAD_DIM)
            key = keys[band, :]
            pad = jnp.zeros((DEPTH - HEAD_DIM - 16, rows), bf16)
            keys_in[h] = jnp.concatenate([key, key_rows[...], pad], axis=0).T
            values_in[h, :HEAD_DIM, :] = values[band, :]
            values_in[h, HEAD_DIM:, :] = ones
            query_full = queries[band, :].astype(f32)
            key_full = key.astype(f32)
            query_top = jnp.max(
                jnp.sum(query_full * query_full, axis=0, keepdims=True), axis=1, keepdims=True
            )
            key_top = jnp.max(
                jnp.sum(key_full * key_full, axis=0, keepdims=True), axis=1, keepdims=True
            )
            worst = jnp.maximum(worst, query_top * key_top)
        safe[0] = jnp.where(worst[0, 0] <= SAFE_SCORE * SAFE_SCORE, 1, 0)

    first = pl.multiple_of(step * TILE_Q, TILE_Q)
    for h in range(heads):
        queries_in[h, :HEAD_DIM, :] = queries[h * HEAD_DIM : (h + 1) * HEAD_DIM, pl.ds(first, TILE_Q)]
        queries_in[h, HEAD_DIM : HEAD_DIM + 16, :] = query_rows[...]
        queries_in[h, HEAD_DIM + 16 :, :] = jnp.zeros((DEPTH - HEAD_DIM - 16, TILE_Q), bf16)

    def finish(peaks, totals):
        for h in range(heads):
            weight = totals[h][HEAD_DIM : HEAD_DIM + 1, :]
            out[h * HEAD_DIM : (h + 1) * HEAD_DIM, :] = (totals[h][:HEAD_DIM, :] / weight).astype(bf16)
            level = jnp.log2(weight)
            logsum[h : h + 1, :] = level if peaks is None else peaks[h] + level

    empty = tuple(jnp.zeros((HEAD_DIM + 16, TILE_Q), f32) for _ in range(heads))

    @pl.when(safe[0] == 1)
    def _():
        def block(j, totals):
            span = pl.ds(pl.multiple_of(j * TILE_K, TILE_K), TILE_K)
            result = [None] * heads
            waiting = {}
            for t in range(heads + FWD_SKEW):
                if t < heads:
                    waiting[t] = dot(keys_in[t, span, :], queries_in[t], NN)
                h = t - FWD_SKEW
                if h >= 0:
                    raised = jnp.exp2(waiting.pop(h)).astype(bf16)
                    result[h] = totals[h] + dot(values_in[h, :, span], raised, NN)
            return tuple(result)

        finish(None, lax.fori_loop(low[step], high[step], block, empty))

    @pl.when(safe[0] == 0)
    def _():
        def block(j, carry):
            peaks, totals = carry
            span = pl.ds(pl.multiple_of(j * TILE_K, TILE_K), TILE_K)
            new_peaks = []
            new_totals = []
            for h in range(heads):
                scores = dot(keys_in[h, span, :], queries_in[h], NN)
                peak = jnp.maximum(peaks[h], jnp.max(scores, axis=0, keepdims=True))
                raised = jnp.exp2(scores - peak).astype(bf16)
                new_totals.append(
                    totals[h] * jnp.exp2(peaks[h] - peak) + dot(values_in[h, :, span], raised, NN)
                )
                new_peaks.append(peak)
            return tuple(new_peaks), tuple(new_totals)

        lowest = tuple(jnp.full((1, TILE_Q), -3e38, f32) for _ in range(heads))
        finish(*lax.fori_loop(low[step], high[step], block, (lowest, empty)))


def attention_forward(low, high, queries, keys, values, key_rows, query_rows):
    width, rows = queries.shape
    heads = width // HEAD_DIM

    def full(count):
        return pl.BlockSpec((count, rows), lambda i, low, high: (0, 0))

    def tile(count):
        return pl.BlockSpec((count, TILE_Q), lambda i, low, high: (0, i))

    return pl.pallas_call(
        forward_kernel,
        out_shape=(
            jax.ShapeDtypeStruct((width, rows), bf16),
            jax.ShapeDtypeStruct((heads, rows), f32),
        ),
        grid_spec=pltpu.PrefetchScalarGridSpec(
            num_scalar_prefetch=2,
            grid=(rows // TILE_Q,),
            in_specs=[full(width), full(width), full(width), full(16), tile(16)],
            out_specs=[tile(width), tile(heads)],
            scratch_shapes=[
                pltpu.VMEM((heads, rows, DEPTH), bf16),
                pltpu.VMEM((heads, HEAD_DIM + 16, rows), bf16),
                pltpu.VMEM((heads, DEPTH, TILE_Q), bf16),
                pltpu.SMEM((1,), jnp.int32),
            ],
        ),
        compiler_params=pltpu.CompilerParams(
            dimension_semantics=("arbitrary",), vmem_limit_bytes=40 << 20
        ),
        name="attention_forward",
    )(low, high, queries, keys, values, key_rows, query_rows)


def backward_kernel(
    low, high, queries, keys, values, grads, outs, logsum, key_rows, query_rows, cosine, sine,
    joined_back, *scratch
):
    heads = queries.shape[0] // HEAD_DIM
    rows = keys.shape[1]
    keys_in, values_in, queries_in, grads_in = scratch[:4]
    key_sum = scratch[4 : 4 + heads]
    value_sum = scratch[4 + heads : 4 + 2 * heads]
    query_sum = scratch[4 + 2 * heads : 4 + 3 * heads]
    step = pl.program_id(0)

    @pl.when(step == 0)
    def _():
        ones = three_ones(rows)
        for h in range(heads):
            band = slice(h * HEAD_DIM, (h + 1) * HEAD_DIM)
            pad = jnp.zeros((DEPTH - HEAD_DIM - 32, rows), bf16)
            keys_in[h] = jnp.concatenate([keys[band, :], key_rows[...], ones, pad], axis=0).T
            pad = jnp.zeros((DEPTH - HEAD_DIM - 16, rows), bf16)
            values_in[h] = jnp.concatenate([values[band, :], ones, pad], axis=0).T
            key_sum[h][...] = jnp.zeros((HEAD_DIM, rows), f32)
            value_sum[h][...] = jnp.zeros((HEAD_DIM, rows), f32)

    for h in range(heads):
        band = slice(h * HEAD_DIM, (h + 1) * HEAD_DIM)
        queries_in[h, :HEAD_DIM, :] = queries[band, :]
        queries_in[h, HEAD_DIM : HEAD_DIM + 16, :] = query_rows[...]
        queries_in[h, HEAD_DIM + 16 : HEAD_DIM + 32, :] = rows16(split3(-logsum[h : h + 1, :]))
        queries_in[h, HEAD_DIM + 32 :, :] = jnp.zeros((DEPTH - HEAD_DIM - 32, TILE_Q), bf16)
        inner = jnp.sum(grads[band, :].astype(f32) * outs[band, :].astype(f32), axis=0, keepdims=True)
        grads_in[h, :HEAD_DIM, :] = grads[band, :]
        grads_in[h, HEAD_DIM : HEAD_DIM + 16, :] = rows16(split3(-inner))
        grads_in[h, HEAD_DIM + 16 :, :] = jnp.zeros((DEPTH - HEAD_DIM - 16, TILE_Q), bf16)
        query_sum[h][...] = jnp.zeros((HEAD_DIM, TILE_Q), f32)

    def block(j, carry):
        span = pl.ds(pl.multiple_of(j * TILE_K, TILE_K), TILE_K)
        waiting = {}
        for t in range(heads + BWD_SKEW):
            if t < heads:
                waiting[t] = (
                    dot(keys_in[t, span, :], queries_in[t], NN),
                    dot(values_in[t, span, :], grads_in[t], NN),
                )
            h = t - BWD_SKEW
            if h < 0:
                continue
            band = slice(h * HEAD_DIM, (h + 1) * HEAD_DIM)
            scores, weight_grad = waiting.pop(h)
            softmax = jnp.exp2(scores)
            score_grad = (softmax * weight_grad).astype(bf16)
            value_sum[h][:, span] += dot(grads[band, :], softmax.astype(bf16), NT)
            key_sum[h][:, span] += dot(queries[band, :], score_grad, NT)
            query_sum[h][...] += dot(keys[band, span], score_grad, NN)
        return carry

    lax.fori_loop(low[step], high[step], block, 0)

    def store(offset, columns, value):
        half = HEAD_DIM // 2
        upper, lower = value[:half], value[half:]
        cos, sin = cosine[:, columns], sine[:, columns]
        joined_back[offset : offset + half, columns] = (upper * cos + lower * sin).astype(bf16)
        joined_back[offset + half : offset + HEAD_DIM, columns] = (lower * cos - upper * sin).astype(bf16)

    width = heads * HEAD_DIM
    columns = pl.ds(pl.multiple_of(step * TILE_Q, TILE_Q), TILE_Q)
    for h in range(heads):
        store(h * HEAD_DIM, columns, query_sum[h][...] * 0.125)

    @pl.when(step == pl.num_programs(0) - 1)
    def _():
        for h in range(heads):
            first = width + h * HEAD_DIM
            store(first, slice(0, rows), key_sum[h][...] * (1.0 / LOG2E))
            first += width
            joined_back[first : first + HEAD_DIM, :] = value_sum[h][...].astype(bf16)


def attention_backward(
    low, high, queries, keys, values, grads, outs, logsum, key_rows, query_rows, cosine, sine
):
    width, rows = queries.shape
    heads = width // HEAD_DIM

    def full(count):
        return pl.BlockSpec((count, rows), lambda i, low, high: (0, 0))

    def tile(count):
        return pl.BlockSpec((count, TILE_Q), lambda i, low, high: (0, i))

    return pl.pallas_call(
        backward_kernel,
        out_shape=jax.ShapeDtypeStruct((3 * width, rows), bf16),
        grid_spec=pltpu.PrefetchScalarGridSpec(
            num_scalar_prefetch=2,
            grid=(rows // TILE_Q,),
            in_specs=[
                tile(width), full(width), full(width), tile(width), tile(width), tile(heads),
                full(16), tile(16), full(HEAD_DIM // 2), full(HEAD_DIM // 2),
            ],
            out_specs=full(3 * width),
            scratch_shapes=[
                pltpu.VMEM((heads, rows, DEPTH), bf16),
                pltpu.VMEM((heads, rows, DEPTH), bf16),
                pltpu.VMEM((heads, DEPTH, TILE_Q), bf16),
                pltpu.VMEM((heads, DEPTH, TILE_Q), bf16),
            ]
            + [pltpu.VMEM((HEAD_DIM, rows), f32)] * (2 * heads)
            + [pltpu.VMEM((HEAD_DIM, TILE_Q), f32)] * heads,
        ),
        compiler_params=pltpu.CompilerParams(
            dimension_semantics=("arbitrary",), vmem_limit_bytes=52 << 20
        ),
        name="attention_backward",
    )(low, high, queries, keys, values, grads, outs, logsum, key_rows, query_rows, cosine, sine)


def layer_norm(values, gain_row):
    centred = values - jnp.mean(values, axis=-1, keepdims=True)
    inverse = lax.rsqrt(jnp.mean(centred * centred, axis=-1, keepdims=True) + norm_epsilon)
    normal = centred * inverse
    return normal * gain_row, normal, inverse


def norm_back(upstream, gain_row, normal, inverse):
    scaled = upstream * gain_row
    inner_mean = jnp.mean(scaled * normal, axis=-1, keepdims=True)
    return inverse * (scaled - jnp.mean(scaled, axis=-1, keepdims=True) - normal * inner_mean)


def horner(square, factors):
    total = factors[0] * square + factors[1]
    for factor in factors[2:]:
        total = total * square + factor
    return total


def error_function(value):
    value = jnp.clip(value, -4.0, 4.0)
    square = value * value
    return value * horner(square, ERF_TOP) / horner(square, ERF_BOTTOM)


def feed_kernel(
    rows, attended, attended_other, upstream, gain, mixer, mixer_other, expand, shrink,
    middle, hidden, second_part, shrink_grad, expand_grad, shrink_sum, expand_sum
):
    step = pl.program_id(0)
    units = shrink.shape[0]
    chunk = units // FEED_CHUNKS

    @pl.when(step == 0)
    def _():
        shrink_sum[...] = jnp.zeros(shrink_sum.shape, f32)
        expand_sum[...] = jnp.zeros(expand_sum.shape, f32)

    total = rows[...].astype(f32) + dot(attended[...].T, mixer[...], NT)
    total = total + dot(attended_other[...].T, mixer_other[...], NT)
    middle[...] = total
    normed = layer_norm(total, gain[...])[0].astype(bf16)
    above = upstream[...]

    def project(c):
        first = slice(c * chunk, (c + 1) * chunk)
        second = slice(units + c * chunk, units + (c + 1) * chunk)
        return (
            dot(expand[first, :], normed, NT),
            dot(expand[second, :], normed, NT),
            dot(shrink[first, :], above, NT),
        )

    waiting = project(0)
    back = jnp.zeros(total.shape, f32)
    for c in range(FEED_CHUNKS):
        active, linear, grad = waiting
        if c + 1 < FEED_CHUNKS:
            waiting = project(c + 1)
        first = slice(c * chunk, (c + 1) * chunk)
        second = slice(units + c * chunk, units + (c + 1) * chunk)
        area = 0.5 * error_function(active * math.sqrt(0.5)) + 0.5
        gate = active * area
        density = jnp.exp(-0.5 * active * active) * (1.0 / math.sqrt(2.0 * math.pi))
        unit = (gate * linear).astype(bf16)
        active_back = (grad * linear * (area + active * density)).astype(bf16)
        linear_back = (grad * gate).astype(bf16)
        hidden[first, :] = unit
        shrink_sum[first, :] += dot(unit, above, NN)
        expand_sum[first, :] += dot(active_back, normed, NN)
        expand_sum[second, :] += dot(linear_back, normed, NN)
        back = back + dot(active_back, expand[first, :], TN) + dot(linear_back, expand[second, :], TN)
    second_part[...] = back.astype(bf16)

    @pl.when(step == pl.num_programs(0) - 1)
    def _():
        shrink_grad[...] = shrink_sum[...].astype(bf16)
        expand_grad[...] = expand_sum[...].astype(bf16)


def feed_forward(rows, attended, attended_other, upstream, gain, mixer, mixer_other, expand, shrink):
    count, width = rows.shape
    mixed, units = attended.shape[0], shrink.shape[0]

    def full(*shape):
        return pl.BlockSpec(shape, lambda i: (0, 0))

    def down(columns):
        return pl.BlockSpec((FEED_ROWS, columns), lambda i: (i, 0))

    def along(lines):
        return pl.BlockSpec((lines, FEED_ROWS), lambda i: (0, i))

    return pl.pallas_call(
        feed_kernel,
        grid=(count // FEED_ROWS,),
        in_specs=[
            down(width), along(mixed), along(mixed), down(width), full(1, width),
            full(width, mixed), full(width, mixed), full(2 * units, width), full(units, width),
        ],
        out_specs=[
            down(width), along(units), down(width), full(units, width), full(2 * units, width),
        ],
        out_shape=(
            jax.ShapeDtypeStruct((count, width), f32),
            jax.ShapeDtypeStruct((units, count), bf16),
            jax.ShapeDtypeStruct((count, width), bf16),
            jax.ShapeDtypeStruct((units, width), bf16),
            jax.ShapeDtypeStruct((2 * units, width), bf16),
        ),
        scratch_shapes=[pltpu.VMEM((units, width), f32), pltpu.VMEM((2 * units, width), f32)],
        compiler_params=pltpu.CompilerParams(
            dimension_semantics=("arbitrary",), vmem_limit_bytes=48 << 20
        ),
        name="feed_forward",
    )(rows, attended, attended_other, upstream, gain, mixer, mixer_other, expand, shrink)


def norm_kernel(
    middle, own, other, upstream, gain, mixer, attended,
    middle_grad, attended_grad, mixer_grad, gain_grad, mixer_turned, mixer_sum
):
    step = pl.program_id(0)

    @pl.when(step == 0)
    def _():
        mixer_turned[...] = mixer[...].T
        mixer_sum[...] = jnp.zeros(mixer_sum.shape, f32)
        gain_grad[...] = jnp.zeros(gain_grad.shape, f32)

    unused, normal, inverse = layer_norm(middle[...], gain[...])
    back = own[...].astype(f32) + other[...].astype(f32)
    grad = upstream[...].astype(f32) + norm_back(back, gain[...], normal, inverse)
    middle_grad[...] = grad
    grad_low = grad.astype(bf16)
    attended_grad[...] = dot(mixer_turned[...], grad_low, NT).astype(bf16)
    mixer_sum[...] += dot(attended[...], grad_low, NN)
    gain_grad[...] += jnp.sum(back * normal, axis=0, keepdims=True)

    @pl.when(step == pl.num_programs(0) - 1)
    def _():
        mixer_grad[...] = mixer_sum[...].T.astype(bf16)


def norm_backward(middle, own, other, upstream, gain, mixer, attended):
    count, width = middle.shape
    mixed = attended.shape[0]

    def full(*shape):
        return pl.BlockSpec(shape, lambda i: (0, 0))

    def down(columns):
        return pl.BlockSpec((FEED_ROWS, columns), lambda i: (i, 0))

    def along(lines):
        return pl.BlockSpec((lines, FEED_ROWS), lambda i: (0, i))

    return pl.pallas_call(
        norm_kernel,
        grid=(count // FEED_ROWS,),
        in_specs=[
            down(width), down(width), down(width), down(width), full(1, width),
            full(width, mixed), along(mixed),
        ],
        out_specs=[down(width), along(mixed), full(width, mixed), full(1, width)],
        out_shape=(
            jax.ShapeDtypeStruct((count, width), f32),
            jax.ShapeDtypeStruct((mixed, count), bf16),
            jax.ShapeDtypeStruct((width, mixed), bf16),
            jax.ShapeDtypeStruct((1, width), f32),
        ),
        scratch_shapes=[pltpu.VMEM((mixed, width), bf16), pltpu.VMEM((mixed, width), f32)],
        compiler_params=pltpu.CompilerParams(
            dimension_semantics=("arbitrary",), vmem_limit_bytes=40 << 20
        ),
        name="norm_backward",
    )(middle, own, other, upstream, gain, mixer, attended)


def swap(value, axis, bit):
    count = lax.axis_size(axis)
    return lax.ppermute(value, axis, [(i, i ^ bit) for i in range(count)])


def bit_orders():
    bits = lax.axis_size("dp").bit_length() - 1
    return [[(start + k) % (bits - 1) for k in range(bits - 1)] + [bits - 1] for start in range(3)]


def steps_count():
    return lax.axis_size("dp").bit_length() - 1


def reduce_start(value):
    bits = steps_count()
    rows = value.shape[0] >> bits
    return value.reshape((2,) * bits + (rows, value.shape[1]))


def reduce_step(held, step, which):
    bits = steps_count()
    bit = bit_orders()[which][step]
    axis = bits - 1 - bit
    side = (lax.axis_index("dp") >> bit) & 1
    kept = lax.dynamic_slice_in_dim(held, side, 1, axis)
    sent = lax.dynamic_slice_in_dim(held, 1 - side, 1, axis)
    total = kept.astype(f32) + swap(sent, "dp", 1 << bit).astype(f32)
    if step + 1 == bits:
        return total.reshape(held.shape[-2:])
    return total.astype(bf16)


def gather_start(value):
    return value[(None,) * steps_count()]


def gather_step(held, step, which):
    bits = steps_count()
    bit = bit_orders()[which][bits - 1 - step]
    return jnp.concatenate([held, swap(held, "dp", 1 << bit)], axis=bits - 1 - bit)


def ordered_step(held, step, which):
    bits = steps_count()
    bit = bit_orders()[which][bits - 1 - step]
    got = swap(held, "dp", 1 << bit)
    low_side = ((lax.axis_index("dp") >> bit) & 1) == 0
    return jnp.concatenate(
        [jnp.where(low_side, held, got), jnp.where(low_side, got, held)], axis=bits - 1 - bit
    )


def gather_rows(held):
    return held.reshape(-1, held.shape[-1])


def thirds(value):
    unit = value.shape[1] // 3 // 128 * 128
    return [value[:, :unit], value[:, unit : 2 * unit], value[:, 2 * unit :]]


def halves_of(value):
    unit = value.shape[1] // 256 * 128
    return [value[:, :unit], value[:, unit:]]


def quarter(step, states, part, first=0):
    bits = steps_count()
    for index in range(bits * part // QUARTERS, bits * (part + 1) // QUARTERS):
        states = [step(state, index, first + which) for which, state in enumerate(states)]
    return states


def tie(*values):
    return lax.optimization_barrier(values)


def total_step(value, part):
    if part == 0:
        return value + swap(value, "head", 1)
    bits = steps_count()
    for bit in range(bits * (part - 1) // QUARTERS, bits * part // QUARTERS):
        value = value + swap(value, "dp", 1 << bit)
    return value


def halves(own, other, head):
    first = jnp.where(head == 0, own, other)
    second = jnp.where(head == 0, other, own)
    return jnp.concatenate([first, second], axis=0)


def schulz_kernel(*refs, count, offset, scale):
    parts = refs[:count]
    own, weight, updated, gram, low, change = refs[count:]
    columns = gram.shape[0]
    lines = 256 if columns % 256 == 0 else columns
    if offset is None:
        held = [part[...] for part in parts]
    else:
        held = [parts[0][:, offset : offset + columns]]
    down = 0
    for left in held:
        along = 0
        for right in held:
            gram[down : down + left.shape[1], along : along + right.shape[1]] = dot(left, right, TN)
            along += right.shape[1]
        down += left.shape[1]
    shape = (columns, columns)
    diagonal = lax.broadcasted_iota(jnp.int32, shape, 0) == lax.broadcasted_iota(jnp.int32, shape, 1)
    trace = jnp.sum(jnp.where(diagonal, gram[...], 0.0), axis=0, keepdims=True)
    norm_value = jnp.sqrt(jnp.sum(trace, axis=1, keepdims=True)) + 1e-07
    rows = own[...] / norm_value
    shrunk = 1.0 / (norm_value * norm_value)
    gram[...] = gram[...] * shrunk
    low[...] = gram[...].astype(bf16)

    def per_block(body):
        def run(index, carry):
            body(pl.ds(pl.multiple_of(index * lines, lines), lines))
            return carry

        lax.fori_loop(0, columns // lines, run, 0)

    def form_change(block):
        squared = dot(low[block, :], low[...], NN)
        change[block, :] = (ns_second * gram[block, :] + ns_third * squared).astype(bf16)

    def next_gram(block):
        once = ns_first * gram[block, :] + dot(low[block, :], change[...], NN)
        twice = ns_first * once + dot(once.astype(bf16), change[...], NN)
        gram[block, :] = twice
        low[block, :] = twice.astype(bf16)

    for iteration in range(NS_ITERS):
        per_block(form_change)
        rows = ns_first * rows + dot(rows.astype(bf16), change[...], NN)
        if iteration + 1 < NS_ITERS:
            per_block(next_gram)
    updated[...] = weight[...] - scale * rows


def schulz(parts, offset, own, weight, name):
    columns = own.shape[1]
    shape_scale = muon_rate * math.sqrt(parts[0].shape[0] / columns)
    kernel = functools.partial(schulz_kernel, count=len(parts), offset=offset, scale=shape_scale)
    return pl.pallas_call(
        kernel,
        out_shape=jax.ShapeDtypeStruct(own.shape, f32),
        scratch_shapes=[
            pltpu.VMEM((columns, columns), f32),
            pltpu.VMEM((columns, columns), bf16),
            pltpu.VMEM((columns, columns), bf16),
        ],
        compiler_params=pltpu.CompilerParams(vmem_limit_bytes=40 << 20),
        name=name,
    )(*parts, own, weight)


def shards(
    tokens,
    lengths,
    norm_gains,
    joined_weight,
    mixer_weight,
    expand_weight,
    shrink_weight,
    joined_momentum,
    mixer_momentum,
    expand_momentum,
    shrink_momentum,
    gain_momentum,
    cotangent,
):
    row_count = cotangent.shape[0]
    local_rows = tokens.shape[0]
    head = lax.axis_index("head")
    mixer_width = mixer_weight.shape[2]

    def own_half(value):
        return lax.dynamic_slice_in_dim(value, head * local_rows, local_rows, 0)

    joined_parts = [gather_start(part) for part in thirds(joined_weight[0].astype(bf16))]
    joined_parts = quarter(ordered_step, joined_parts, 0)
    others = [gather_start(part) for part in halves_of(expand_weight[0].astype(bf16))] + [
        gather_start(jnp.concatenate([mixer_weight[0], shrink_weight[0]], axis=1).astype(bf16))
    ]
    key_rows, query_rows, cosine, sine = doc_tables(lengths[0], row_count)
    low, high = key_bounds(lengths[0], row_count)
    rows_low = halves(tokens, swap(tokens, "head", 1), head)
    first_normed, first_normal, first_inverse = layer_norm(rows_low.astype(f32), norm_gains[0])
    first_low = first_normed.astype(bf16)

    joined_parts, others = tie(joined_parts, others)
    joined_parts = quarter(ordered_step, joined_parts, 1)
    others = quarter(ordered_step, others, 0)
    joined_parts, others = tie(joined_parts, others)
    joined_parts = quarter(ordered_step, joined_parts, 2)
    others = quarter(ordered_step, others, 1)
    joined_parts, others, first_low = tie(joined_parts, others, first_low)
    joined_parts = quarter(ordered_step, joined_parts, 3)
    moved = quarter(ordered_step, others, 2)

    joined_low = jnp.concatenate([gather_rows(part) for part in joined_parts], axis=1)
    joined = dot(joined_low, first_low, NT)
    width = joined.shape[0] // 3
    queries = (rotate(joined[:width], cosine, sine) * QUERY_SCALE).astype(bf16)
    keys = rotate(joined[width : 2 * width], cosine, sine).astype(bf16)
    values = joined[2 * width :].astype(bf16)
    others, queries, keys, values, low = tie(moved, queries, keys, values, low)
    moved = quarter(ordered_step, others, 3)
    attended, logsum = attention_forward(low, high, queries, keys, values, key_rows, query_rows)
    others, attended, logsum = tie(moved, attended, logsum)
    attended_other = swap(attended, "head", 1)
    expand_low = jnp.concatenate([gather_rows(part) for part in others[:2]], axis=1)
    both_low = gather_rows(others[2])
    mixer_low, shrink_turned = both_low[:, :mixer_width], both_low[:, mixer_width:].T
    mixer_other = swap(mixer_low, "head", 1)

    second_gain = norm_gains[1:2]
    middle, hidden, second_part, shrink_grad, expand_grad = feed_forward(
        rows_low, attended, attended_other, cotangent, second_gain,
        mixer_low, mixer_other, expand_low, shrink_turned,
    )
    second_other = swap(second_part, "head", 1)

    sums, second_other = tie([reduce_start(part) for part in halves_of(expand_grad)], second_other)
    moved = quarter(reduce_step, sums, 0)
    middle_grad, attended_grad, mixer_grad, second_gain_grad = norm_backward(
        middle, second_part, second_other, cotangent, second_gain, mixer_low, attended
    )
    second_gain_grad = 0.5 * second_gain_grad[0]
    both_sum = [reduce_start(jnp.concatenate([mixer_grad, shrink_grad.T], axis=1))]

    sums, attended_grad, shrink_now = tie(moved, attended_grad, shrink_turned)
    moved = quarter(reduce_step, sums, 1)

    def fed(columns):
        return dot(lax.dynamic_slice_in_dim(hidden, columns, local_rows, 1), shrink_now, TN)

    fed_other = fed((1 - head) * local_rows).astype(bf16)
    fed_own = fed(head * local_rows)

    sums, both_sum, fed_other, fed_own, low = tie(moved, both_sum, fed_other, fed_own, low)
    moved = quarter(reduce_step, sums, 2)
    both_moved = quarter(reduce_step, both_sum, 0, 2)
    fed_other = swap(fed_other, "head", 1)
    joined_back = attention_backward(
        low, high, queries, keys, values, attended_grad, attended, logsum, key_rows, query_rows,
        cosine, sine,
    )
    sums, both_sum, joined_back = tie(moved, both_moved, joined_back)
    moved = quarter(reduce_step, sums, 3)
    both_moved = quarter(reduce_step, both_sum, 1, 2)
    joined_grad = dot(joined_back, first_low, NN).astype(bf16)

    def first_part(start, weight):
        columns = lax.dynamic_slice_in_dim(joined_back, start, local_rows, 1)
        return dot(columns, weight, TN)

    sums, both_sum, joined_grad, joined_now = tie(moved, both_moved, joined_grad, joined_low)
    expand_next = 0.5 * expand_momentum[0] + jnp.concatenate(sums, axis=1)
    gathers = [gather_start(part) for part in halves_of(expand_next.astype(bf16))]
    sums = quarter(reduce_step, [reduce_start(part) for part in thirds(joined_grad)], 0)
    moved = quarter(gather_step, gathers, 0)
    both_moved = quarter(reduce_step, both_sum, 2, 2)
    first_other = swap(
        first_part((1 - head) * local_rows, joined_now).astype(bf16), "head", 1
    )
    first_mine = first_part(head * local_rows, joined_now)

    sums, gathers, both_sum, first_other, first_mine = tie(
        sums, moved, both_moved, first_other, first_mine
    )
    moved = quarter(reduce_step, sums, 1)
    gathers_moved = quarter(gather_step, gathers, 1)
    both_moved = quarter(reduce_step, both_sum, 3, 2)
    first_back = first_mine + first_other.astype(f32)
    own_normal = own_half(first_normal)
    first_gain_grad = jnp.sum(first_back * own_normal, axis=0)

    sums, gathers, both_sum, first_gain_grad, first_gain = tie(
        moved, gathers_moved, both_moved, first_gain_grad, norm_gains[0]
    )
    mixer_next = 0.5 * mixer_momentum[0] + both_sum[0][:, :mixer_width]
    shrink_next = 0.5 * shrink_momentum[0] + both_sum[0][:, mixer_width:]
    both_gather = [gather_start(jnp.concatenate([mixer_next, shrink_next], axis=1).astype(bf16))]
    gain_totals = jnp.stack([first_gain_grad, second_gain_grad])
    moved = quarter(reduce_step, sums, 2)
    gathers_moved = quarter(gather_step, gathers, 2)
    both_moved = quarter(gather_step, both_gather, 0, 2)
    gain_moved = total_step(gain_totals, 0)
    input_gradient = own_half(middle_grad) + norm_back(
        first_back, first_gain, own_normal, own_half(first_inverse)
    )

    sums, gathers, both_gather, gain_totals, input_gradient, fed_own = tie(
        moved, gathers_moved, both_moved, gain_moved, input_gradient, fed_own
    )
    moved = quarter(reduce_step, sums, 3)
    gathers_moved = quarter(gather_step, gathers, 3)
    both_moved = quarter(gather_step, both_gather, 1, 2)
    gain_moved = total_step(gain_totals, 1)
    layer_output = (own_half(middle) + fed_own + fed_other.astype(f32)).astype(bf16)

    sums, gathers, both_gather, gain_totals, layer_output = tie(
        moved, gathers_moved, both_moved, gain_moved, layer_output
    )
    joined_next = 0.5 * joined_momentum[0] + jnp.concatenate(sums, axis=1)
    joined_gather = [gather_start(part) for part in thirds(joined_next.astype(bf16))]
    moved = quarter(gather_step, joined_gather, 0)
    both_moved = quarter(gather_step, both_gather, 2, 2)
    gain_moved = total_step(gain_totals, 2)
    updated_expand = schulz(
        [gather_rows(part) for part in gathers], None, expand_next, expand_weight[0], "schulz_expand"
    )
    joined_gather, both_gather, gain_totals, updated_expand = tie(
        moved, both_moved, gain_moved, updated_expand
    )
    moved = quarter(gather_step, joined_gather, 1)
    both_moved = quarter(gather_step, both_gather, 3, 2)
    gain_moved = total_step(gain_totals, 3)
    joined_gather, both_gather, gain_totals = tie(moved, both_moved, gain_moved)
    both_full = [gather_rows(both_gather[0])]
    moved = quarter(gather_step, joined_gather, 2)
    gain_totals = total_step(gain_totals, 4)
    updated_shrink = schulz(
        both_full, mixer_width, shrink_next, shrink_weight[0], "schulz_shrink"
    )
    joined_gather, both_full, updated_shrink = tie(moved, both_full, updated_shrink)
    moved = quarter(gather_step, joined_gather, 3)
    updated_mixer = schulz(both_full, 0, mixer_next, mixer_weight[0], "schulz_mixer")
    joined_gather, updated_mixer = tie(moved, updated_mixer)
    updated_joined = schulz(
        [gather_rows(part) for part in joined_gather],
        None, joined_next, joined_weight[0], "schulz_joined",
    )

    momentum_gains = 0.5 * gain_momentum + gain_totals
    updated_gains = norm_gains - gain_rate * momentum_gains * lax.rsqrt(
        jnp.mean(momentum_gains * momentum_gains, axis=-1, keepdims=True) + 1e-06
    )
    return (
        layer_output,
        input_gradient,
        joined_next[None],
        mixer_next[None],
        expand_next[None],
        shrink_next[None],
        updated_joined[None],
        updated_mixer[None],
        updated_expand[None],
        updated_shrink[None],
        momentum_gains,
        updated_gains,
    )


def solution(mesh):
    rows = P(("dp", "head"), None)
    weight = P("head", "dp", None)
    return jax.shard_map(
        shards,
        mesh=mesh,
        in_specs=(rows, P("dp", None), P()) + (weight,) * 8 + (P(), P("dp", None)),
        out_specs=(rows, rows) + (weight,) * 8 + (P(), P()),
        check_vma=False,
    )
```

```python
import functools
import math

import jax
import jax.numpy as jnp
from jax import lax
from jax.experimental import pallas as pl
from jax.experimental.pallas import tpu as pltpu
from jax.sharding import PartitionSpec as P

HEAD_DIM = 64
NS_ITERS = 3

theta_base = 160000.0
norm_epsilon = 1e-05
ns_first = 3.4445
ns_second = -4.775
ns_third = 2.0315
muon_rate = 1.0
gain_rate = 0.3

bf16 = jnp.bfloat16
f32 = jnp.float32
LOG2E = math.log2(math.e)
QUERY_SCALE = 0.125 * LOG2E
SAFE_SCORE = 60.0
DEPTH = 128
TILE_Q = 256
TILE_K = 256
FWD_SKEW = 6
BWD_SKEW = 2

NN = (((1,), (0,)), ((), ()))
NT = (((1,), (1,)), ((), ()))
TN = (((0,), (0,)), ((), ()))
TT = (((0,), (1,)), ((), ()))
QUARTERS = 4
FEED_ROWS = 256
FEED_CHUNKS = 3
ERF_TOP = (
    -2.72614225801306e-10, 2.77068142495902e-08, -2.10102402082508e-06, -5.69250639462346e-05,
    -7.34990630326855e-04, -2.95459980854025e-03, -1.60960333262415e-02,
)
ERF_BOTTOM = (
    -1.45660718464996e-05, -2.13374055278905e-04, -1.68282697438203e-03, -7.37332916720468e-03,
    -1.42647390514189e-02,
)


def dot(left, right, dims):
    return lax.dot_general(left, right, dims, preferred_element_type=f32)


def key_bounds(length_row, row_count):
    ends = jnp.cumsum(length_row)
    starts = ends - length_row
    first = jnp.arange(row_count // TILE_Q, dtype=jnp.int32) * TILE_Q
    labels = jnp.arange(length_row.shape[0], dtype=jnp.int32)

    def pick(places, table):
        segment = jnp.sum((places[:, None] >= ends[None, :]).astype(jnp.int32), axis=1)
        return jnp.sum(jnp.where(segment[:, None] == labels[None, :], table[None, :], 0), axis=1)

    low = pick(first, starts) // TILE_K
    high = (pick(first + TILE_Q - 1, ends) + TILE_K - 1) // TILE_K
    return low.astype(jnp.int32), high.astype(jnp.int32)


def doc_tables(length_row, row_count):
    ends = jnp.cumsum(length_row)
    starts = ends - length_row
    count = length_row.shape[0]
    places = jnp.arange(row_count, dtype=jnp.int32)[None, :]
    member = (places >= starts[:, None]) & (places < ends[:, None])
    rest = jnp.zeros((16 - count, row_count), f32)
    key_rows = jnp.concatenate([member.astype(f32), rest], axis=0).astype(bf16)
    query_rows = jnp.concatenate([jnp.where(member, 0.0, -1e30), rest], axis=0).astype(bf16)
    doc_first = jnp.sum(jnp.where(member, starts[:, None], 0), axis=0, keepdims=True)
    position = (places - doc_first).astype(f32)
    half_dim = HEAD_DIM // 2
    frequency = jnp.exp(
        jnp.arange(half_dim, dtype=f32) * (-2.0 * math.log(theta_base) / HEAD_DIM)
    )
    angles = frequency[:, None] * position
    return key_rows, query_rows, jnp.cos(angles), jnp.sin(angles)


def rotate(values, cosine, sine):
    half = HEAD_DIM // 2
    heads = values.reshape(-1, HEAD_DIM, values.shape[1])
    low, high = heads[:, :half], heads[:, half:]
    turned = jnp.concatenate([low * cosine - high * sine, high * cosine + low * sine], axis=1)
    return turned.reshape(values.shape)


def rows16(parts):
    rest = jnp.zeros((16 - len(parts), parts[0].shape[1]), f32)
    return jnp.concatenate([part.astype(f32) for part in parts] + [rest], axis=0).astype(bf16)


def split3(value):
    first = value.astype(bf16)
    left = value - first.astype(f32)
    second = left.astype(bf16)
    third = (left - second.astype(f32)).astype(bf16)
    return [first, second, third]


def three_ones(count):
    return jnp.concatenate([jnp.ones((3, count), f32), jnp.zeros((13, count), f32)], axis=0).astype(
        bf16
    )


def forward_kernel(
    low, high, queries, keys, values, key_rows, query_rows, out, logsum, keys_in, values_in, queries_in, safe
):
    heads = queries.shape[0] // HEAD_DIM
    rows = keys.shape[1]
    step = pl.program_id(0)

    @pl.when(step == 0)
    def _():
        worst = jnp.zeros((1, 1), f32)
        ones = rows16([jnp.ones((1, rows), f32)])
        for h in range(heads):
            band = slice(h * HEAD_DIM, (h + 1) * HEAD_DIM)
            key = keys[band, :]
            pad = jnp.zeros((DEPTH - HEAD_DIM - 16, rows), bf16)
            keys_in[h] = jnp.concatenate([key, key_rows[...], pad], axis=0).T
            values_in[h, :HEAD_DIM, :] = values[band, :]
            values_in[h, HEAD_DIM:, :] = ones
            query_full = queries[band, :].astype(f32)
            key_full = key.astype(f32)
            query_top = jnp.max(
                jnp.sum(query_full * query_full, axis=0, keepdims=True), axis=1, keepdims=True
            )
            key_top = jnp.max(
                jnp.sum(key_full * key_full, axis=0, keepdims=True), axis=1, keepdims=True
            )
            worst = jnp.maximum(worst, query_top * key_top)
        safe[0] = jnp.where(worst[0, 0] <= SAFE_SCORE * SAFE_SCORE, 1, 0)

    first = pl.multiple_of(step * TILE_Q, TILE_Q)
    for h in range(heads):
        queries_in[h, :HEAD_DIM, :] = queries[h * HEAD_DIM : (h + 1) * HEAD_DIM, pl.ds(first, TILE_Q)]
        queries_in[h, HEAD_DIM : HEAD_DIM + 16, :] = query_rows[...]
        queries_in[h, HEAD_DIM + 16 :, :] = jnp.zeros((DEPTH - HEAD_DIM - 16, TILE_Q), bf16)

    def finish(peaks, totals):
        for h in range(heads):
            weight = totals[h][HEAD_DIM : HEAD_DIM + 1, :]
            out[h * HEAD_DIM : (h + 1) * HEAD_DIM, :] = (totals[h][:HEAD_DIM, :] / weight).astype(bf16)
            level = jnp.log2(weight)
            logsum[h : h + 1, :] = level if peaks is None else peaks[h] + level

    empty = tuple(jnp.zeros((HEAD_DIM + 16, TILE_Q), f32) for _ in range(heads))

    @pl.when(safe[0] == 1)
    def _():
        def block(j, totals):
            span = pl.ds(pl.multiple_of(j * TILE_K, TILE_K), TILE_K)
            result = [None] * heads
            waiting = {}
            for t in range(heads + FWD_SKEW):
                if t < heads:
                    waiting[t] = dot(keys_in[t, span, :], queries_in[t], NN)
                h = t - FWD_SKEW
                if h >= 0:
                    raised = jnp.exp2(waiting.pop(h)).astype(bf16)
                    result[h] = totals[h] + dot(values_in[h, :, span], raised, NN)
            return tuple(result)

        finish(None, lax.fori_loop(low[step], high[step], block, empty))

    @pl.when(safe[0] == 0)
    def _():
        def block(j, carry):
            peaks, totals = carry
            span = pl.ds(pl.multiple_of(j * TILE_K, TILE_K), TILE_K)
            new_peaks = []
            new_totals = []
            for h in range(heads):
                scores = dot(keys_in[h, span, :], queries_in[h], NN)
                peak = jnp.maximum(peaks[h], jnp.max(scores, axis=0, keepdims=True))
                raised = jnp.exp2(scores - peak).astype(bf16)
                new_totals.append(
                    totals[h] * jnp.exp2(peaks[h] - peak) + dot(values_in[h, :, span], raised, NN)
                )
                new_peaks.append(peak)
            return tuple(new_peaks), tuple(new_totals)

        lowest = tuple(jnp.full((1, TILE_Q), -3e38, f32) for _ in range(heads))
        finish(*lax.fori_loop(low[step], high[step], block, (lowest, empty)))


def attention_forward(low, high, queries, keys, values, key_rows, query_rows):
    width, rows = queries.shape
    heads = width // HEAD_DIM

    def full(count):
        return pl.BlockSpec((count, rows), lambda i, low, high: (0, 0))

    def tile(count):
        return pl.BlockSpec((count, TILE_Q), lambda i, low, high: (0, i))

    return pl.pallas_call(
        forward_kernel,
        out_shape=(
            jax.ShapeDtypeStruct((width, rows), bf16),
            jax.ShapeDtypeStruct((heads, rows), f32),
        ),
        grid_spec=pltpu.PrefetchScalarGridSpec(
            num_scalar_prefetch=2,
            grid=(rows // TILE_Q,),
            in_specs=[full(width), full(width), full(width), full(16), tile(16)],
            out_specs=[tile(width), tile(heads)],
            scratch_shapes=[
                pltpu.VMEM((heads, rows, DEPTH), bf16),
                pltpu.VMEM((heads, HEAD_DIM + 16, rows), bf16),
                pltpu.VMEM((heads, DEPTH, TILE_Q), bf16),
                pltpu.SMEM((1,), jnp.int32),
            ],
        ),
        compiler_params=pltpu.CompilerParams(
            dimension_semantics=("arbitrary",), vmem_limit_bytes=40 << 20
        ),
        name="attention_forward",
    )(low, high, queries, keys, values, key_rows, query_rows)


def backward_kernel(
    low, high, queries, keys, values, grads, outs, logsum, key_rows, query_rows, cosine, sine,
    joined_back, *scratch
):
    heads = queries.shape[0] // HEAD_DIM
    rows = keys.shape[1]
    keys_in, values_in, queries_in, grads_in = scratch[:4]
    key_sum = scratch[4 : 4 + heads]
    value_sum = scratch[4 + heads : 4 + 2 * heads]
    query_sum = scratch[4 + 2 * heads : 4 + 3 * heads]
    step = pl.program_id(0)

    @pl.when(step == 0)
    def _():
        ones = three_ones(rows)
        for h in range(heads):
            band = slice(h * HEAD_DIM, (h + 1) * HEAD_DIM)
            pad = jnp.zeros((DEPTH - HEAD_DIM - 32, rows), bf16)
            keys_in[h] = jnp.concatenate([keys[band, :], key_rows[...], ones, pad], axis=0).T
            pad = jnp.zeros((DEPTH - HEAD_DIM - 16, rows), bf16)
            values_in[h] = jnp.concatenate([values[band, :], ones, pad], axis=0).T
            key_sum[h][...] = jnp.zeros((HEAD_DIM, rows), f32)
            value_sum[h][...] = jnp.zeros((HEAD_DIM, rows), f32)

    for h in range(heads):
        band = slice(h * HEAD_DIM, (h + 1) * HEAD_DIM)
        queries_in[h, :HEAD_DIM, :] = queries[band, :]
        queries_in[h, HEAD_DIM : HEAD_DIM + 16, :] = query_rows[...]
        queries_in[h, HEAD_DIM + 16 : HEAD_DIM + 32, :] = rows16(split3(-logsum[h : h + 1, :]))
        queries_in[h, HEAD_DIM + 32 :, :] = jnp.zeros((DEPTH - HEAD_DIM - 32, TILE_Q), bf16)
        inner = jnp.sum(grads[band, :].astype(f32) * outs[band, :].astype(f32), axis=0, keepdims=True)
        grads_in[h, :HEAD_DIM, :] = grads[band, :]
        grads_in[h, HEAD_DIM : HEAD_DIM + 16, :] = rows16(split3(-inner))
        grads_in[h, HEAD_DIM + 16 :, :] = jnp.zeros((DEPTH - HEAD_DIM - 16, TILE_Q), bf16)
        query_sum[h][...] = jnp.zeros((HEAD_DIM, TILE_Q), f32)

    def block(j, carry):
        span = pl.ds(pl.multiple_of(j * TILE_K, TILE_K), TILE_K)
        waiting = {}
        for t in range(heads + BWD_SKEW):
            if t < heads:
                waiting[t] = (
                    dot(keys_in[t, span, :], queries_in[t], NN),
                    dot(values_in[t, span, :], grads_in[t], NN),
                )
            h = t - BWD_SKEW
            if h < 0:
                continue
            band = slice(h * HEAD_DIM, (h + 1) * HEAD_DIM)
            scores, weight_grad = waiting.pop(h)
            softmax = jnp.exp2(scores)
            score_grad = (softmax * weight_grad).astype(bf16)
            value_sum[h][:, span] += dot(grads[band, :], softmax.astype(bf16), NT)
            key_sum[h][:, span] += dot(queries[band, :], score_grad, NT)
            query_sum[h][...] += dot(keys[band, span], score_grad, NN)
        return carry

    lax.fori_loop(low[step], high[step], block, 0)

    def store(offset, columns, value):
        half = HEAD_DIM // 2
        upper, lower = value[:half], value[half:]
        cos, sin = cosine[:, columns], sine[:, columns]
        joined_back[offset : offset + half, columns] = (upper * cos + lower * sin).astype(bf16)
        joined_back[offset + half : offset + HEAD_DIM, columns] = (lower * cos - upper * sin).astype(bf16)

    width = heads * HEAD_DIM
    columns = pl.ds(pl.multiple_of(step * TILE_Q, TILE_Q), TILE_Q)
    for h in range(heads):
        store(h * HEAD_DIM, columns, query_sum[h][...] * 0.125)

    @pl.when(step == pl.num_programs(0) - 1)
    def _():
        for h in range(heads):
            first = width + h * HEAD_DIM
            store(first, slice(0, rows), key_sum[h][...] * (1.0 / LOG2E))
            first += width
            joined_back[first : first + HEAD_DIM, :] = value_sum[h][...].astype(bf16)


def attention_backward(
    low, high, queries, keys, values, grads, outs, logsum, key_rows, query_rows, cosine, sine
):
    width, rows = queries.shape
    heads = width // HEAD_DIM

    def full(count):
        return pl.BlockSpec((count, rows), lambda i, low, high: (0, 0))

    def tile(count):
        return pl.BlockSpec((count, TILE_Q), lambda i, low, high: (0, i))

    return pl.pallas_call(
        backward_kernel,
        out_shape=jax.ShapeDtypeStruct((3 * width, rows), bf16),
        grid_spec=pltpu.PrefetchScalarGridSpec(
            num_scalar_prefetch=2,
            grid=(rows // TILE_Q,),
            in_specs=[
                tile(width), full(width), full(width), tile(width), tile(width), tile(heads),
                full(16), tile(16), full(HEAD_DIM // 2), full(HEAD_DIM // 2),
            ],
            out_specs=full(3 * width),
            scratch_shapes=[
                pltpu.VMEM((heads, rows, DEPTH), bf16),
                pltpu.VMEM((heads, rows, DEPTH), bf16),
                pltpu.VMEM((heads, DEPTH, TILE_Q), bf16),
                pltpu.VMEM((heads, DEPTH, TILE_Q), bf16),
            ]
            + [pltpu.VMEM((HEAD_DIM, rows), f32)] * (2 * heads)
            + [pltpu.VMEM((HEAD_DIM, TILE_Q), f32)] * heads,
        ),
        compiler_params=pltpu.CompilerParams(
            dimension_semantics=("arbitrary",), vmem_limit_bytes=52 << 20
        ),
        name="attention_backward",
    )(low, high, queries, keys, values, grads, outs, logsum, key_rows, query_rows, cosine, sine)


def layer_norm(values, gain_row):
    centred = values - jnp.mean(values, axis=-1, keepdims=True)
    inverse = lax.rsqrt(jnp.mean(centred * centred, axis=-1, keepdims=True) + norm_epsilon)
    normal = centred * inverse
    return normal * gain_row, normal, inverse


def norm_back(upstream, gain_row, normal, inverse):
    scaled = upstream * gain_row
    inner_mean = jnp.mean(scaled * normal, axis=-1, keepdims=True)
    return inverse * (scaled - jnp.mean(scaled, axis=-1, keepdims=True) - normal * inner_mean)


def horner(square, factors):
    total = factors[0] * square + factors[1]
    for factor in factors[2:]:
        total = total * square + factor
    return total


def error_function(value):
    value = jnp.clip(value, -4.0, 4.0)
    square = value * value
    return value * horner(square, ERF_TOP) / horner(square, ERF_BOTTOM)


def turn(value):
    columns = value.shape[1]
    rest = jnp.zeros((value.shape[0], -columns % 128), value.dtype)
    return jnp.concatenate([value, rest], axis=1).T[:columns, :]


def turn_back(value):
    lines = value.shape[0]
    rest = jnp.zeros((-lines % 128, value.shape[1]), value.dtype)
    return jnp.concatenate([value, rest], axis=0).T[:, :lines]


def first_kernel(head, own, other, gain, rows, normed):
    tiles = pl.num_programs(0) // 2
    mine = pl.program_id(0) // tiles == head[0]
    value = jnp.where(mine, own[...].astype(f32), other[...].astype(f32))
    rows[...] = value.astype(bf16)
    normed[...] = layer_norm(value, gain[...])[0].astype(bf16)


def first_norm(head, own, other, gain):
    half, width = own.shape
    tiles = half // FEED_ROWS
    result = jax.ShapeDtypeStruct((2 * half, width), bf16)
    spec = pl.BlockSpec((FEED_ROWS, width), lambda i, head: (i, 0))
    return pl.pallas_call(
        first_kernel,
        out_shape=(result, result),
        grid_spec=pltpu.PrefetchScalarGridSpec(
            num_scalar_prefetch=1,
            grid=(2 * tiles,),
            in_specs=[
                pl.BlockSpec(
                    (FEED_ROWS, width),
                    lambda i, head: (jnp.clip(i - head[0] * tiles, 0, tiles - 1), 0),
                ),
                pl.BlockSpec(
                    (FEED_ROWS, width),
                    lambda i, head: (jnp.clip(i - (1 - head[0]) * tiles, 0, tiles - 1), 0),
                ),
                pl.BlockSpec((1, width), lambda i, head: (0, 0)),
            ],
            out_specs=[spec, spec],
        ),
        compiler_params=pltpu.CompilerParams(dimension_semantics=("arbitrary",)),
        name="first_norm",
    )(head, own, other, gain)


def gradient_kernel(back, normed, grad, total):
    step = pl.program_id(0)

    @pl.when(step == 0)
    def _():
        total[...] = dot(back[...], normed[...], NN)

    @pl.when(step > 0)
    def _():
        total[...] += dot(back[...], normed[...], NN)

    @pl.when(step == pl.num_programs(0) - 1)
    def _():
        grad[...] = total[...].astype(bf16)


def joined_gradient(back, normed):
    lines, count = back.shape
    width = normed.shape[1]
    tile = 2 * FEED_ROWS
    return pl.pallas_call(
        gradient_kernel,
        grid=(count // tile,),
        in_specs=[
            pl.BlockSpec((lines, tile), lambda i: (0, i)),
            pl.BlockSpec((tile, width), lambda i: (i, 0)),
        ],
        out_specs=pl.BlockSpec((lines, width), lambda i: (0, 0)),
        out_shape=jax.ShapeDtypeStruct((lines, width), bf16),
        scratch_shapes=[pltpu.VMEM((lines, width), f32)],
        compiler_params=pltpu.CompilerParams(
            dimension_semantics=("arbitrary",), vmem_limit_bytes=32 << 20
        ),
        name="joined_gradient",
    )(back, normed)


def pull_kernel(head, back, weight, out):
    out[...] = dot(back[...].T, weight[...], NN).astype(bf16)


def pull_other(head, back, weight):
    lines, count = back.shape
    width = weight.shape[1]
    tiles = count // 2 // FEED_ROWS
    return pl.pallas_call(
        pull_kernel,
        out_shape=jax.ShapeDtypeStruct((count // 2, width), bf16),
        grid_spec=pltpu.PrefetchScalarGridSpec(
            num_scalar_prefetch=1,
            grid=(tiles,),
            in_specs=[
                pl.BlockSpec((lines, FEED_ROWS), lambda i, head: (0, (1 - head[0]) * tiles + i)),
                pl.BlockSpec((lines, width), lambda i, head: (0, 0)),
            ],
            out_specs=pl.BlockSpec((FEED_ROWS, width), lambda i, head: (i, 0)),
        ),
        compiler_params=pltpu.CompilerParams(
            dimension_semantics=("arbitrary",), vmem_limit_bytes=24 << 20
        ),
        name="pull_other",
    )(head, back, weight)


def input_kernel(head, back, weight, other, rows, middle_grad, gain, input_grad, gain_grad):
    @pl.when(pl.program_id(0) == 0)
    def _():
        gain_grad[...] = jnp.zeros(gain_grad.shape, f32)

    pulled = dot(back[...].T, weight[...], NN) + other[...].astype(f32)
    unused, normal, inverse = layer_norm(rows[...].astype(f32), gain[...])
    input_grad[...] = middle_grad[...] + norm_back(pulled, gain[...], normal, inverse)
    gain_grad[...] += jnp.sum(pulled * normal, axis=0, keepdims=True)


def input_backward(head, back, weight, other, rows, middle_grad, gain):
    lines, count = back.shape
    width = weight.shape[1]
    tiles = count // 2 // FEED_ROWS

    def down():
        return pl.BlockSpec((FEED_ROWS, width), lambda i, head: (i, 0))

    return pl.pallas_call(
        input_kernel,
        out_shape=(
            jax.ShapeDtypeStruct((count // 2, width), f32),
            jax.ShapeDtypeStruct((1, width), f32),
        ),
        grid_spec=pltpu.PrefetchScalarGridSpec(
            num_scalar_prefetch=1,
            grid=(tiles,),
            in_specs=[
                pl.BlockSpec((lines, FEED_ROWS), lambda i, head: (0, head[0] * tiles + i)),
                pl.BlockSpec((lines, width), lambda i, head: (0, 0)),
                down(),
                down(),
                pl.BlockSpec((FEED_ROWS, width), lambda i, head: (head[0] * tiles + i, 0)),
                pl.BlockSpec((1, width), lambda i, head: (0, 0)),
            ],
            out_specs=[down(), pl.BlockSpec((1, width), lambda i, head: (0, 0))],
        ),
        compiler_params=pltpu.CompilerParams(
            dimension_semantics=("arbitrary",), vmem_limit_bytes=24 << 20
        ),
        name="input_backward",
    )(head, back, weight, other, rows, middle_grad, gain)


def feed_kernel(
    rows, attended, attended_other, upstream, gain, both, mixer_other, expand_left, expand_right,
    middle, hidden, second_part, shrink_grad, expand_grad, shrink_sum, expand_sum, expand, shrink
):
    step = pl.program_id(0)
    mixed, units = attended.shape[0], shrink.shape[0]
    chunk = units // FEED_CHUNKS

    @pl.when(step == 0)
    def _():
        expand[:, : expand_left.shape[1]] = expand_left[...]
        expand[:, expand_left.shape[1] :] = expand_right[...]
        shrink[...] = turn(both[:, mixed:])
        shrink_sum[...] = jnp.zeros(shrink_sum.shape, f32)
        expand_sum[...] = jnp.zeros(expand_sum.shape, f32)

    total = rows[...].astype(f32) + dot(attended[...].T, both[:, :mixed], NT)
    total = total + dot(attended_other[...].T, mixer_other[...], NT)
    middle[...] = total
    normed = layer_norm(total, gain[...])[0].astype(bf16)
    above = upstream[...]

    def project(c):
        first = slice(c * chunk, (c + 1) * chunk)
        second = slice(units + c * chunk, units + (c + 1) * chunk)
        return (
            dot(expand[first, :], normed, NT),
            dot(expand[second, :], normed, NT),
            dot(shrink[first, :], above, NT),
        )

    waiting = project(0)
    back = jnp.zeros(total.shape, f32)
    for c in range(FEED_CHUNKS):
        active, linear, grad = waiting
        if c + 1 < FEED_CHUNKS:
            waiting = project(c + 1)
        first = slice(c * chunk, (c + 1) * chunk)
        second = slice(units + c * chunk, units + (c + 1) * chunk)
        area = 0.5 * error_function(active * math.sqrt(0.5)) + 0.5
        gate = active * area
        density = jnp.exp(-0.5 * active * active) * (1.0 / math.sqrt(2.0 * math.pi))
        unit = (gate * linear).astype(bf16)
        active_back = (grad * linear * (area + active * density)).astype(bf16)
        linear_back = (grad * gate).astype(bf16)
        hidden[first, :] = unit
        shrink_sum[first, :] += dot(unit, above, NN)
        expand_sum[first, :] += dot(active_back, normed, NN)
        expand_sum[second, :] += dot(linear_back, normed, NN)
        back = back + dot(active_back, expand[first, :], TN) + dot(linear_back, expand[second, :], TN)
    second_part[...] = back.astype(bf16)

    @pl.when(step == pl.num_programs(0) - 1)
    def _():
        shrink_grad[...] = shrink_sum[...].astype(bf16)
        expand_grad[...] = expand_sum[...].astype(bf16)


def feed_forward(rows, attended, attended_other, upstream, gain, both, mixer_other, expand):
    count, width = rows.shape
    mixed, units = attended.shape[0], expand[0].shape[0] // 2

    def full(*shape):
        return pl.BlockSpec(shape, lambda i: (0, 0))

    def down(columns):
        return pl.BlockSpec((FEED_ROWS, columns), lambda i: (i, 0))

    def along(lines):
        return pl.BlockSpec((lines, FEED_ROWS), lambda i: (0, i))

    return pl.pallas_call(
        feed_kernel,
        grid=(count // FEED_ROWS,),
        in_specs=[
            down(width), along(mixed), along(mixed), down(width), full(1, width),
            full(*both.shape), full(width, mixed), full(*expand[0].shape), full(*expand[1].shape),
        ],
        out_specs=[
            down(width), along(units), down(width), full(units, width), full(2 * units, width),
        ],
        out_shape=(
            jax.ShapeDtypeStruct((count, width), f32),
            jax.ShapeDtypeStruct((units, count), bf16),
            jax.ShapeDtypeStruct((count, width), bf16),
            jax.ShapeDtypeStruct((units, width), bf16),
            jax.ShapeDtypeStruct((2 * units, width), bf16),
        ),
        scratch_shapes=[
            pltpu.VMEM((units, width), f32),
            pltpu.VMEM((2 * units, width), f32),
            pltpu.VMEM((2 * units, width), bf16),
            pltpu.VMEM((units, width), bf16),
        ],
        compiler_params=pltpu.CompilerParams(
            dimension_semantics=("arbitrary",), vmem_limit_bytes=48 << 20
        ),
        name="feed_forward",
    )(rows, attended, attended_other, upstream, gain, both, mixer_other, *expand)


def norm_kernel(
    middle, own, other, upstream, gain, both, attended, shrink_grad,
    middle_grad, attended_grad, both_grad, gain_grad, mixer_turned, mixer_sum
):
    step = pl.program_id(0)

    @pl.when(step == 0)
    def _():
        mixer_turned[...] = both[:, : attended.shape[0]].T
        mixer_sum[...] = jnp.zeros(mixer_sum.shape, f32)
        gain_grad[...] = jnp.zeros(gain_grad.shape, f32)

    unused, normal, inverse = layer_norm(middle[...], gain[...])
    back = own[...].astype(f32) + other[...].astype(f32)
    grad = upstream[...].astype(f32) + norm_back(back, gain[...], normal, inverse)
    middle_grad[...] = grad
    grad_low = grad.astype(bf16)
    attended_grad[...] = dot(mixer_turned[...], grad_low, NT).astype(bf16)
    mixer_sum[...] += dot(attended[...], grad_low, NN)
    gain_grad[...] += jnp.sum(back * normal, axis=0, keepdims=True)

    @pl.when(step == pl.num_programs(0) - 1)
    def _():
        mixed = attended.shape[0]
        both_grad[:, :mixed] = mixer_sum[...].T.astype(bf16)
        both_grad[:, mixed:] = turn_back(shrink_grad[...])


def norm_backward(middle, own, other, upstream, gain, both, attended, shrink_grad):
    count, width = middle.shape
    mixed = attended.shape[0]

    def full(*shape):
        return pl.BlockSpec(shape, lambda i: (0, 0))

    def down(columns):
        return pl.BlockSpec((FEED_ROWS, columns), lambda i: (i, 0))

    def along(lines):
        return pl.BlockSpec((lines, FEED_ROWS), lambda i: (0, i))

    return pl.pallas_call(
        norm_kernel,
        grid=(count // FEED_ROWS,),
        in_specs=[
            down(width), down(width), down(width), down(width), full(1, width),
            full(*both.shape), along(mixed), full(*shrink_grad.shape),
        ],
        out_specs=[down(width), along(mixed), full(*both.shape), full(1, width)],
        out_shape=(
            jax.ShapeDtypeStruct((count, width), f32),
            jax.ShapeDtypeStruct((mixed, count), bf16),
            jax.ShapeDtypeStruct(both.shape, bf16),
            jax.ShapeDtypeStruct((1, width), f32),
        ),
        scratch_shapes=[pltpu.VMEM((mixed, width), bf16), pltpu.VMEM((mixed, width), f32)],
        compiler_params=pltpu.CompilerParams(
            dimension_semantics=("arbitrary",), vmem_limit_bytes=40 << 20
        ),
        name="norm_backward",
    )(middle, own, other, upstream, gain, both, attended, shrink_grad)


def swap(value, axis, bit):
    count = lax.axis_size(axis)
    return lax.ppermute(value, axis, [(i, i ^ bit) for i in range(count)])


def bit_orders():
    bits = lax.axis_size("dp").bit_length() - 1
    return [[(start + k) % (bits - 1) for k in range(bits - 1)] + [bits - 1] for start in range(3)]


def steps_count():
    return lax.axis_size("dp").bit_length() - 1


def reduce_start(value):
    bits = steps_count()
    rows = value.shape[0] >> bits
    return value.reshape((2,) * bits + (rows, value.shape[1]))


def reduce_step(held, step, which):
    bits = steps_count()
    bit = bit_orders()[which][step]
    axis = bits - 1 - bit
    side = (lax.axis_index("dp") >> bit) & 1
    kept = lax.dynamic_slice_in_dim(held, side, 1, axis)
    sent = lax.dynamic_slice_in_dim(held, 1 - side, 1, axis)
    total = kept.astype(f32) + swap(sent, "dp", 1 << bit).astype(f32)
    if step + 1 == bits:
        return total.reshape(held.shape[-2:])
    return total.astype(bf16)


def gather_start(value):
    return value[(None,) * steps_count()]


def gather_step(held, step, which):
    bits = steps_count()
    bit = bit_orders()[which][bits - 1 - step]
    return jnp.concatenate([held, swap(held, "dp", 1 << bit)], axis=bits - 1 - bit)


def ordered_step(held, step, which):
    bits = steps_count()
    bit = bit_orders()[which][bits - 1 - step]
    got = swap(held, "dp", 1 << bit)
    low_side = ((lax.axis_index("dp") >> bit) & 1) == 0
    return jnp.concatenate(
        [jnp.where(low_side, held, got), jnp.where(low_side, got, held)], axis=bits - 1 - bit
    )


def gather_rows(held):
    return held.reshape(-1, held.shape[-1])


def thirds(value):
    unit = value.shape[1] // 3 // 128 * 128
    return [value[:, :unit], value[:, unit : 2 * unit], value[:, 2 * unit :]]


def halves_of(value):
    unit = value.shape[1] // 256 * 128
    return [value[:, :unit], value[:, unit:]]


def quarter(step, states, part, first=0):
    bits = steps_count()
    for index in range(bits * part // QUARTERS, bits * (part + 1) // QUARTERS):
        states = [step(state, index, first + which) for which, state in enumerate(states)]
    return states


def tie(*values):
    return lax.optimization_barrier(values)


def total_step(value, part):
    if part == 0:
        return value + swap(value, "head", 1)
    bits = steps_count()
    for bit in range(bits * (part - 1) // QUARTERS, bits * part // QUARTERS):
        value = value + swap(value, "dp", 1 << bit)
    return value


def schulz_start(held, own, gram, low):
    down = 0
    for left in held:
        along = 0
        for right in held:
            gram[down : down + left.shape[1], along : along + right.shape[1]] = dot(left, right, TN)
            along += right.shape[1]
        down += left.shape[1]
    shape = gram.shape
    diagonal = lax.broadcasted_iota(jnp.int32, shape, 0) == lax.broadcasted_iota(jnp.int32, shape, 1)
    trace = jnp.sum(jnp.where(diagonal, gram[...], 0.0), axis=0, keepdims=True)
    norm_value = jnp.sqrt(jnp.sum(trace, axis=1, keepdims=True)) + 1e-07
    gram[...] = gram[...] * (1.0 / (norm_value * norm_value))
    low[...] = gram[...].astype(bf16)
    return own[...] / norm_value


def schulz_steps(rows, gram, low, change, first, stop):
    columns = gram.shape[0]
    lines = 256 if columns % 256 == 0 else columns

    def per_block(body):
        def run(index, carry):
            body(pl.ds(pl.multiple_of(index * lines, lines), lines))
            return carry

        lax.fori_loop(0, columns // lines, run, 0)

    def form_change(block):
        squared = dot(low[block, :], low[...], NN)
        change[block, :] = (ns_second * gram[block, :] + ns_third * squared).astype(bf16)

    def next_gram(block):
        once = ns_first * gram[block, :] + dot(low[block, :], change[...], NN)
        twice = ns_first * once + dot(once.astype(bf16), change[...], NN)
        gram[block, :] = twice
        low[block, :] = twice.astype(bf16)

    for iteration in range(first, stop):
        per_block(form_change)
        rows = ns_first * rows + dot(rows.astype(bf16), change[...], NN)
        if iteration + 1 < NS_ITERS:
            per_block(next_gram)
    return rows


def whole_kernel(*refs, count, offset, scale):
    parts = refs[:count]
    own, weight, updated, gram, low, change = refs[count:]
    if offset is None:
        held = [part[...] for part in parts]
    else:
        held = [parts[0][:, offset : offset + gram.shape[0]]]
    rows = schulz_start(held, own, gram, low)
    updated[...] = weight[...] - scale * schulz_steps(rows, gram, low, change, 0, NS_ITERS)


def early_kernel(*refs, count):
    own, rows, gram_out, low_out, gram, low, change = refs[count:]
    start = schulz_start([part[...] for part in refs[:count]], own, gram, low)
    rows[...] = start
    gram_out[...] = gram[...]
    low_out[...] = low[...]


def late_kernel(rows, gram_in, low_in, weight, updated, gram, low, change, *, scale):
    gram[...] = gram_in[...]
    low[...] = low_in[...]
    done = schulz_steps(rows[...], gram, low, change, 0, NS_ITERS)
    updated[...] = weight[...] - scale * done


def square_scratch(columns):
    return [
        pltpu.VMEM((columns, columns), f32),
        pltpu.VMEM((columns, columns), bf16),
        pltpu.VMEM((columns, columns), bf16),
    ]


def shape_scale(rows, columns):
    return muon_rate * math.sqrt(rows / columns)


def schulz(parts, offset, own, weight, name):
    columns = own.shape[1]
    return pl.pallas_call(
        functools.partial(
            whole_kernel, count=len(parts), offset=offset, scale=shape_scale(parts[0].shape[0], columns)
        ),
        out_shape=jax.ShapeDtypeStruct(own.shape, f32),
        scratch_shapes=square_scratch(columns),
        compiler_params=pltpu.CompilerParams(vmem_limit_bytes=40 << 20),
        name=name,
    )(*parts, own, weight)


def schulz_early(parts, own):
    columns = own.shape[1]
    return pl.pallas_call(
        functools.partial(early_kernel, count=len(parts)),
        out_shape=(
            jax.ShapeDtypeStruct(own.shape, f32),
            jax.ShapeDtypeStruct((columns, columns), f32),
            jax.ShapeDtypeStruct((columns, columns), bf16),
        ),
        scratch_shapes=square_scratch(columns),
        compiler_params=pltpu.CompilerParams(vmem_limit_bytes=40 << 20),
        name="schulz_early",
    )(*parts, own)


def schulz_late(state, weight, rows):
    columns = weight.shape[1]
    return pl.pallas_call(
        functools.partial(late_kernel, scale=shape_scale(rows, columns)),
        out_shape=jax.ShapeDtypeStruct(weight.shape, f32),
        scratch_shapes=square_scratch(columns),
        compiler_params=pltpu.CompilerParams(vmem_limit_bytes=40 << 20),
        name="schulz_late",
    )(*state, weight)


def shards(
    tokens,
    lengths,
    norm_gains,
    joined_weight,
    mixer_weight,
    expand_weight,
    shrink_weight,
    joined_momentum,
    mixer_momentum,
    expand_momentum,
    shrink_momentum,
    gain_momentum,
    cotangent,
):
    row_count = cotangent.shape[0]
    local_rows = tokens.shape[0]
    head = lax.axis_index("head")
    mixer_width = mixer_weight.shape[2]

    def own_half(value):
        return lax.dynamic_slice_in_dim(value, head * local_rows, local_rows, 0)

    joined_parts = [gather_start(part) for part in thirds(joined_weight[0].astype(bf16))]
    joined_parts = quarter(ordered_step, joined_parts, 0)
    others = [gather_start(part) for part in halves_of(expand_weight[0].astype(bf16))] + [
        gather_start(jnp.concatenate([mixer_weight[0], shrink_weight[0]], axis=1).astype(bf16))
    ]
    key_rows, query_rows, cosine, sine = doc_tables(lengths[0], row_count)
    low, high = key_bounds(lengths[0], row_count)
    head_place = head[None]
    rows_low, first_low = first_norm(head_place, tokens, swap(tokens, "head", 1), norm_gains[0:1])

    joined_parts, others = tie(joined_parts, others)
    joined_parts = quarter(ordered_step, joined_parts, 1)
    others = quarter(ordered_step, others, 0)
    joined_parts, others = tie(joined_parts, others)
    joined_parts = quarter(ordered_step, joined_parts, 2)
    others = quarter(ordered_step, others, 1)
    joined_parts, others, first_low = tie(joined_parts, others, first_low)
    joined_parts = quarter(ordered_step, joined_parts, 3)
    moved = quarter(ordered_step, others, 2)

    joined_low = jnp.concatenate([gather_rows(part) for part in joined_parts], axis=1)
    joined = dot(joined_low, first_low, NT)
    width = joined.shape[0] // 3
    queries = (rotate(joined[:width], cosine, sine) * QUERY_SCALE).astype(bf16)
    keys = rotate(joined[width : 2 * width], cosine, sine).astype(bf16)
    values = joined[2 * width :].astype(bf16)
    others, queries, keys, values, low = tie(moved, queries, keys, values, low)
    moved = quarter(ordered_step, others, 3)
    attended, logsum = attention_forward(low, high, queries, keys, values, key_rows, query_rows)
    others, attended, logsum = tie(moved, attended, logsum)
    attended_other = swap(attended, "head", 1)
    both_low = gather_rows(others[2])
    mixer_other = swap(both_low[:, :mixer_width], "head", 1)

    second_gain = norm_gains[1:2]
    middle, hidden, second_part, shrink_grad, expand_grad = feed_forward(
        rows_low, attended, attended_other, cotangent, second_gain,
        both_low, mixer_other, [gather_rows(part) for part in others[:2]],
    )
    second_other = swap(second_part, "head", 1)

    moved = quarter(reduce_step, [reduce_start(part) for part in halves_of(expand_grad)], 0)
    middle_grad, attended_grad, both_grad, second_gain_grad = norm_backward(
        middle, second_part, second_other, cotangent, second_gain, both_low, attended, shrink_grad
    )
    both_sum = [reduce_start(both_grad)]

    sums, attended_grad, both_now = tie(moved, attended_grad, both_low)
    moved = quarter(reduce_step, sums, 1)

    def fed(columns):
        units = lax.dynamic_slice_in_dim(hidden, columns, local_rows, 1)
        return dot(units, both_now[:, mixer_width:], TT)

    fed_other = fed((1 - head) * local_rows).astype(bf16)
    fed_own = fed(head * local_rows)

    sums, both_sum, fed_other, fed_own, low = tie(moved, both_sum, fed_other, fed_own, low)
    moved = quarter(reduce_step, sums, 2)
    both_moved = quarter(reduce_step, both_sum, 0, 2)
    fed_other = swap(fed_other, "head", 1)
    joined_back = attention_backward(
        low, high, queries, keys, values, attended_grad, attended, logsum, key_rows, query_rows,
        cosine, sine,
    )
    sums, both_sum, joined_back = tie(moved, both_moved, joined_back)
    moved = quarter(reduce_step, sums, 3)
    both_moved = quarter(reduce_step, both_sum, 1, 2)
    joined_grad = joined_gradient(joined_back, first_low)

    sums, both_sum, joined_grad, joined_now = tie(moved, both_moved, joined_grad, joined_low)
    expand_next = 0.5 * expand_momentum[0] + jnp.concatenate(sums, axis=1)
    gathers = [gather_start(part) for part in halves_of(expand_next.astype(bf16))]
    sums = quarter(reduce_step, [reduce_start(part) for part in thirds(joined_grad)], 0)
    moved = quarter(gather_step, gathers, 0)
    both_moved = quarter(reduce_step, both_sum, 2, 2)
    first_other = pull_other(head_place, joined_back, joined_now)

    sums, gathers, both_sum, first_other, fed_own = tie(sums, moved, both_moved, first_other, fed_own)
    first_other = swap(first_other, "head", 1)
    moved = quarter(reduce_step, sums, 1)
    gathers_moved = quarter(gather_step, gathers, 1)
    both_moved = quarter(reduce_step, both_sum, 3, 2)
    layer_output = (own_half(middle) + fed_own + fed_other.astype(f32)).astype(bf16)

    sums, gathers, both_sum, first_other, layer_output = tie(
        moved, gathers_moved, both_moved, first_other, layer_output
    )
    mixer_next = 0.5 * mixer_momentum[0] + both_sum[0][:, :mixer_width]
    shrink_next = 0.5 * shrink_momentum[0] + both_sum[0][:, mixer_width:]
    both_gather = [gather_start(jnp.concatenate([mixer_next, shrink_next], axis=1).astype(bf16))]
    moved = quarter(reduce_step, sums, 2)
    gathers_moved = quarter(gather_step, gathers, 2)
    both_moved = quarter(gather_step, both_gather, 0, 2)
    input_gradient, first_gain_grad = input_backward(
        head_place, joined_back, joined_now, first_other, tokens, middle_grad, norm_gains[0:1]
    )

    sums, gathers, both_gather, first_gain_grad = tie(
        moved, gathers_moved, both_moved, first_gain_grad
    )
    gain_totals = jnp.concatenate([first_gain_grad, 0.5 * second_gain_grad], axis=0)
    moved = quarter(reduce_step, sums, 3)
    gathers_moved = quarter(gather_step, gathers, 3)
    both_moved = quarter(gather_step, both_gather, 1, 2)
    gain_moved = total_step(gain_totals, 0)

    sums, gathers, both_gather, gain_totals = tie(moved, gathers_moved, both_moved, gain_moved)
    joined_next = 0.5 * joined_momentum[0] + jnp.concatenate(sums, axis=1)
    joined_gather = [gather_start(part) for part in thirds(joined_next.astype(bf16))]
    moved = quarter(gather_step, joined_gather, 0)
    both_moved = quarter(gather_step, both_gather, 2, 2)
    gain_moved = total_step(gain_totals, 1)
    expand_state = schulz_early([gather_rows(part) for part in gathers], expand_next)
    joined_gather, both_gather, gain_totals, expand_state = tie(
        moved, both_moved, gain_moved, expand_state
    )
    moved = quarter(gather_step, joined_gather, 1)
    both_moved = quarter(gather_step, both_gather, 3, 2)
    gain_moved = total_step(gain_totals, 2)
    updated_expand = schulz_late(expand_state, expand_weight[0], expand_grad.shape[0])
    joined_gather, both_gather, gain_totals, updated_expand = tie(
        moved, both_moved, gain_moved, updated_expand
    )
    both_full = [gather_rows(both_gather[0])]
    moved = quarter(gather_step, joined_gather, 2)
    gain_moved = total_step(gain_totals, 3)
    updated_shrink = schulz(
        both_full, mixer_width, shrink_next, shrink_weight[0], "schulz_shrink"
    )
    joined_gather, both_full, gain_totals, updated_shrink = tie(
        moved, both_full, gain_moved, updated_shrink
    )
    moved = quarter(gather_step, joined_gather, 3)
    gain_totals = total_step(gain_totals, 4)
    updated_mixer = schulz(both_full, 0, mixer_next, mixer_weight[0], "schulz_mixer")
    joined_gather, updated_mixer = tie(moved, updated_mixer)
    updated_joined = schulz(
        [gather_rows(part) for part in joined_gather],
        None, joined_next, joined_weight[0], "schulz_joined",
    )

    momentum_gains = 0.5 * gain_momentum + gain_totals
    updated_gains = norm_gains - gain_rate * momentum_gains * lax.rsqrt(
        jnp.mean(momentum_gains * momentum_gains, axis=-1, keepdims=True) + 1e-06
    )
    return (
        layer_output,
        input_gradient,
        joined_next[None],
        mixer_next[None],
        expand_next[None],
        shrink_next[None],
        updated_joined[None],
        updated_mixer[None],
        updated_expand[None],
        updated_shrink[None],
        momentum_gains,
        updated_gains,
    )


def solution(mesh):
    rows = P(("dp", "head"), None)
    weight = P("head", "dp", None)
    return jax.shard_map(
        shards,
        mesh=mesh,
        in_specs=(rows, P("dp", None), P()) + (weight,) * 8 + (P(), P("dp", None)),
        out_specs=(rows, rows) + (weight,) * 8 + (P(), P()),
        check_vma=False,
    )
```

```python
import functools
import math

import jax
import jax.numpy as jnp
from jax import lax
from jax.experimental import pallas as pl
from jax.experimental.pallas import tpu as pltpu
from jax.sharding import PartitionSpec as P

HEAD_DIM = 64
NS_ITERS = 3

theta_base = 160000.0
norm_epsilon = 1e-05
ns_first = 3.4445
ns_second = -4.775
ns_third = 2.0315
muon_rate = 1.0
gain_rate = 0.3

bf16 = jnp.bfloat16
f32 = jnp.float32
LOG2E = math.log2(math.e)
QUERY_SCALE = 0.125 * LOG2E
SAFE_SCORE = 60.0
DEPTH = 128
TILE_Q = 256
TILE_K = 256
FWD_SKEW = 6
BWD_SKEW = 2

NN = (((1,), (0,)), ((), ()))
NT = (((1,), (1,)), ((), ()))
TN = (((0,), (0,)), ((), ()))
TT = (((0,), (1,)), ((), ()))
QUARTERS = 4
FEED_ROWS = 256
FEED_CHUNKS = 3
ERF_TOP = (
    -2.72614225801306e-10, 2.77068142495902e-08, -2.10102402082508e-06, -5.69250639462346e-05,
    -7.34990630326855e-04, -2.95459980854025e-03, -1.60960333262415e-02,
)
ERF_BOTTOM = (
    -1.45660718464996e-05, -2.13374055278905e-04, -1.68282697438203e-03, -7.37332916720468e-03,
    -1.42647390514189e-02,
)


def dot(left, right, dims):
    return lax.dot_general(left, right, dims, preferred_element_type=f32)


def key_bounds(length_row, row_count):
    ends = jnp.cumsum(length_row)
    starts = ends - length_row
    first = jnp.arange(row_count // TILE_Q, dtype=jnp.int32) * TILE_Q
    labels = jnp.arange(length_row.shape[0], dtype=jnp.int32)

    def pick(places, table):
        segment = jnp.sum((places[:, None] >= ends[None, :]).astype(jnp.int32), axis=1)
        return jnp.sum(jnp.where(segment[:, None] == labels[None, :], table[None, :], 0), axis=1)

    low = pick(first, starts) // TILE_K
    high = (pick(first + TILE_Q - 1, ends) + TILE_K - 1) // TILE_K
    return low.astype(jnp.int32), high.astype(jnp.int32)


def doc_tables(length_row, row_count):
    ends = jnp.cumsum(length_row)
    starts = ends - length_row
    count = length_row.shape[0]
    places = jnp.arange(row_count, dtype=jnp.int32)[None, :]
    member = (places >= starts[:, None]) & (places < ends[:, None])
    rest = jnp.zeros((16 - count, row_count), f32)
    key_rows = jnp.concatenate([member.astype(f32), rest], axis=0).astype(bf16)
    query_rows = jnp.concatenate([jnp.where(member, 0.0, -1e30), rest], axis=0).astype(bf16)
    doc_first = jnp.sum(jnp.where(member, starts[:, None], 0), axis=0, keepdims=True)
    position = (places - doc_first).astype(f32)
    half_dim = HEAD_DIM // 2
    frequency = jnp.exp(
        jnp.arange(half_dim, dtype=f32) * (-2.0 * math.log(theta_base) / HEAD_DIM)
    )
    angles = frequency[:, None] * position
    return key_rows, query_rows, jnp.cos(angles), jnp.sin(angles)


def rotate(values, cosine, sine):
    half = HEAD_DIM // 2
    heads = values.reshape(-1, HEAD_DIM, values.shape[1])
    low, high = heads[:, :half], heads[:, half:]
    turned = jnp.concatenate([low * cosine - high * sine, high * cosine + low * sine], axis=1)
    return turned.reshape(values.shape)


def rows16(parts):
    rest = jnp.zeros((16 - len(parts), parts[0].shape[1]), f32)
    return jnp.concatenate([part.astype(f32) for part in parts] + [rest], axis=0).astype(bf16)


def split3(value):
    first = value.astype(bf16)
    left = value - first.astype(f32)
    second = left.astype(bf16)
    third = (left - second.astype(f32)).astype(bf16)
    return [first, second, third]


def three_ones(count):
    return jnp.concatenate([jnp.ones((3, count), f32), jnp.zeros((13, count), f32)], axis=0).astype(
        bf16
    )


def forward_kernel(
    low, high, queries, keys, values, key_rows, query_rows, out, logsum, keys_in, values_in, queries_in, safe
):
    heads = queries.shape[0] // HEAD_DIM
    rows = keys.shape[1]
    step = pl.program_id(0)

    @pl.when(step == 0)
    def _():
        worst = jnp.zeros((1, 1), f32)
        ones = rows16([jnp.ones((1, rows), f32)])
        for h in range(heads):
            band = slice(h * HEAD_DIM, (h + 1) * HEAD_DIM)
            key = keys[band, :]
            pad = jnp.zeros((DEPTH - HEAD_DIM - 16, rows), bf16)
            keys_in[h] = jnp.concatenate([key, key_rows[...], pad], axis=0).T
            values_in[h, :HEAD_DIM, :] = values[band, :]
            values_in[h, HEAD_DIM:, :] = ones
            query_full = queries[band, :].astype(f32)
            key_full = key.astype(f32)
            query_top = jnp.max(
                jnp.sum(query_full * query_full, axis=0, keepdims=True), axis=1, keepdims=True
            )
            key_top = jnp.max(
                jnp.sum(key_full * key_full, axis=0, keepdims=True), axis=1, keepdims=True
            )
            worst = jnp.maximum(worst, query_top * key_top)
        safe[0] = jnp.where(worst[0, 0] <= SAFE_SCORE * SAFE_SCORE, 1, 0)

    first = pl.multiple_of(step * TILE_Q, TILE_Q)
    for h in range(heads):
        queries_in[h, :HEAD_DIM, :] = queries[h * HEAD_DIM : (h + 1) * HEAD_DIM, pl.ds(first, TILE_Q)]
        queries_in[h, HEAD_DIM : HEAD_DIM + 16, :] = query_rows[...]
        queries_in[h, HEAD_DIM + 16 :, :] = jnp.zeros((DEPTH - HEAD_DIM - 16, TILE_Q), bf16)

    def finish(peaks, totals):
        for h in range(heads):
            weight = totals[h][HEAD_DIM : HEAD_DIM + 1, :]
            out[h * HEAD_DIM : (h + 1) * HEAD_DIM, :] = (totals[h][:HEAD_DIM, :] / weight).astype(bf16)
            level = jnp.log2(weight)
            logsum[h : h + 1, :] = level if peaks is None else peaks[h] + level

    empty = tuple(jnp.zeros((HEAD_DIM + 16, TILE_Q), f32) for _ in range(heads))

    @pl.when(safe[0] == 1)
    def _():
        def block(j, totals):
            span = pl.ds(pl.multiple_of(j * TILE_K, TILE_K), TILE_K)
            result = [None] * heads
            waiting = {}
            for t in range(heads + FWD_SKEW):
                if t < heads:
                    waiting[t] = dot(keys_in[t, span, :], queries_in[t], NN)
                h = t - FWD_SKEW
                if h >= 0:
                    raised = jnp.exp2(waiting.pop(h)).astype(bf16)
                    result[h] = totals[h] + dot(values_in[h, :, span], raised, NN)
            return tuple(result)

        finish(None, lax.fori_loop(low[step], high[step], block, empty))

    @pl.when(safe[0] == 0)
    def _():
        def block(j, carry):
            peaks, totals = carry
            span = pl.ds(pl.multiple_of(j * TILE_K, TILE_K), TILE_K)
            new_peaks = []
            new_totals = []
            for h in range(heads):
                scores = dot(keys_in[h, span, :], queries_in[h], NN)
                peak = jnp.maximum(peaks[h], jnp.max(scores, axis=0, keepdims=True))
                raised = jnp.exp2(scores - peak).astype(bf16)
                new_totals.append(
                    totals[h] * jnp.exp2(peaks[h] - peak) + dot(values_in[h, :, span], raised, NN)
                )
                new_peaks.append(peak)
            return tuple(new_peaks), tuple(new_totals)

        lowest = tuple(jnp.full((1, TILE_Q), -3e38, f32) for _ in range(heads))
        finish(*lax.fori_loop(low[step], high[step], block, (lowest, empty)))


def attention_forward(low, high, queries, keys, values, key_rows, query_rows):
    width, rows = queries.shape
    heads = width // HEAD_DIM

    def full(count):
        return pl.BlockSpec((count, rows), lambda i, low, high: (0, 0))

    def tile(count):
        return pl.BlockSpec((count, TILE_Q), lambda i, low, high: (0, i))

    return pl.pallas_call(
        forward_kernel,
        out_shape=(
            jax.ShapeDtypeStruct((width, rows), bf16),
            jax.ShapeDtypeStruct((heads, rows), f32),
        ),
        grid_spec=pltpu.PrefetchScalarGridSpec(
            num_scalar_prefetch=2,
            grid=(rows // TILE_Q,),
            in_specs=[full(width), full(width), full(width), full(16), tile(16)],
            out_specs=[tile(width), tile(heads)],
            scratch_shapes=[
                pltpu.VMEM((heads, rows, DEPTH), bf16),
                pltpu.VMEM((heads, HEAD_DIM + 16, rows), bf16),
                pltpu.VMEM((heads, DEPTH, TILE_Q), bf16),
                pltpu.SMEM((1,), jnp.int32),
            ],
        ),
        compiler_params=pltpu.CompilerParams(
            dimension_semantics=("arbitrary",), vmem_limit_bytes=40 << 20
        ),
        name="attention_forward",
    )(low, high, queries, keys, values, key_rows, query_rows)


def backward_kernel(
    low, high, queries, keys, values, grads, outs, logsum, key_rows, query_rows, cosine, sine,
    joined_back, *scratch
):
    heads = queries.shape[0] // HEAD_DIM
    rows = keys.shape[1]
    keys_in, values_in, queries_in, grads_in = scratch[:4]
    key_sum = scratch[4 : 4 + heads]
    value_sum = scratch[4 + heads : 4 + 2 * heads]
    query_sum = scratch[4 + 2 * heads : 4 + 3 * heads]
    step = pl.program_id(0)

    @pl.when(step == 0)
    def _():
        ones = three_ones(rows)
        for h in range(heads):
            band = slice(h * HEAD_DIM, (h + 1) * HEAD_DIM)
            pad = jnp.zeros((DEPTH - HEAD_DIM - 32, rows), bf16)
            keys_in[h] = jnp.concatenate([keys[band, :], key_rows[...], ones, pad], axis=0).T
            pad = jnp.zeros((DEPTH - HEAD_DIM - 16, rows), bf16)
            values_in[h] = jnp.concatenate([values[band, :], ones, pad], axis=0).T
            key_sum[h][...] = jnp.zeros((HEAD_DIM, rows), f32)
            value_sum[h][...] = jnp.zeros((HEAD_DIM, rows), f32)

    for h in range(heads):
        band = slice(h * HEAD_DIM, (h + 1) * HEAD_DIM)
        queries_in[h, :HEAD_DIM, :] = queries[band, :]
        queries_in[h, HEAD_DIM : HEAD_DIM + 16, :] = query_rows[...]
        queries_in[h, HEAD_DIM + 16 : HEAD_DIM + 32, :] = rows16(split3(-logsum[h : h + 1, :]))
        queries_in[h, HEAD_DIM + 32 :, :] = jnp.zeros((DEPTH - HEAD_DIM - 32, TILE_Q), bf16)
        inner = jnp.sum(grads[band, :].astype(f32) * outs[band, :].astype(f32), axis=0, keepdims=True)
        grads_in[h, :HEAD_DIM, :] = grads[band, :]
        grads_in[h, HEAD_DIM : HEAD_DIM + 16, :] = rows16(split3(-inner))
        grads_in[h, HEAD_DIM + 16 :, :] = jnp.zeros((DEPTH - HEAD_DIM - 16, TILE_Q), bf16)
        query_sum[h][...] = jnp.zeros((HEAD_DIM, TILE_Q), f32)

    def block(j, carry):
        span = pl.ds(pl.multiple_of(j * TILE_K, TILE_K), TILE_K)
        waiting = {}
        for t in range(heads + BWD_SKEW):
            if t < heads:
                waiting[t] = (
                    dot(keys_in[t, span, :], queries_in[t], NN),
                    dot(values_in[t, span, :], grads_in[t], NN),
                )
            h = t - BWD_SKEW
            if h < 0:
                continue
            band = slice(h * HEAD_DIM, (h + 1) * HEAD_DIM)
            scores, weight_grad = waiting.pop(h)
            softmax = jnp.exp2(scores)
            score_grad = (softmax * weight_grad).astype(bf16)
            value_sum[h][:, span] += dot(grads[band, :], softmax.astype(bf16), NT)
            key_sum[h][:, span] += dot(queries[band, :], score_grad, NT)
            query_sum[h][...] += dot(keys[band, span], score_grad, NN)
        return carry

    lax.fori_loop(low[step], high[step], block, 0)

    def store(offset, columns, value):
        half = HEAD_DIM // 2
        upper, lower = value[:half], value[half:]
        cos, sin = cosine[:, columns], sine[:, columns]
        joined_back[offset : offset + half, columns] = (upper * cos + lower * sin).astype(bf16)
        joined_back[offset + half : offset + HEAD_DIM, columns] = (lower * cos - upper * sin).astype(bf16)

    width = heads * HEAD_DIM
    columns = pl.ds(pl.multiple_of(step * TILE_Q, TILE_Q), TILE_Q)
    for h in range(heads):
        store(h * HEAD_DIM, columns, query_sum[h][...] * 0.125)

    @pl.when(step == pl.num_programs(0) - 1)
    def _():
        for h in range(heads):
            first = width + h * HEAD_DIM
            store(first, slice(0, rows), key_sum[h][...] * (1.0 / LOG2E))
            first += width
            joined_back[first : first + HEAD_DIM, :] = value_sum[h][...].astype(bf16)


def attention_backward(
    low, high, queries, keys, values, grads, outs, logsum, key_rows, query_rows, cosine, sine
):
    width, rows = queries.shape
    heads = width // HEAD_DIM

    def full(count):
        return pl.BlockSpec((count, rows), lambda i, low, high: (0, 0))

    def tile(count):
        return pl.BlockSpec((count, TILE_Q), lambda i, low, high: (0, i))

    return pl.pallas_call(
        backward_kernel,
        out_shape=jax.ShapeDtypeStruct((3 * width, rows), bf16),
        grid_spec=pltpu.PrefetchScalarGridSpec(
            num_scalar_prefetch=2,
            grid=(rows // TILE_Q,),
            in_specs=[
                tile(width), full(width), full(width), tile(width), tile(width), tile(heads),
                full(16), tile(16), full(HEAD_DIM // 2), full(HEAD_DIM // 2),
            ],
            out_specs=full(3 * width),
            scratch_shapes=[
                pltpu.VMEM((heads, rows, DEPTH), bf16),
                pltpu.VMEM((heads, rows, DEPTH), bf16),
                pltpu.VMEM((heads, DEPTH, TILE_Q), bf16),
                pltpu.VMEM((heads, DEPTH, TILE_Q), bf16),
            ]
            + [pltpu.VMEM((HEAD_DIM, rows), f32)] * (2 * heads)
            + [pltpu.VMEM((HEAD_DIM, TILE_Q), f32)] * heads,
        ),
        compiler_params=pltpu.CompilerParams(
            dimension_semantics=("arbitrary",), vmem_limit_bytes=52 << 20
        ),
        name="attention_backward",
    )(low, high, queries, keys, values, grads, outs, logsum, key_rows, query_rows, cosine, sine)


def layer_norm(values, gain_row):
    centred = values - jnp.mean(values, axis=-1, keepdims=True)
    inverse = lax.rsqrt(jnp.mean(centred * centred, axis=-1, keepdims=True) + norm_epsilon)
    normal = centred * inverse
    return normal * gain_row, normal, inverse


def norm_back(upstream, gain_row, normal, inverse):
    scaled = upstream * gain_row
    inner_mean = jnp.mean(scaled * normal, axis=-1, keepdims=True)
    return inverse * (scaled - jnp.mean(scaled, axis=-1, keepdims=True) - normal * inner_mean)


def horner(square, factors):
    total = factors[0] * square + factors[1]
    for factor in factors[2:]:
        total = total * square + factor
    return total


def error_function(value):
    value = jnp.clip(value, -4.0, 4.0)
    square = value * value
    return value * horner(square, ERF_TOP) / horner(square, ERF_BOTTOM)


def turn(value):
    columns = value.shape[1]
    rest = jnp.zeros((value.shape[0], -columns % 128), value.dtype)
    return jnp.concatenate([value, rest], axis=1).T[:columns, :]


def turn_back(value):
    lines = value.shape[0]
    rest = jnp.zeros((-lines % 128, value.shape[1]), value.dtype)
    return jnp.concatenate([value, rest], axis=0).T[:, :lines]


def first_kernel(head, own, other, gain, rows, normed):
    tiles = pl.num_programs(0) // 2
    mine = pl.program_id(0) // tiles == head[0]
    value = jnp.where(mine, own[...].astype(f32), other[...].astype(f32))
    rows[...] = value.astype(bf16)
    normed[...] = layer_norm(value, gain[...])[0].astype(bf16)


def first_norm(head, own, other, gain):
    half, width = own.shape
    tiles = half // FEED_ROWS
    result = jax.ShapeDtypeStruct((2 * half, width), bf16)
    spec = pl.BlockSpec((FEED_ROWS, width), lambda i, head: (i, 0))
    return pl.pallas_call(
        first_kernel,
        out_shape=(result, result),
        grid_spec=pltpu.PrefetchScalarGridSpec(
            num_scalar_prefetch=1,
            grid=(2 * tiles,),
            in_specs=[
                pl.BlockSpec(
                    (FEED_ROWS, width),
                    lambda i, head: (jnp.clip(i - head[0] * tiles, 0, tiles - 1), 0),
                ),
                pl.BlockSpec(
                    (FEED_ROWS, width),
                    lambda i, head: (jnp.clip(i - (1 - head[0]) * tiles, 0, tiles - 1), 0),
                ),
                pl.BlockSpec((1, width), lambda i, head: (0, 0)),
            ],
            out_specs=[spec, spec],
        ),
        compiler_params=pltpu.CompilerParams(dimension_semantics=("arbitrary",)),
        name="first_norm",
    )(head, own, other, gain)


def gradient_kernel(back, normed, *refs):
    grads, total = refs[:-1], refs[-1]
    step = pl.program_id(0)

    @pl.when(step == 0)
    def _():
        total[...] = dot(back[...], normed[...], NN)

    @pl.when(step > 0)
    def _():
        total[...] += dot(back[...], normed[...], NN)

    @pl.when(step == pl.num_programs(0) - 1)
    def _():
        first = 0
        for grad in grads:
            grad[...] = total[:, first : first + grad.shape[1]].astype(bf16)
            first += grad.shape[1]


def joined_gradient(back, normed):
    lines, count = back.shape
    width = normed.shape[1]
    tile = 2 * FEED_ROWS
    half = width // 256 * 128
    parts = [half, width - half]
    return pl.pallas_call(
        gradient_kernel,
        grid=(count // tile,),
        in_specs=[
            pl.BlockSpec((lines, tile), lambda i: (0, i)),
            pl.BlockSpec((tile, width), lambda i: (i, 0)),
        ],
        out_specs=[pl.BlockSpec((lines, part), lambda i: (0, 0)) for part in parts],
        out_shape=[jax.ShapeDtypeStruct((lines, part), bf16) for part in parts],
        scratch_shapes=[pltpu.VMEM((lines, width), f32)],
        compiler_params=pltpu.CompilerParams(
            dimension_semantics=("arbitrary",), vmem_limit_bytes=32 << 20
        ),
        name="joined_gradient",
    )(back, normed)


def pull_kernel(head, back, weight, out):
    out[...] = dot(back[...].T, weight[...], NN).astype(bf16)


def pull_other(head, back, weight):
    lines, count = back.shape
    width = weight.shape[1]
    tiles = count // 2 // FEED_ROWS
    return pl.pallas_call(
        pull_kernel,
        out_shape=jax.ShapeDtypeStruct((count // 2, width), bf16),
        grid_spec=pltpu.PrefetchScalarGridSpec(
            num_scalar_prefetch=1,
            grid=(tiles,),
            in_specs=[
                pl.BlockSpec((lines, FEED_ROWS), lambda i, head: (0, (1 - head[0]) * tiles + i)),
                pl.BlockSpec((lines, width), lambda i, head: (0, 0)),
            ],
            out_specs=pl.BlockSpec((FEED_ROWS, width), lambda i, head: (i, 0)),
        ),
        compiler_params=pltpu.CompilerParams(
            dimension_semantics=("arbitrary",), vmem_limit_bytes=24 << 20
        ),
        name="pull_other",
    )(head, back, weight)


def input_kernel(head, back, weight, other, rows, middle_grad, gain, input_grad, gain_grad):
    @pl.when(pl.program_id(0) == 0)
    def _():
        gain_grad[...] = jnp.zeros(gain_grad.shape, f32)

    pulled = dot(back[...].T, weight[...], NN) + other[...].astype(f32)
    unused, normal, inverse = layer_norm(rows[...].astype(f32), gain[...])
    input_grad[...] = middle_grad[...] + norm_back(pulled, gain[...], normal, inverse)
    gain_grad[...] += jnp.sum(pulled * normal, axis=0, keepdims=True)


def input_backward(head, back, weight, other, rows, middle_grad, gain):
    lines, count = back.shape
    width = weight.shape[1]
    tiles = count // 2 // FEED_ROWS

    def down():
        return pl.BlockSpec((FEED_ROWS, width), lambda i, head: (i, 0))

    return pl.pallas_call(
        input_kernel,
        out_shape=(
            jax.ShapeDtypeStruct((count // 2, width), f32),
            jax.ShapeDtypeStruct((1, width), f32),
        ),
        grid_spec=pltpu.PrefetchScalarGridSpec(
            num_scalar_prefetch=1,
            grid=(tiles,),
            in_specs=[
                pl.BlockSpec((lines, FEED_ROWS), lambda i, head: (0, head[0] * tiles + i)),
                pl.BlockSpec((lines, width), lambda i, head: (0, 0)),
                down(),
                down(),
                pl.BlockSpec((FEED_ROWS, width), lambda i, head: (head[0] * tiles + i, 0)),
                pl.BlockSpec((1, width), lambda i, head: (0, 0)),
            ],
            out_specs=[down(), pl.BlockSpec((1, width), lambda i, head: (0, 0))],
        ),
        compiler_params=pltpu.CompilerParams(
            dimension_semantics=("arbitrary",), vmem_limit_bytes=24 << 20
        ),
        name="input_backward",
    )(head, back, weight, other, rows, middle_grad, gain)


def feed_kernel(
    rows, attended, attended_other, upstream, gain, both, mixer_other, expand_left, expand_right,
    middle, hidden, second_part, shrink_grad, left_grad, right_grad, shrink,
    shrink_sum, expand_sum, expand
):
    step = pl.program_id(0)
    mixed, units = attended.shape[0], shrink.shape[0]
    chunk = units // FEED_CHUNKS

    @pl.when(step == 0)
    def _():
        expand[:, : expand_left.shape[1]] = expand_left[...]
        expand[:, expand_left.shape[1] :] = expand_right[...]
        shrink[...] = turn(both[:, mixed:])
        shrink_sum[...] = jnp.zeros(shrink_sum.shape, f32)
        expand_sum[...] = jnp.zeros(expand_sum.shape, f32)

    total = rows[...].astype(f32) + dot(attended[...].T, both[:, :mixed], NT)
    total = total + dot(attended_other[...].T, mixer_other[...], NT)
    middle[...] = total
    normed = layer_norm(total, gain[...])[0].astype(bf16)
    above = upstream[...]

    def project(c):
        first = slice(c * chunk, (c + 1) * chunk)
        second = slice(units + c * chunk, units + (c + 1) * chunk)
        return (
            dot(expand[first, :], normed, NT),
            dot(expand[second, :], normed, NT),
            dot(shrink[first, :], above, NT),
        )

    waiting = project(0)
    back = jnp.zeros(total.shape, f32)
    for c in range(FEED_CHUNKS):
        active, linear, grad = waiting
        if c + 1 < FEED_CHUNKS:
            waiting = project(c + 1)
        first = slice(c * chunk, (c + 1) * chunk)
        second = slice(units + c * chunk, units + (c + 1) * chunk)
        area = 0.5 * error_function(active * math.sqrt(0.5)) + 0.5
        gate = active * area
        density = jnp.exp(-0.5 * active * active) * (1.0 / math.sqrt(2.0 * math.pi))
        unit = (gate * linear).astype(bf16)
        active_back = (grad * linear * (area + active * density)).astype(bf16)
        linear_back = (grad * gate).astype(bf16)
        hidden[first, :] = unit
        shrink_sum[first, :] += dot(unit, above, NN)
        expand_sum[first, :] += dot(active_back, normed, NN)
        expand_sum[second, :] += dot(linear_back, normed, NN)
        back = back + dot(active_back, expand[first, :], TN) + dot(linear_back, expand[second, :], TN)
    second_part[...] = back.astype(bf16)

    @pl.when(step == pl.num_programs(0) - 1)
    def _():
        shrink_grad[...] = shrink_sum[...].astype(bf16)
        cut = left_grad.shape[1]
        left_grad[...] = expand_sum[:, :cut].astype(bf16)
        right_grad[...] = expand_sum[:, cut:].astype(bf16)


def feed_forward(rows, attended, attended_other, upstream, gain, both, mixer_other, expand):
    count, width = rows.shape
    mixed, units = attended.shape[0], expand[0].shape[0] // 2

    def full(*shape):
        return pl.BlockSpec(shape, lambda i: (0, 0))

    def down(columns):
        return pl.BlockSpec((FEED_ROWS, columns), lambda i: (i, 0))

    def along(lines):
        return pl.BlockSpec((lines, FEED_ROWS), lambda i: (0, i))

    return pl.pallas_call(
        feed_kernel,
        grid=(count // FEED_ROWS,),
        in_specs=[
            down(width), along(mixed), along(mixed), down(width), full(1, width),
            full(*both.shape), full(width, mixed), full(*expand[0].shape), full(*expand[1].shape),
        ],
        out_specs=[
            down(width), along(units), down(width), full(units, width),
            full(*expand[0].shape), full(*expand[1].shape), full(units, width),
        ],
        out_shape=(
            jax.ShapeDtypeStruct((count, width), f32),
            jax.ShapeDtypeStruct((units, count), bf16),
            jax.ShapeDtypeStruct((count, width), bf16),
            jax.ShapeDtypeStruct((units, width), bf16),
            jax.ShapeDtypeStruct(expand[0].shape, bf16),
            jax.ShapeDtypeStruct(expand[1].shape, bf16),
            jax.ShapeDtypeStruct((units, width), bf16),
        ),
        scratch_shapes=[
            pltpu.VMEM((units, width), f32),
            pltpu.VMEM((2 * units, width), f32),
            pltpu.VMEM((2 * units, width), bf16),
        ],
        compiler_params=pltpu.CompilerParams(
            dimension_semantics=("arbitrary",), vmem_limit_bytes=48 << 20
        ),
        name="feed_forward",
    )(rows, attended, attended_other, upstream, gain, both, mixer_other, *expand)


def norm_kernel(
    middle, own, other, upstream, gain, both, attended, shrink_grad,
    middle_grad, attended_grad, both_grad, gain_grad, mixer_turned, mixer_sum
):
    step = pl.program_id(0)

    @pl.when(step == 0)
    def _():
        mixer_turned[...] = both[:, : attended.shape[0]].T
        mixer_sum[...] = jnp.zeros(mixer_sum.shape, f32)
        gain_grad[...] = jnp.zeros(gain_grad.shape, f32)

    unused, normal, inverse = layer_norm(middle[...], gain[...])
    back = own[...].astype(f32) + other[...].astype(f32)
    grad = upstream[...].astype(f32) + norm_back(back, gain[...], normal, inverse)
    middle_grad[...] = grad
    grad_low = grad.astype(bf16)
    attended_grad[...] = dot(mixer_turned[...], grad_low, NT).astype(bf16)
    mixer_sum[...] += dot(attended[...], grad_low, NN)
    gain_grad[...] += jnp.sum(back * normal, axis=0, keepdims=True)

    @pl.when(step == pl.num_programs(0) - 1)
    def _():
        mixed = attended.shape[0]
        both_grad[:, :mixed] = mixer_sum[...].T.astype(bf16)
        both_grad[:, mixed:] = turn_back(shrink_grad[...])


def norm_backward(middle, own, other, upstream, gain, both, attended, shrink_grad):
    count, width = middle.shape
    mixed = attended.shape[0]

    def full(*shape):
        return pl.BlockSpec(shape, lambda i: (0, 0))

    def down(columns):
        return pl.BlockSpec((FEED_ROWS, columns), lambda i: (i, 0))

    def along(lines):
        return pl.BlockSpec((lines, FEED_ROWS), lambda i: (0, i))

    return pl.pallas_call(
        norm_kernel,
        grid=(count // FEED_ROWS,),
        in_specs=[
            down(width), down(width), down(width), down(width), full(1, width),
            full(*both.shape), along(mixed), full(*shrink_grad.shape),
        ],
        out_specs=[down(width), along(mixed), full(*both.shape), full(1, width)],
        out_shape=(
            jax.ShapeDtypeStruct((count, width), f32),
            jax.ShapeDtypeStruct((mixed, count), bf16),
            jax.ShapeDtypeStruct(both.shape, bf16),
            jax.ShapeDtypeStruct((1, width), f32),
        ),
        scratch_shapes=[pltpu.VMEM((mixed, width), bf16), pltpu.VMEM((mixed, width), f32)],
        compiler_params=pltpu.CompilerParams(
            dimension_semantics=("arbitrary",), vmem_limit_bytes=40 << 20
        ),
        name="norm_backward",
    )(middle, own, other, upstream, gain, both, attended, shrink_grad)


def swap(value, axis, bit):
    count = lax.axis_size(axis)
    return lax.ppermute(value, axis, [(i, i ^ bit) for i in range(count)])


def bit_orders():
    bits = lax.axis_size("dp").bit_length() - 1
    return [[(start + k) % (bits - 1) for k in range(bits - 1)] + [bits - 1] for start in range(3)]


def steps_count():
    return lax.axis_size("dp").bit_length() - 1


def reduce_start(value):
    bits = steps_count()
    rows = value.shape[0] >> bits
    return value.reshape((2,) * bits + (rows, value.shape[1]))


def reduce_step(held, step, which):
    bits = steps_count()
    bit = bit_orders()[which][step]
    axis = bits - 1 - bit
    side = (lax.axis_index("dp") >> bit) & 1
    kept = lax.dynamic_slice_in_dim(held, side, 1, axis)
    sent = lax.dynamic_slice_in_dim(held, 1 - side, 1, axis)
    total = kept.astype(f32) + swap(sent, "dp", 1 << bit).astype(f32)
    if step + 1 == bits:
        return total.reshape(held.shape[-2:])
    return total.astype(bf16)


def gather_start(value):
    return value[(None,) * steps_count()]


def gather_step(held, step, which):
    bits = steps_count()
    bit = bit_orders()[which][bits - 1 - step]
    return jnp.concatenate([held, swap(held, "dp", 1 << bit)], axis=bits - 1 - bit)


def ordered_step(held, step, which):
    bits = steps_count()
    bit = bit_orders()[which][bits - 1 - step]
    got = swap(held, "dp", 1 << bit)
    low_side = ((lax.axis_index("dp") >> bit) & 1) == 0
    return jnp.concatenate(
        [jnp.where(low_side, held, got), jnp.where(low_side, got, held)], axis=bits - 1 - bit
    )


def gather_rows(held):
    return held.reshape(-1, held.shape[-1])


def halves_of(value):
    unit = value.shape[1] // 256 * 128
    return [value[:, :unit], value[:, unit:]]


def quarter(step, states, part, first=0):
    bits = steps_count()
    for index in range(bits * part // QUARTERS, bits * (part + 1) // QUARTERS):
        states = [step(state, index, first + which) for which, state in enumerate(states)]
    return states


def tie(*values):
    return lax.optimization_barrier(values)


def total_step(value, part):
    if part == 0:
        return value + swap(value, "head", 1)
    bits = steps_count()
    for bit in range(bits * (part - 1) // QUARTERS, bits * part // QUARTERS):
        value = value + swap(value, "dp", 1 << bit)
    return value


def schulz_start(held, own, gram, low):
    down = 0
    for left in held:
        along = 0
        for right in held:
            gram[down : down + left.shape[1], along : along + right.shape[1]] = dot(left, right, TN)
            along += right.shape[1]
        down += left.shape[1]
    shape = gram.shape
    diagonal = lax.broadcasted_iota(jnp.int32, shape, 0) == lax.broadcasted_iota(jnp.int32, shape, 1)
    trace = jnp.sum(jnp.where(diagonal, gram[...], 0.0), axis=0, keepdims=True)
    norm_value = jnp.sqrt(jnp.sum(trace, axis=1, keepdims=True)) + 1e-07
    gram[...] = gram[...] * (1.0 / (norm_value * norm_value))
    low[...] = gram[...].astype(bf16)
    return own[...] / norm_value


def schulz_steps(rows, gram, low, change, first, stop):
    columns = gram.shape[0]
    lines = 256 if columns % 256 == 0 else columns

    def per_block(body):
        def run(index, carry):
            body(pl.ds(pl.multiple_of(index * lines, lines), lines))
            return carry

        lax.fori_loop(0, columns // lines, run, 0)

    def form_change(block):
        squared = dot(low[block, :], low[...], NN)
        change[block, :] = (ns_second * gram[block, :] + ns_third * squared).astype(bf16)

    def next_gram(block):
        once = ns_first * gram[block, :] + dot(low[block, :], change[...], NN)
        twice = ns_first * once + dot(once.astype(bf16), change[...], NN)
        gram[block, :] = twice
        low[block, :] = twice.astype(bf16)

    for iteration in range(first, stop):
        per_block(form_change)
        rows = ns_first * rows + dot(rows.astype(bf16), change[...], NN)
        if iteration + 1 < NS_ITERS:
            per_block(next_gram)
    return rows


def whole_kernel(*refs, count, offset, scale):
    parts = refs[:count]
    own, weight, updated, gram, low, change = refs[count:]
    if offset is None:
        held = [part[...] for part in parts]
    else:
        held = [parts[0][:, offset : offset + gram.shape[0]]]
    rows = schulz_start(held, own, gram, low)
    updated[...] = weight[...] - scale * schulz_steps(rows, gram, low, change, 0, NS_ITERS)


def early_kernel(*refs, count):
    own, rows, gram_out, low_out, gram, low, change = refs[count:]
    start = schulz_start([part[...] for part in refs[:count]], own, gram, low)
    rows[...] = start
    gram_out[...] = gram[...]
    low_out[...] = low[...]


def late_kernel(rows, gram_in, low_in, weight, updated, gram, low, change, *, scale):
    gram[...] = gram_in[...]
    low[...] = low_in[...]
    done = schulz_steps(rows[...], gram, low, change, 0, NS_ITERS)
    updated[...] = weight[...] - scale * done


def square_scratch(columns):
    return [
        pltpu.VMEM((columns, columns), f32),
        pltpu.VMEM((columns, columns), bf16),
        pltpu.VMEM((columns, columns), bf16),
    ]


def shape_scale(rows, columns):
    return muon_rate * math.sqrt(rows / columns)


def schulz(parts, offset, own, weight, name):
    columns = own.shape[1]
    return pl.pallas_call(
        functools.partial(
            whole_kernel, count=len(parts), offset=offset, scale=shape_scale(parts[0].shape[0], columns)
        ),
        out_shape=jax.ShapeDtypeStruct(own.shape, f32),
        scratch_shapes=square_scratch(columns),
        compiler_params=pltpu.CompilerParams(vmem_limit_bytes=40 << 20),
        name=name,
    )(*parts, own, weight)


def schulz_early(parts, own):
    columns = own.shape[1]
    return pl.pallas_call(
        functools.partial(early_kernel, count=len(parts)),
        out_shape=(
            jax.ShapeDtypeStruct(own.shape, f32),
            jax.ShapeDtypeStruct((columns, columns), f32),
            jax.ShapeDtypeStruct((columns, columns), bf16),
        ),
        scratch_shapes=square_scratch(columns),
        compiler_params=pltpu.CompilerParams(vmem_limit_bytes=40 << 20),
        name="schulz_early",
    )(*parts, own)


def schulz_late(state, weight, rows):
    columns = weight.shape[1]
    return pl.pallas_call(
        functools.partial(late_kernel, scale=shape_scale(rows, columns)),
        out_shape=jax.ShapeDtypeStruct(weight.shape, f32),
        scratch_shapes=square_scratch(columns),
        compiler_params=pltpu.CompilerParams(vmem_limit_bytes=40 << 20),
        name="schulz_late",
    )(*state, weight)


def shards(
    tokens,
    lengths,
    norm_gains,
    joined_weight,
    mixer_weight,
    expand_weight,
    shrink_weight,
    joined_momentum,
    mixer_momentum,
    expand_momentum,
    shrink_momentum,
    gain_momentum,
    cotangent,
):
    row_count = cotangent.shape[0]
    local_rows = tokens.shape[0]
    head = lax.axis_index("head")
    mixer_width = mixer_weight.shape[2]

    def own_half(value):
        return lax.dynamic_slice_in_dim(value, head * local_rows, local_rows, 0)

    joined_parts = [gather_start(part) for part in halves_of(joined_weight[0].astype(bf16))]
    joined_parts = quarter(ordered_step, joined_parts, 0)
    others = [gather_start(part) for part in halves_of(expand_weight[0].astype(bf16))] + [
        gather_start(jnp.concatenate([mixer_weight[0], shrink_weight[0]], axis=1).astype(bf16))
    ]
    key_rows, query_rows, cosine, sine = doc_tables(lengths[0], row_count)
    low, high = key_bounds(lengths[0], row_count)
    head_place = head[None]
    tokens_other = swap(tokens, "head", 1)

    joined_parts, others, tokens_other = tie(joined_parts, others, tokens_other)
    joined_parts = quarter(ordered_step, joined_parts, 1)
    others = quarter(ordered_step, others, 0)
    rows_low, first_low = first_norm(head_place, tokens, tokens_other, norm_gains[0:1])
    joined_parts, others, first_low = tie(joined_parts, others, first_low)
    joined_parts = quarter(ordered_step, joined_parts, 2)
    others = quarter(ordered_step, others, 1)
    joined_parts, others = tie(joined_parts, others)
    joined_parts = quarter(ordered_step, joined_parts, 3)
    moved = quarter(ordered_step, others, 2)

    joined_low = jnp.concatenate([gather_rows(part) for part in joined_parts], axis=1)
    joined = dot(joined_low, first_low, NT)
    width = joined.shape[0] // 3
    queries = (rotate(joined[:width], cosine, sine) * QUERY_SCALE).astype(bf16)
    keys = rotate(joined[width : 2 * width], cosine, sine).astype(bf16)
    values = joined[2 * width :].astype(bf16)
    others, queries, keys, values, low = tie(moved, queries, keys, values, low)
    moved = quarter(ordered_step, others, 3)
    attended, logsum = attention_forward(low, high, queries, keys, values, key_rows, query_rows)
    others, attended, logsum = tie(moved, attended, logsum)
    attended_other = swap(attended, "head", 1)
    both_low = gather_rows(others[2])
    mixer_other = swap(both_low[:, :mixer_width], "head", 1)

    second_gain = norm_gains[1:2]
    middle, hidden, second_part, shrink_grad, left_grad, right_grad, shrink_turned = feed_forward(
        rows_low, attended, attended_other, cotangent, second_gain,
        both_low, mixer_other, [gather_rows(part) for part in others[:2]],
    )
    second_other = swap(second_part, "head", 1)

    sums, second_other = tie([reduce_start(left_grad), reduce_start(right_grad)], second_other)
    moved = quarter(reduce_step, sums, 0)
    middle_grad, attended_grad, both_grad, second_gain_grad = norm_backward(
        middle, second_part, second_other, cotangent, second_gain, both_low, attended, shrink_grad
    )
    both_sum = [reduce_start(both_grad)]

    sums, attended_grad, shrink_now = tie(moved, attended_grad, shrink_turned)
    moved = quarter(reduce_step, sums, 1)

    def fed(columns):
        units = lax.dynamic_slice_in_dim(hidden, columns, local_rows, 1)
        return dot(units, shrink_now, TN)

    fed_other = fed((1 - head) * local_rows).astype(bf16)
    fed_own = fed(head * local_rows)

    sums, both_sum, fed_other, fed_own, low = tie(moved, both_sum, fed_other, fed_own, low)
    moved = quarter(reduce_step, sums, 2)
    both_moved = quarter(reduce_step, both_sum, 0, 2)
    fed_other = swap(fed_other, "head", 1)
    joined_back = attention_backward(
        low, high, queries, keys, values, attended_grad, attended, logsum, key_rows, query_rows,
        cosine, sine,
    )
    sums, both_sum, joined_back = tie(moved, both_moved, joined_back)
    moved = quarter(reduce_step, sums, 3)
    both_moved = quarter(reduce_step, both_sum, 1, 2)
    joined_grad = joined_gradient(joined_back, first_low)

    sums, both_sum, joined_grad, joined_now = tie(moved, both_moved, joined_grad, joined_low)
    expand_next = 0.5 * expand_momentum[0] + jnp.concatenate(sums, axis=1)
    gathers = [gather_start(part) for part in halves_of(expand_next.astype(bf16))]
    sums = quarter(reduce_step, [reduce_start(part) for part in joined_grad], 0)
    moved = quarter(gather_step, gathers, 0)
    both_moved = quarter(reduce_step, both_sum, 2, 2)
    first_other = pull_other(head_place, joined_back, joined_now)

    sums, gathers, both_sum, first_other, fed_own = tie(sums, moved, both_moved, first_other, fed_own)
    first_other = swap(first_other, "head", 1)
    moved = quarter(reduce_step, sums, 1)
    gathers_moved = quarter(gather_step, gathers, 1)
    both_moved = quarter(reduce_step, both_sum, 3, 2)

    sums, gathers, both_sum, first_other, fed_own = tie(
        moved, gathers_moved, both_moved, first_other, fed_own
    )
    mixer_next = 0.5 * mixer_momentum[0] + both_sum[0][:, :mixer_width]
    shrink_next = 0.5 * shrink_momentum[0] + both_sum[0][:, mixer_width:]
    both_gather = [gather_start(jnp.concatenate([mixer_next, shrink_next], axis=1).astype(bf16))]
    moved = quarter(reduce_step, sums, 2)
    gathers_moved = quarter(gather_step, gathers, 2)
    both_moved = quarter(gather_step, both_gather, 0, 2)
    layer_output = (own_half(middle) + fed_own + fed_other.astype(f32)).astype(bf16)

    sums, gathers, both_gather, first_other, layer_output = tie(
        moved, gathers_moved, both_moved, first_other, layer_output
    )
    moved = quarter(reduce_step, sums, 3)
    gathers_moved = quarter(gather_step, gathers, 3)
    both_moved = quarter(gather_step, both_gather, 1, 2)
    input_gradient, first_gain_grad = input_backward(
        head_place, joined_back, joined_now, first_other, tokens, middle_grad, norm_gains[0:1]
    )
    gain_totals = jnp.concatenate([first_gain_grad, 0.5 * second_gain_grad], axis=0)

    sums, gathers, both_gather, gain_totals = tie(moved, gathers_moved, both_moved, gain_totals)
    joined_next = 0.5 * joined_momentum[0] + jnp.concatenate(sums, axis=1)
    joined_gather = [gather_start(part) for part in halves_of(joined_next.astype(bf16))]
    moved = quarter(gather_step, joined_gather, 0)
    both_moved = quarter(gather_step, both_gather, 2, 2)
    gain_moved = total_step(gain_totals, 0)
    expand_state = schulz_early([gather_rows(part) for part in gathers], expand_next)
    joined_gather, both_gather, gain_totals, expand_state = tie(
        moved, both_moved, gain_moved, expand_state
    )
    moved = quarter(gather_step, joined_gather, 1)
    both_moved = quarter(gather_step, both_gather, 3, 2)
    gain_moved = total_step(gain_totals, 1)
    updated_expand = schulz_late(expand_state, expand_weight[0], left_grad.shape[0])
    joined_gather, both_gather, gain_totals, updated_expand = tie(
        moved, both_moved, gain_moved, updated_expand
    )
    both_full = [gather_rows(both_gather[0])]
    moved = quarter(gather_step, joined_gather, 2)
    gain_moved = total_step(gain_totals, 2)
    updated_shrink = schulz(
        both_full, mixer_width, shrink_next, shrink_weight[0], "schulz_shrink"
    )
    joined_gather, both_full, gain_totals, updated_shrink = tie(
        moved, both_full, gain_moved, updated_shrink
    )
    moved = quarter(gather_step, joined_gather, 3)
    gain_moved = total_step(gain_totals, 3)
    updated_mixer = schulz(both_full, 0, mixer_next, mixer_weight[0], "schulz_mixer")
    joined_gather, gain_totals, updated_mixer = tie(moved, gain_moved, updated_mixer)
    gain_totals = total_step(gain_totals, 4)
    updated_joined = schulz(
        [gather_rows(part) for part in joined_gather],
        None, joined_next, joined_weight[0], "schulz_joined",
    )

    momentum_gains = 0.5 * gain_momentum + gain_totals
    updated_gains = norm_gains - gain_rate * momentum_gains * lax.rsqrt(
        jnp.mean(momentum_gains * momentum_gains, axis=-1, keepdims=True) + 1e-06
    )
    return (
        layer_output,
        input_gradient,
        joined_next[None],
        mixer_next[None],
        expand_next[None],
        shrink_next[None],
        updated_joined[None],
        updated_mixer[None],
        updated_expand[None],
        updated_shrink[None],
        momentum_gains,
        updated_gains,
    )


def solution(mesh):
    rows = P(("dp", "head"), None)
    weight = P("head", "dp", None)
    return jax.shard_map(
        shards,
        mesh=mesh,
        in_specs=(rows, P("dp", None), P()) + (weight,) * 8 + (P(), P("dp", None)),
        out_specs=(rows, rows) + (weight,) * 8 + (P(), P()),
        check_vma=False,
    )
```

```python
import functools
import math

import jax
import jax.numpy as jnp
from jax import lax
from jax.experimental import pallas as pl
from jax.experimental.pallas import tpu as pltpu
from jax.sharding import PartitionSpec as P

HEAD_DIM = 64
NS_ITERS = 3

theta_base = 160000.0
norm_epsilon = 1e-05
ns_first = 3.4445
ns_second = -4.775
ns_third = 2.0315
muon_rate = 1.0
gain_rate = 0.3

bf16 = jnp.bfloat16
f32 = jnp.float32
LOG2E = math.log2(math.e)
QUERY_SCALE = 0.125 * LOG2E
SAFE_SCORE = 60.0
DEPTH = 128
TILE_Q = 256
TILE_K = 256
FWD_SKEW = 6
BWD_SKEW = 2

NN = (((1,), (0,)), ((), ()))
NT = (((1,), (1,)), ((), ()))
TN = (((0,), (0,)), ((), ()))
TT = (((0,), (1,)), ((), ()))
QUARTERS = 4
PAIR = ("012", "102")
JOINED_FIRST = ("012", "120")
OTHERS_FIRST = ("021", "201", "120")
ONE = ("012",)
FEED_ROWS = 256
FEED_CHUNKS = 3
ERF_TOP = (
    -2.72614225801306e-10, 2.77068142495902e-08, -2.10102402082508e-06, -5.69250639462346e-05,
    -7.34990630326855e-04, -2.95459980854025e-03, -1.60960333262415e-02,
)
ERF_BOTTOM = (
    -1.45660718464996e-05, -2.13374055278905e-04, -1.68282697438203e-03, -7.37332916720468e-03,
    -1.42647390514189e-02,
)


def dot(left, right, dims):
    return lax.dot_general(left, right, dims, preferred_element_type=f32)


def key_bounds(length_row, row_count):
    ends = jnp.cumsum(length_row)
    starts = ends - length_row
    first = jnp.arange(row_count // TILE_Q, dtype=jnp.int32) * TILE_Q
    labels = jnp.arange(length_row.shape[0], dtype=jnp.int32)

    def pick(places, table):
        segment = jnp.sum((places[:, None] >= ends[None, :]).astype(jnp.int32), axis=1)
        return jnp.sum(jnp.where(segment[:, None] == labels[None, :], table[None, :], 0), axis=1)

    low = pick(first, starts) // TILE_K
    high = (pick(first + TILE_Q - 1, ends) + TILE_K - 1) // TILE_K
    return low.astype(jnp.int32), high.astype(jnp.int32)


def doc_tables(length_row, row_count):
    ends = jnp.cumsum(length_row)
    starts = ends - length_row
    count = length_row.shape[0]
    places = jnp.arange(row_count, dtype=jnp.int32)[None, :]
    member = (places >= starts[:, None]) & (places < ends[:, None])
    rest = jnp.zeros((16 - count, row_count), f32)
    key_rows = jnp.concatenate([member.astype(f32), rest], axis=0).astype(bf16)
    query_rows = jnp.concatenate([jnp.where(member, 0.0, -1e30), rest], axis=0).astype(bf16)
    doc_first = jnp.sum(jnp.where(member, starts[:, None], 0), axis=0, keepdims=True)
    position = (places - doc_first).astype(f32)
    half_dim = HEAD_DIM // 2
    frequency = jnp.exp(
        jnp.arange(half_dim, dtype=f32) * (-2.0 * math.log(theta_base) / HEAD_DIM)
    )
    angles = frequency[:, None] * position
    return key_rows, query_rows, jnp.cos(angles), jnp.sin(angles)


def rotate(values, cosine, sine):
    half = HEAD_DIM // 2
    heads = values.reshape(-1, HEAD_DIM, values.shape[1])
    low, high = heads[:, :half], heads[:, half:]
    turned = jnp.concatenate([low * cosine - high * sine, high * cosine + low * sine], axis=1)
    return turned.reshape(values.shape)


def rows16(parts):
    rest = jnp.zeros((16 - len(parts), parts[0].shape[1]), f32)
    return jnp.concatenate([part.astype(f32) for part in parts] + [rest], axis=0).astype(bf16)


def split3(value):
    first = value.astype(bf16)
    left = value - first.astype(f32)
    second = left.astype(bf16)
    third = (left - second.astype(f32)).astype(bf16)
    return [first, second, third]


def three_ones(count):
    return jnp.concatenate([jnp.ones((3, count), f32), jnp.zeros((13, count), f32)], axis=0).astype(
        bf16
    )


def forward_kernel(
    low, high, queries, keys, values, key_rows, query_rows, out, logsum, keys_in, values_in, queries_in, safe
):
    heads = queries.shape[0] // HEAD_DIM
    rows = keys.shape[1]
    step = pl.program_id(0)

    @pl.when(step == 0)
    def _():
        worst = jnp.zeros((1, 1), f32)
        ones = rows16([jnp.ones((1, rows), f32)])
        for h in range(heads):
            band = slice(h * HEAD_DIM, (h + 1) * HEAD_DIM)
            key = keys[band, :]
            pad = jnp.zeros((DEPTH - HEAD_DIM - 16, rows), bf16)
            keys_in[h] = jnp.concatenate([key, key_rows[...], pad], axis=0).T
            values_in[h, :HEAD_DIM, :] = values[band, :]
            values_in[h, HEAD_DIM:, :] = ones
            query_full = queries[band, :].astype(f32)
            key_full = key.astype(f32)
            query_top = jnp.max(
                jnp.sum(query_full * query_full, axis=0, keepdims=True), axis=1, keepdims=True
            )
            key_top = jnp.max(
                jnp.sum(key_full * key_full, axis=0, keepdims=True), axis=1, keepdims=True
            )
            worst = jnp.maximum(worst, query_top * key_top)
        safe[0] = jnp.where(worst[0, 0] <= SAFE_SCORE * SAFE_SCORE, 1, 0)

    first = pl.multiple_of(step * TILE_Q, TILE_Q)
    for h in range(heads):
        queries_in[h, :HEAD_DIM, :] = queries[h * HEAD_DIM : (h + 1) * HEAD_DIM, pl.ds(first, TILE_Q)]
        queries_in[h, HEAD_DIM : HEAD_DIM + 16, :] = query_rows[...]
        queries_in[h, HEAD_DIM + 16 :, :] = jnp.zeros((DEPTH - HEAD_DIM - 16, TILE_Q), bf16)

    def finish(peaks, totals):
        for h in range(heads):
            weight = totals[h][HEAD_DIM : HEAD_DIM + 1, :]
            out[h * HEAD_DIM : (h + 1) * HEAD_DIM, :] = (totals[h][:HEAD_DIM, :] / weight).astype(bf16)
            level = jnp.log2(weight)
            logsum[h : h + 1, :] = level if peaks is None else peaks[h] + level

    empty = tuple(jnp.zeros((HEAD_DIM + 16, TILE_Q), f32) for _ in range(heads))

    @pl.when(safe[0] == 1)
    def _():
        def block(j, totals):
            span = pl.ds(pl.multiple_of(j * TILE_K, TILE_K), TILE_K)
            result = [None] * heads
            waiting = {}
            for t in range(heads + FWD_SKEW):
                if t < heads:
                    waiting[t] = dot(keys_in[t, span, :], queries_in[t], NN)
                h = t - FWD_SKEW
                if h >= 0:
                    raised = jnp.exp2(waiting.pop(h)).astype(bf16)
                    result[h] = totals[h] + dot(values_in[h, :, span], raised, NN)
            return tuple(result)

        finish(None, lax.fori_loop(low[step], high[step], block, empty))

    @pl.when(safe[0] == 0)
    def _():
        def block(j, carry):
            peaks, totals = carry
            span = pl.ds(pl.multiple_of(j * TILE_K, TILE_K), TILE_K)
            new_peaks = []
            new_totals = []
            for h in range(heads):
                scores = dot(keys_in[h, span, :], queries_in[h], NN)
                peak = jnp.maximum(peaks[h], jnp.max(scores, axis=0, keepdims=True))
                raised = jnp.exp2(scores - peak).astype(bf16)
                new_totals.append(
                    totals[h] * jnp.exp2(peaks[h] - peak) + dot(values_in[h, :, span], raised, NN)
                )
                new_peaks.append(peak)
            return tuple(new_peaks), tuple(new_totals)

        lowest = tuple(jnp.full((1, TILE_Q), -3e38, f32) for _ in range(heads))
        finish(*lax.fori_loop(low[step], high[step], block, (lowest, empty)))


def attention_forward(low, high, queries, keys, values, key_rows, query_rows):
    width, rows = queries.shape
    heads = width // HEAD_DIM

    def full(count):
        return pl.BlockSpec((count, rows), lambda i, low, high: (0, 0))

    def tile(count):
        return pl.BlockSpec((count, TILE_Q), lambda i, low, high: (0, i))

    return pl.pallas_call(
        forward_kernel,
        out_shape=(
            jax.ShapeDtypeStruct((width, rows), bf16),
            jax.ShapeDtypeStruct((heads, rows), f32),
        ),
        grid_spec=pltpu.PrefetchScalarGridSpec(
            num_scalar_prefetch=2,
            grid=(rows // TILE_Q,),
            in_specs=[full(width), full(width), full(width), full(16), tile(16)],
            out_specs=[tile(width), tile(heads)],
            scratch_shapes=[
                pltpu.VMEM((heads, rows, DEPTH), bf16),
                pltpu.VMEM((heads, HEAD_DIM + 16, rows), bf16),
                pltpu.VMEM((heads, DEPTH, TILE_Q), bf16),
                pltpu.SMEM((1,), jnp.int32),
            ],
        ),
        compiler_params=pltpu.CompilerParams(
            dimension_semantics=("arbitrary",), vmem_limit_bytes=40 << 20
        ),
        name="attention_forward",
    )(low, high, queries, keys, values, key_rows, query_rows)


def backward_kernel(
    low, high, queries, keys, values, grads, outs, logsum, key_rows, query_rows, cosine, sine,
    joined_back, *scratch
):
    heads = queries.shape[0] // HEAD_DIM
    rows = keys.shape[1]
    keys_in, values_in, queries_in, grads_in = scratch[:4]
    key_sum = scratch[4 : 4 + heads]
    value_sum = scratch[4 + heads : 4 + 2 * heads]
    query_sum = scratch[4 + 2 * heads : 4 + 3 * heads]
    step = pl.program_id(0)

    @pl.when(step == 0)
    def _():
        ones = three_ones(rows)
        for h in range(heads):
            band = slice(h * HEAD_DIM, (h + 1) * HEAD_DIM)
            pad = jnp.zeros((DEPTH - HEAD_DIM - 32, rows), bf16)
            keys_in[h] = jnp.concatenate([keys[band, :], key_rows[...], ones, pad], axis=0).T
            pad = jnp.zeros((DEPTH - HEAD_DIM - 16, rows), bf16)
            values_in[h] = jnp.concatenate([values[band, :], ones, pad], axis=0).T
            key_sum[h][...] = jnp.zeros((HEAD_DIM, rows), f32)
            value_sum[h][...] = jnp.zeros((HEAD_DIM, rows), f32)

    for h in range(heads):
        band = slice(h * HEAD_DIM, (h + 1) * HEAD_DIM)
        queries_in[h, :HEAD_DIM, :] = queries[band, :]
        queries_in[h, HEAD_DIM : HEAD_DIM + 16, :] = query_rows[...]
        queries_in[h, HEAD_DIM + 16 : HEAD_DIM + 32, :] = rows16(split3(-logsum[h : h + 1, :]))
        queries_in[h, HEAD_DIM + 32 :, :] = jnp.zeros((DEPTH - HEAD_DIM - 32, TILE_Q), bf16)
        inner = jnp.sum(grads[band, :].astype(f32) * outs[band, :].astype(f32), axis=0, keepdims=True)
        grads_in[h, :HEAD_DIM, :] = grads[band, :]
        grads_in[h, HEAD_DIM : HEAD_DIM + 16, :] = rows16(split3(-inner))
        grads_in[h, HEAD_DIM + 16 :, :] = jnp.zeros((DEPTH - HEAD_DIM - 16, TILE_Q), bf16)
        query_sum[h][...] = jnp.zeros((HEAD_DIM, TILE_Q), f32)

    def block(j, carry):
        span = pl.ds(pl.multiple_of(j * TILE_K, TILE_K), TILE_K)
        waiting = {}
        for t in range(heads + BWD_SKEW):
            if t < heads:
                waiting[t] = (
                    dot(keys_in[t, span, :], queries_in[t], NN),
                    dot(values_in[t, span, :], grads_in[t], NN),
                )
            h = t - BWD_SKEW
            if h < 0:
                continue
            band = slice(h * HEAD_DIM, (h + 1) * HEAD_DIM)
            scores, weight_grad = waiting.pop(h)
            softmax = jnp.exp2(scores)
            score_grad = (softmax * weight_grad).astype(bf16)
            value_sum[h][:, span] += dot(grads[band, :], softmax.astype(bf16), NT)
            key_sum[h][:, span] += dot(queries[band, :], score_grad, NT)
            query_sum[h][...] += dot(keys[band, span], score_grad, NN)
        return carry

    lax.fori_loop(low[step], high[step], block, 0)

    def store(offset, columns, value):
        half = HEAD_DIM // 2
        upper, lower = value[:half], value[half:]
        cos, sin = cosine[:, columns], sine[:, columns]
        joined_back[offset : offset + half, columns] = (upper * cos + lower * sin).astype(bf16)
        joined_back[offset + half : offset + HEAD_DIM, columns] = (lower * cos - upper * sin).astype(bf16)

    width = heads * HEAD_DIM
    columns = pl.ds(pl.multiple_of(step * TILE_Q, TILE_Q), TILE_Q)
    for h in range(heads):
        store(h * HEAD_DIM, columns, query_sum[h][...] * 0.125)

    @pl.when(step == pl.num_programs(0) - 1)
    def _():
        for h in range(heads):
            first = width + h * HEAD_DIM
            store(first, slice(0, rows), key_sum[h][...] * (1.0 / LOG2E))
            first += width
            joined_back[first : first + HEAD_DIM, :] = value_sum[h][...].astype(bf16)


def attention_backward(
    low, high, queries, keys, values, grads, outs, logsum, key_rows, query_rows, cosine, sine
):
    width, rows = queries.shape
    heads = width // HEAD_DIM

    def full(count):
        return pl.BlockSpec((count, rows), lambda i, low, high: (0, 0))

    def tile(count):
        return pl.BlockSpec((count, TILE_Q), lambda i, low, high: (0, i))

    return pl.pallas_call(
        backward_kernel,
        out_shape=jax.ShapeDtypeStruct((3 * width, rows), bf16),
        grid_spec=pltpu.PrefetchScalarGridSpec(
            num_scalar_prefetch=2,
            grid=(rows // TILE_Q,),
            in_specs=[
                tile(width), full(width), full(width), tile(width), tile(width), tile(heads),
                full(16), tile(16), full(HEAD_DIM // 2), full(HEAD_DIM // 2),
            ],
            out_specs=full(3 * width),
            scratch_shapes=[
                pltpu.VMEM((heads, rows, DEPTH), bf16),
                pltpu.VMEM((heads, rows, DEPTH), bf16),
                pltpu.VMEM((heads, DEPTH, TILE_Q), bf16),
                pltpu.VMEM((heads, DEPTH, TILE_Q), bf16),
            ]
            + [pltpu.VMEM((HEAD_DIM, rows), f32)] * (2 * heads)
            + [pltpu.VMEM((HEAD_DIM, TILE_Q), f32)] * heads,
        ),
        compiler_params=pltpu.CompilerParams(
            dimension_semantics=("arbitrary",), vmem_limit_bytes=52 << 20
        ),
        name="attention_backward",
    )(low, high, queries, keys, values, grads, outs, logsum, key_rows, query_rows, cosine, sine)


def layer_norm(values, gain_row):
    centred = values - jnp.mean(values, axis=-1, keepdims=True)
    inverse = lax.rsqrt(jnp.mean(centred * centred, axis=-1, keepdims=True) + norm_epsilon)
    normal = centred * inverse
    return normal * gain_row, normal, inverse


def norm_back(upstream, gain_row, normal, inverse):
    scaled = upstream * gain_row
    inner_mean = jnp.mean(scaled * normal, axis=-1, keepdims=True)
    return inverse * (scaled - jnp.mean(scaled, axis=-1, keepdims=True) - normal * inner_mean)


def horner(square, factors):
    total = factors[0] * square + factors[1]
    for factor in factors[2:]:
        total = total * square + factor
    return total


def error_function(value):
    value = jnp.clip(value, -4.0, 4.0)
    square = value * value
    return value * horner(square, ERF_TOP) / horner(square, ERF_BOTTOM)


def turn(value):
    columns = value.shape[1]
    rest = jnp.zeros((value.shape[0], -columns % 128), value.dtype)
    return jnp.concatenate([value, rest], axis=1).T[:columns, :]


def turn_back(value):
    lines = value.shape[0]
    rest = jnp.zeros((-lines % 128, value.shape[1]), value.dtype)
    return jnp.concatenate([value, rest], axis=0).T[:, :lines]


def first_kernel(head, own, other, gain, rows, normed):
    tiles = pl.num_programs(0) // 2
    mine = pl.program_id(0) // tiles == head[0]
    value = jnp.where(mine, own[...].astype(f32), other[...].astype(f32))
    rows[...] = value.astype(bf16)
    normed[...] = layer_norm(value, gain[...])[0].astype(bf16)


def first_norm(head, own, other, gain):
    half, width = own.shape
    tiles = half // FEED_ROWS
    result = jax.ShapeDtypeStruct((2 * half, width), bf16)
    spec = pl.BlockSpec((FEED_ROWS, width), lambda i, head: (i, 0))
    return pl.pallas_call(
        first_kernel,
        out_shape=(result, result),
        grid_spec=pltpu.PrefetchScalarGridSpec(
            num_scalar_prefetch=1,
            grid=(2 * tiles,),
            in_specs=[
                pl.BlockSpec(
                    (FEED_ROWS, width),
                    lambda i, head: (jnp.clip(i - head[0] * tiles, 0, tiles - 1), 0),
                ),
                pl.BlockSpec(
                    (FEED_ROWS, width),
                    lambda i, head: (jnp.clip(i - (1 - head[0]) * tiles, 0, tiles - 1), 0),
                ),
                pl.BlockSpec((1, width), lambda i, head: (0, 0)),
            ],
            out_specs=[spec, spec],
        ),
        compiler_params=pltpu.CompilerParams(dimension_semantics=("arbitrary",)),
        name="first_norm",
    )(head, own, other, gain)


def gradient_kernel(back, normed, *refs):
    grads, total = refs[:-1], refs[-1]
    step = pl.program_id(0)

    @pl.when(step == 0)
    def _():
        total[...] = dot(back[...], normed[...], NN)

    @pl.when(step > 0)
    def _():
        total[...] += dot(back[...], normed[...], NN)

    @pl.when(step == pl.num_programs(0) - 1)
    def _():
        first = 0
        for grad in grads:
            grad[...] = total[:, first : first + grad.shape[1]].astype(bf16)
            first += grad.shape[1]


def joined_gradient(back, normed):
    lines, count = back.shape
    width = normed.shape[1]
    tile = 2 * FEED_ROWS
    half = width // 256 * 128
    parts = [half, width - half]
    return pl.pallas_call(
        gradient_kernel,
        grid=(count // tile,),
        in_specs=[
            pl.BlockSpec((lines, tile), lambda i: (0, i)),
            pl.BlockSpec((tile, width), lambda i: (i, 0)),
        ],
        out_specs=[pl.BlockSpec((lines, part), lambda i: (0, 0)) for part in parts],
        out_shape=[jax.ShapeDtypeStruct((lines, part), bf16) for part in parts],
        scratch_shapes=[pltpu.VMEM((lines, width), f32)],
        compiler_params=pltpu.CompilerParams(
            dimension_semantics=("arbitrary",), vmem_limit_bytes=32 << 20
        ),
        name="joined_gradient",
    )(back, normed)


def pull_kernel(head, back, weight, out):
    out[...] = dot(back[...].T, weight[...], NN).astype(bf16)


def pull_other(head, back, weight):
    lines, count = back.shape
    width = weight.shape[1]
    tiles = count // 2 // FEED_ROWS
    return pl.pallas_call(
        pull_kernel,
        out_shape=jax.ShapeDtypeStruct((count // 2, width), bf16),
        grid_spec=pltpu.PrefetchScalarGridSpec(
            num_scalar_prefetch=1,
            grid=(tiles,),
            in_specs=[
                pl.BlockSpec((lines, FEED_ROWS), lambda i, head: (0, (1 - head[0]) * tiles + i)),
                pl.BlockSpec((lines, width), lambda i, head: (0, 0)),
            ],
            out_specs=pl.BlockSpec((FEED_ROWS, width), lambda i, head: (i, 0)),
        ),
        compiler_params=pltpu.CompilerParams(
            dimension_semantics=("arbitrary",), vmem_limit_bytes=24 << 20
        ),
        name="pull_other",
    )(head, back, weight)


def input_kernel(head, back, weight, other, rows, middle_grad, gain, input_grad, gain_grad):
    @pl.when(pl.program_id(0) == 0)
    def _():
        gain_grad[...] = jnp.zeros(gain_grad.shape, f32)

    pulled = dot(back[...].T, weight[...], NN) + other[...].astype(f32)
    unused, normal, inverse = layer_norm(rows[...].astype(f32), gain[...])
    input_grad[...] = middle_grad[...] + norm_back(pulled, gain[...], normal, inverse)
    gain_grad[...] += jnp.sum(pulled * normal, axis=0, keepdims=True)


def input_backward(head, back, weight, other, rows, middle_grad, gain):
    lines, count = back.shape
    width = weight.shape[1]
    tiles = count // 2 // FEED_ROWS

    def down():
        return pl.BlockSpec((FEED_ROWS, width), lambda i, head: (i, 0))

    return pl.pallas_call(
        input_kernel,
        out_shape=(
            jax.ShapeDtypeStruct((count // 2, width), f32),
            jax.ShapeDtypeStruct((1, width), f32),
        ),
        grid_spec=pltpu.PrefetchScalarGridSpec(
            num_scalar_prefetch=1,
            grid=(tiles,),
            in_specs=[
                pl.BlockSpec((lines, FEED_ROWS), lambda i, head: (0, head[0] * tiles + i)),
                pl.BlockSpec((lines, width), lambda i, head: (0, 0)),
                down(),
                down(),
                pl.BlockSpec((FEED_ROWS, width), lambda i, head: (head[0] * tiles + i, 0)),
                pl.BlockSpec((1, width), lambda i, head: (0, 0)),
            ],
            out_specs=[down(), pl.BlockSpec((1, width), lambda i, head: (0, 0))],
        ),
        compiler_params=pltpu.CompilerParams(
            dimension_semantics=("arbitrary",), vmem_limit_bytes=24 << 20
        ),
        name="input_backward",
    )(head, back, weight, other, rows, middle_grad, gain)


def feed_kernel(
    rows, attended, attended_other, upstream, gain, both, mixer_other, expand_left, expand_right,
    middle, hidden, second_part, shrink_grad, left_grad, right_grad, shrink,
    shrink_sum, expand_sum, expand
):
    step = pl.program_id(0)
    mixed, units = attended.shape[0], shrink.shape[0]
    chunk = units // FEED_CHUNKS

    @pl.when(step == 0)
    def _():
        expand[:, : expand_left.shape[1]] = expand_left[...]
        expand[:, expand_left.shape[1] :] = expand_right[...]
        shrink[...] = turn(both[:, mixed:])
        shrink_sum[...] = jnp.zeros(shrink_sum.shape, f32)
        expand_sum[...] = jnp.zeros(expand_sum.shape, f32)

    total = rows[...].astype(f32) + dot(attended[...].T, both[:, :mixed], NT)
    total = total + dot(attended_other[...].T, mixer_other[...], NT)
    middle[...] = total
    normed = layer_norm(total, gain[...])[0].astype(bf16)
    above = upstream[...]

    def project(c):
        first = slice(c * chunk, (c + 1) * chunk)
        second = slice(units + c * chunk, units + (c + 1) * chunk)
        return (
            dot(expand[first, :], normed, NT),
            dot(expand[second, :], normed, NT),
            dot(shrink[first, :], above, NT),
        )

    waiting = project(0)
    back = jnp.zeros(total.shape, f32)
    for c in range(FEED_CHUNKS):
        active, linear, grad = waiting
        if c + 1 < FEED_CHUNKS:
            waiting = project(c + 1)
        first = slice(c * chunk, (c + 1) * chunk)
        second = slice(units + c * chunk, units + (c + 1) * chunk)
        area = 0.5 * error_function(active * math.sqrt(0.5)) + 0.5
        gate = active * area
        density = jnp.exp(-0.5 * active * active) * (1.0 / math.sqrt(2.0 * math.pi))
        unit = (gate * linear).astype(bf16)
        active_back = (grad * linear * (area + active * density)).astype(bf16)
        linear_back = (grad * gate).astype(bf16)
        hidden[first, :] = unit
        shrink_sum[first, :] += dot(unit, above, NN)
        expand_sum[first, :] += dot(active_back, normed, NN)
        expand_sum[second, :] += dot(linear_back, normed, NN)
        back = back + dot(active_back, expand[first, :], TN) + dot(linear_back, expand[second, :], TN)
    second_part[...] = back.astype(bf16)

    @pl.when(step == pl.num_programs(0) - 1)
    def _():
        shrink_grad[...] = shrink_sum[...].astype(bf16)
        cut = left_grad.shape[1]
        left_grad[...] = expand_sum[:, :cut].astype(bf16)
        right_grad[...] = expand_sum[:, cut:].astype(bf16)


def feed_forward(rows, attended, attended_other, upstream, gain, both, mixer_other, expand):
    count, width = rows.shape
    mixed, units = attended.shape[0], expand[0].shape[0] // 2

    def full(*shape):
        return pl.BlockSpec(shape, lambda i: (0, 0))

    def down(columns):
        return pl.BlockSpec((FEED_ROWS, columns), lambda i: (i, 0))

    def along(lines):
        return pl.BlockSpec((lines, FEED_ROWS), lambda i: (0, i))

    return pl.pallas_call(
        feed_kernel,
        grid=(count // FEED_ROWS,),
        in_specs=[
            down(width), along(mixed), along(mixed), down(width), full(1, width),
            full(*both.shape), full(width, mixed), full(*expand[0].shape), full(*expand[1].shape),
        ],
        out_specs=[
            down(width), along(units), down(width), full(units, width),
            full(*expand[0].shape), full(*expand[1].shape), full(units, width),
        ],
        out_shape=(
            jax.ShapeDtypeStruct((count, width), f32),
            jax.ShapeDtypeStruct((units, count), bf16),
            jax.ShapeDtypeStruct((count, width), bf16),
            jax.ShapeDtypeStruct((units, width), bf16),
            jax.ShapeDtypeStruct(expand[0].shape, bf16),
            jax.ShapeDtypeStruct(expand[1].shape, bf16),
            jax.ShapeDtypeStruct((units, width), bf16),
        ),
        scratch_shapes=[
            pltpu.VMEM((units, width), f32),
            pltpu.VMEM((2 * units, width), f32),
            pltpu.VMEM((2 * units, width), bf16),
        ],
        compiler_params=pltpu.CompilerParams(
            dimension_semantics=("arbitrary",), vmem_limit_bytes=48 << 20
        ),
        name="feed_forward",
    )(rows, attended, attended_other, upstream, gain, both, mixer_other, *expand)


def norm_kernel(
    middle, own, other, upstream, gain, both, attended, shrink_grad,
    middle_grad, attended_grad, both_grad, gain_grad, mixer_turned, mixer_sum
):
    step = pl.program_id(0)

    @pl.when(step == 0)
    def _():
        mixer_turned[...] = both[:, : attended.shape[0]].T
        mixer_sum[...] = jnp.zeros(mixer_sum.shape, f32)
        gain_grad[...] = jnp.zeros(gain_grad.shape, f32)

    unused, normal, inverse = layer_norm(middle[...], gain[...])
    back = own[...].astype(f32) + other[...].astype(f32)
    grad = upstream[...].astype(f32) + norm_back(back, gain[...], normal, inverse)
    middle_grad[...] = grad
    grad_low = grad.astype(bf16)
    attended_grad[...] = dot(mixer_turned[...], grad_low, NT).astype(bf16)
    mixer_sum[...] += dot(attended[...], grad_low, NN)
    gain_grad[...] += jnp.sum(back * normal, axis=0, keepdims=True)

    @pl.when(step == pl.num_programs(0) - 1)
    def _():
        mixed = attended.shape[0]
        both_grad[:, :mixed] = mixer_sum[...].T.astype(bf16)
        both_grad[:, mixed:] = turn_back(shrink_grad[...])


def norm_backward(middle, own, other, upstream, gain, both, attended, shrink_grad):
    count, width = middle.shape
    mixed = attended.shape[0]

    def full(*shape):
        return pl.BlockSpec(shape, lambda i: (0, 0))

    def down(columns):
        return pl.BlockSpec((FEED_ROWS, columns), lambda i: (i, 0))

    def along(lines):
        return pl.BlockSpec((lines, FEED_ROWS), lambda i: (0, i))

    return pl.pallas_call(
        norm_kernel,
        grid=(count // FEED_ROWS,),
        in_specs=[
            down(width), down(width), down(width), down(width), full(1, width),
            full(*both.shape), along(mixed), full(*shrink_grad.shape),
        ],
        out_specs=[down(width), along(mixed), full(*both.shape), full(1, width)],
        out_shape=(
            jax.ShapeDtypeStruct((count, width), f32),
            jax.ShapeDtypeStruct((mixed, count), bf16),
            jax.ShapeDtypeStruct(both.shape, bf16),
            jax.ShapeDtypeStruct((1, width), f32),
        ),
        scratch_shapes=[pltpu.VMEM((mixed, width), bf16), pltpu.VMEM((mixed, width), f32)],
        compiler_params=pltpu.CompilerParams(
            dimension_semantics=("arbitrary",), vmem_limit_bytes=40 << 20
        ),
        name="norm_backward",
    )(middle, own, other, upstream, gain, both, attended, shrink_grad)


def swap(value, axis, bit):
    count = lax.axis_size(axis)
    return lax.ppermute(value, axis, [(i, i ^ bit) for i in range(count)])


def bit_order(lead):
    bits = lax.axis_size("dp").bit_length() - 1
    return [int(bit) for bit in lead] + list(range(len(lead), bits))


def steps_count():
    return lax.axis_size("dp").bit_length() - 1


def cut(held, bit):
    axis = steps_count() - 1 - bit
    side = (lax.axis_index("dp") >> bit) & 1
    kept = lax.dynamic_slice_in_dim(held, side, 1, axis)
    return kept, lax.dynamic_slice_in_dim(held, 1 - side, 1, axis)


def reduce_start(value, lead):
    bits = steps_count()
    rows = value.shape[0] >> bits
    return cut(value.reshape((2,) * bits + (rows, value.shape[1])), bit_order(lead)[0])


def reduce_step(held, step, lead):
    bits = steps_count()
    kept, sent = held if step == 0 else cut(held, bit_order(lead)[step])
    total = kept.astype(f32) + swap(sent, "dp", 1 << bit_order(lead)[step]).astype(f32)
    if step + 1 == bits:
        return total.reshape(kept.shape[-2:])
    return total.astype(bf16)


def gather_start(value):
    return value[(None,) * steps_count()]


def gather_step(held, step, lead):
    bits = steps_count()
    bit = bit_order(lead)[bits - 1 - step]
    return jnp.concatenate([held, swap(held, "dp", 1 << bit)], axis=bits - 1 - bit)


def ordered_step(held, step, lead):
    bits = steps_count()
    bit = bit_order(lead)[bits - 1 - step]
    got = swap(held, "dp", 1 << bit)
    low_side = ((lax.axis_index("dp") >> bit) & 1) == 0
    return jnp.concatenate(
        [jnp.where(low_side, held, got), jnp.where(low_side, got, held)], axis=bits - 1 - bit
    )


def gather_rows(held):
    return held.reshape(-1, held.shape[-1])


def halves_of(value):
    unit = value.shape[1] // 256 * 128
    return [value[:, :unit], value[:, unit:]]


def quarter(step, states, part, leads):
    bits = steps_count()
    for index in range(bits * part // QUARTERS, bits * (part + 1) // QUARTERS):
        states = [step(state, index, lead) for state, lead in zip(states, leads)]
    return states


def tie(*values):
    return lax.optimization_barrier(values)


def total_step(value, part):
    if part == 0:
        return value + swap(value, "head", 1)
    bits = steps_count()
    for bit in range(bits * (part - 1) // QUARTERS, bits * part // QUARTERS):
        value = value + swap(value, "dp", 1 << bit)
    return value


def schulz_start(held, own, gram, low):
    down = 0
    for left in held:
        along = 0
        for right in held:
            gram[down : down + left.shape[1], along : along + right.shape[1]] = dot(left, right, TN)
            along += right.shape[1]
        down += left.shape[1]
    shape = gram.shape
    diagonal = lax.broadcasted_iota(jnp.int32, shape, 0) == lax.broadcasted_iota(jnp.int32, shape, 1)
    trace = jnp.sum(jnp.where(diagonal, gram[...], 0.0), axis=0, keepdims=True)
    norm_value = jnp.sqrt(jnp.sum(trace, axis=1, keepdims=True)) + 1e-07
    gram[...] = gram[...] * (1.0 / (norm_value * norm_value))
    low[...] = gram[...].astype(bf16)
    return own[...] / norm_value


def schulz_steps(rows, gram, low, change, first, stop):
    columns = gram.shape[0]
    lines = 256 if columns % 256 == 0 else columns

    def per_block(body):
        def run(index, carry):
            body(pl.ds(pl.multiple_of(index * lines, lines), lines))
            return carry

        lax.fori_loop(0, columns // lines, run, 0)

    def form_change(block):
        squared = dot(low[block, :], low[...], NN)
        change[block, :] = (ns_second * gram[block, :] + ns_third * squared).astype(bf16)

    def next_gram(block):
        once = ns_first * gram[block, :] + dot(low[block, :], change[...], NN)
        twice = ns_first * once + dot(once.astype(bf16), change[...], NN)
        gram[block, :] = twice
        low[block, :] = twice.astype(bf16)

    for iteration in range(first, stop):
        per_block(form_change)
        rows = ns_first * rows + dot(rows.astype(bf16), change[...], NN)
        if iteration + 1 < NS_ITERS:
            per_block(next_gram)
    return rows


def whole_kernel(*refs, count, offset, scale):
    parts = refs[:count]
    own, weight, updated, gram, low, change = refs[count:]
    if offset is None:
        held = [part[...] for part in parts]
    else:
        held = [parts[0][:, offset : offset + gram.shape[0]]]
    rows = schulz_start(held, own, gram, low)
    updated[...] = weight[...] - scale * schulz_steps(rows, gram, low, change, 0, NS_ITERS)


def early_kernel(*refs, count):
    own, rows, gram_out, low_out, gram, low, change = refs[count:]
    start = schulz_start([part[...] for part in refs[:count]], own, gram, low)
    rows[...] = start
    gram_out[...] = gram[...]
    low_out[...] = low[...]


def late_kernel(rows, gram_in, low_in, weight, updated, gram, low, change, *, scale):
    gram[...] = gram_in[...]
    low[...] = low_in[...]
    done = schulz_steps(rows[...], gram, low, change, 0, NS_ITERS)
    updated[...] = weight[...] - scale * done


def square_scratch(columns):
    return [
        pltpu.VMEM((columns, columns), f32),
        pltpu.VMEM((columns, columns), bf16),
        pltpu.VMEM((columns, columns), bf16),
    ]


def shape_scale(rows, columns):
    return muon_rate * math.sqrt(rows / columns)


def schulz(parts, offset, own, weight, name):
    columns = own.shape[1]
    return pl.pallas_call(
        functools.partial(
            whole_kernel, count=len(parts), offset=offset, scale=shape_scale(parts[0].shape[0], columns)
        ),
        out_shape=jax.ShapeDtypeStruct(own.shape, f32),
        scratch_shapes=square_scratch(columns),
        compiler_params=pltpu.CompilerParams(vmem_limit_bytes=40 << 20),
        name=name,
    )(*parts, own, weight)


def schulz_early(parts, own):
    columns = own.shape[1]
    return pl.pallas_call(
        functools.partial(early_kernel, count=len(parts)),
        out_shape=(
            jax.ShapeDtypeStruct(own.shape, f32),
            jax.ShapeDtypeStruct((columns, columns), f32),
            jax.ShapeDtypeStruct((columns, columns), bf16),
        ),
        scratch_shapes=square_scratch(columns),
        compiler_params=pltpu.CompilerParams(vmem_limit_bytes=40 << 20),
        name="schulz_early",
    )(*parts, own)


def schulz_late(state, weight, rows):
    columns = weight.shape[1]
    return pl.pallas_call(
        functools.partial(late_kernel, scale=shape_scale(rows, columns)),
        out_shape=jax.ShapeDtypeStruct(weight.shape, f32),
        scratch_shapes=square_scratch(columns),
        compiler_params=pltpu.CompilerParams(vmem_limit_bytes=40 << 20),
        name="schulz_late",
    )(*state, weight)


def shards(
    tokens,
    lengths,
    norm_gains,
    joined_weight,
    mixer_weight,
    expand_weight,
    shrink_weight,
    joined_momentum,
    mixer_momentum,
    expand_momentum,
    shrink_momentum,
    gain_momentum,
    cotangent,
):
    row_count = cotangent.shape[0]
    local_rows = tokens.shape[0]
    head = lax.axis_index("head")
    mixer_width = mixer_weight.shape[2]

    def own_half(value):
        return lax.dynamic_slice_in_dim(value, head * local_rows, local_rows, 0)

    joined_parts = [gather_start(part) for part in halves_of(joined_weight[0].astype(bf16))]
    joined_parts = quarter(ordered_step, joined_parts, 0, JOINED_FIRST)
    others = [gather_start(part) for part in halves_of(expand_weight[0].astype(bf16))] + [
        gather_start(jnp.concatenate([mixer_weight[0], shrink_weight[0]], axis=1).astype(bf16))
    ]
    key_rows, query_rows, cosine, sine = doc_tables(lengths[0], row_count)
    low, high = key_bounds(lengths[0], row_count)
    head_place = head[None]
    tokens_other = swap(tokens, "head", 1)

    joined_parts, others, tokens_other = tie(joined_parts, others, tokens_other)
    joined_parts = quarter(ordered_step, joined_parts, 1, JOINED_FIRST)
    others = quarter(ordered_step, others, 0, OTHERS_FIRST)
    rows_low, first_low = first_norm(head_place, tokens, tokens_other, norm_gains[0:1])
    joined_parts, others, first_low = tie(joined_parts, others, first_low)
    joined_parts = quarter(ordered_step, joined_parts, 2, JOINED_FIRST)
    others = quarter(ordered_step, others, 1, OTHERS_FIRST)
    joined_parts, others = tie(joined_parts, others)
    joined_parts = quarter(ordered_step, joined_parts, 3, JOINED_FIRST)
    moved = quarter(ordered_step, others, 2, OTHERS_FIRST)

    joined_low = jnp.concatenate([gather_rows(part) for part in joined_parts], axis=1)
    joined = dot(joined_low, first_low, NT)
    width = joined.shape[0] // 3
    queries = (rotate(joined[:width], cosine, sine) * QUERY_SCALE).astype(bf16)
    keys = rotate(joined[width : 2 * width], cosine, sine).astype(bf16)
    values = joined[2 * width :].astype(bf16)
    others, queries, keys, values, low = tie(moved, queries, keys, values, low)
    moved = quarter(ordered_step, others, 3, OTHERS_FIRST)
    attended, logsum = attention_forward(low, high, queries, keys, values, key_rows, query_rows)
    others, attended, logsum = tie(moved, attended, logsum)
    attended_other = swap(attended, "head", 1)
    both_low = gather_rows(others[2])
    mixer_other = swap(both_low[:, :mixer_width], "head", 1)

    second_gain = norm_gains[1:2]
    middle, hidden, second_part, shrink_grad, left_grad, right_grad, shrink_turned = feed_forward(
        rows_low, attended, attended_other, cotangent, second_gain,
        both_low, mixer_other, [gather_rows(part) for part in others[:2]],
    )
    second_other = swap(second_part, "head", 1)

    sums = [reduce_start(part, lead) for part, lead in zip((left_grad, right_grad), PAIR)]
    sums, second_other = tie(sums, second_other)
    moved = quarter(reduce_step, sums, 0, PAIR)
    middle_grad, attended_grad, both_grad, second_gain_grad = norm_backward(
        middle, second_part, second_other, cotangent, second_gain, both_low, attended, shrink_grad
    )
    both_sum = [reduce_start(both_grad, ONE[0])]

    sums, attended_grad, shrink_now = tie(moved, attended_grad, shrink_turned)
    moved = quarter(reduce_step, sums, 1, PAIR)

    def fed(columns):
        units = lax.dynamic_slice_in_dim(hidden, columns, local_rows, 1)
        return dot(units, shrink_now, TN)

    fed_other = fed((1 - head) * local_rows).astype(bf16)
    fed_own = fed(head * local_rows)

    sums, both_sum, fed_other, fed_own, low = tie(moved, both_sum, fed_other, fed_own, low)
    moved = quarter(reduce_step, sums, 2, PAIR)
    both_moved = quarter(reduce_step, both_sum, 0, ONE)
    fed_other = swap(fed_other, "head", 1)
    joined_back = attention_backward(
        low, high, queries, keys, values, attended_grad, attended, logsum, key_rows, query_rows,
        cosine, sine,
    )
    sums, both_sum, joined_back = tie(moved, both_moved, joined_back)
    moved = quarter(reduce_step, sums, 3, PAIR)
    both_moved = quarter(reduce_step, both_sum, 1, ONE)
    joined_grad = joined_gradient(joined_back, first_low)

    sums, both_sum, joined_grad, joined_now = tie(moved, both_moved, joined_grad, joined_low)
    expand_next = 0.5 * expand_momentum[0] + jnp.concatenate(sums, axis=1)
    gathers = [gather_start(part) for part in halves_of(expand_next.astype(bf16))]
    sums = [reduce_start(part, lead) for part, lead in zip(joined_grad, PAIR)]
    sums = quarter(reduce_step, sums, 0, PAIR)
    moved = quarter(gather_step, gathers, 0, PAIR)
    both_moved = quarter(reduce_step, both_sum, 2, ONE)
    first_other = pull_other(head_place, joined_back, joined_now)

    sums, gathers, both_sum, first_other, fed_own = tie(sums, moved, both_moved, first_other, fed_own)
    first_other = swap(first_other, "head", 1)
    moved = quarter(reduce_step, sums, 1, PAIR)
    gathers_moved = quarter(gather_step, gathers, 1, PAIR)
    both_moved = quarter(reduce_step, both_sum, 3, ONE)

    sums, gathers, both_sum, first_other, fed_own = tie(
        moved, gathers_moved, both_moved, first_other, fed_own
    )
    mixer_next = 0.5 * mixer_momentum[0] + both_sum[0][:, :mixer_width]
    shrink_next = 0.5 * shrink_momentum[0] + both_sum[0][:, mixer_width:]
    both_gather = [gather_start(jnp.concatenate([mixer_next, shrink_next], axis=1).astype(bf16))]
    moved = quarter(reduce_step, sums, 2, PAIR)
    gathers_moved = quarter(gather_step, gathers, 2, PAIR)
    both_moved = quarter(gather_step, both_gather, 0, ONE)
    layer_output = (own_half(middle) + fed_own + fed_other.astype(f32)).astype(bf16)

    sums, gathers, both_gather, first_other, layer_output = tie(
        moved, gathers_moved, both_moved, first_other, layer_output
    )
    moved = quarter(reduce_step, sums, 3, PAIR)
    gathers_moved = quarter(gather_step, gathers, 3, PAIR)
    both_moved = quarter(gather_step, both_gather, 1, ONE)
    input_gradient, first_gain_grad = input_backward(
        head_place, joined_back, joined_now, first_other, tokens, middle_grad, norm_gains[0:1]
    )
    gain_totals = jnp.concatenate([first_gain_grad, 0.5 * second_gain_grad], axis=0)

    sums, gathers, both_gather, gain_totals = tie(moved, gathers_moved, both_moved, gain_totals)
    joined_next = 0.5 * joined_momentum[0] + jnp.concatenate(sums, axis=1)
    joined_gather = [gather_start(part) for part in halves_of(joined_next.astype(bf16))]
    moved = quarter(gather_step, joined_gather, 0, PAIR)
    both_moved = quarter(gather_step, both_gather, 2, ONE)
    gain_moved = total_step(gain_totals, 0)
    expand_state = schulz_early([gather_rows(part) for part in gathers], expand_next)
    joined_gather, both_gather, gain_totals, expand_state = tie(
        moved, both_moved, gain_moved, expand_state
    )
    moved = quarter(gather_step, joined_gather, 1, PAIR)
    both_moved = quarter(gather_step, both_gather, 3, ONE)
    gain_moved = total_step(gain_totals, 1)
    updated_expand = schulz_late(expand_state, expand_weight[0], left_grad.shape[0])
    joined_gather, both_gather, gain_totals, updated_expand = tie(
        moved, both_moved, gain_moved, updated_expand
    )
    both_full = [gather_rows(both_gather[0])]
    moved = quarter(gather_step, joined_gather, 2, PAIR)
    gain_moved = total_step(gain_totals, 2)
    updated_shrink = schulz(
        both_full, mixer_width, shrink_next, shrink_weight[0], "schulz_shrink"
    )
    joined_gather, both_full, gain_totals, updated_shrink = tie(
        moved, both_full, gain_moved, updated_shrink
    )
    moved = quarter(gather_step, joined_gather, 3, PAIR)
    gain_moved = total_step(gain_totals, 3)
    updated_mixer = schulz(both_full, 0, mixer_next, mixer_weight[0], "schulz_mixer")
    joined_gather, gain_totals, updated_mixer = tie(moved, gain_moved, updated_mixer)
    gain_totals = total_step(gain_totals, 4)
    updated_joined = schulz(
        [gather_rows(part) for part in joined_gather],
        None, joined_next, joined_weight[0], "schulz_joined",
    )

    momentum_gains = 0.5 * gain_momentum + gain_totals
    updated_gains = norm_gains - gain_rate * momentum_gains * lax.rsqrt(
        jnp.mean(momentum_gains * momentum_gains, axis=-1, keepdims=True) + 1e-06
    )
    return (
        layer_output,
        input_gradient,
        joined_next[None],
        mixer_next[None],
        expand_next[None],
        shrink_next[None],
        updated_joined[None],
        updated_mixer[None],
        updated_expand[None],
        updated_shrink[None],
        momentum_gains,
        updated_gains,
    )


def solution(mesh):
    rows = P(("dp", "head"), None)
    weight = P("head", "dp", None)
    return jax.shard_map(
        shards,
        mesh=mesh,
        in_specs=(rows, P("dp", None), P()) + (weight,) * 8 + (P(), P("dp", None)),
        out_specs=(rows, rows) + (weight,) * 8 + (P(), P()),
        check_vma=False,
    )
```

```python
import functools
import math

import jax
import jax.numpy as jnp
from jax import lax
from jax.experimental import pallas as pl
from jax.experimental.pallas import tpu as pltpu
from jax.sharding import PartitionSpec as P

HEAD_DIM = 64
NS_ITERS = 3

theta_base = 160000.0
norm_epsilon = 1e-05
ns_first = 3.4445
ns_second = -4.775
ns_third = 2.0315
muon_rate = 1.0
gain_rate = 0.3

bf16 = jnp.bfloat16
f32 = jnp.float32
LOG2E = math.log2(math.e)
QUERY_SCALE = 0.125 * LOG2E
SAFE_SCORE = 60.0
DEPTH = 128
TILE_Q = 256
TILE_K = 256
FWD_SKEW = 6
BWD_SKEW = 2

NN = (((1,), (0,)), ((), ()))
NT = (((1,), (1,)), ((), ()))
TN = (((0,), (0,)), ((), ()))
TT = (((0,), (1,)), ((), ()))
QUARTERS = 4
PAIR = ("012", "102")
JOINED_FIRST = ("012", "120")
OTHERS_FIRST = ("021", "201", "120")
ONE = ("012",)
FEED_ROWS = 256
FEED_TILE = 512
FEED_CHUNKS = 2
ERF_TOP = (
    -2.72614225801306e-10, 2.77068142495902e-08, -2.10102402082508e-06, -5.69250639462346e-05,
    -7.34990630326855e-04, -2.95459980854025e-03, -1.60960333262415e-02,
)
ERF_BOTTOM = (
    -1.45660718464996e-05, -2.13374055278905e-04, -1.68282697438203e-03, -7.37332916720468e-03,
    -1.42647390514189e-02,
)


def dot(left, right, dims):
    return lax.dot_general(left, right, dims, preferred_element_type=f32)


def key_bounds(length_row, row_count):
    ends = jnp.cumsum(length_row)
    starts = ends - length_row
    first = jnp.arange(row_count // TILE_Q, dtype=jnp.int32) * TILE_Q
    labels = jnp.arange(length_row.shape[0], dtype=jnp.int32)

    def pick(places, table):
        segment = jnp.sum((places[:, None] >= ends[None, :]).astype(jnp.int32), axis=1)
        return jnp.sum(jnp.where(segment[:, None] == labels[None, :], table[None, :], 0), axis=1)

    low = pick(first, starts) // TILE_K
    high = (pick(first + TILE_Q - 1, ends) + TILE_K - 1) // TILE_K
    return low.astype(jnp.int32), high.astype(jnp.int32)


def doc_tables(length_row, row_count):
    ends = jnp.cumsum(length_row)
    starts = ends - length_row
    count = length_row.shape[0]
    places = jnp.arange(row_count, dtype=jnp.int32)[None, :]
    member = (places >= starts[:, None]) & (places < ends[:, None])
    rest = jnp.zeros((16 - count, row_count), f32)
    key_rows = jnp.concatenate([member.astype(f32), rest], axis=0).astype(bf16)
    query_rows = jnp.concatenate([jnp.where(member, 0.0, -1e30), rest], axis=0).astype(bf16)
    doc_first = jnp.sum(jnp.where(member, starts[:, None], 0), axis=0, keepdims=True)
    position = (places - doc_first).astype(f32)
    half_dim = HEAD_DIM // 2
    frequency = jnp.exp(
        jnp.arange(half_dim, dtype=f32) * (-2.0 * math.log(theta_base) / HEAD_DIM)
    )
    angles = frequency[:, None] * position
    return key_rows, query_rows, jnp.cos(angles), jnp.sin(angles)


def rotate(values, cosine, sine):
    half = HEAD_DIM // 2
    heads = values.reshape(-1, HEAD_DIM, values.shape[1])
    low, high = heads[:, :half], heads[:, half:]
    turned = jnp.concatenate([low * cosine - high * sine, high * cosine + low * sine], axis=1)
    return turned.reshape(values.shape)


def rows16(parts):
    rest = jnp.zeros((16 - len(parts), parts[0].shape[1]), f32)
    return jnp.concatenate([part.astype(f32) for part in parts] + [rest], axis=0).astype(bf16)


def split3(value):
    first = value.astype(bf16)
    left = value - first.astype(f32)
    second = left.astype(bf16)
    third = (left - second.astype(f32)).astype(bf16)
    return [first, second, third]


def three_ones(count):
    return jnp.concatenate([jnp.ones((3, count), f32), jnp.zeros((13, count), f32)], axis=0).astype(
        bf16
    )


def tile_loop(low, high, block, carry):
    pairs = (high - low) // 2

    def two(index, carry):
        first = low + 2 * index
        return block([first, first + 1], carry)

    carry = lax.fori_loop(0, pairs, two, carry)
    return lax.fori_loop(low + 2 * pairs, high, lambda j, carry: block([j], carry), carry)


def forward_kernel(
    low, high, queries, keys, values, key_rows, query_rows, out, logsum, keys_in, values_in, queries_in, safe
):
    heads = queries.shape[0] // HEAD_DIM
    rows = keys.shape[1]
    step = pl.program_id(0)

    @pl.when(step == 0)
    def _():
        worst = jnp.zeros((1, 1), f32)
        ones = rows16([jnp.ones((1, rows), f32)])
        for h in range(heads):
            band = slice(h * HEAD_DIM, (h + 1) * HEAD_DIM)
            key = keys[band, :]
            pad = jnp.zeros((DEPTH - HEAD_DIM - 16, rows), bf16)
            keys_in[h] = jnp.concatenate([key, key_rows[...], pad], axis=0).T
            values_in[h, :HEAD_DIM, :] = values[band, :]
            values_in[h, HEAD_DIM:, :] = ones
            query_full = queries[band, :].astype(f32)
            key_full = key.astype(f32)
            query_top = jnp.max(
                jnp.sum(query_full * query_full, axis=0, keepdims=True), axis=1, keepdims=True
            )
            key_top = jnp.max(
                jnp.sum(key_full * key_full, axis=0, keepdims=True), axis=1, keepdims=True
            )
            worst = jnp.maximum(worst, query_top * key_top)
        safe[0] = jnp.where(worst[0, 0] <= SAFE_SCORE * SAFE_SCORE, 1, 0)

    first = pl.multiple_of(step * TILE_Q, TILE_Q)
    for h in range(heads):
        queries_in[h, :HEAD_DIM, :] = queries[h * HEAD_DIM : (h + 1) * HEAD_DIM, pl.ds(first, TILE_Q)]
        queries_in[h, HEAD_DIM : HEAD_DIM + 16, :] = query_rows[...]
        queries_in[h, HEAD_DIM + 16 :, :] = jnp.zeros((DEPTH - HEAD_DIM - 16, TILE_Q), bf16)

    def finish(peaks, totals):
        for h in range(heads):
            weight = totals[h][HEAD_DIM : HEAD_DIM + 1, :]
            out[h * HEAD_DIM : (h + 1) * HEAD_DIM, :] = (totals[h][:HEAD_DIM, :] / weight).astype(bf16)
            level = jnp.log2(weight)
            logsum[h : h + 1, :] = level if peaks is None else peaks[h] + level

    empty = tuple(jnp.zeros((HEAD_DIM + 16, TILE_Q), f32) for _ in range(heads))

    @pl.when(safe[0] == 1)
    def _():
        def block(tiles, totals):
            spans = [pl.ds(pl.multiple_of(j * TILE_K, TILE_K), TILE_K) for j in tiles]
            units = [(span, h) for span in spans for h in range(heads)]
            totals = list(totals)
            waiting = {}
            for t in range(len(units) + FWD_SKEW):
                if t < len(units):
                    span, h = units[t]
                    waiting[t] = dot(keys_in[h, span, :], queries_in[h], NN)
                if t >= FWD_SKEW:
                    span, h = units[t - FWD_SKEW]
                    raised = jnp.exp2(waiting.pop(t - FWD_SKEW)).astype(bf16)
                    totals[h] = totals[h] + dot(values_in[h, :, span], raised, NN)
            return tuple(totals)

        finish(None, tile_loop(low[step], high[step], block, empty))

    @pl.when(safe[0] == 0)
    def _():
        def block(j, carry):
            peaks, totals = carry
            span = pl.ds(pl.multiple_of(j * TILE_K, TILE_K), TILE_K)
            new_peaks = []
            new_totals = []
            for h in range(heads):
                scores = dot(keys_in[h, span, :], queries_in[h], NN)
                peak = jnp.maximum(peaks[h], jnp.max(scores, axis=0, keepdims=True))
                raised = jnp.exp2(scores - peak).astype(bf16)
                new_totals.append(
                    totals[h] * jnp.exp2(peaks[h] - peak) + dot(values_in[h, :, span], raised, NN)
                )
                new_peaks.append(peak)
            return tuple(new_peaks), tuple(new_totals)

        lowest = tuple(jnp.full((1, TILE_Q), -3e38, f32) for _ in range(heads))
        finish(*lax.fori_loop(low[step], high[step], block, (lowest, empty)))


def attention_forward(low, high, queries, keys, values, key_rows, query_rows):
    width, rows = queries.shape
    heads = width // HEAD_DIM

    def full(count):
        return pl.BlockSpec((count, rows), lambda i, low, high: (0, 0))

    def tile(count):
        return pl.BlockSpec((count, TILE_Q), lambda i, low, high: (0, i))

    return pl.pallas_call(
        forward_kernel,
        out_shape=(
            jax.ShapeDtypeStruct((width, rows), bf16),
            jax.ShapeDtypeStruct((heads, rows), f32),
        ),
        grid_spec=pltpu.PrefetchScalarGridSpec(
            num_scalar_prefetch=2,
            grid=(rows // TILE_Q,),
            in_specs=[full(width), full(width), full(width), full(16), tile(16)],
            out_specs=[tile(width), tile(heads)],
            scratch_shapes=[
                pltpu.VMEM((heads, rows, DEPTH), bf16),
                pltpu.VMEM((heads, HEAD_DIM + 16, rows), bf16),
                pltpu.VMEM((heads, DEPTH, TILE_Q), bf16),
                pltpu.SMEM((1,), jnp.int32),
            ],
        ),
        compiler_params=pltpu.CompilerParams(
            dimension_semantics=("arbitrary",), vmem_limit_bytes=40 << 20
        ),
        name="attention_forward",
    )(low, high, queries, keys, values, key_rows, query_rows)


def backward_kernel(
    low, high, queries, keys, values, grads, outs, logsum, key_rows, query_rows, cosine, sine,
    joined_back, *scratch
):
    heads = queries.shape[0] // HEAD_DIM
    rows = keys.shape[1]
    keys_in, values_in, queries_in, grads_in = scratch[:4]
    key_sum = scratch[4 : 4 + heads]
    value_sum = scratch[4 + heads : 4 + 2 * heads]
    query_sum = scratch[4 + 2 * heads : 4 + 3 * heads]
    step = pl.program_id(0)

    @pl.when(step == 0)
    def _():
        ones = three_ones(rows)
        for h in range(heads):
            band = slice(h * HEAD_DIM, (h + 1) * HEAD_DIM)
            pad = jnp.zeros((DEPTH - HEAD_DIM - 32, rows), bf16)
            keys_in[h] = jnp.concatenate([keys[band, :], key_rows[...], ones, pad], axis=0).T
            pad = jnp.zeros((DEPTH - HEAD_DIM - 16, rows), bf16)
            values_in[h] = jnp.concatenate([values[band, :], ones, pad], axis=0).T
            key_sum[h][...] = jnp.zeros((HEAD_DIM, rows), f32)
            value_sum[h][...] = jnp.zeros((HEAD_DIM, rows), f32)

    for h in range(heads):
        band = slice(h * HEAD_DIM, (h + 1) * HEAD_DIM)
        queries_in[h, :HEAD_DIM, :] = queries[band, :]
        queries_in[h, HEAD_DIM : HEAD_DIM + 16, :] = query_rows[...]
        queries_in[h, HEAD_DIM + 16 : HEAD_DIM + 32, :] = rows16(split3(-logsum[h : h + 1, :]))
        queries_in[h, HEAD_DIM + 32 :, :] = jnp.zeros((DEPTH - HEAD_DIM - 32, TILE_Q), bf16)
        inner = jnp.sum(grads[band, :].astype(f32) * outs[band, :].astype(f32), axis=0, keepdims=True)
        grads_in[h, :HEAD_DIM, :] = grads[band, :]
        grads_in[h, HEAD_DIM : HEAD_DIM + 16, :] = rows16(split3(-inner))
        grads_in[h, HEAD_DIM + 16 :, :] = jnp.zeros((DEPTH - HEAD_DIM - 16, TILE_Q), bf16)
        query_sum[h][...] = jnp.zeros((HEAD_DIM, TILE_Q), f32)

    def block(tiles, carry):
        spans = [pl.ds(pl.multiple_of(j * TILE_K, TILE_K), TILE_K) for j in tiles]
        units = [(span, h) for span in spans for h in range(heads)]
        waiting = {}
        for t in range(len(units) + BWD_SKEW):
            if t < len(units):
                span, h = units[t]
                waiting[t] = (
                    dot(keys_in[h, span, :], queries_in[h], NN),
                    dot(values_in[h, span, :], grads_in[h], NN),
                )
            if t < BWD_SKEW:
                continue
            span, h = units[t - BWD_SKEW]
            band = slice(h * HEAD_DIM, (h + 1) * HEAD_DIM)
            scores, weight_grad = waiting.pop(t - BWD_SKEW)
            softmax = jnp.exp2(scores)
            score_grad = (softmax * weight_grad).astype(bf16)
            value_sum[h][:, span] += dot(grads[band, :], softmax.astype(bf16), NT)
            key_sum[h][:, span] += dot(queries[band, :], score_grad, NT)
            query_sum[h][...] += dot(keys[band, span], score_grad, NN)
        return carry

    tile_loop(low[step], high[step], block, 0)

    def store(offset, columns, value):
        half = HEAD_DIM // 2
        upper, lower = value[:half], value[half:]
        cos, sin = cosine[:, columns], sine[:, columns]
        joined_back[offset : offset + half, columns] = (upper * cos + lower * sin).astype(bf16)
        joined_back[offset + half : offset + HEAD_DIM, columns] = (lower * cos - upper * sin).astype(bf16)

    width = heads * HEAD_DIM
    columns = pl.ds(pl.multiple_of(step * TILE_Q, TILE_Q), TILE_Q)
    for h in range(heads):
        store(h * HEAD_DIM, columns, query_sum[h][...] * 0.125)

    @pl.when(step == pl.num_programs(0) - 1)
    def _():
        for h in range(heads):
            first = width + h * HEAD_DIM
            store(first, slice(0, rows), key_sum[h][...] * (1.0 / LOG2E))
            first += width
            joined_back[first : first + HEAD_DIM, :] = value_sum[h][...].astype(bf16)


def attention_backward(
    low, high, queries, keys, values, grads, outs, logsum, key_rows, query_rows, cosine, sine
):
    width, rows = queries.shape
    heads = width // HEAD_DIM

    def full(count):
        return pl.BlockSpec((count, rows), lambda i, low, high: (0, 0))

    def tile(count):
        return pl.BlockSpec((count, TILE_Q), lambda i, low, high: (0, i))

    return pl.pallas_call(
        backward_kernel,
        out_shape=jax.ShapeDtypeStruct((3 * width, rows), bf16),
        grid_spec=pltpu.PrefetchScalarGridSpec(
            num_scalar_prefetch=2,
            grid=(rows // TILE_Q,),
            in_specs=[
                tile(width), full(width), full(width), tile(width), tile(width), tile(heads),
                full(16), tile(16), full(HEAD_DIM // 2), full(HEAD_DIM // 2),
            ],
            out_specs=full(3 * width),
            scratch_shapes=[
                pltpu.VMEM((heads, rows, DEPTH), bf16),
                pltpu.VMEM((heads, rows, DEPTH), bf16),
                pltpu.VMEM((heads, DEPTH, TILE_Q), bf16),
                pltpu.VMEM((heads, DEPTH, TILE_Q), bf16),
            ]
            + [pltpu.VMEM((HEAD_DIM, rows), f32)] * (2 * heads)
            + [pltpu.VMEM((HEAD_DIM, TILE_Q), f32)] * heads,
        ),
        compiler_params=pltpu.CompilerParams(
            dimension_semantics=("arbitrary",), vmem_limit_bytes=52 << 20
        ),
        name="attention_backward",
    )(low, high, queries, keys, values, grads, outs, logsum, key_rows, query_rows, cosine, sine)


def layer_norm(values, gain_row):
    centred = values - jnp.mean(values, axis=-1, keepdims=True)
    inverse = lax.rsqrt(jnp.mean(centred * centred, axis=-1, keepdims=True) + norm_epsilon)
    normal = centred * inverse
    return normal * gain_row, normal, inverse


def norm_back(upstream, gain_row, normal, inverse):
    scaled = upstream * gain_row
    inner_mean = jnp.mean(scaled * normal, axis=-1, keepdims=True)
    return inverse * (scaled - jnp.mean(scaled, axis=-1, keepdims=True) - normal * inner_mean)


def horner(square, factors):
    total = factors[0] * square + factors[1]
    for factor in factors[2:]:
        total = total * square + factor
    return total


def error_function(value):
    value = jnp.clip(value, -4.0, 4.0)
    square = value * value
    return value * horner(square, ERF_TOP) / horner(square, ERF_BOTTOM)


def turn(value):
    columns = value.shape[1]
    rest = jnp.zeros((value.shape[0], -columns % 128), value.dtype)
    return jnp.concatenate([value, rest], axis=1).T[:columns, :]


def turn_back(value):
    lines = value.shape[0]
    rest = jnp.zeros((-lines % 128, value.shape[1]), value.dtype)
    return jnp.concatenate([value, rest], axis=0).T[:, :lines]


def first_kernel(head, own, other, gain, rows, normed):
    tiles = pl.num_programs(0) // 2
    mine = pl.program_id(0) // tiles == head[0]
    value = jnp.where(mine, own[...].astype(f32), other[...].astype(f32))
    rows[...] = value.astype(bf16)
    normed[...] = layer_norm(value, gain[...])[0].astype(bf16)


def first_norm(head, own, other, gain):
    half, width = own.shape
    tiles = half // FEED_ROWS
    result = jax.ShapeDtypeStruct((2 * half, width), bf16)
    spec = pl.BlockSpec((FEED_ROWS, width), lambda i, head: (i, 0))
    return pl.pallas_call(
        first_kernel,
        out_shape=(result, result),
        grid_spec=pltpu.PrefetchScalarGridSpec(
            num_scalar_prefetch=1,
            grid=(2 * tiles,),
            in_specs=[
                pl.BlockSpec(
                    (FEED_ROWS, width),
                    lambda i, head: (jnp.clip(i - head[0] * tiles, 0, tiles - 1), 0),
                ),
                pl.BlockSpec(
                    (FEED_ROWS, width),
                    lambda i, head: (jnp.clip(i - (1 - head[0]) * tiles, 0, tiles - 1), 0),
                ),
                pl.BlockSpec((1, width), lambda i, head: (0, 0)),
            ],
            out_specs=[spec, spec],
        ),
        compiler_params=pltpu.CompilerParams(dimension_semantics=("arbitrary",)),
        name="first_norm",
    )(head, own, other, gain)


def gradient_kernel(back, normed, *refs):
    grads, total = refs[:-1], refs[-1]
    step = pl.program_id(0)

    @pl.when(step == 0)
    def _():
        total[...] = dot(back[...], normed[...], NN)

    @pl.when(step > 0)
    def _():
        total[...] += dot(back[...], normed[...], NN)

    @pl.when(step == pl.num_programs(0) - 1)
    def _():
        first = 0
        for grad in grads:
            grad[...] = total[:, first : first + grad.shape[1]].astype(bf16)
            first += grad.shape[1]


def joined_gradient(back, normed):
    lines, count = back.shape
    width = normed.shape[1]
    tile = 2 * FEED_ROWS
    half = width // 256 * 128
    parts = [half, width - half]
    return pl.pallas_call(
        gradient_kernel,
        grid=(count // tile,),
        in_specs=[
            pl.BlockSpec((lines, tile), lambda i: (0, i)),
            pl.BlockSpec((tile, width), lambda i: (i, 0)),
        ],
        out_specs=[pl.BlockSpec((lines, part), lambda i: (0, 0)) for part in parts],
        out_shape=[jax.ShapeDtypeStruct((lines, part), bf16) for part in parts],
        scratch_shapes=[pltpu.VMEM((lines, width), f32)],
        compiler_params=pltpu.CompilerParams(
            dimension_semantics=("arbitrary",), vmem_limit_bytes=32 << 20
        ),
        name="joined_gradient",
    )(back, normed)


def pull_kernel(head, back, weight, out):
    out[...] = dot(back[...].T, weight[...], NN).astype(bf16)


def pull_other(head, back, weight):
    lines, count = back.shape
    width = weight.shape[1]
    tiles = count // 2 // FEED_ROWS
    return pl.pallas_call(
        pull_kernel,
        out_shape=jax.ShapeDtypeStruct((count // 2, width), bf16),
        grid_spec=pltpu.PrefetchScalarGridSpec(
            num_scalar_prefetch=1,
            grid=(tiles,),
            in_specs=[
                pl.BlockSpec((lines, FEED_ROWS), lambda i, head: (0, (1 - head[0]) * tiles + i)),
                pl.BlockSpec((lines, width), lambda i, head: (0, 0)),
            ],
            out_specs=pl.BlockSpec((FEED_ROWS, width), lambda i, head: (i, 0)),
        ),
        compiler_params=pltpu.CompilerParams(
            dimension_semantics=("arbitrary",), vmem_limit_bytes=24 << 20
        ),
        name="pull_other",
    )(head, back, weight)


def input_kernel(head, back, weight, other, rows, middle_grad, gain, input_grad, gain_grad):
    @pl.when(pl.program_id(0) == 0)
    def _():
        gain_grad[...] = jnp.zeros(gain_grad.shape, f32)

    pulled = dot(back[...].T, weight[...], NN) + other[...].astype(f32)
    unused, normal, inverse = layer_norm(rows[...].astype(f32), gain[...])
    input_grad[...] = middle_grad[...] + norm_back(pulled, gain[...], normal, inverse)
    gain_grad[...] += jnp.sum(pulled * normal, axis=0, keepdims=True)


def input_backward(head, back, weight, other, rows, middle_grad, gain):
    lines, count = back.shape
    width = weight.shape[1]
    tiles = count // 2 // FEED_ROWS

    def down():
        return pl.BlockSpec((FEED_ROWS, width), lambda i, head: (i, 0))

    return pl.pallas_call(
        input_kernel,
        out_shape=(
            jax.ShapeDtypeStruct((count // 2, width), f32),
            jax.ShapeDtypeStruct((1, width), f32),
        ),
        grid_spec=pltpu.PrefetchScalarGridSpec(
            num_scalar_prefetch=1,
            grid=(tiles,),
            in_specs=[
                pl.BlockSpec((lines, FEED_ROWS), lambda i, head: (0, head[0] * tiles + i)),
                pl.BlockSpec((lines, width), lambda i, head: (0, 0)),
                down(),
                down(),
                pl.BlockSpec((FEED_ROWS, width), lambda i, head: (head[0] * tiles + i, 0)),
                pl.BlockSpec((1, width), lambda i, head: (0, 0)),
            ],
            out_specs=[down(), pl.BlockSpec((1, width), lambda i, head: (0, 0))],
        ),
        compiler_params=pltpu.CompilerParams(
            dimension_semantics=("arbitrary",), vmem_limit_bytes=24 << 20
        ),
        name="input_backward",
    )(head, back, weight, other, rows, middle_grad, gain)


def feed_kernel(
    rows, attended, attended_other, upstream, gain, both, mixer_other, expand_left, expand_right,
    middle, hidden, second_part, shrink_grad, left_grad, right_grad, shrink,
    shrink_sum, expand_sum, expand
):
    step = pl.program_id(0)
    mixed, units = attended.shape[0], shrink.shape[0]
    chunk = units // FEED_CHUNKS

    @pl.when(step == 0)
    def _():
        expand[:, : expand_left.shape[1]] = expand_left[...]
        expand[:, expand_left.shape[1] :] = expand_right[...]
        shrink[...] = turn(both[:, mixed:])
        shrink_sum[...] = jnp.zeros(shrink_sum.shape, f32)
        expand_sum[...] = jnp.zeros(expand_sum.shape, f32)

    total = rows[...].astype(f32) + dot(attended[...].T, both[:, :mixed], NT)
    total = total + dot(attended_other[...].T, mixer_other[...], NT)
    middle[...] = total
    normed = layer_norm(total, gain[...])[0].astype(bf16)
    above = upstream[...]

    def project(c):
        first = slice(c * chunk, (c + 1) * chunk)
        second = slice(units + c * chunk, units + (c + 1) * chunk)
        return (
            dot(expand[first, :], normed, NT),
            dot(expand[second, :], normed, NT),
            dot(shrink[first, :], above, NT),
        )

    waiting = project(0)
    back = jnp.zeros(total.shape, f32)
    for c in range(FEED_CHUNKS):
        active, linear, grad = waiting
        if c + 1 < FEED_CHUNKS:
            waiting = project(c + 1)
        first = slice(c * chunk, (c + 1) * chunk)
        second = slice(units + c * chunk, units + (c + 1) * chunk)
        area = 0.5 * error_function(active * math.sqrt(0.5)) + 0.5
        gate = active * area
        density = jnp.exp(-0.5 * active * active) * (1.0 / math.sqrt(2.0 * math.pi))
        unit = (gate * linear).astype(bf16)
        active_back = (grad * linear * (area + active * density)).astype(bf16)
        linear_back = (grad * gate).astype(bf16)
        hidden[first, :] = unit
        shrink_sum[first, :] += dot(unit, above, NN)
        expand_sum[first, :] += dot(active_back, normed, NN)
        expand_sum[second, :] += dot(linear_back, normed, NN)
        back = back + dot(active_back, expand[first, :], TN) + dot(linear_back, expand[second, :], TN)
    second_part[...] = back.astype(bf16)

    @pl.when(step == pl.num_programs(0) - 1)
    def _():
        shrink_grad[...] = shrink_sum[...].astype(bf16)
        cut = left_grad.shape[1]
        left_grad[...] = expand_sum[:, :cut].astype(bf16)
        right_grad[...] = expand_sum[:, cut:].astype(bf16)


def feed_forward(rows, attended, attended_other, upstream, gain, both, mixer_other, expand):
    count, width = rows.shape
    mixed, units = attended.shape[0], expand[0].shape[0] // 2

    def full(*shape):
        return pl.BlockSpec(shape, lambda i: (0, 0))

    def down(columns):
        return pl.BlockSpec((FEED_TILE, columns), lambda i: (i, 0))

    def along(lines):
        return pl.BlockSpec((lines, FEED_TILE), lambda i: (0, i))

    return pl.pallas_call(
        feed_kernel,
        grid=(count // FEED_TILE,),
        in_specs=[
            down(width), along(mixed), along(mixed), down(width), full(1, width),
            full(*both.shape), full(width, mixed), full(*expand[0].shape), full(*expand[1].shape),
        ],
        out_specs=[
            down(width), along(units), down(width), full(units, width),
            full(*expand[0].shape), full(*expand[1].shape), full(units, width),
        ],
        out_shape=(
            jax.ShapeDtypeStruct((count, width), f32),
            jax.ShapeDtypeStruct((units, count), bf16),
            jax.ShapeDtypeStruct((count, width), bf16),
            jax.ShapeDtypeStruct((units, width), bf16),
            jax.ShapeDtypeStruct(expand[0].shape, bf16),
            jax.ShapeDtypeStruct(expand[1].shape, bf16),
            jax.ShapeDtypeStruct((units, width), bf16),
        ),
        scratch_shapes=[
            pltpu.VMEM((units, width), f32),
            pltpu.VMEM((2 * units, width), f32),
            pltpu.VMEM((2 * units, width), bf16),
        ],
        compiler_params=pltpu.CompilerParams(
            dimension_semantics=("arbitrary",), vmem_limit_bytes=48 << 20
        ),
        name="feed_forward",
    )(rows, attended, attended_other, upstream, gain, both, mixer_other, *expand)


def norm_kernel(
    middle, own, other, upstream, gain, both, attended, shrink_grad,
    middle_grad, attended_grad, both_grad, gain_grad, mixer_turned, mixer_sum
):
    step = pl.program_id(0)

    @pl.when(step == 0)
    def _():
        mixer_turned[...] = both[:, : attended.shape[0]].T
        mixer_sum[...] = jnp.zeros(mixer_sum.shape, f32)
        gain_grad[...] = jnp.zeros(gain_grad.shape, f32)

    unused, normal, inverse = layer_norm(middle[...], gain[...])
    back = own[...].astype(f32) + other[...].astype(f32)
    grad = upstream[...].astype(f32) + norm_back(back, gain[...], normal, inverse)
    middle_grad[...] = grad
    grad_low = grad.astype(bf16)
    attended_grad[...] = dot(mixer_turned[...], grad_low, NT).astype(bf16)
    mixer_sum[...] += dot(attended[...], grad_low, NN)
    gain_grad[...] += jnp.sum(back * normal, axis=0, keepdims=True)

    @pl.when(step == pl.num_programs(0) - 1)
    def _():
        mixed = attended.shape[0]
        both_grad[:, :mixed] = mixer_sum[...].T.astype(bf16)
        both_grad[:, mixed:] = turn_back(shrink_grad[...])


def norm_backward(middle, own, other, upstream, gain, both, attended, shrink_grad):
    count, width = middle.shape
    mixed = attended.shape[0]

    def full(*shape):
        return pl.BlockSpec(shape, lambda i: (0, 0))

    def down(columns):
        return pl.BlockSpec((FEED_TILE, columns), lambda i: (i, 0))

    def along(lines):
        return pl.BlockSpec((lines, FEED_TILE), lambda i: (0, i))

    return pl.pallas_call(
        norm_kernel,
        grid=(count // FEED_TILE,),
        in_specs=[
            down(width), down(width), down(width), down(width), full(1, width),
            full(*both.shape), along(mixed), full(*shrink_grad.shape),
        ],
        out_specs=[down(width), along(mixed), full(*both.shape), full(1, width)],
        out_shape=(
            jax.ShapeDtypeStruct((count, width), f32),
            jax.ShapeDtypeStruct((mixed, count), bf16),
            jax.ShapeDtypeStruct(both.shape, bf16),
            jax.ShapeDtypeStruct((1, width), f32),
        ),
        scratch_shapes=[pltpu.VMEM((mixed, width), bf16), pltpu.VMEM((mixed, width), f32)],
        compiler_params=pltpu.CompilerParams(
            dimension_semantics=("arbitrary",), vmem_limit_bytes=40 << 20
        ),
        name="norm_backward",
    )(middle, own, other, upstream, gain, both, attended, shrink_grad)


def swap(value, axis, bit):
    count = lax.axis_size(axis)
    return lax.ppermute(value, axis, [(i, i ^ bit) for i in range(count)])


def bit_order(lead):
    bits = lax.axis_size("dp").bit_length() - 1
    return [int(bit) for bit in lead] + list(range(len(lead), bits))


def steps_count():
    return lax.axis_size("dp").bit_length() - 1


def cut(held, bit):
    axis = steps_count() - 1 - bit
    side = (lax.axis_index("dp") >> bit) & 1
    kept = lax.dynamic_slice_in_dim(held, side, 1, axis)
    return kept, lax.dynamic_slice_in_dim(held, 1 - side, 1, axis)


def reduce_start(value, lead):
    bits = steps_count()
    rows = value.shape[0] >> bits
    return cut(value.reshape((2,) * bits + (rows, value.shape[1])), bit_order(lead)[0])


def reduce_step(held, step, lead):
    bits = steps_count()
    kept, sent = held if step == 0 else cut(held, bit_order(lead)[step])
    total = kept.astype(f32) + swap(sent, "dp", 1 << bit_order(lead)[step]).astype(f32)
    if step + 1 == bits:
        return total.reshape(kept.shape[-2:])
    return total.astype(bf16)


def gather_start(value):
    return value[(None,) * steps_count()]


def gather_step(held, step, lead):
    bits = steps_count()
    bit = bit_order(lead)[bits - 1 - step]
    return jnp.concatenate([held, swap(held, "dp", 1 << bit)], axis=bits - 1 - bit)


def ordered_step(held, step, lead):
    bits = steps_count()
    bit = bit_order(lead)[bits - 1 - step]
    got = swap(held, "dp", 1 << bit)
    low_side = ((lax.axis_index("dp") >> bit) & 1) == 0
    return jnp.concatenate(
        [jnp.where(low_side, held, got), jnp.where(low_side, got, held)], axis=bits - 1 - bit
    )


def gather_rows(held):
    return held.reshape(-1, held.shape[-1])


def halves_of(value):
    unit = value.shape[1] // 256 * 128
    return [value[:, :unit], value[:, unit:]]


def quarter(step, states, part, leads):
    bits = steps_count()
    for index in range(bits * part // QUARTERS, bits * (part + 1) // QUARTERS):
        states = [step(state, index, lead) for state, lead in zip(states, leads)]
    return states


def tie(*values):
    return lax.optimization_barrier(values)


def total_step(value, part):
    if part == 0:
        return value + swap(value, "head", 1)
    bits = steps_count()
    for bit in range(bits * (part - 1) // QUARTERS, bits * part // QUARTERS):
        value = value + swap(value, "dp", 1 << bit)
    return value


def schulz_start(held, own, gram, low):
    down = 0
    for left in held:
        along = 0
        for right in held:
            gram[down : down + left.shape[1], along : along + right.shape[1]] = dot(left, right, TN)
            along += right.shape[1]
        down += left.shape[1]
    shape = gram.shape
    diagonal = lax.broadcasted_iota(jnp.int32, shape, 0) == lax.broadcasted_iota(jnp.int32, shape, 1)
    trace = jnp.sum(jnp.where(diagonal, gram[...], 0.0), axis=0, keepdims=True)
    norm_value = jnp.sqrt(jnp.sum(trace, axis=1, keepdims=True)) + 1e-07
    gram[...] = gram[...] * (1.0 / (norm_value * norm_value))
    low[...] = gram[...].astype(bf16)
    return own[...] / norm_value


def schulz_steps(rows, gram, low, change, first, stop):
    columns = gram.shape[0]
    lines = 256 if columns % 256 == 0 else columns

    def per_block(body):
        def run(index, carry):
            body(pl.ds(pl.multiple_of(index * lines, lines), lines))
            return carry

        lax.fori_loop(0, columns // lines, run, 0)

    def form_change(block):
        squared = dot(low[block, :], low[...], NN)
        change[block, :] = (ns_second * gram[block, :] + ns_third * squared).astype(bf16)

    def next_gram(block):
        once = ns_first * gram[block, :] + dot(low[block, :], change[...], NN)
        twice = ns_first * once + dot(once.astype(bf16), change[...], NN)
        gram[block, :] = twice
        low[block, :] = twice.astype(bf16)

    for iteration in range(first, stop):
        per_block(form_change)
        rows = ns_first * rows + dot(rows.astype(bf16), change[...], NN)
        if iteration + 1 < NS_ITERS:
            per_block(next_gram)
    return rows


def whole_kernel(*refs, count, offset, scale):
    parts = refs[:count]
    own, weight, updated, gram, low, change = refs[count:]
    if offset is None:
        held = [part[...] for part in parts]
    else:
        held = [parts[0][:, offset : offset + gram.shape[0]]]
    rows = schulz_start(held, own, gram, low)
    updated[...] = weight[...] - scale * schulz_steps(rows, gram, low, change, 0, NS_ITERS)


def early_kernel(*refs, count):
    own, rows, gram_out, low_out, gram, low, change = refs[count:]
    start = schulz_start([part[...] for part in refs[:count]], own, gram, low)
    rows[...] = start
    gram_out[...] = gram[...]
    low_out[...] = low[...]


def late_kernel(rows, gram_in, low_in, weight, updated, gram, low, change, *, scale):
    gram[...] = gram_in[...]
    low[...] = low_in[...]
    done = schulz_steps(rows[...], gram, low, change, 0, NS_ITERS)
    updated[...] = weight[...] - scale * done


def square_scratch(columns):
    return [
        pltpu.VMEM((columns, columns), f32),
        pltpu.VMEM((columns, columns), bf16),
        pltpu.VMEM((columns, columns), bf16),
    ]


def shape_scale(rows, columns):
    return muon_rate * math.sqrt(rows / columns)


def schulz(parts, offset, own, weight, name):
    columns = own.shape[1]
    return pl.pallas_call(
        functools.partial(
            whole_kernel, count=len(parts), offset=offset, scale=shape_scale(parts[0].shape[0], columns)
        ),
        out_shape=jax.ShapeDtypeStruct(own.shape, f32),
        scratch_shapes=square_scratch(columns),
        compiler_params=pltpu.CompilerParams(vmem_limit_bytes=40 << 20),
        name=name,
    )(*parts, own, weight)


def schulz_early(parts, own):
    columns = own.shape[1]
    return pl.pallas_call(
        functools.partial(early_kernel, count=len(parts)),
        out_shape=(
            jax.ShapeDtypeStruct(own.shape, f32),
            jax.ShapeDtypeStruct((columns, columns), f32),
            jax.ShapeDtypeStruct((columns, columns), bf16),
        ),
        scratch_shapes=square_scratch(columns),
        compiler_params=pltpu.CompilerParams(vmem_limit_bytes=40 << 20),
        name="schulz_early",
    )(*parts, own)


def schulz_late(state, weight, rows):
    columns = weight.shape[1]
    return pl.pallas_call(
        functools.partial(late_kernel, scale=shape_scale(rows, columns)),
        out_shape=jax.ShapeDtypeStruct(weight.shape, f32),
        scratch_shapes=square_scratch(columns),
        compiler_params=pltpu.CompilerParams(vmem_limit_bytes=40 << 20),
        name="schulz_late",
    )(*state, weight)


def shards(
    tokens,
    lengths,
    norm_gains,
    joined_weight,
    mixer_weight,
    expand_weight,
    shrink_weight,
    joined_momentum,
    mixer_momentum,
    expand_momentum,
    shrink_momentum,
    gain_momentum,
    cotangent,
):
    row_count = cotangent.shape[0]
    local_rows = tokens.shape[0]
    head = lax.axis_index("head")
    mixer_width = mixer_weight.shape[2]

    def own_half(value):
        return lax.dynamic_slice_in_dim(value, head * local_rows, local_rows, 0)

    joined_parts = [gather_start(part) for part in halves_of(joined_weight[0].astype(bf16))]
    joined_parts = quarter(ordered_step, joined_parts, 0, JOINED_FIRST)
    others = [gather_start(part) for part in halves_of(expand_weight[0].astype(bf16))] + [
        gather_start(jnp.concatenate([mixer_weight[0], shrink_weight[0]], axis=1).astype(bf16))
    ]
    key_rows, query_rows, cosine, sine = doc_tables(lengths[0], row_count)
    low, high = key_bounds(lengths[0], row_count)
    head_place = head[None]
    tokens_other = swap(tokens, "head", 1)

    joined_parts, others, tokens_other = tie(joined_parts, others, tokens_other)
    joined_parts = quarter(ordered_step, joined_parts, 1, JOINED_FIRST)
    others = quarter(ordered_step, others, 0, OTHERS_FIRST)
    rows_low, first_low = first_norm(head_place, tokens, tokens_other, norm_gains[0:1])
    joined_parts, others, first_low = tie(joined_parts, others, first_low)
    joined_parts = quarter(ordered_step, joined_parts, 2, JOINED_FIRST)
    others = quarter(ordered_step, others, 1, OTHERS_FIRST)
    joined_parts, others = tie(joined_parts, others)
    joined_parts = quarter(ordered_step, joined_parts, 3, JOINED_FIRST)
    moved = quarter(ordered_step, others, 2, OTHERS_FIRST)

    joined_low = jnp.concatenate([gather_rows(part) for part in joined_parts], axis=1)
    joined = dot(joined_low, first_low, NT)
    width = joined.shape[0] // 3
    queries = (rotate(joined[:width], cosine, sine) * QUERY_SCALE).astype(bf16)
    keys = rotate(joined[width : 2 * width], cosine, sine).astype(bf16)
    values = joined[2 * width :].astype(bf16)
    others, queries, keys, values, low = tie(moved, queries, keys, values, low)
    moved = quarter(ordered_step, others, 3, OTHERS_FIRST)
    attended, logsum = attention_forward(low, high, queries, keys, values, key_rows, query_rows)
    others, attended, logsum = tie(moved, attended, logsum)
    attended_other = swap(attended, "head", 1)
    both_low = gather_rows(others[2])
    mixer_other = swap(both_low[:, :mixer_width], "head", 1)

    second_gain = norm_gains[1:2]
    middle, hidden, second_part, shrink_grad, left_grad, right_grad, shrink_turned = feed_forward(
        rows_low, attended, attended_other, cotangent, second_gain,
        both_low, mixer_other, [gather_rows(part) for part in others[:2]],
    )
    second_other = swap(second_part, "head", 1)

    sums = [reduce_start(part, lead) for part, lead in zip((left_grad, right_grad), PAIR)]
    sums, second_other = tie(sums, second_other)
    moved = quarter(reduce_step, sums, 0, PAIR)
    middle_grad, attended_grad, both_grad, second_gain_grad = norm_backward(
        middle, second_part, second_other, cotangent, second_gain, both_low, attended, shrink_grad
    )
    both_sum = [reduce_start(both_grad, ONE[0])]

    sums, attended_grad, shrink_now = tie(moved, attended_grad, shrink_turned)
    moved = quarter(reduce_step, sums, 1, PAIR)

    def fed(columns):
        units = lax.dynamic_slice_in_dim(hidden, columns, local_rows, 1)
        return dot(units, shrink_now, TN)

    fed_other = fed((1 - head) * local_rows).astype(bf16)
    fed_own = fed(head * local_rows)

    sums, both_sum, fed_other, fed_own, low = tie(moved, both_sum, fed_other, fed_own, low)
    moved = quarter(reduce_step, sums, 2, PAIR)
    both_moved = quarter(reduce_step, both_sum, 0, ONE)
    fed_other = swap(fed_other, "head", 1)
    joined_back = attention_backward(
        low, high, queries, keys, values, attended_grad, attended, logsum, key_rows, query_rows,
        cosine, sine,
    )
    sums, both_sum, joined_back = tie(moved, both_moved, joined_back)
    moved = quarter(reduce_step, sums, 3, PAIR)
    both_moved = quarter(reduce_step, both_sum, 1, ONE)
    joined_grad = joined_gradient(joined_back, first_low)

    sums, both_sum, joined_grad, joined_now = tie(moved, both_moved, joined_grad, joined_low)
    expand_next = 0.5 * expand_momentum[0] + jnp.concatenate(sums, axis=1)
    gathers = [gather_start(part) for part in halves_of(expand_next.astype(bf16))]
    sums = [reduce_start(part, lead) for part, lead in zip(joined_grad, PAIR)]
    sums = quarter(reduce_step, sums, 0, PAIR)
    moved = quarter(gather_step, gathers, 0, PAIR)
    both_moved = quarter(reduce_step, both_sum, 2, ONE)
    first_other = pull_other(head_place, joined_back, joined_now)

    sums, gathers, both_sum, first_other, fed_own = tie(sums, moved, both_moved, first_other, fed_own)
    first_other = swap(first_other, "head", 1)
    moved = quarter(reduce_step, sums, 1, PAIR)
    gathers_moved = quarter(gather_step, gathers, 1, PAIR)
    both_moved = quarter(reduce_step, both_sum, 3, ONE)

    sums, gathers, both_sum, first_other, fed_own = tie(
        moved, gathers_moved, both_moved, first_other, fed_own
    )
    mixer_next = 0.5 * mixer_momentum[0] + both_sum[0][:, :mixer_width]
    shrink_next = 0.5 * shrink_momentum[0] + both_sum[0][:, mixer_width:]
    both_gather = [gather_start(jnp.concatenate([mixer_next, shrink_next], axis=1).astype(bf16))]
    moved = quarter(reduce_step, sums, 2, PAIR)
    gathers_moved = quarter(gather_step, gathers, 2, PAIR)
    both_moved = quarter(gather_step, both_gather, 0, ONE)
    layer_output = (own_half(middle) + fed_own + fed_other.astype(f32)).astype(bf16)

    sums, gathers, both_gather, first_other, layer_output = tie(
        moved, gathers_moved, both_moved, first_other, layer_output
    )
    moved = quarter(reduce_step, sums, 3, PAIR)
    gathers_moved = quarter(gather_step, gathers, 3, PAIR)
    both_moved = quarter(gather_step, both_gather, 1, ONE)
    input_gradient, first_gain_grad = input_backward(
        head_place, joined_back, joined_now, first_other, tokens, middle_grad, norm_gains[0:1]
    )
    gain_totals = jnp.concatenate([first_gain_grad, 0.5 * second_gain_grad], axis=0)

    sums, gathers, both_gather, gain_totals = tie(moved, gathers_moved, both_moved, gain_totals)
    joined_next = 0.5 * joined_momentum[0] + jnp.concatenate(sums, axis=1)
    joined_gather = [gather_start(part) for part in halves_of(joined_next.astype(bf16))]
    moved = quarter(gather_step, joined_gather, 0, PAIR)
    both_moved = quarter(gather_step, both_gather, 2, ONE)
    gain_moved = total_step(gain_totals, 0)
    expand_state = schulz_early([gather_rows(part) for part in gathers], expand_next)
    joined_gather, both_gather, gain_totals, expand_state = tie(
        moved, both_moved, gain_moved, expand_state
    )
    moved = quarter(gather_step, joined_gather, 1, PAIR)
    both_moved = quarter(gather_step, both_gather, 3, ONE)
    gain_moved = total_step(gain_totals, 1)
    updated_expand = schulz_late(expand_state, expand_weight[0], left_grad.shape[0])
    joined_gather, both_gather, gain_totals, updated_expand = tie(
        moved, both_moved, gain_moved, updated_expand
    )
    both_full = [gather_rows(both_gather[0])]
    moved = quarter(gather_step, joined_gather, 2, PAIR)
    gain_moved = total_step(gain_totals, 2)
    updated_shrink = schulz(
        both_full, mixer_width, shrink_next, shrink_weight[0], "schulz_shrink"
    )
    joined_gather, both_full, gain_totals, updated_shrink = tie(
        moved, both_full, gain_moved, updated_shrink
    )
    moved = quarter(gather_step, joined_gather, 3, PAIR)
    gain_moved = total_step(gain_totals, 3)
    updated_mixer = schulz(both_full, 0, mixer_next, mixer_weight[0], "schulz_mixer")
    joined_gather, gain_totals, updated_mixer = tie(moved, gain_moved, updated_mixer)
    gain_totals = total_step(gain_totals, 4)
    updated_joined = schulz(
        [gather_rows(part) for part in joined_gather],
        None, joined_next, joined_weight[0], "schulz_joined",
    )

    momentum_gains = 0.5 * gain_momentum + gain_totals
    updated_gains = norm_gains - gain_rate * momentum_gains * lax.rsqrt(
        jnp.mean(momentum_gains * momentum_gains, axis=-1, keepdims=True) + 1e-06
    )
    return (
        layer_output,
        input_gradient,
        joined_next[None],
        mixer_next[None],
        expand_next[None],
        shrink_next[None],
        updated_joined[None],
        updated_mixer[None],
        updated_expand[None],
        updated_shrink[None],
        momentum_gains,
        updated_gains,
    )


def solution(mesh):
    rows = P(("dp", "head"), None)
    weight = P("head", "dp", None)
    return jax.shard_map(
        shards,
        mesh=mesh,
        in_specs=(rows, P("dp", None), P()) + (weight,) * 8 + (P(), P("dp", None)),
        out_specs=(rows, rows) + (weight,) * 8 + (P(), P()),
        check_vma=False,
    )
```

```python
import functools
import math

import jax
import jax.numpy as jnp
from jax import lax
from jax.experimental import pallas as pl
from jax.experimental.pallas import tpu as pltpu
from jax.sharding import PartitionSpec as P

HEAD_DIM = 64
NS_ITERS = 3

theta_base = 160000.0
norm_epsilon = 1e-05
ns_first = 3.4445
ns_second = -4.775
ns_third = 2.0315
muon_rate = 1.0
gain_rate = 0.3

bf16 = jnp.bfloat16
f32 = jnp.float32
LOG2E = math.log2(math.e)
QUERY_SCALE = 0.125 * LOG2E
SAFE_SCORE = 60.0
DEPTH = 128
TILE_Q = 256
TILE_K = 256
FWD_SKEW = 6
BWD_SKEW = 2

NN = (((1,), (0,)), ((), ()))
NT = (((1,), (1,)), ((), ()))
TN = (((0,), (0,)), ((), ()))
TT = (((0,), (1,)), ((), ()))
QUARTERS = 4
PAIR = ("012", "102")
JOINED_FIRST = ("012", "120")
OTHERS_FIRST = ("021", "201", "120")
ONE = ("012",)
FEED_ROWS = 512
FEED_TILE = 512
FEED_CHUNKS = 2
ERF_TOP = (
    -2.72614225801306e-10, 2.77068142495902e-08, -2.10102402082508e-06, -5.69250639462346e-05,
    -7.34990630326855e-04, -2.95459980854025e-03, -1.60960333262415e-02,
)
ERF_BOTTOM = (
    -1.45660718464996e-05, -2.13374055278905e-04, -1.68282697438203e-03, -7.37332916720468e-03,
    -1.42647390514189e-02,
)


def dot(left, right, dims):
    return lax.dot_general(left, right, dims, preferred_element_type=f32)


def key_bounds(length_row, row_count):
    ends = jnp.cumsum(length_row)
    starts = ends - length_row
    first = jnp.arange(row_count // TILE_Q, dtype=jnp.int32) * TILE_Q
    labels = jnp.arange(length_row.shape[0], dtype=jnp.int32)

    def pick(places, table):
        segment = jnp.sum((places[:, None] >= ends[None, :]).astype(jnp.int32), axis=1)
        return jnp.sum(jnp.where(segment[:, None] == labels[None, :], table[None, :], 0), axis=1)

    low = pick(first, starts) // TILE_K
    high = (pick(first + TILE_Q - 1, ends) + TILE_K - 1) // TILE_K
    return low.astype(jnp.int32), high.astype(jnp.int32)


def doc_tables(length_row, row_count):
    ends = jnp.cumsum(length_row)
    starts = ends - length_row
    count = length_row.shape[0]
    places = jnp.arange(row_count, dtype=jnp.int32)[None, :]
    member = (places >= starts[:, None]) & (places < ends[:, None])
    rest = jnp.zeros((16 - count, row_count), f32)
    key_rows = jnp.concatenate([member.astype(f32), rest], axis=0).astype(bf16)
    query_rows = jnp.concatenate([jnp.where(member, 0.0, -1e30), rest], axis=0).astype(bf16)
    doc_first = jnp.sum(jnp.where(member, starts[:, None], 0), axis=0, keepdims=True)
    position = (places - doc_first).astype(f32)
    half_dim = HEAD_DIM // 2
    frequency = jnp.exp(
        jnp.arange(half_dim, dtype=f32) * (-2.0 * math.log(theta_base) / HEAD_DIM)
    )
    angles = frequency[:, None] * position
    return key_rows, query_rows, jnp.cos(angles), jnp.sin(angles)


def rotate(values, cosine, sine):
    half = HEAD_DIM // 2
    heads = values.reshape(-1, HEAD_DIM, values.shape[1])
    low, high = heads[:, :half], heads[:, half:]
    turned = jnp.concatenate([low * cosine - high * sine, high * cosine + low * sine], axis=1)
    return turned.reshape(values.shape)


def rows16(parts):
    rest = jnp.zeros((16 - len(parts), parts[0].shape[1]), f32)
    return jnp.concatenate([part.astype(f32) for part in parts] + [rest], axis=0).astype(bf16)


def split3(value):
    first = value.astype(bf16)
    left = value - first.astype(f32)
    second = left.astype(bf16)
    third = (left - second.astype(f32)).astype(bf16)
    return [first, second, third]


def three_ones(count):
    return jnp.concatenate([jnp.ones((3, count), f32), jnp.zeros((13, count), f32)], axis=0).astype(
        bf16
    )


def tile_loop(low, high, block, carry):
    pairs = (high - low) // 2

    def two(index, carry):
        first = low + 2 * index
        return block([first, first + 1], carry)

    carry = lax.fori_loop(0, pairs, two, carry)
    return lax.fori_loop(low + 2 * pairs, high, lambda j, carry: block([j], carry), carry)


def forward_kernel(
    low, high, queries, keys, values, key_rows, query_rows, out, logsum, keys_in, values_in, queries_in, safe
):
    heads = queries.shape[0] // HEAD_DIM
    rows = keys.shape[1]
    step = pl.program_id(0)

    @pl.when(step == 0)
    def _():
        worst = jnp.zeros((1, 1), f32)
        ones = rows16([jnp.ones((1, rows), f32)])
        for h in range(heads):
            band = slice(h * HEAD_DIM, (h + 1) * HEAD_DIM)
            key = keys[band, :]
            pad = jnp.zeros((DEPTH - HEAD_DIM - 16, rows), bf16)
            keys_in[h] = jnp.concatenate([key, key_rows[...], pad], axis=0).T
            values_in[h, :HEAD_DIM, :] = values[band, :]
            values_in[h, HEAD_DIM:, :] = ones
            query_full = queries[band, :].astype(f32)
            key_full = key.astype(f32)
            query_top = jnp.max(
                jnp.sum(query_full * query_full, axis=0, keepdims=True), axis=1, keepdims=True
            )
            key_top = jnp.max(
                jnp.sum(key_full * key_full, axis=0, keepdims=True), axis=1, keepdims=True
            )
            worst = jnp.maximum(worst, query_top * key_top)
        safe[0] = jnp.where(worst[0, 0] <= SAFE_SCORE * SAFE_SCORE, 1, 0)

    first = pl.multiple_of(step * TILE_Q, TILE_Q)
    for h in range(heads):
        queries_in[h, :HEAD_DIM, :] = queries[h * HEAD_DIM : (h + 1) * HEAD_DIM, pl.ds(first, TILE_Q)]
        queries_in[h, HEAD_DIM : HEAD_DIM + 16, :] = query_rows[...]
        queries_in[h, HEAD_DIM + 16 :, :] = jnp.zeros((DEPTH - HEAD_DIM - 16, TILE_Q), bf16)

    def finish(peaks, totals):
        for h in range(heads):
            weight = totals[h][HEAD_DIM : HEAD_DIM + 1, :]
            out[h * HEAD_DIM : (h + 1) * HEAD_DIM, :] = (totals[h][:HEAD_DIM, :] / weight).astype(bf16)
            level = jnp.log2(weight)
            logsum[h : h + 1, :] = level if peaks is None else peaks[h] + level

    empty = tuple(jnp.zeros((HEAD_DIM + 16, TILE_Q), f32) for _ in range(heads))

    @pl.when(safe[0] == 1)
    def _():
        def block(tiles, totals):
            spans = [pl.ds(pl.multiple_of(j * TILE_K, TILE_K), TILE_K) for j in tiles]
            units = [(span, h) for span in spans for h in range(heads)]
            totals = list(totals)
            waiting = {}
            for t in range(len(units) + FWD_SKEW):
                if t < len(units):
                    span, h = units[t]
                    waiting[t] = dot(keys_in[h, span, :], queries_in[h], NN)
                if t >= FWD_SKEW:
                    span, h = units[t - FWD_SKEW]
                    raised = jnp.exp2(waiting.pop(t - FWD_SKEW)).astype(bf16)
                    totals[h] = totals[h] + dot(values_in[h, :, span], raised, NN)
            return tuple(totals)

        finish(None, tile_loop(low[step], high[step], block, empty))

    @pl.when(safe[0] == 0)
    def _():
        def block(j, carry):
            peaks, totals = carry
            span = pl.ds(pl.multiple_of(j * TILE_K, TILE_K), TILE_K)
            new_peaks = []
            new_totals = []
            for h in range(heads):
                scores = dot(keys_in[h, span, :], queries_in[h], NN)
                peak = jnp.maximum(peaks[h], jnp.max(scores, axis=0, keepdims=True))
                raised = jnp.exp2(scores - peak).astype(bf16)
                new_totals.append(
                    totals[h] * jnp.exp2(peaks[h] - peak) + dot(values_in[h, :, span], raised, NN)
                )
                new_peaks.append(peak)
            return tuple(new_peaks), tuple(new_totals)

        lowest = tuple(jnp.full((1, TILE_Q), -3e38, f32) for _ in range(heads))
        finish(*lax.fori_loop(low[step], high[step], block, (lowest, empty)))


def attention_forward(low, high, queries, keys, values, key_rows, query_rows):
    width, rows = queries.shape
    heads = width // HEAD_DIM

    def full(count):
        return pl.BlockSpec((count, rows), lambda i, low, high: (0, 0))

    def tile(count):
        return pl.BlockSpec((count, TILE_Q), lambda i, low, high: (0, i))

    return pl.pallas_call(
        forward_kernel,
        out_shape=(
            jax.ShapeDtypeStruct((width, rows), bf16),
            jax.ShapeDtypeStruct((heads, rows), f32),
        ),
        grid_spec=pltpu.PrefetchScalarGridSpec(
            num_scalar_prefetch=2,
            grid=(rows // TILE_Q,),
            in_specs=[full(width), full(width), full(width), full(16), tile(16)],
            out_specs=[tile(width), tile(heads)],
            scratch_shapes=[
                pltpu.VMEM((heads, rows, DEPTH), bf16),
                pltpu.VMEM((heads, HEAD_DIM + 16, rows), bf16),
                pltpu.VMEM((heads, DEPTH, TILE_Q), bf16),
                pltpu.SMEM((1,), jnp.int32),
            ],
        ),
        compiler_params=pltpu.CompilerParams(
            dimension_semantics=("arbitrary",), vmem_limit_bytes=40 << 20
        ),
        name="attention_forward",
    )(low, high, queries, keys, values, key_rows, query_rows)


def backward_kernel(
    low, high, queries, keys, values, grads, outs, logsum, key_rows, query_rows, cosine, sine,
    joined_back, *scratch
):
    heads = queries.shape[0] // HEAD_DIM
    rows = keys.shape[1]
    keys_in, values_in, queries_in, grads_in = scratch[:4]
    key_sum = scratch[4 : 4 + heads]
    value_sum = scratch[4 + heads : 4 + 2 * heads]
    query_sum = scratch[4 + 2 * heads : 4 + 3 * heads]
    step = pl.program_id(0)

    @pl.when(step == 0)
    def _():
        ones = three_ones(rows)
        for h in range(heads):
            band = slice(h * HEAD_DIM, (h + 1) * HEAD_DIM)
            pad = jnp.zeros((DEPTH - HEAD_DIM - 32, rows), bf16)
            keys_in[h] = jnp.concatenate([keys[band, :], key_rows[...], ones, pad], axis=0).T
            pad = jnp.zeros((DEPTH - HEAD_DIM - 16, rows), bf16)
            values_in[h] = jnp.concatenate([values[band, :], ones, pad], axis=0).T
            key_sum[h][...] = jnp.zeros((HEAD_DIM, rows), f32)
            value_sum[h][...] = jnp.zeros((HEAD_DIM, rows), f32)

    for h in range(heads):
        band = slice(h * HEAD_DIM, (h + 1) * HEAD_DIM)
        queries_in[h, :HEAD_DIM, :] = queries[band, :]
        queries_in[h, HEAD_DIM : HEAD_DIM + 16, :] = query_rows[...]
        queries_in[h, HEAD_DIM + 16 : HEAD_DIM + 32, :] = rows16(split3(-logsum[h : h + 1, :]))
        queries_in[h, HEAD_DIM + 32 :, :] = jnp.zeros((DEPTH - HEAD_DIM - 32, TILE_Q), bf16)
        inner = jnp.sum(grads[band, :].astype(f32) * outs[band, :].astype(f32), axis=0, keepdims=True)
        grads_in[h, :HEAD_DIM, :] = grads[band, :]
        grads_in[h, HEAD_DIM : HEAD_DIM + 16, :] = rows16(split3(-inner))
        grads_in[h, HEAD_DIM + 16 :, :] = jnp.zeros((DEPTH - HEAD_DIM - 16, TILE_Q), bf16)
        query_sum[h][...] = jnp.zeros((HEAD_DIM, TILE_Q), f32)

    def block(tiles, carry):
        spans = [pl.ds(pl.multiple_of(j * TILE_K, TILE_K), TILE_K) for j in tiles]
        units = [(span, h) for span in spans for h in range(heads)]
        waiting = {}
        for t in range(len(units) + BWD_SKEW):
            if t < len(units):
                span, h = units[t]
                waiting[t] = (
                    dot(keys_in[h, span, :], queries_in[h], NN),
                    dot(values_in[h, span, :], grads_in[h], NN),
                )
            if t < BWD_SKEW:
                continue
            span, h = units[t - BWD_SKEW]
            band = slice(h * HEAD_DIM, (h + 1) * HEAD_DIM)
            scores, weight_grad = waiting.pop(t - BWD_SKEW)
            softmax = jnp.exp2(scores)
            score_grad = (softmax * weight_grad).astype(bf16)
            value_sum[h][:, span] += dot(grads[band, :], softmax.astype(bf16), NT)
            key_sum[h][:, span] += dot(queries[band, :], score_grad, NT)
            query_sum[h][...] += dot(keys[band, span], score_grad, NN)
        return carry

    tile_loop(low[step], high[step], block, 0)

    def store(offset, columns, value):
        half = HEAD_DIM // 2
        upper, lower = value[:half], value[half:]
        cos, sin = cosine[:, columns], sine[:, columns]
        joined_back[offset : offset + half, columns] = (upper * cos + lower * sin).astype(bf16)
        joined_back[offset + half : offset + HEAD_DIM, columns] = (lower * cos - upper * sin).astype(bf16)

    width = heads * HEAD_DIM
    columns = pl.ds(pl.multiple_of(step * TILE_Q, TILE_Q), TILE_Q)
    for h in range(heads):
        store(h * HEAD_DIM, columns, query_sum[h][...] * 0.125)

    @pl.when(step == pl.num_programs(0) - 1)
    def _():
        for h in range(heads):
            first = width + h * HEAD_DIM
            store(first, slice(0, rows), key_sum[h][...] * (1.0 / LOG2E))
            first += width
            joined_back[first : first + HEAD_DIM, :] = value_sum[h][...].astype(bf16)


def attention_backward(
    low, high, queries, keys, values, grads, outs, logsum, key_rows, query_rows, cosine, sine
):
    width, rows = queries.shape
    heads = width // HEAD_DIM

    def full(count):
        return pl.BlockSpec((count, rows), lambda i, low, high: (0, 0))

    def tile(count):
        return pl.BlockSpec((count, TILE_Q), lambda i, low, high: (0, i))

    return pl.pallas_call(
        backward_kernel,
        out_shape=jax.ShapeDtypeStruct((3 * width, rows), bf16),
        grid_spec=pltpu.PrefetchScalarGridSpec(
            num_scalar_prefetch=2,
            grid=(rows // TILE_Q,),
            in_specs=[
                tile(width), full(width), full(width), tile(width), tile(width), tile(heads),
                full(16), tile(16), full(HEAD_DIM // 2), full(HEAD_DIM // 2),
            ],
            out_specs=full(3 * width),
            scratch_shapes=[
                pltpu.VMEM((heads, rows, DEPTH), bf16),
                pltpu.VMEM((heads, rows, DEPTH), bf16),
                pltpu.VMEM((heads, DEPTH, TILE_Q), bf16),
                pltpu.VMEM((heads, DEPTH, TILE_Q), bf16),
            ]
            + [pltpu.VMEM((HEAD_DIM, rows), f32)] * (2 * heads)
            + [pltpu.VMEM((HEAD_DIM, TILE_Q), f32)] * heads,
        ),
        compiler_params=pltpu.CompilerParams(
            dimension_semantics=("arbitrary",), vmem_limit_bytes=52 << 20
        ),
        name="attention_backward",
    )(low, high, queries, keys, values, grads, outs, logsum, key_rows, query_rows, cosine, sine)


def layer_norm(values, gain_row):
    centred = values - jnp.mean(values, axis=-1, keepdims=True)
    inverse = lax.rsqrt(jnp.mean(centred * centred, axis=-1, keepdims=True) + norm_epsilon)
    normal = centred * inverse
    return normal * gain_row, normal, inverse


def norm_back(upstream, gain_row, normal, inverse):
    scaled = upstream * gain_row
    inner_mean = jnp.mean(scaled * normal, axis=-1, keepdims=True)
    return inverse * (scaled - jnp.mean(scaled, axis=-1, keepdims=True) - normal * inner_mean)


def horner(square, factors):
    total = factors[0] * square + factors[1]
    for factor in factors[2:]:
        total = total * square + factor
    return total


def error_function(value):
    value = jnp.clip(value, -4.0, 4.0)
    square = value * value
    return value * horner(square, ERF_TOP) / horner(square, ERF_BOTTOM)


def turn(value):
    columns = value.shape[1]
    rest = jnp.zeros((value.shape[0], -columns % 128), value.dtype)
    return jnp.concatenate([value, rest], axis=1).T[:columns, :]


def turn_back(value):
    lines = value.shape[0]
    rest = jnp.zeros((-lines % 128, value.shape[1]), value.dtype)
    return jnp.concatenate([value, rest], axis=0).T[:, :lines]


def first_kernel(head, own, other, gain, rows, normed):
    tiles = pl.num_programs(0) // 2
    mine = pl.program_id(0) // tiles == head[0]
    value = jnp.where(mine, own[...].astype(f32), other[...].astype(f32))
    rows[...] = value.astype(bf16)
    normed[...] = layer_norm(value, gain[...])[0].astype(bf16)


def first_norm(head, own, other, gain):
    half, width = own.shape
    tiles = half // FEED_ROWS
    result = jax.ShapeDtypeStruct((2 * half, width), bf16)
    spec = pl.BlockSpec((FEED_ROWS, width), lambda i, head: (i, 0))
    return pl.pallas_call(
        first_kernel,
        out_shape=(result, result),
        grid_spec=pltpu.PrefetchScalarGridSpec(
            num_scalar_prefetch=1,
            grid=(2 * tiles,),
            in_specs=[
                pl.BlockSpec(
                    (FEED_ROWS, width),
                    lambda i, head: (jnp.clip(i - head[0] * tiles, 0, tiles - 1), 0),
                ),
                pl.BlockSpec(
                    (FEED_ROWS, width),
                    lambda i, head: (jnp.clip(i - (1 - head[0]) * tiles, 0, tiles - 1), 0),
                ),
                pl.BlockSpec((1, width), lambda i, head: (0, 0)),
            ],
            out_specs=[spec, spec],
        ),
        compiler_params=pltpu.CompilerParams(dimension_semantics=("arbitrary",)),
        name="first_norm",
    )(head, own, other, gain)


def gradient_kernel(back, normed, *refs):
    grads, total = refs[:-1], refs[-1]
    step = pl.program_id(0)

    @pl.when(step == 0)
    def _():
        total[...] = dot(back[...], normed[...], NN)

    @pl.when(step > 0)
    def _():
        total[...] += dot(back[...], normed[...], NN)

    @pl.when(step == pl.num_programs(0) - 1)
    def _():
        first = 0
        for grad in grads:
            grad[...] = total[:, first : first + grad.shape[1]].astype(bf16)
            first += grad.shape[1]


def joined_gradient(back, normed):
    lines, count = back.shape
    width = normed.shape[1]
    tile = 2 * FEED_ROWS
    half = width // 256 * 128
    parts = [half, width - half]
    return pl.pallas_call(
        gradient_kernel,
        grid=(count // tile,),
        in_specs=[
            pl.BlockSpec((lines, tile), lambda i: (0, i)),
            pl.BlockSpec((tile, width), lambda i: (i, 0)),
        ],
        out_specs=[pl.BlockSpec((lines, part), lambda i: (0, 0)) for part in parts],
        out_shape=[jax.ShapeDtypeStruct((lines, part), bf16) for part in parts],
        scratch_shapes=[pltpu.VMEM((lines, width), f32)],
        compiler_params=pltpu.CompilerParams(
            dimension_semantics=("arbitrary",), vmem_limit_bytes=32 << 20
        ),
        name="joined_gradient",
    )(back, normed)


def pull_kernel(head, back, weight, out):
    out[...] = dot(back[...].T, weight[...], NN).astype(bf16)


def pull_other(head, back, weight):
    lines, count = back.shape
    width = weight.shape[1]
    tiles = count // 2 // FEED_ROWS
    return pl.pallas_call(
        pull_kernel,
        out_shape=jax.ShapeDtypeStruct((count // 2, width), bf16),
        grid_spec=pltpu.PrefetchScalarGridSpec(
            num_scalar_prefetch=1,
            grid=(tiles,),
            in_specs=[
                pl.BlockSpec((lines, FEED_ROWS), lambda i, head: (0, (1 - head[0]) * tiles + i)),
                pl.BlockSpec((lines, width), lambda i, head: (0, 0)),
            ],
            out_specs=pl.BlockSpec((FEED_ROWS, width), lambda i, head: (i, 0)),
        ),
        compiler_params=pltpu.CompilerParams(
            dimension_semantics=("arbitrary",), vmem_limit_bytes=24 << 20
        ),
        name="pull_other",
    )(head, back, weight)


def input_kernel(head, back, weight, other, rows, middle_grad, gain, input_grad, gain_grad):
    @pl.when(pl.program_id(0) == 0)
    def _():
        gain_grad[...] = jnp.zeros(gain_grad.shape, f32)

    pulled = dot(back[...].T, weight[...], NN) + other[...].astype(f32)
    unused, normal, inverse = layer_norm(rows[...].astype(f32), gain[...])
    input_grad[...] = middle_grad[...] + norm_back(pulled, gain[...], normal, inverse)
    gain_grad[...] += jnp.sum(pulled * normal, axis=0, keepdims=True)


def input_backward(head, back, weight, other, rows, middle_grad, gain):
    lines, count = back.shape
    width = weight.shape[1]
    tiles = count // 2 // FEED_ROWS

    def down():
        return pl.BlockSpec((FEED_ROWS, width), lambda i, head: (i, 0))

    return pl.pallas_call(
        input_kernel,
        out_shape=(
            jax.ShapeDtypeStruct((count // 2, width), f32),
            jax.ShapeDtypeStruct((1, width), f32),
        ),
        grid_spec=pltpu.PrefetchScalarGridSpec(
            num_scalar_prefetch=1,
            grid=(tiles,),
            in_specs=[
                pl.BlockSpec((lines, FEED_ROWS), lambda i, head: (0, head[0] * tiles + i)),
                pl.BlockSpec((lines, width), lambda i, head: (0, 0)),
                down(),
                down(),
                pl.BlockSpec((FEED_ROWS, width), lambda i, head: (head[0] * tiles + i, 0)),
                pl.BlockSpec((1, width), lambda i, head: (0, 0)),
            ],
            out_specs=[down(), pl.BlockSpec((1, width), lambda i, head: (0, 0))],
        ),
        compiler_params=pltpu.CompilerParams(
            dimension_semantics=("arbitrary",), vmem_limit_bytes=24 << 20
        ),
        name="input_backward",
    )(head, back, weight, other, rows, middle_grad, gain)


def feed_kernel(
    rows, attended, attended_other, upstream, gain, both, mixer_other, expand_left, expand_right,
    middle, hidden, second_part, shrink_grad, left_grad, right_grad, shrink,
    shrink_sum, expand_sum, expand
):
    step = pl.program_id(0)
    mixed, units = attended.shape[0], shrink.shape[0]
    chunk = units // FEED_CHUNKS

    @pl.when(step == 0)
    def _():
        expand[:, : expand_left.shape[1]] = expand_left[...]
        expand[:, expand_left.shape[1] :] = expand_right[...]
        shrink[...] = turn(both[:, mixed:])
        shrink_sum[...] = jnp.zeros(shrink_sum.shape, f32)
        expand_sum[...] = jnp.zeros(expand_sum.shape, f32)

    total = rows[...].astype(f32) + dot(attended[...].T, both[:, :mixed], NT)
    total = total + dot(attended_other[...].T, mixer_other[...], NT)
    middle[...] = total
    normed = layer_norm(total, gain[...])[0].astype(bf16)
    above = upstream[...]

    def project(c):
        first = slice(c * chunk, (c + 1) * chunk)
        second = slice(units + c * chunk, units + (c + 1) * chunk)
        return (
            dot(expand[first, :], normed, NT),
            dot(expand[second, :], normed, NT),
            dot(shrink[first, :], above, NT),
        )

    waiting = project(0)
    back = jnp.zeros(total.shape, f32)
    for c in range(FEED_CHUNKS):
        active, linear, grad = waiting
        if c + 1 < FEED_CHUNKS:
            waiting = project(c + 1)
        first = slice(c * chunk, (c + 1) * chunk)
        second = slice(units + c * chunk, units + (c + 1) * chunk)
        area = 0.5 * error_function(active * math.sqrt(0.5)) + 0.5
        gate = active * area
        density = jnp.exp(-0.5 * active * active) * (1.0 / math.sqrt(2.0 * math.pi))
        unit = (gate * linear).astype(bf16)
        active_back = (grad * linear * (area + active * density)).astype(bf16)
        linear_back = (grad * gate).astype(bf16)
        hidden[first, :] = unit
        shrink_sum[first, :] += dot(unit, above, NN)
        expand_sum[first, :] += dot(active_back, normed, NN)
        expand_sum[second, :] += dot(linear_back, normed, NN)
        back = back + dot(active_back, expand[first, :], TN) + dot(linear_back, expand[second, :], TN)
    second_part[...] = back.astype(bf16)

    @pl.when(step == pl.num_programs(0) - 1)
    def _():
        shrink_grad[...] = shrink_sum[...].astype(bf16)
        cut = left_grad.shape[1]
        left_grad[...] = expand_sum[:, :cut].astype(bf16)
        right_grad[...] = expand_sum[:, cut:].astype(bf16)


def feed_forward(rows, attended, attended_other, upstream, gain, both, mixer_other, expand):
    count, width = rows.shape
    mixed, units = attended.shape[0], expand[0].shape[0] // 2

    def full(*shape):
        return pl.BlockSpec(shape, lambda i: (0, 0))

    def down(columns):
        return pl.BlockSpec((FEED_TILE, columns), lambda i: (i, 0))

    def along(lines):
        return pl.BlockSpec((lines, FEED_TILE), lambda i: (0, i))

    return pl.pallas_call(
        feed_kernel,
        grid=(count // FEED_TILE,),
        in_specs=[
            down(width), along(mixed), along(mixed), down(width), full(1, width),
            full(*both.shape), full(width, mixed), full(*expand[0].shape), full(*expand[1].shape),
        ],
        out_specs=[
            down(width), along(units), down(width), full(units, width),
            full(*expand[0].shape), full(*expand[1].shape), full(units, width),
        ],
        out_shape=(
            jax.ShapeDtypeStruct((count, width), f32),
            jax.ShapeDtypeStruct((units, count), bf16),
            jax.ShapeDtypeStruct((count, width), bf16),
            jax.ShapeDtypeStruct((units, width), bf16),
            jax.ShapeDtypeStruct(expand[0].shape, bf16),
            jax.ShapeDtypeStruct(expand[1].shape, bf16),
            jax.ShapeDtypeStruct((units, width), bf16),
        ),
        scratch_shapes=[
            pltpu.VMEM((units, width), f32),
            pltpu.VMEM((2 * units, width), f32),
            pltpu.VMEM((2 * units, width), bf16),
        ],
        compiler_params=pltpu.CompilerParams(
            dimension_semantics=("arbitrary",), vmem_limit_bytes=48 << 20
        ),
        name="feed_forward",
    )(rows, attended, attended_other, upstream, gain, both, mixer_other, *expand)


def norm_kernel(
    middle, own, other, upstream, gain, both, attended, shrink_grad,
    middle_grad, attended_grad, both_grad, gain_grad, mixer_turned, mixer_sum
):
    step = pl.program_id(0)

    @pl.when(step == 0)
    def _():
        mixer_turned[...] = both[:, : attended.shape[0]].T
        mixer_sum[...] = jnp.zeros(mixer_sum.shape, f32)
        gain_grad[...] = jnp.zeros(gain_grad.shape, f32)

    unused, normal, inverse = layer_norm(middle[...], gain[...])
    back = own[...].astype(f32) + other[...].astype(f32)
    grad = upstream[...].astype(f32) + norm_back(back, gain[...], normal, inverse)
    middle_grad[...] = grad
    grad_low = grad.astype(bf16)
    attended_grad[...] = dot(mixer_turned[...], grad_low, NT).astype(bf16)
    mixer_sum[...] += dot(attended[...], grad_low, NN)
    gain_grad[...] += jnp.sum(back * normal, axis=0, keepdims=True)

    @pl.when(step == pl.num_programs(0) - 1)
    def _():
        mixed = attended.shape[0]
        both_grad[:, :mixed] = mixer_sum[...].T.astype(bf16)
        both_grad[:, mixed:] = turn_back(shrink_grad[...])


def norm_backward(middle, own, other, upstream, gain, both, attended, shrink_grad):
    count, width = middle.shape
    mixed = attended.shape[0]

    def full(*shape):
        return pl.BlockSpec(shape, lambda i: (0, 0))

    def down(columns):
        return pl.BlockSpec((FEED_TILE, columns), lambda i: (i, 0))

    def along(lines):
        return pl.BlockSpec((lines, FEED_TILE), lambda i: (0, i))

    return pl.pallas_call(
        norm_kernel,
        grid=(count // FEED_TILE,),
        in_specs=[
            down(width), down(width), down(width), down(width), full(1, width),
            full(*both.shape), along(mixed), full(*shrink_grad.shape),
        ],
        out_specs=[down(width), along(mixed), full(*both.shape), full(1, width)],
        out_shape=(
            jax.ShapeDtypeStruct((count, width), f32),
            jax.ShapeDtypeStruct((mixed, count), bf16),
            jax.ShapeDtypeStruct(both.shape, bf16),
            jax.ShapeDtypeStruct((1, width), f32),
        ),
        scratch_shapes=[pltpu.VMEM((mixed, width), bf16), pltpu.VMEM((mixed, width), f32)],
        compiler_params=pltpu.CompilerParams(
            dimension_semantics=("arbitrary",), vmem_limit_bytes=40 << 20
        ),
        name="norm_backward",
    )(middle, own, other, upstream, gain, both, attended, shrink_grad)


def swap(value, axis, bit):
    count = lax.axis_size(axis)
    return lax.ppermute(value, axis, [(i, i ^ bit) for i in range(count)])


def bit_order(lead):
    bits = lax.axis_size("dp").bit_length() - 1
    return [int(bit) for bit in lead] + list(range(len(lead), bits))


def steps_count():
    return lax.axis_size("dp").bit_length() - 1


def cut(held, bit):
    axis = steps_count() - 1 - bit
    side = (lax.axis_index("dp") >> bit) & 1
    kept = lax.dynamic_slice_in_dim(held, side, 1, axis)
    return kept, lax.dynamic_slice_in_dim(held, 1 - side, 1, axis)


def reduce_start(value, lead):
    bits = steps_count()
    rows = value.shape[0] >> bits
    return cut(value.reshape((2,) * bits + (rows, value.shape[1])), bit_order(lead)[0])


def reduce_step(held, step, lead):
    bits = steps_count()
    kept, sent = held if step == 0 else cut(held, bit_order(lead)[step])
    total = kept.astype(f32) + swap(sent, "dp", 1 << bit_order(lead)[step]).astype(f32)
    if step + 1 == bits:
        return total.reshape(kept.shape[-2:])
    return total.astype(bf16)


def gather_start(value):
    return value[(None,) * steps_count()]


def gather_step(held, step, lead):
    bits = steps_count()
    bit = bit_order(lead)[bits - 1 - step]
    return jnp.concatenate([held, swap(held, "dp", 1 << bit)], axis=bits - 1 - bit)


def ordered_step(held, step, lead):
    bits = steps_count()
    bit = bit_order(lead)[bits - 1 - step]
    got = swap(held, "dp", 1 << bit)
    low_side = ((lax.axis_index("dp") >> bit) & 1) == 0
    return jnp.concatenate(
        [jnp.where(low_side, held, got), jnp.where(low_side, got, held)], axis=bits - 1 - bit
    )


def gather_rows(held):
    return held.reshape(-1, held.shape[-1])


def halves_of(value):
    unit = value.shape[1] // 256 * 128
    return [value[:, :unit], value[:, unit:]]


def quarter(step, states, part, leads):
    bits = steps_count()
    for index in range(bits * part // QUARTERS, bits * (part + 1) // QUARTERS):
        states = [step(state, index, lead) for state, lead in zip(states, leads)]
    return states


def tie(*values):
    return lax.optimization_barrier(values)


def total_step(value, part):
    if part == 0:
        return value + swap(value, "head", 1)
    bits = steps_count()
    for bit in range(bits * (part - 1) // QUARTERS, bits * part // QUARTERS):
        value = value + swap(value, "dp", 1 << bit)
    return value


def schulz_start(held, own, gram, low):
    down = 0
    for left in held:
        along = 0
        for right in held:
            gram[down : down + left.shape[1], along : along + right.shape[1]] = dot(left, right, TN)
            along += right.shape[1]
        down += left.shape[1]
    shape = gram.shape
    diagonal = lax.broadcasted_iota(jnp.int32, shape, 0) == lax.broadcasted_iota(jnp.int32, shape, 1)
    trace = jnp.sum(jnp.where(diagonal, gram[...], 0.0), axis=0, keepdims=True)
    norm_value = jnp.sqrt(jnp.sum(trace, axis=1, keepdims=True)) + 1e-07
    gram[...] = gram[...] * (1.0 / (norm_value * norm_value))
    low[...] = gram[...].astype(bf16)
    return own[...] / norm_value


def schulz_steps(rows, gram, low, change, first, stop):
    columns = gram.shape[0]
    lines = 256 if columns % 256 == 0 else columns

    def per_block(body):
        def run(index, carry):
            body(pl.ds(pl.multiple_of(index * lines, lines), lines))
            return carry

        lax.fori_loop(0, columns // lines, run, 0, unroll=True)

    def form_change(block):
        squared = dot(low[block, :], low[...], NN)
        change[block, :] = (ns_second * gram[block, :] + ns_third * squared).astype(bf16)

    def next_gram(block):
        once = ns_first * gram[block, :] + dot(low[block, :], change[...], NN)
        twice = ns_first * once + dot(once.astype(bf16), change[...], NN)
        gram[block, :] = twice
        low[block, :] = twice.astype(bf16)

    for iteration in range(first, stop):
        per_block(form_change)
        rows = ns_first * rows + dot(rows.astype(bf16), change[...], NN)
        if iteration + 1 < NS_ITERS:
            per_block(next_gram)
    return rows


def whole_kernel(*refs, count, offset, scale):
    parts = refs[:count]
    own, weight, updated, gram, low, change = refs[count:]
    if offset is None:
        held = [part[...] for part in parts]
    else:
        held = [parts[0][:, offset : offset + gram.shape[0]]]
    rows = schulz_start(held, own, gram, low)
    updated[...] = weight[...] - scale * schulz_steps(rows, gram, low, change, 0, NS_ITERS)


def early_kernel(*refs, count):
    own, rows, gram_out, low_out, gram, low, change = refs[count:]
    start = schulz_start([part[...] for part in refs[:count]], own, gram, low)
    rows[...] = start
    gram_out[...] = gram[...]
    low_out[...] = low[...]


def late_kernel(rows, gram_in, low_in, weight, updated, gram, low, change, *, scale):
    gram[...] = gram_in[...]
    low[...] = low_in[...]
    done = schulz_steps(rows[...], gram, low, change, 0, NS_ITERS)
    updated[...] = weight[...] - scale * done


def square_scratch(columns):
    return [
        pltpu.VMEM((columns, columns), f32),
        pltpu.VMEM((columns, columns), bf16),
        pltpu.VMEM((columns, columns), bf16),
    ]


def shape_scale(rows, columns):
    return muon_rate * math.sqrt(rows / columns)


def schulz(parts, offset, own, weight, name):
    columns = own.shape[1]
    return pl.pallas_call(
        functools.partial(
            whole_kernel, count=len(parts), offset=offset, scale=shape_scale(parts[0].shape[0], columns)
        ),
        out_shape=jax.ShapeDtypeStruct(own.shape, f32),
        scratch_shapes=square_scratch(columns),
        compiler_params=pltpu.CompilerParams(vmem_limit_bytes=40 << 20),
        name=name,
    )(*parts, own, weight)


def schulz_early(parts, own):
    columns = own.shape[1]
    return pl.pallas_call(
        functools.partial(early_kernel, count=len(parts)),
        out_shape=(
            jax.ShapeDtypeStruct(own.shape, f32),
            jax.ShapeDtypeStruct((columns, columns), f32),
            jax.ShapeDtypeStruct((columns, columns), bf16),
        ),
        scratch_shapes=square_scratch(columns),
        compiler_params=pltpu.CompilerParams(vmem_limit_bytes=40 << 20),
        name="schulz_early",
    )(*parts, own)


def schulz_late(state, weight, rows):
    columns = weight.shape[1]
    return pl.pallas_call(
        functools.partial(late_kernel, scale=shape_scale(rows, columns)),
        out_shape=jax.ShapeDtypeStruct(weight.shape, f32),
        scratch_shapes=square_scratch(columns),
        compiler_params=pltpu.CompilerParams(vmem_limit_bytes=40 << 20),
        name="schulz_late",
    )(*state, weight)


def shards(
    tokens,
    lengths,
    norm_gains,
    joined_weight,
    mixer_weight,
    expand_weight,
    shrink_weight,
    joined_momentum,
    mixer_momentum,
    expand_momentum,
    shrink_momentum,
    gain_momentum,
    cotangent,
):
    row_count = cotangent.shape[0]
    local_rows = tokens.shape[0]
    head = lax.axis_index("head")
    mixer_width = mixer_weight.shape[2]

    def own_half(value):
        return lax.dynamic_slice_in_dim(value, head * local_rows, local_rows, 0)

    joined_parts = [gather_start(part) for part in halves_of(joined_weight[0].astype(bf16))]
    joined_parts = quarter(ordered_step, joined_parts, 0, JOINED_FIRST)
    others = [gather_start(part) for part in halves_of(expand_weight[0].astype(bf16))] + [
        gather_start(jnp.concatenate([mixer_weight[0], shrink_weight[0]], axis=1).astype(bf16))
    ]
    key_rows, query_rows, cosine, sine = doc_tables(lengths[0], row_count)
    low, high = key_bounds(lengths[0], row_count)
    head_place = head[None]
    tokens_other = swap(tokens, "head", 1)

    joined_parts, others, tokens_other = tie(joined_parts, others, tokens_other)
    joined_parts = quarter(ordered_step, joined_parts, 1, JOINED_FIRST)
    others = quarter(ordered_step, others, 0, OTHERS_FIRST)
    rows_low, first_low = first_norm(head_place, tokens, tokens_other, norm_gains[0:1])
    joined_parts, others, first_low = tie(joined_parts, others, first_low)
    joined_parts = quarter(ordered_step, joined_parts, 2, JOINED_FIRST)
    others = quarter(ordered_step, others, 1, OTHERS_FIRST)
    joined_parts, others = tie(joined_parts, others)
    joined_parts = quarter(ordered_step, joined_parts, 3, JOINED_FIRST)
    moved = quarter(ordered_step, others, 2, OTHERS_FIRST)

    joined_low = jnp.concatenate([gather_rows(part) for part in joined_parts], axis=1)
    joined = dot(joined_low, first_low, NT)
    width = joined.shape[0] // 3
    queries = (rotate(joined[:width], cosine, sine) * QUERY_SCALE).astype(bf16)
    keys = rotate(joined[width : 2 * width], cosine, sine).astype(bf16)
    values = joined[2 * width :].astype(bf16)
    others, queries, keys, values, low = tie(moved, queries, keys, values, low)
    moved = quarter(ordered_step, others, 3, OTHERS_FIRST)
    attended, logsum = attention_forward(low, high, queries, keys, values, key_rows, query_rows)
    others, attended, logsum = tie(moved, attended, logsum)
    attended_other = swap(attended, "head", 1)
    both_low = gather_rows(others[2])
    mixer_other = swap(both_low[:, :mixer_width], "head", 1)

    second_gain = norm_gains[1:2]
    middle, hidden, second_part, shrink_grad, left_grad, right_grad, shrink_turned = feed_forward(
        rows_low, attended, attended_other, cotangent, second_gain,
        both_low, mixer_other, [gather_rows(part) for part in others[:2]],
    )
    second_other = swap(second_part, "head", 1)

    sums = [reduce_start(part, lead) for part, lead in zip((left_grad, right_grad), PAIR)]
    sums, second_other = tie(sums, second_other)
    moved = quarter(reduce_step, sums, 0, PAIR)
    middle_grad, attended_grad, both_grad, second_gain_grad = norm_backward(
        middle, second_part, second_other, cotangent, second_gain, both_low, attended, shrink_grad
    )
    both_sum = [reduce_start(both_grad, ONE[0])]

    sums, attended_grad, shrink_now = tie(moved, attended_grad, shrink_turned)
    moved = quarter(reduce_step, sums, 1, PAIR)

    def fed(columns):
        units = lax.dynamic_slice_in_dim(hidden, columns, local_rows, 1)
        return dot(units, shrink_now, TN)

    fed_other = fed((1 - head) * local_rows).astype(bf16)
    fed_own = fed(head * local_rows)

    sums, both_sum, fed_other, fed_own, low = tie(moved, both_sum, fed_other, fed_own, low)
    moved = quarter(reduce_step, sums, 2, PAIR)
    both_moved = quarter(reduce_step, both_sum, 0, ONE)
    fed_other = swap(fed_other, "head", 1)
    joined_back = attention_backward(
        low, high, queries, keys, values, attended_grad, attended, logsum, key_rows, query_rows,
        cosine, sine,
    )
    sums, both_sum, joined_back, fed_other = tie(moved, both_moved, joined_back, fed_other)
    moved = quarter(reduce_step, sums, 3, PAIR)
    both_moved = quarter(reduce_step, both_sum, 1, ONE)
    joined_grad = joined_gradient(joined_back, first_low)

    sums, both_sum, joined_grad, joined_now = tie(moved, both_moved, joined_grad, joined_low)
    expand_next = 0.5 * expand_momentum[0] + jnp.concatenate(sums, axis=1)
    gathers = [gather_start(part) for part in halves_of(expand_next.astype(bf16))]
    sums = [reduce_start(part, lead) for part, lead in zip(joined_grad, PAIR)]
    sums = quarter(reduce_step, sums, 0, PAIR)
    moved = quarter(gather_step, gathers, 0, PAIR)
    both_moved = quarter(reduce_step, both_sum, 2, ONE)
    first_other = pull_other(head_place, joined_back, joined_now)

    sums, gathers, both_sum, first_other, fed_own = tie(sums, moved, both_moved, first_other, fed_own)
    first_other = swap(first_other, "head", 1)
    moved = quarter(reduce_step, sums, 1, PAIR)
    gathers_moved = quarter(gather_step, gathers, 1, PAIR)
    both_moved = quarter(reduce_step, both_sum, 3, ONE)

    sums, gathers, both_sum, first_other, fed_own = tie(
        moved, gathers_moved, both_moved, first_other, fed_own
    )
    mixer_next = 0.5 * mixer_momentum[0] + both_sum[0][:, :mixer_width]
    shrink_next = 0.5 * shrink_momentum[0] + both_sum[0][:, mixer_width:]
    both_gather = [gather_start(jnp.concatenate([mixer_next, shrink_next], axis=1).astype(bf16))]
    moved = quarter(reduce_step, sums, 2, PAIR)
    gathers_moved = quarter(gather_step, gathers, 2, PAIR)
    both_moved = quarter(gather_step, both_gather, 0, ONE)
    layer_output = (own_half(middle) + fed_own + fed_other.astype(f32)).astype(bf16)

    sums, gathers, both_gather, first_other, layer_output = tie(
        moved, gathers_moved, both_moved, first_other, layer_output
    )
    moved = quarter(reduce_step, sums, 3, PAIR)
    gathers_moved = quarter(gather_step, gathers, 3, PAIR)
    both_moved = quarter(gather_step, both_gather, 1, ONE)
    input_gradient, first_gain_grad = input_backward(
        head_place, joined_back, joined_now, first_other, tokens, middle_grad, norm_gains[0:1]
    )
    gain_totals = jnp.concatenate([first_gain_grad, 0.5 * second_gain_grad], axis=0)

    sums, gathers, both_gather, gain_totals = tie(moved, gathers_moved, both_moved, gain_totals)
    joined_next = 0.5 * joined_momentum[0] + jnp.concatenate(sums, axis=1)
    joined_gather = [gather_start(part) for part in halves_of(joined_next.astype(bf16))]
    moved = quarter(gather_step, joined_gather, 0, PAIR)
    both_moved = quarter(gather_step, both_gather, 2, ONE)
    gain_moved = total_step(gain_totals, 0)
    expand_state = schulz_early([gather_rows(part) for part in gathers], expand_next)
    joined_gather, both_gather, gain_totals, expand_state = tie(
        moved, both_moved, gain_moved, expand_state
    )
    moved = quarter(gather_step, joined_gather, 1, PAIR)
    both_moved = quarter(gather_step, both_gather, 3, ONE)
    gain_moved = total_step(gain_totals, 1)
    updated_expand = schulz_late(expand_state, expand_weight[0], left_grad.shape[0])
    joined_gather, both_gather, gain_totals, updated_expand = tie(
        moved, both_moved, gain_moved, updated_expand
    )
    both_full = [gather_rows(both_gather[0])]
    moved = quarter(gather_step, joined_gather, 2, PAIR)
    gain_moved = total_step(gain_totals, 2)
    updated_shrink = schulz(
        both_full, mixer_width, shrink_next, shrink_weight[0], "schulz_shrink"
    )
    joined_gather, both_full, gain_totals, updated_shrink = tie(
        moved, both_full, gain_moved, updated_shrink
    )
    moved = quarter(gather_step, joined_gather, 3, PAIR)
    gain_moved = total_step(gain_totals, 3)
    updated_mixer = schulz(both_full, 0, mixer_next, mixer_weight[0], "schulz_mixer")
    joined_gather, gain_totals, updated_mixer = tie(moved, gain_moved, updated_mixer)
    gain_totals = total_step(gain_totals, 4)
    updated_joined = schulz(
        [gather_rows(part) for part in joined_gather],
        None, joined_next, joined_weight[0], "schulz_joined",
    )

    momentum_gains = 0.5 * gain_momentum + gain_totals
    updated_gains = norm_gains - gain_rate * momentum_gains * lax.rsqrt(
        jnp.mean(momentum_gains * momentum_gains, axis=-1, keepdims=True) + 1e-06
    )
    return (
        layer_output,
        input_gradient,
        joined_next[None],
        mixer_next[None],
        expand_next[None],
        shrink_next[None],
        updated_joined[None],
        updated_mixer[None],
        updated_expand[None],
        updated_shrink[None],
        momentum_gains,
        updated_gains,
    )


def solution(mesh):
    rows = P(("dp", "head"), None)
    weight = P("head", "dp", None)
    return jax.shard_map(
        shards,
        mesh=mesh,
        in_specs=(rows, P("dp", None), P()) + (weight,) * 8 + (P(), P("dp", None)),
        out_specs=(rows, rows) + (weight,) * 8 + (P(), P()),
        check_vma=False,
    )
```

```python
import functools
import math

import jax
import jax.numpy as jnp
from jax import lax
from jax.experimental import pallas as pl
from jax.experimental.pallas import tpu as pltpu
from jax.sharding import PartitionSpec as P

HEAD_DIM = 64
NS_ITERS = 3

theta_base = 160000.0
norm_epsilon = 1e-05
ns_first = 3.4445
ns_second = -4.775
ns_third = 2.0315
muon_rate = 1.0
gain_rate = 0.3

bf16 = jnp.bfloat16
f32 = jnp.float32
LOG2E = math.log2(math.e)
QUERY_SCALE = 0.125 * LOG2E
SAFE_SCORE = 60.0
DEPTH = 128
TILE_Q = 256
TILE_K = 256
FWD_SKEW = 6
BWD_SKEW = 2

NN = (((1,), (0,)), ((), ()))
NT = (((1,), (1,)), ((), ()))
TN = (((0,), (0,)), ((), ()))
TT = (((0,), (1,)), ((), ()))
QUARTERS = 4
PAIR = ("012", "102")
JOINED_FIRST = ("012", "120")
OTHERS_FIRST = ("021", "201", "120")
ONE = ("012",)
FEED_ROWS = 512
FEED_TILE = 512
FEED_CHUNKS = 2
ERF_TOP = (
    -2.72614225801306e-10, 2.77068142495902e-08, -2.10102402082508e-06, -5.69250639462346e-05,
    -7.34990630326855e-04, -2.95459980854025e-03, -1.60960333262415e-02,
)
ERF_BOTTOM = (
    -1.45660718464996e-05, -2.13374055278905e-04, -1.68282697438203e-03, -7.37332916720468e-03,
    -1.42647390514189e-02,
)


def dot(left, right, dims):
    return lax.dot_general(left, right, dims, preferred_element_type=f32)


def key_bounds(length_row, row_count):
    ends = jnp.cumsum(length_row)
    starts = ends - length_row
    first = jnp.arange(row_count // TILE_Q, dtype=jnp.int32) * TILE_Q
    labels = jnp.arange(length_row.shape[0], dtype=jnp.int32)

    def pick(places, table):
        segment = jnp.sum((places[:, None] >= ends[None, :]).astype(jnp.int32), axis=1)
        return jnp.sum(jnp.where(segment[:, None] == labels[None, :], table[None, :], 0), axis=1)

    low = pick(first, starts) // TILE_K
    high = (pick(first + TILE_Q - 1, ends) + TILE_K - 1) // TILE_K
    return low.astype(jnp.int32), high.astype(jnp.int32)


def doc_tables(length_row, row_count):
    ends = jnp.cumsum(length_row)
    starts = ends - length_row
    count = length_row.shape[0]
    places = jnp.arange(row_count, dtype=jnp.int32)[None, :]
    member = (places >= starts[:, None]) & (places < ends[:, None])
    rest = jnp.zeros((16 - count, row_count), f32)
    key_rows = jnp.concatenate([member.astype(f32), rest], axis=0).astype(bf16)
    query_rows = jnp.concatenate([jnp.where(member, 0.0, -1e30), rest], axis=0).astype(bf16)
    doc_first = jnp.sum(jnp.where(member, starts[:, None], 0), axis=0, keepdims=True)
    position = (places - doc_first).astype(f32)
    half_dim = HEAD_DIM // 2
    frequency = jnp.exp(
        jnp.arange(half_dim, dtype=f32) * (-2.0 * math.log(theta_base) / HEAD_DIM)
    )
    angles = frequency[:, None] * position
    return key_rows, query_rows, jnp.cos(angles), jnp.sin(angles)


def rotate(values, cosine, sine):
    half = HEAD_DIM // 2
    heads = values.reshape(-1, HEAD_DIM, values.shape[1])
    low, high = heads[:, :half], heads[:, half:]
    turned = jnp.concatenate([low * cosine - high * sine, high * cosine + low * sine], axis=1)
    return turned.reshape(values.shape)


def rows16(parts):
    rest = jnp.zeros((16 - len(parts), parts[0].shape[1]), f32)
    return jnp.concatenate([part.astype(f32) for part in parts] + [rest], axis=0).astype(bf16)


def split3(value):
    first = value.astype(bf16)
    left = value - first.astype(f32)
    second = left.astype(bf16)
    third = (left - second.astype(f32)).astype(bf16)
    return [first, second, third]


def three_ones(count):
    return jnp.concatenate([jnp.ones((3, count), f32), jnp.zeros((13, count), f32)], axis=0).astype(
        bf16
    )


def tile_loop(low, high, block, carry):
    pairs = (high - low) // 2

    def two(index, carry):
        first = low + 2 * index
        return block([first, first + 1], carry)

    carry = lax.fori_loop(0, pairs, two, carry)
    return lax.fori_loop(low + 2 * pairs, high, lambda j, carry: block([j], carry), carry)


def forward_kernel(
    low, high, queries, keys, values, key_rows, query_rows, out, logsum, keys_in, values_in, queries_in, safe
):
    heads = queries.shape[0] // HEAD_DIM
    rows = keys.shape[1]
    step = pl.program_id(0)

    @pl.when(step == 0)
    def _():
        worst = jnp.zeros((1, 1), f32)
        ones = rows16([jnp.ones((1, rows), f32)])
        for h in range(heads):
            band = slice(h * HEAD_DIM, (h + 1) * HEAD_DIM)
            key = keys[band, :]
            pad = jnp.zeros((DEPTH - HEAD_DIM - 16, rows), bf16)
            keys_in[h] = jnp.concatenate([key, key_rows[...], pad], axis=0).T
            values_in[h, :HEAD_DIM, :] = values[band, :]
            values_in[h, HEAD_DIM:, :] = ones
            query_full = queries[band, :].astype(f32)
            key_full = key.astype(f32)
            query_top = jnp.max(
                jnp.sum(query_full * query_full, axis=0, keepdims=True), axis=1, keepdims=True
            )
            key_top = jnp.max(
                jnp.sum(key_full * key_full, axis=0, keepdims=True), axis=1, keepdims=True
            )
            worst = jnp.maximum(worst, query_top * key_top)
        safe[0] = jnp.where(worst[0, 0] <= SAFE_SCORE * SAFE_SCORE, 1, 0)

    first = pl.multiple_of(step * TILE_Q, TILE_Q)
    for h in range(heads):
        queries_in[h, :HEAD_DIM, :] = queries[h * HEAD_DIM : (h + 1) * HEAD_DIM, pl.ds(first, TILE_Q)]
        queries_in[h, HEAD_DIM : HEAD_DIM + 16, :] = query_rows[...]
        queries_in[h, HEAD_DIM + 16 :, :] = jnp.zeros((DEPTH - HEAD_DIM - 16, TILE_Q), bf16)

    def finish(peaks, totals):
        for h in range(heads):
            weight = totals[h][HEAD_DIM : HEAD_DIM + 1, :]
            out[h * HEAD_DIM : (h + 1) * HEAD_DIM, :] = (totals[h][:HEAD_DIM, :] / weight).astype(bf16)
            level = jnp.log2(weight)
            logsum[h : h + 1, :] = level if peaks is None else peaks[h] + level

    empty = tuple(jnp.zeros((HEAD_DIM + 16, TILE_Q), f32) for _ in range(heads))

    @pl.when(safe[0] == 1)
    def _():
        def block(tiles, totals):
            spans = [pl.ds(pl.multiple_of(j * TILE_K, TILE_K), TILE_K) for j in tiles]
            units = [(span, h) for span in spans for h in range(heads)]
            totals = list(totals)
            waiting = {}
            for t in range(len(units) + FWD_SKEW):
                if t < len(units):
                    span, h = units[t]
                    waiting[t] = dot(keys_in[h, span, :], queries_in[h], NN)
                if t >= FWD_SKEW:
                    span, h = units[t - FWD_SKEW]
                    raised = jnp.exp2(waiting.pop(t - FWD_SKEW)).astype(bf16)
                    totals[h] = totals[h] + dot(values_in[h, :, span], raised, NN)
            return tuple(totals)

        finish(None, tile_loop(low[step], high[step], block, empty))

    @pl.when(safe[0] == 0)
    def _():
        def block(j, carry):
            peaks, totals = carry
            span = pl.ds(pl.multiple_of(j * TILE_K, TILE_K), TILE_K)
            new_peaks = []
            new_totals = []
            for h in range(heads):
                scores = dot(keys_in[h, span, :], queries_in[h], NN)
                peak = jnp.maximum(peaks[h], jnp.max(scores, axis=0, keepdims=True))
                raised = jnp.exp2(scores - peak).astype(bf16)
                new_totals.append(
                    totals[h] * jnp.exp2(peaks[h] - peak) + dot(values_in[h, :, span], raised, NN)
                )
                new_peaks.append(peak)
            return tuple(new_peaks), tuple(new_totals)

        lowest = tuple(jnp.full((1, TILE_Q), -3e38, f32) for _ in range(heads))
        finish(*lax.fori_loop(low[step], high[step], block, (lowest, empty)))


def attention_forward(low, high, queries, keys, values, key_rows, query_rows):
    width, rows = queries.shape
    heads = width // HEAD_DIM

    def full(count):
        return pl.BlockSpec((count, rows), lambda i, low, high: (0, 0))

    def tile(count):
        return pl.BlockSpec((count, TILE_Q), lambda i, low, high: (0, i))

    return pl.pallas_call(
        forward_kernel,
        out_shape=(
            jax.ShapeDtypeStruct((width, rows), bf16),
            jax.ShapeDtypeStruct((heads, rows), f32),
        ),
        grid_spec=pltpu.PrefetchScalarGridSpec(
            num_scalar_prefetch=2,
            grid=(rows // TILE_Q,),
            in_specs=[full(width), full(width), full(width), full(16), tile(16)],
            out_specs=[tile(width), tile(heads)],
            scratch_shapes=[
                pltpu.VMEM((heads, rows, DEPTH), bf16),
                pltpu.VMEM((heads, HEAD_DIM + 16, rows), bf16),
                pltpu.VMEM((heads, DEPTH, TILE_Q), bf16),
                pltpu.SMEM((1,), jnp.int32),
            ],
        ),
        compiler_params=pltpu.CompilerParams(
            dimension_semantics=("arbitrary",), vmem_limit_bytes=40 << 20
        ),
        name="attention_forward",
    )(low, high, queries, keys, values, key_rows, query_rows)


def backward_kernel(
    low, high, queries, keys, values, grads, outs, logsum, key_rows, query_rows, cosine, sine,
    joined_back, *scratch
):
    heads = queries.shape[0] // HEAD_DIM
    rows = keys.shape[1]
    keys_in, values_in, queries_in, grads_in = scratch[:4]
    key_sum = scratch[4 : 4 + heads]
    value_sum = scratch[4 + heads : 4 + 2 * heads]
    query_sum = scratch[4 + 2 * heads : 4 + 3 * heads]
    step = pl.program_id(0)

    @pl.when(step == 0)
    def _():
        ones = three_ones(rows)
        for h in range(heads):
            band = slice(h * HEAD_DIM, (h + 1) * HEAD_DIM)
            pad = jnp.zeros((DEPTH - HEAD_DIM - 32, rows), bf16)
            keys_in[h] = jnp.concatenate([keys[band, :], key_rows[...], ones, pad], axis=0).T
            pad = jnp.zeros((DEPTH - HEAD_DIM - 16, rows), bf16)
            values_in[h] = jnp.concatenate([values[band, :], ones, pad], axis=0).T
            key_sum[h][...] = jnp.zeros((HEAD_DIM, rows), f32)
            value_sum[h][...] = jnp.zeros((HEAD_DIM, rows), f32)

    for h in range(heads):
        band = slice(h * HEAD_DIM, (h + 1) * HEAD_DIM)
        queries_in[h, :HEAD_DIM, :] = queries[band, :]
        queries_in[h, HEAD_DIM : HEAD_DIM + 16, :] = query_rows[...]
        queries_in[h, HEAD_DIM + 16 : HEAD_DIM + 32, :] = rows16(split3(-logsum[h : h + 1, :]))
        queries_in[h, HEAD_DIM + 32 :, :] = jnp.zeros((DEPTH - HEAD_DIM - 32, TILE_Q), bf16)
        inner = jnp.sum(grads[band, :].astype(f32) * outs[band, :].astype(f32), axis=0, keepdims=True)
        grads_in[h, :HEAD_DIM, :] = grads[band, :]
        grads_in[h, HEAD_DIM : HEAD_DIM + 16, :] = rows16(split3(-inner))
        grads_in[h, HEAD_DIM + 16 :, :] = jnp.zeros((DEPTH - HEAD_DIM - 16, TILE_Q), bf16)
        query_sum[h][...] = jnp.zeros((HEAD_DIM, TILE_Q), f32)

    def block(tiles, carry):
        spans = [pl.ds(pl.multiple_of(j * TILE_K, TILE_K), TILE_K) for j in tiles]
        units = [(span, h) for span in spans for h in range(heads)]
        waiting = {}
        for t in range(len(units) + BWD_SKEW):
            if t < len(units):
                span, h = units[t]
                waiting[t] = (
                    dot(keys_in[h, span, :], queries_in[h], NN),
                    dot(values_in[h, span, :], grads_in[h], NN),
                )
            if t < BWD_SKEW:
                continue
            span, h = units[t - BWD_SKEW]
            band = slice(h * HEAD_DIM, (h + 1) * HEAD_DIM)
            scores, weight_grad = waiting.pop(t - BWD_SKEW)
            softmax = jnp.exp2(scores)
            score_grad = (softmax * weight_grad).astype(bf16)
            value_sum[h][:, span] += dot(grads[band, :], softmax.astype(bf16), NT)
            key_sum[h][:, span] += dot(queries[band, :], score_grad, NT)
            query_sum[h][...] += dot(keys[band, span], score_grad, NN)
        return carry

    tile_loop(low[step], high[step], block, 0)

    def store(offset, columns, value):
        half = HEAD_DIM // 2
        upper, lower = value[:half], value[half:]
        cos, sin = cosine[:, columns], sine[:, columns]
        joined_back[offset : offset + half, columns] = (upper * cos + lower * sin).astype(bf16)
        joined_back[offset + half : offset + HEAD_DIM, columns] = (lower * cos - upper * sin).astype(bf16)

    width = heads * HEAD_DIM
    columns = pl.ds(pl.multiple_of(step * TILE_Q, TILE_Q), TILE_Q)
    for h in range(heads):
        store(h * HEAD_DIM, columns, query_sum[h][...] * 0.125)

    @pl.when(step == pl.num_programs(0) - 1)
    def _():
        for h in range(heads):
            first = width + h * HEAD_DIM
            store(first, slice(0, rows), key_sum[h][...] * (1.0 / LOG2E))
            first += width
            joined_back[first : first + HEAD_DIM, :] = value_sum[h][...].astype(bf16)


def attention_backward(
    low, high, queries, keys, values, grads, outs, logsum, key_rows, query_rows, cosine, sine
):
    width, rows = queries.shape
    heads = width // HEAD_DIM

    def full(count):
        return pl.BlockSpec((count, rows), lambda i, low, high: (0, 0))

    def tile(count):
        return pl.BlockSpec((count, TILE_Q), lambda i, low, high: (0, i))

    return pl.pallas_call(
        backward_kernel,
        out_shape=jax.ShapeDtypeStruct((3 * width, rows), bf16),
        grid_spec=pltpu.PrefetchScalarGridSpec(
            num_scalar_prefetch=2,
            grid=(rows // TILE_Q,),
            in_specs=[
                tile(width), full(width), full(width), tile(width), tile(width), tile(heads),
                full(16), tile(16), full(HEAD_DIM // 2), full(HEAD_DIM // 2),
            ],
            out_specs=full(3 * width),
            scratch_shapes=[
                pltpu.VMEM((heads, rows, DEPTH), bf16),
                pltpu.VMEM((heads, rows, DEPTH), bf16),
                pltpu.VMEM((heads, DEPTH, TILE_Q), bf16),
                pltpu.VMEM((heads, DEPTH, TILE_Q), bf16),
            ]
            + [pltpu.VMEM((HEAD_DIM, rows), f32)] * (2 * heads)
            + [pltpu.VMEM((HEAD_DIM, TILE_Q), f32)] * heads,
        ),
        compiler_params=pltpu.CompilerParams(
            dimension_semantics=("arbitrary",), vmem_limit_bytes=52 << 20
        ),
        name="attention_backward",
    )(low, high, queries, keys, values, grads, outs, logsum, key_rows, query_rows, cosine, sine)


def layer_norm(values, gain_row):
    centred = values - jnp.mean(values, axis=-1, keepdims=True)
    inverse = lax.rsqrt(jnp.mean(centred * centred, axis=-1, keepdims=True) + norm_epsilon)
    normal = centred * inverse
    return normal * gain_row, normal, inverse


def norm_back(upstream, gain_row, normal, inverse):
    scaled = upstream * gain_row
    inner_mean = jnp.mean(scaled * normal, axis=-1, keepdims=True)
    return inverse * (scaled - jnp.mean(scaled, axis=-1, keepdims=True) - normal * inner_mean)


def horner(square, factors):
    total = factors[0] * square + factors[1]
    for factor in factors[2:]:
        total = total * square + factor
    return total


def error_function(value):
    value = jnp.clip(value, -4.0, 4.0)
    square = value * value
    return value * horner(square, ERF_TOP) / horner(square, ERF_BOTTOM)


def turn(value):
    columns = value.shape[1]
    rest = jnp.zeros((value.shape[0], -columns % 128), value.dtype)
    return jnp.concatenate([value, rest], axis=1).T[:columns, :]


def turn_back(value):
    lines = value.shape[0]
    rest = jnp.zeros((-lines % 128, value.shape[1]), value.dtype)
    return jnp.concatenate([value, rest], axis=0).T[:, :lines]


def first_kernel(head, own, other, gain, rows, normed):
    tiles = pl.num_programs(0) // 2
    mine = pl.program_id(0) // tiles == head[0]
    value = jnp.where(mine, own[...].astype(f32), other[...].astype(f32))
    rows[...] = value.astype(bf16)
    normed[...] = layer_norm(value, gain[...])[0].astype(bf16)


def first_norm(head, own, other, gain):
    half, width = own.shape
    tiles = half // FEED_ROWS
    result = jax.ShapeDtypeStruct((2 * half, width), bf16)
    spec = pl.BlockSpec((FEED_ROWS, width), lambda i, head: (i, 0))
    return pl.pallas_call(
        first_kernel,
        out_shape=(result, result),
        grid_spec=pltpu.PrefetchScalarGridSpec(
            num_scalar_prefetch=1,
            grid=(2 * tiles,),
            in_specs=[
                pl.BlockSpec(
                    (FEED_ROWS, width),
                    lambda i, head: (jnp.clip(i - head[0] * tiles, 0, tiles - 1), 0),
                ),
                pl.BlockSpec(
                    (FEED_ROWS, width),
                    lambda i, head: (jnp.clip(i - (1 - head[0]) * tiles, 0, tiles - 1), 0),
                ),
                pl.BlockSpec((1, width), lambda i, head: (0, 0)),
            ],
            out_specs=[spec, spec],
        ),
        compiler_params=pltpu.CompilerParams(dimension_semantics=("arbitrary",)),
        name="first_norm",
    )(head, own, other, gain)


def gradient_kernel(back, normed, *refs):
    grads, total = refs[:-1], refs[-1]
    step = pl.program_id(0)

    @pl.when(step == 0)
    def _():
        total[...] = dot(back[...], normed[...], NN)

    @pl.when(step > 0)
    def _():
        total[...] += dot(back[...], normed[...], NN)

    @pl.when(step == pl.num_programs(0) - 1)
    def _():
        first = 0
        for grad in grads:
            grad[...] = total[:, first : first + grad.shape[1]].astype(bf16)
            first += grad.shape[1]


def joined_gradient(back, normed):
    lines, count = back.shape
    width = normed.shape[1]
    tile = 2 * FEED_ROWS
    half = width // 256 * 128
    parts = [half, width - half]
    return pl.pallas_call(
        gradient_kernel,
        grid=(count // tile,),
        in_specs=[
            pl.BlockSpec((lines, tile), lambda i: (0, i)),
            pl.BlockSpec((tile, width), lambda i: (i, 0)),
        ],
        out_specs=[pl.BlockSpec((lines, part), lambda i: (0, 0)) for part in parts],
        out_shape=[jax.ShapeDtypeStruct((lines, part), bf16) for part in parts],
        scratch_shapes=[pltpu.VMEM((lines, width), f32)],
        compiler_params=pltpu.CompilerParams(
            dimension_semantics=("arbitrary",), vmem_limit_bytes=32 << 20
        ),
        name="joined_gradient",
    )(back, normed)


def pull_kernel(head, back, weight, out):
    out[...] = dot(back[...].T, weight[...], NN).astype(bf16)


def pull_other(head, back, weight):
    lines, count = back.shape
    width = weight.shape[1]
    tiles = count // 2 // FEED_ROWS
    return pl.pallas_call(
        pull_kernel,
        out_shape=jax.ShapeDtypeStruct((count // 2, width), bf16),
        grid_spec=pltpu.PrefetchScalarGridSpec(
            num_scalar_prefetch=1,
            grid=(tiles,),
            in_specs=[
                pl.BlockSpec((lines, FEED_ROWS), lambda i, head: (0, (1 - head[0]) * tiles + i)),
                pl.BlockSpec((lines, width), lambda i, head: (0, 0)),
            ],
            out_specs=pl.BlockSpec((FEED_ROWS, width), lambda i, head: (i, 0)),
        ),
        compiler_params=pltpu.CompilerParams(
            dimension_semantics=("arbitrary",), vmem_limit_bytes=24 << 20
        ),
        name="pull_other",
    )(head, back, weight)


def input_kernel(head, back, weight, other, rows, middle_grad, gain, input_grad, gain_grad):
    @pl.when(pl.program_id(0) == 0)
    def _():
        gain_grad[...] = jnp.zeros(gain_grad.shape, f32)

    pulled = dot(back[...].T, weight[...], NN) + other[...].astype(f32)
    unused, normal, inverse = layer_norm(rows[...].astype(f32), gain[...])
    input_grad[...] = middle_grad[...] + norm_back(pulled, gain[...], normal, inverse)
    gain_grad[...] += jnp.sum(pulled * normal, axis=0, keepdims=True)


def input_backward(head, back, weight, other, rows, middle_grad, gain):
    lines, count = back.shape
    width = weight.shape[1]
    tiles = count // 2 // FEED_ROWS

    def down():
        return pl.BlockSpec((FEED_ROWS, width), lambda i, head: (i, 0))

    return pl.pallas_call(
        input_kernel,
        out_shape=(
            jax.ShapeDtypeStruct((count // 2, width), f32),
            jax.ShapeDtypeStruct((1, width), f32),
        ),
        grid_spec=pltpu.PrefetchScalarGridSpec(
            num_scalar_prefetch=1,
            grid=(tiles,),
            in_specs=[
                pl.BlockSpec((lines, FEED_ROWS), lambda i, head: (0, head[0] * tiles + i)),
                pl.BlockSpec((lines, width), lambda i, head: (0, 0)),
                down(),
                down(),
                pl.BlockSpec((FEED_ROWS, width), lambda i, head: (head[0] * tiles + i, 0)),
                pl.BlockSpec((1, width), lambda i, head: (0, 0)),
            ],
            out_specs=[down(), pl.BlockSpec((1, width), lambda i, head: (0, 0))],
        ),
        compiler_params=pltpu.CompilerParams(
            dimension_semantics=("arbitrary",), vmem_limit_bytes=24 << 20
        ),
        name="input_backward",
    )(head, back, weight, other, rows, middle_grad, gain)


def feed_kernel(
    rows, attended, attended_other, upstream, gain, both, mixer_other, expand_left, expand_right,
    middle, hidden, second_part, shrink_grad, left_grad, right_grad, shrink,
    shrink_sum, expand_sum, expand
):
    step = pl.program_id(0)
    mixed, units = attended.shape[0], shrink.shape[0]
    chunk = units // FEED_CHUNKS

    @pl.when(step == 0)
    def _():
        expand[:, : expand_left.shape[1]] = expand_left[...]
        expand[:, expand_left.shape[1] :] = expand_right[...]
        shrink[...] = turn(both[:, mixed:])
        shrink_sum[...] = jnp.zeros(shrink_sum.shape, f32)
        expand_sum[...] = jnp.zeros(expand_sum.shape, f32)

    total = rows[...].astype(f32) + dot(attended[...].T, both[:, :mixed], NT)
    total = total + dot(attended_other[...].T, mixer_other[...], NT)
    middle[...] = total
    normed = layer_norm(total, gain[...])[0].astype(bf16)
    above = upstream[...]

    def project(c):
        first = slice(c * chunk, (c + 1) * chunk)
        second = slice(units + c * chunk, units + (c + 1) * chunk)
        return (
            dot(expand[first, :], normed, NT),
            dot(expand[second, :], normed, NT),
            dot(shrink[first, :], above, NT),
        )

    waiting = project(0)
    back = jnp.zeros(total.shape, f32)
    for c in range(FEED_CHUNKS):
        active, linear, grad = waiting
        if c + 1 < FEED_CHUNKS:
            waiting = project(c + 1)
        first = slice(c * chunk, (c + 1) * chunk)
        second = slice(units + c * chunk, units + (c + 1) * chunk)
        area = 0.5 * error_function(active * math.sqrt(0.5)) + 0.5
        gate = active * area
        density = jnp.exp(-0.5 * active * active) * (1.0 / math.sqrt(2.0 * math.pi))
        unit = (gate * linear).astype(bf16)
        active_back = (grad * linear * (area + active * density)).astype(bf16)
        linear_back = (grad * gate).astype(bf16)
        hidden[first, :] = unit
        shrink_sum[first, :] += dot(unit, above, NN)
        expand_sum[first, :] += dot(active_back, normed, NN)
        expand_sum[second, :] += dot(linear_back, normed, NN)
        back = back + dot(active_back, expand[first, :], TN) + dot(linear_back, expand[second, :], TN)
    second_part[...] = back.astype(bf16)

    @pl.when(step == pl.num_programs(0) - 1)
    def _():
        shrink_grad[...] = shrink_sum[...].astype(bf16)
        cut = left_grad.shape[1]
        left_grad[...] = expand_sum[:, :cut].astype(bf16)
        right_grad[...] = expand_sum[:, cut:].astype(bf16)


def feed_forward(rows, attended, attended_other, upstream, gain, both, mixer_other, expand):
    count, width = rows.shape
    mixed, units = attended.shape[0], expand[0].shape[0] // 2

    def full(*shape):
        return pl.BlockSpec(shape, lambda i: (0, 0))

    def down(columns):
        return pl.BlockSpec((FEED_TILE, columns), lambda i: (i, 0))

    def along(lines):
        return pl.BlockSpec((lines, FEED_TILE), lambda i: (0, i))

    return pl.pallas_call(
        feed_kernel,
        grid=(count // FEED_TILE,),
        in_specs=[
            down(width), along(mixed), along(mixed), down(width), full(1, width),
            full(*both.shape), full(width, mixed), full(*expand[0].shape), full(*expand[1].shape),
        ],
        out_specs=[
            down(width), along(units), down(width), full(units, width),
            full(*expand[0].shape), full(*expand[1].shape), full(units, width),
        ],
        out_shape=(
            jax.ShapeDtypeStruct((count, width), f32),
            jax.ShapeDtypeStruct((units, count), bf16),
            jax.ShapeDtypeStruct((count, width), bf16),
            jax.ShapeDtypeStruct((units, width), bf16),
            jax.ShapeDtypeStruct(expand[0].shape, bf16),
            jax.ShapeDtypeStruct(expand[1].shape, bf16),
            jax.ShapeDtypeStruct((units, width), bf16),
        ),
        scratch_shapes=[
            pltpu.VMEM((units, width), f32),
            pltpu.VMEM((2 * units, width), f32),
            pltpu.VMEM((2 * units, width), bf16),
        ],
        compiler_params=pltpu.CompilerParams(
            dimension_semantics=("arbitrary",), vmem_limit_bytes=48 << 20
        ),
        name="feed_forward",
    )(rows, attended, attended_other, upstream, gain, both, mixer_other, *expand)


def norm_kernel(
    middle, own, other, upstream, gain, both, attended, shrink_grad,
    middle_grad, attended_grad, both_grad, gain_grad, mixer_turned, mixer_sum
):
    step = pl.program_id(0)

    @pl.when(step == 0)
    def _():
        mixer_turned[...] = both[:, : attended.shape[0]].T
        mixer_sum[...] = jnp.zeros(mixer_sum.shape, f32)
        gain_grad[...] = jnp.zeros(gain_grad.shape, f32)

    unused, normal, inverse = layer_norm(middle[...], gain[...])
    back = own[...].astype(f32) + other[...].astype(f32)
    grad = upstream[...].astype(f32) + norm_back(back, gain[...], normal, inverse)
    middle_grad[...] = grad
    grad_low = grad.astype(bf16)
    attended_grad[...] = dot(mixer_turned[...], grad_low, NT).astype(bf16)
    mixer_sum[...] += dot(attended[...], grad_low, NN)
    gain_grad[...] += jnp.sum(back * normal, axis=0, keepdims=True)

    @pl.when(step == pl.num_programs(0) - 1)
    def _():
        mixed = attended.shape[0]
        both_grad[:, :mixed] = mixer_sum[...].T.astype(bf16)
        both_grad[:, mixed:] = turn_back(shrink_grad[...])


def norm_backward(middle, own, other, upstream, gain, both, attended, shrink_grad):
    count, width = middle.shape
    mixed = attended.shape[0]

    def full(*shape):
        return pl.BlockSpec(shape, lambda i: (0, 0))

    def down(columns):
        return pl.BlockSpec((FEED_TILE, columns), lambda i: (i, 0))

    def along(lines):
        return pl.BlockSpec((lines, FEED_TILE), lambda i: (0, i))

    return pl.pallas_call(
        norm_kernel,
        grid=(count // FEED_TILE,),
        in_specs=[
            down(width), down(width), down(width), down(width), full(1, width),
            full(*both.shape), along(mixed), full(*shrink_grad.shape),
        ],
        out_specs=[down(width), along(mixed), full(*both.shape), full(1, width)],
        out_shape=(
            jax.ShapeDtypeStruct((count, width), f32),
            jax.ShapeDtypeStruct((mixed, count), bf16),
            jax.ShapeDtypeStruct(both.shape, bf16),
            jax.ShapeDtypeStruct((1, width), f32),
        ),
        scratch_shapes=[pltpu.VMEM((mixed, width), bf16), pltpu.VMEM((mixed, width), f32)],
        compiler_params=pltpu.CompilerParams(
            dimension_semantics=("arbitrary",), vmem_limit_bytes=40 << 20
        ),
        name="norm_backward",
    )(middle, own, other, upstream, gain, both, attended, shrink_grad)


def swap(value, axis, bit):
    count = lax.axis_size(axis)
    return lax.ppermute(value, axis, [(i, i ^ bit) for i in range(count)])


def bit_order(lead):
    bits = lax.axis_size("dp").bit_length() - 1
    return [int(bit) for bit in lead] + list(range(len(lead), bits))


def steps_count():
    return lax.axis_size("dp").bit_length() - 1


def cut(held, bit):
    axis = steps_count() - 1 - bit
    side = (lax.axis_index("dp") >> bit) & 1
    kept = lax.dynamic_slice_in_dim(held, side, 1, axis)
    return kept, lax.dynamic_slice_in_dim(held, 1 - side, 1, axis)


def reduce_start(value, lead):
    bits = steps_count()
    rows = value.shape[0] >> bits
    return cut(value.reshape((2,) * bits + (rows, value.shape[1])), bit_order(lead)[0])


def reduce_step(held, step, lead):
    bits = steps_count()
    kept, sent = held if step == 0 else cut(held, bit_order(lead)[step])
    total = kept.astype(f32) + swap(sent, "dp", 1 << bit_order(lead)[step]).astype(f32)
    if step + 1 == bits:
        return total.reshape(kept.shape[-2:])
    return total.astype(bf16)


def gather_start(value):
    return value[(None,) * steps_count()]


def gather_step(held, step, lead):
    bits = steps_count()
    bit = bit_order(lead)[bits - 1 - step]
    return jnp.concatenate([held, swap(held, "dp", 1 << bit)], axis=bits - 1 - bit)


def ordered_step(held, step, lead):
    bits = steps_count()
    bit = bit_order(lead)[bits - 1 - step]
    got = swap(held, "dp", 1 << bit)
    low_side = ((lax.axis_index("dp") >> bit) & 1) == 0
    return jnp.concatenate(
        [jnp.where(low_side, held, got), jnp.where(low_side, got, held)], axis=bits - 1 - bit
    )


def gather_rows(held):
    return held.reshape(-1, held.shape[-1])


def halves_of(value):
    unit = value.shape[1] // 256 * 128
    return [value[:, :unit], value[:, unit:]]


def quarter(step, states, part, leads):
    bits = steps_count()
    for index in range(bits * part // QUARTERS, bits * (part + 1) // QUARTERS):
        states = [step(state, index, lead) for state, lead in zip(states, leads)]
    return states


def tie(*values):
    return lax.optimization_barrier(values)


def total_step(value, part):
    if part == 0:
        return value + swap(value, "head", 1)
    bits = steps_count()
    for bit in range(bits * (part - 1) // QUARTERS, bits * part // QUARTERS):
        value = value + swap(value, "dp", 1 << bit)
    return value


def schulz_start(held, own, gram, low):
    down = 0
    for left in held:
        along = 0
        for right in held:
            gram[down : down + left.shape[1], along : along + right.shape[1]] = dot(left, right, TN)
            along += right.shape[1]
        down += left.shape[1]
    shape = gram.shape
    diagonal = lax.broadcasted_iota(jnp.int32, shape, 0) == lax.broadcasted_iota(jnp.int32, shape, 1)
    trace = jnp.sum(jnp.where(diagonal, gram[...], 0.0), axis=0, keepdims=True)
    norm_value = jnp.sqrt(jnp.sum(trace, axis=1, keepdims=True)) + 1e-07
    gram[...] = gram[...] * (1.0 / (norm_value * norm_value))
    low[...] = gram[...].astype(bf16)
    return own[...] / norm_value


def schulz_steps(rows, gram, low, change, first, stop):
    columns = gram.shape[0]
    lines = 256 if columns % 256 == 0 else columns

    def per_block(body):
        def run(index, carry):
            body(pl.ds(pl.multiple_of(index * lines, lines), lines))
            return carry

        lax.fori_loop(0, columns // lines, run, 0, unroll=True)

    def form_change(block):
        squared = dot(low[block, :], low[...], NN)
        change[block, :] = (ns_second * gram[block, :] + ns_third * squared).astype(bf16)

    def next_gram(block):
        once = ns_first * gram[block, :] + dot(low[block, :], change[...], NN)
        twice = ns_first * once + dot(once.astype(bf16), change[...], NN)
        gram[block, :] = twice
        low[block, :] = twice.astype(bf16)

    for iteration in range(first, stop):
        per_block(form_change)
        rows = ns_first * rows + dot(rows.astype(bf16), change[...], NN)
        if iteration + 1 < NS_ITERS:
            per_block(next_gram)
    return rows


def whole_kernel(*refs, count, offset, scale):
    parts = refs[:count]
    own, weight, updated, gram, low, change = refs[count:]
    if offset is None:
        held = [part[...] for part in parts]
    else:
        held = [parts[0][:, offset : offset + gram.shape[0]]]
    rows = schulz_start(held, own, gram, low)
    updated[...] = weight[...] - scale * schulz_steps(rows, gram, low, change, 0, NS_ITERS)


def square_scratch(columns):
    return [
        pltpu.VMEM((columns, columns), f32),
        pltpu.VMEM((columns, columns), bf16),
        pltpu.VMEM((columns, columns), bf16),
    ]


def shape_scale(rows, columns):
    return muon_rate * math.sqrt(rows / columns)


def schulz(parts, offset, own, weight, name):
    columns = own.shape[1]
    return pl.pallas_call(
        functools.partial(
            whole_kernel, count=len(parts), offset=offset, scale=shape_scale(parts[0].shape[0], columns)
        ),
        out_shape=jax.ShapeDtypeStruct(own.shape, f32),
        scratch_shapes=square_scratch(columns),
        compiler_params=pltpu.CompilerParams(vmem_limit_bytes=40 << 20),
        name=name,
    )(*parts, own, weight)


def shards(
    tokens,
    lengths,
    norm_gains,
    joined_weight,
    mixer_weight,
    expand_weight,
    shrink_weight,
    joined_momentum,
    mixer_momentum,
    expand_momentum,
    shrink_momentum,
    gain_momentum,
    cotangent,
):
    row_count = cotangent.shape[0]
    local_rows = tokens.shape[0]
    head = lax.axis_index("head")
    mixer_width = mixer_weight.shape[2]

    def own_half(value):
        return lax.dynamic_slice_in_dim(value, head * local_rows, local_rows, 0)

    joined_parts = [gather_start(part) for part in halves_of(joined_weight[0].astype(bf16))]
    joined_parts = quarter(ordered_step, joined_parts, 0, JOINED_FIRST)
    others = [gather_start(part) for part in halves_of(expand_weight[0].astype(bf16))] + [
        gather_start(jnp.concatenate([mixer_weight[0], shrink_weight[0]], axis=1).astype(bf16))
    ]
    key_rows, query_rows, cosine, sine = doc_tables(lengths[0], row_count)
    low, high = key_bounds(lengths[0], row_count)
    head_place = head[None]
    tokens_other = swap(tokens, "head", 1)

    joined_parts, others, tokens_other = tie(joined_parts, others, tokens_other)
    joined_parts = quarter(ordered_step, joined_parts, 1, JOINED_FIRST)
    others = quarter(ordered_step, others, 0, OTHERS_FIRST)
    rows_low, first_low = first_norm(head_place, tokens, tokens_other, norm_gains[0:1])
    joined_parts, others, first_low = tie(joined_parts, others, first_low)
    joined_parts = quarter(ordered_step, joined_parts, 2, JOINED_FIRST)
    others = quarter(ordered_step, others, 1, OTHERS_FIRST)
    joined_parts, others = tie(joined_parts, others)
    joined_parts = quarter(ordered_step, joined_parts, 3, JOINED_FIRST)
    moved = quarter(ordered_step, others, 2, OTHERS_FIRST)

    joined_low = jnp.concatenate([gather_rows(part) for part in joined_parts], axis=1)
    joined = dot(joined_low, first_low, NT)
    width = joined.shape[0] // 3
    queries = (rotate(joined[:width], cosine, sine) * QUERY_SCALE).astype(bf16)
    keys = rotate(joined[width : 2 * width], cosine, sine).astype(bf16)
    values = joined[2 * width :].astype(bf16)
    others, queries, keys, values, low = tie(moved, queries, keys, values, low)
    moved = quarter(ordered_step, others, 3, OTHERS_FIRST)
    attended, logsum = attention_forward(low, high, queries, keys, values, key_rows, query_rows)
    others, attended, logsum = tie(moved, attended, logsum)
    attended_other = swap(attended, "head", 1)
    both_low = gather_rows(others[2])
    mixer_other = swap(both_low[:, :mixer_width], "head", 1)

    second_gain = norm_gains[1:2]
    middle, hidden, second_part, shrink_grad, left_grad, right_grad, shrink_turned = feed_forward(
        rows_low, attended, attended_other, cotangent, second_gain,
        both_low, mixer_other, [gather_rows(part) for part in others[:2]],
    )
    second_other = swap(second_part, "head", 1)

    sums = [reduce_start(part, lead) for part, lead in zip((left_grad, right_grad), PAIR)]
    sums, second_other = tie(sums, second_other)
    moved = quarter(reduce_step, sums, 0, PAIR)
    middle_grad, attended_grad, both_grad, second_gain_grad = norm_backward(
        middle, second_part, second_other, cotangent, second_gain, both_low, attended, shrink_grad
    )
    both_sum = [reduce_start(both_grad, ONE[0])]

    sums, attended_grad, shrink_now = tie(moved, attended_grad, shrink_turned)
    moved = quarter(reduce_step, sums, 1, PAIR)

    def fed(columns):
        units = lax.dynamic_slice_in_dim(hidden, columns, local_rows, 1)
        return dot(units, shrink_now, TN)

    fed_other = fed((1 - head) * local_rows).astype(bf16)
    fed_own = fed(head * local_rows)

    sums, both_sum, fed_other, fed_own, low = tie(moved, both_sum, fed_other, fed_own, low)
    moved = quarter(reduce_step, sums, 2, PAIR)
    both_moved = quarter(reduce_step, both_sum, 0, ONE)
    fed_other = swap(fed_other, "head", 1)
    joined_back = attention_backward(
        low, high, queries, keys, values, attended_grad, attended, logsum, key_rows, query_rows,
        cosine, sine,
    )
    sums, both_sum, joined_back, fed_other = tie(moved, both_moved, joined_back, fed_other)
    moved = quarter(reduce_step, sums, 3, PAIR)
    both_moved = quarter(reduce_step, both_sum, 1, ONE)
    joined_grad = joined_gradient(joined_back, first_low)

    sums, both_sum, joined_grad, joined_now = tie(moved, both_moved, joined_grad, joined_low)
    expand_next = 0.5 * expand_momentum[0] + jnp.concatenate(sums, axis=1)
    gathers = [gather_start(part) for part in halves_of(expand_next.astype(bf16))]
    sums = [reduce_start(part, lead) for part, lead in zip(joined_grad, PAIR)]
    sums = quarter(reduce_step, sums, 0, PAIR)
    moved = quarter(gather_step, gathers, 0, PAIR)
    both_moved = quarter(reduce_step, both_sum, 2, ONE)
    first_other = pull_other(head_place, joined_back, joined_now)

    sums, gathers, both_sum, first_other, fed_own = tie(sums, moved, both_moved, first_other, fed_own)
    first_other = swap(first_other, "head", 1)
    moved = quarter(reduce_step, sums, 1, PAIR)
    gathers_moved = quarter(gather_step, gathers, 1, PAIR)
    both_moved = quarter(reduce_step, both_sum, 3, ONE)

    sums, gathers, both_sum, first_other, fed_own = tie(
        moved, gathers_moved, both_moved, first_other, fed_own
    )
    mixer_next = 0.5 * mixer_momentum[0] + both_sum[0][:, :mixer_width]
    shrink_next = 0.5 * shrink_momentum[0] + both_sum[0][:, mixer_width:]
    both_gather = [gather_start(jnp.concatenate([mixer_next, shrink_next], axis=1).astype(bf16))]
    moved = quarter(reduce_step, sums, 2, PAIR)
    gathers_moved = quarter(gather_step, gathers, 2, PAIR)
    both_moved = quarter(gather_step, both_gather, 0, ONE)
    layer_output = (own_half(middle) + fed_own + fed_other.astype(f32)).astype(bf16)

    sums, gathers, both_gather, first_other, layer_output = tie(
        moved, gathers_moved, both_moved, first_other, layer_output
    )
    moved = quarter(reduce_step, sums, 3, PAIR)
    gathers_moved = quarter(gather_step, gathers, 3, PAIR)
    both_moved = quarter(gather_step, both_gather, 1, ONE)
    input_gradient, first_gain_grad = input_backward(
        head_place, joined_back, joined_now, first_other, tokens, middle_grad, norm_gains[0:1]
    )
    gain_totals = jnp.concatenate([first_gain_grad, 0.5 * second_gain_grad], axis=0)

    sums, gathers, both_gather, gain_totals = tie(moved, gathers_moved, both_moved, gain_totals)
    joined_next = 0.5 * joined_momentum[0] + jnp.concatenate(sums, axis=1)
    joined_gather = [gather_start(part) for part in halves_of(joined_next.astype(bf16))]
    moved = quarter(gather_step, joined_gather, 0, PAIR)
    both_moved = quarter(gather_step, both_gather, 2, ONE)
    gain_moved = total_step(gain_totals, 0)
    joined_gather, both_gather, gain_totals, gathers = tie(moved, both_moved, gain_moved, gathers)
    moved = quarter(gather_step, joined_gather, 1, PAIR)
    both_moved = quarter(gather_step, both_gather, 3, ONE)
    gain_moved = total_step(gain_totals, 1)
    updated_expand = schulz(
        [gather_rows(part) for part in gathers], None, expand_next, expand_weight[0], "schulz_expand"
    )
    joined_gather, both_gather, gain_totals, updated_expand = tie(
        moved, both_moved, gain_moved, updated_expand
    )
    both_full = [gather_rows(both_gather[0])]
    moved = quarter(gather_step, joined_gather, 2, PAIR)
    gain_moved = total_step(gain_totals, 2)
    updated_shrink = schulz(
        both_full, mixer_width, shrink_next, shrink_weight[0], "schulz_shrink"
    )
    joined_gather, both_full, gain_totals, updated_shrink = tie(
        moved, both_full, gain_moved, updated_shrink
    )
    moved = quarter(gather_step, joined_gather, 3, PAIR)
    gain_moved = total_step(gain_totals, 3)
    updated_mixer = schulz(both_full, 0, mixer_next, mixer_weight[0], "schulz_mixer")
    joined_gather, gain_totals, updated_mixer = tie(moved, gain_moved, updated_mixer)
    gain_totals = total_step(gain_totals, 4)
    updated_joined = schulz(
        [gather_rows(part) for part in joined_gather],
        None, joined_next, joined_weight[0], "schulz_joined",
    )

    momentum_gains = 0.5 * gain_momentum + gain_totals
    updated_gains = norm_gains - gain_rate * momentum_gains * lax.rsqrt(
        jnp.mean(momentum_gains * momentum_gains, axis=-1, keepdims=True) + 1e-06
    )
    return (
        layer_output,
        input_gradient,
        joined_next[None],
        mixer_next[None],
        expand_next[None],
        shrink_next[None],
        updated_joined[None],
        updated_mixer[None],
        updated_expand[None],
        updated_shrink[None],
        momentum_gains,
        updated_gains,
    )


def solution(mesh):
    rows = P(("dp", "head"), None)
    weight = P("head", "dp", None)
    return jax.shard_map(
        shards,
        mesh=mesh,
        in_specs=(rows, P("dp", None), P()) + (weight,) * 8 + (P(), P("dp", None)),
        out_specs=(rows, rows) + (weight,) * 8 + (P(), P()),
        check_vma=False,
    )
```

```python
import functools
import math

import jax
import jax.numpy as jnp
from jax import lax
from jax.experimental import pallas as pl
from jax.experimental.pallas import tpu as pltpu
from jax.sharding import PartitionSpec as P

HEAD_DIM = 64
NS_ITERS = 3

theta_base = 160000.0
norm_epsilon = 1e-05
ns_first = 3.4445
ns_second = -4.775
ns_third = 2.0315
muon_rate = 1.0
gain_rate = 0.3

bf16 = jnp.bfloat16
f32 = jnp.float32
LOG2E = math.log2(math.e)
QUERY_SCALE = 0.125 * LOG2E
SAFE_SCORE = 60.0
DEPTH = 128
TILE_Q = 256
TILE_K = 256
FWD_SKEW = 6
BWD_SKEW = 2

NN = (((1,), (0,)), ((), ()))
NT = (((1,), (1,)), ((), ()))
TN = (((0,), (0,)), ((), ()))
TT = (((0,), (1,)), ((), ()))
QUARTERS = 4
PAIR = ("012", "102")
JOINED_FIRST = ("012", "120")
OTHERS_FIRST = ("021", "201", "120")
ONE = ("012",)
FEED_ROWS = 512
FEED_TILE = 512
FEED_CHUNKS = 1
ERF_TOP = (
    -2.72614225801306e-10, 2.77068142495902e-08, -2.10102402082508e-06, -5.69250639462346e-05,
    -7.34990630326855e-04, -2.95459980854025e-03, -1.60960333262415e-02,
)
ERF_BOTTOM = (
    -1.45660718464996e-05, -2.13374055278905e-04, -1.68282697438203e-03, -7.37332916720468e-03,
    -1.42647390514189e-02,
)


def dot(left, right, dims):
    return lax.dot_general(left, right, dims, preferred_element_type=f32)


def key_bounds(length_row, row_count):
    ends = jnp.cumsum(length_row)
    starts = ends - length_row
    first = jnp.arange(row_count // TILE_Q, dtype=jnp.int32) * TILE_Q
    labels = jnp.arange(length_row.shape[0], dtype=jnp.int32)

    def pick(places, table):
        segment = jnp.sum((places[:, None] >= ends[None, :]).astype(jnp.int32), axis=1)
        return jnp.sum(jnp.where(segment[:, None] == labels[None, :], table[None, :], 0), axis=1)

    low = pick(first, starts) // TILE_K
    high = (pick(first + TILE_Q - 1, ends) + TILE_K - 1) // TILE_K
    return low.astype(jnp.int32), high.astype(jnp.int32)


def doc_tables(length_row, row_count):
    ends = jnp.cumsum(length_row)
    starts = ends - length_row
    count = length_row.shape[0]
    places = jnp.arange(row_count, dtype=jnp.int32)[None, :]
    member = (places >= starts[:, None]) & (places < ends[:, None])
    rest = jnp.zeros((16 - count, row_count), f32)
    key_rows = jnp.concatenate([member.astype(f32), rest], axis=0).astype(bf16)
    query_rows = jnp.concatenate([jnp.where(member, 0.0, -1e30), rest], axis=0).astype(bf16)
    doc_first = jnp.sum(jnp.where(member, starts[:, None], 0), axis=0, keepdims=True)
    position = (places - doc_first).astype(f32)
    half_dim = HEAD_DIM // 2
    frequency = jnp.exp(
        jnp.arange(half_dim, dtype=f32) * (-2.0 * math.log(theta_base) / HEAD_DIM)
    )
    angles = frequency[:, None] * position
    return key_rows, query_rows, jnp.cos(angles), jnp.sin(angles)


def rotate(values, cosine, sine):
    half = HEAD_DIM // 2
    heads = values.reshape(-1, HEAD_DIM, values.shape[1])
    low, high = heads[:, :half], heads[:, half:]
    turned = jnp.concatenate([low * cosine - high * sine, high * cosine + low * sine], axis=1)
    return turned.reshape(values.shape)


def rows16(parts):
    rest = jnp.zeros((16 - len(parts), parts[0].shape[1]), f32)
    return jnp.concatenate([part.astype(f32) for part in parts] + [rest], axis=0).astype(bf16)


def split3(value):
    first = value.astype(bf16)
    left = value - first.astype(f32)
    second = left.astype(bf16)
    third = (left - second.astype(f32)).astype(bf16)
    return [first, second, third]


def three_ones(count):
    return jnp.concatenate([jnp.ones((3, count), f32), jnp.zeros((13, count), f32)], axis=0).astype(
        bf16
    )


def tile_loop(low, high, block, carry):
    pairs = (high - low) // 2

    def two(index, carry):
        first = low + 2 * index
        return block([first, first + 1], carry)

    carry = lax.fori_loop(0, pairs, two, carry)
    return lax.fori_loop(low + 2 * pairs, high, lambda j, carry: block([j], carry), carry)


def forward_kernel(
    low, high, queries, keys, values, key_rows, query_rows, out, logsum, keys_in, values_in, queries_in, safe
):
    heads = queries.shape[0] // HEAD_DIM
    rows = keys.shape[1]
    step = pl.program_id(0)

    @pl.when(step == 0)
    def _():
        worst = jnp.zeros((1, 1), f32)
        ones = rows16([jnp.ones((1, rows), f32)])
        for h in range(heads):
            band = slice(h * HEAD_DIM, (h + 1) * HEAD_DIM)
            key = keys[band, :]
            pad = jnp.zeros((DEPTH - HEAD_DIM - 16, rows), bf16)
            keys_in[h] = jnp.concatenate([key, key_rows[...], pad], axis=0).T
            values_in[h, :HEAD_DIM, :] = values[band, :]
            values_in[h, HEAD_DIM:, :] = ones
            query_full = queries[band, :].astype(f32)
            key_full = key.astype(f32)
            query_top = jnp.max(
                jnp.sum(query_full * query_full, axis=0, keepdims=True), axis=1, keepdims=True
            )
            key_top = jnp.max(
                jnp.sum(key_full * key_full, axis=0, keepdims=True), axis=1, keepdims=True
            )
            worst = jnp.maximum(worst, query_top * key_top)
        safe[0] = jnp.where(worst[0, 0] <= SAFE_SCORE * SAFE_SCORE, 1, 0)

    first = pl.multiple_of(step * TILE_Q, TILE_Q)
    for h in range(heads):
        queries_in[h, :HEAD_DIM, :] = queries[h * HEAD_DIM : (h + 1) * HEAD_DIM, pl.ds(first, TILE_Q)]
        queries_in[h, HEAD_DIM : HEAD_DIM + 16, :] = query_rows[...]
        queries_in[h, HEAD_DIM + 16 :, :] = jnp.zeros((DEPTH - HEAD_DIM - 16, TILE_Q), bf16)

    def finish(peaks, totals):
        for h in range(heads):
            weight = totals[h][HEAD_DIM : HEAD_DIM + 1, :]
            out[h * HEAD_DIM : (h + 1) * HEAD_DIM, :] = (totals[h][:HEAD_DIM, :] / weight).astype(bf16)
            level = jnp.log2(weight)
            logsum[h : h + 1, :] = level if peaks is None else peaks[h] + level

    empty = tuple(jnp.zeros((HEAD_DIM + 16, TILE_Q), f32) for _ in range(heads))

    @pl.when(safe[0] == 1)
    def _():
        def block(tiles, totals):
            spans = [pl.ds(pl.multiple_of(j * TILE_K, TILE_K), TILE_K) for j in tiles]
            units = [(span, h) for span in spans for h in range(heads)]
            totals = list(totals)
            waiting = {}
            for t in range(len(units) + FWD_SKEW):
                if t < len(units):
                    span, h = units[t]
                    waiting[t] = dot(keys_in[h, span, :], queries_in[h], NN)
                if t >= FWD_SKEW:
                    span, h = units[t - FWD_SKEW]
                    raised = jnp.exp2(waiting.pop(t - FWD_SKEW)).astype(bf16)
                    totals[h] = totals[h] + dot(values_in[h, :, span], raised, NN)
            return tuple(totals)

        finish(None, tile_loop(low[step], high[step], block, empty))

    @pl.when(safe[0] == 0)
    def _():
        def block(j, carry):
            peaks, totals = carry
            span = pl.ds(pl.multiple_of(j * TILE_K, TILE_K), TILE_K)
            new_peaks = []
            new_totals = []
            for h in range(heads):
                scores = dot(keys_in[h, span, :], queries_in[h], NN)
                peak = jnp.maximum(peaks[h], jnp.max(scores, axis=0, keepdims=True))
                raised = jnp.exp2(scores - peak).astype(bf16)
                new_totals.append(
                    totals[h] * jnp.exp2(peaks[h] - peak) + dot(values_in[h, :, span], raised, NN)
                )
                new_peaks.append(peak)
            return tuple(new_peaks), tuple(new_totals)

        lowest = tuple(jnp.full((1, TILE_Q), -3e38, f32) for _ in range(heads))
        finish(*lax.fori_loop(low[step], high[step], block, (lowest, empty)))


def attention_forward(low, high, queries, keys, values, key_rows, query_rows):
    width, rows = queries.shape
    heads = width // HEAD_DIM

    def full(count):
        return pl.BlockSpec((count, rows), lambda i, low, high: (0, 0))

    def tile(count):
        return pl.BlockSpec((count, TILE_Q), lambda i, low, high: (0, i))

    return pl.pallas_call(
        forward_kernel,
        out_shape=(
            jax.ShapeDtypeStruct((width, rows), bf16),
            jax.ShapeDtypeStruct((heads, rows), f32),
        ),
        grid_spec=pltpu.PrefetchScalarGridSpec(
            num_scalar_prefetch=2,
            grid=(rows // TILE_Q,),
            in_specs=[full(width), full(width), full(width), full(16), tile(16)],
            out_specs=[tile(width), tile(heads)],
            scratch_shapes=[
                pltpu.VMEM((heads, rows, DEPTH), bf16),
                pltpu.VMEM((heads, HEAD_DIM + 16, rows), bf16),
                pltpu.VMEM((heads, DEPTH, TILE_Q), bf16),
                pltpu.SMEM((1,), jnp.int32),
            ],
        ),
        compiler_params=pltpu.CompilerParams(
            dimension_semantics=("arbitrary",), vmem_limit_bytes=40 << 20
        ),
        name="attention_forward",
    )(low, high, queries, keys, values, key_rows, query_rows)


def backward_kernel(
    low, high, queries, keys, values, grads, outs, logsum, key_rows, query_rows, cosine, sine,
    joined_back, *scratch
):
    heads = queries.shape[0] // HEAD_DIM
    rows = keys.shape[1]
    keys_in, values_in, queries_in, grads_in = scratch[:4]
    key_sum = scratch[4 : 4 + heads]
    value_sum = scratch[4 + heads : 4 + 2 * heads]
    query_sum = scratch[4 + 2 * heads : 4 + 3 * heads]
    step = pl.program_id(0)

    @pl.when(step == 0)
    def _():
        ones = three_ones(rows)
        for h in range(heads):
            band = slice(h * HEAD_DIM, (h + 1) * HEAD_DIM)
            pad = jnp.zeros((DEPTH - HEAD_DIM - 32, rows), bf16)
            keys_in[h] = jnp.concatenate([keys[band, :], key_rows[...], ones, pad], axis=0).T
            pad = jnp.zeros((DEPTH - HEAD_DIM - 16, rows), bf16)
            values_in[h] = jnp.concatenate([values[band, :], ones, pad], axis=0).T
            key_sum[h][...] = jnp.zeros((HEAD_DIM, rows), f32)
            value_sum[h][...] = jnp.zeros((HEAD_DIM, rows), f32)

    for h in range(heads):
        band = slice(h * HEAD_DIM, (h + 1) * HEAD_DIM)
        queries_in[h, :HEAD_DIM, :] = queries[band, :]
        queries_in[h, HEAD_DIM : HEAD_DIM + 16, :] = query_rows[...]
        queries_in[h, HEAD_DIM + 16 : HEAD_DIM + 32, :] = rows16(split3(-logsum[h : h + 1, :]))
        queries_in[h, HEAD_DIM + 32 :, :] = jnp.zeros((DEPTH - HEAD_DIM - 32, TILE_Q), bf16)
        inner = jnp.sum(grads[band, :].astype(f32) * outs[band, :].astype(f32), axis=0, keepdims=True)
        grads_in[h, :HEAD_DIM, :] = grads[band, :]
        grads_in[h, HEAD_DIM : HEAD_DIM + 16, :] = rows16(split3(-inner))
        grads_in[h, HEAD_DIM + 16 :, :] = jnp.zeros((DEPTH - HEAD_DIM - 16, TILE_Q), bf16)
        query_sum[h][...] = jnp.zeros((HEAD_DIM, TILE_Q), f32)

    def block(tiles, carry):
        spans = [pl.ds(pl.multiple_of(j * TILE_K, TILE_K), TILE_K) for j in tiles]
        units = [(span, h) for span in spans for h in range(heads)]
        waiting = {}
        for t in range(len(units) + BWD_SKEW):
            if t < len(units):
                span, h = units[t]
                waiting[t] = (
                    dot(keys_in[h, span, :], queries_in[h], NN),
                    dot(values_in[h, span, :], grads_in[h], NN),
                )
            if t < BWD_SKEW:
                continue
            span, h = units[t - BWD_SKEW]
            band = slice(h * HEAD_DIM, (h + 1) * HEAD_DIM)
            scores, weight_grad = waiting.pop(t - BWD_SKEW)
            softmax = jnp.exp2(scores)
            score_grad = (softmax * weight_grad).astype(bf16)
            value_sum[h][:, span] += dot(grads[band, :], softmax.astype(bf16), NT)
            key_sum[h][:, span] += dot(queries[band, :], score_grad, NT)
            query_sum[h][...] += dot(keys[band, span], score_grad, NN)
        return carry

    tile_loop(low[step], high[step], block, 0)

    def store(offset, columns, value):
        half = HEAD_DIM // 2
        upper, lower = value[:half], value[half:]
        cos, sin = cosine[:, columns], sine[:, columns]
        joined_back[offset : offset + half, columns] = (upper * cos + lower * sin).astype(bf16)
        joined_back[offset + half : offset + HEAD_DIM, columns] = (lower * cos - upper * sin).astype(bf16)

    width = heads * HEAD_DIM
    columns = pl.ds(pl.multiple_of(step * TILE_Q, TILE_Q), TILE_Q)
    for h in range(heads):
        store(h * HEAD_DIM, columns, query_sum[h][...] * 0.125)

    @pl.when(step == pl.num_programs(0) - 1)
    def _():
        for h in range(heads):
            first = width + h * HEAD_DIM
            store(first, slice(0, rows), key_sum[h][...] * (1.0 / LOG2E))
            first += width
            joined_back[first : first + HEAD_DIM, :] = value_sum[h][...].astype(bf16)


def attention_backward(
    low, high, queries, keys, values, grads, outs, logsum, key_rows, query_rows, cosine, sine
):
    width, rows = queries.shape
    heads = width // HEAD_DIM

    def full(count):
        return pl.BlockSpec((count, rows), lambda i, low, high: (0, 0))

    def tile(count):
        return pl.BlockSpec((count, TILE_Q), lambda i, low, high: (0, i))

    return pl.pallas_call(
        backward_kernel,
        out_shape=jax.ShapeDtypeStruct((3 * width, rows), bf16),
        grid_spec=pltpu.PrefetchScalarGridSpec(
            num_scalar_prefetch=2,
            grid=(rows // TILE_Q,),
            in_specs=[
                tile(width), full(width), full(width), tile(width), tile(width), tile(heads),
                full(16), tile(16), full(HEAD_DIM // 2), full(HEAD_DIM // 2),
            ],
            out_specs=full(3 * width),
            scratch_shapes=[
                pltpu.VMEM((heads, rows, DEPTH), bf16),
                pltpu.VMEM((heads, rows, DEPTH), bf16),
                pltpu.VMEM((heads, DEPTH, TILE_Q), bf16),
                pltpu.VMEM((heads, DEPTH, TILE_Q), bf16),
            ]
            + [pltpu.VMEM((HEAD_DIM, rows), f32)] * (2 * heads)
            + [pltpu.VMEM((HEAD_DIM, TILE_Q), f32)] * heads,
        ),
        compiler_params=pltpu.CompilerParams(
            dimension_semantics=("arbitrary",), vmem_limit_bytes=52 << 20
        ),
        name="attention_backward",
    )(low, high, queries, keys, values, grads, outs, logsum, key_rows, query_rows, cosine, sine)


def layer_norm(values, gain_row):
    centred = values - jnp.mean(values, axis=-1, keepdims=True)
    inverse = lax.rsqrt(jnp.mean(centred * centred, axis=-1, keepdims=True) + norm_epsilon)
    normal = centred * inverse
    return normal * gain_row, normal, inverse


def norm_back(upstream, gain_row, normal, inverse):
    scaled = upstream * gain_row
    inner_mean = jnp.mean(scaled * normal, axis=-1, keepdims=True)
    return inverse * (scaled - jnp.mean(scaled, axis=-1, keepdims=True) - normal * inner_mean)


def horner(square, factors):
    total = factors[0] * square + factors[1]
    for factor in factors[2:]:
        total = total * square + factor
    return total


def error_function(value):
    value = jnp.clip(value, -4.0, 4.0)
    square = value * value
    return value * horner(square, ERF_TOP) / horner(square, ERF_BOTTOM)


def turn(value):
    columns = value.shape[1]
    rest = jnp.zeros((value.shape[0], -columns % 128), value.dtype)
    return jnp.concatenate([value, rest], axis=1).T[:columns, :]


def turn_back(value):
    lines = value.shape[0]
    rest = jnp.zeros((-lines % 128, value.shape[1]), value.dtype)
    return jnp.concatenate([value, rest], axis=0).T[:, :lines]


def first_kernel(head, own, other, gain, rows, normed):
    tiles = pl.num_programs(0) // 2
    mine = pl.program_id(0) // tiles == head[0]
    value = jnp.where(mine, own[...].astype(f32), other[...].astype(f32))
    rows[...] = value.astype(bf16)
    normed[...] = layer_norm(value, gain[...])[0].astype(bf16)


def first_norm(head, own, other, gain):
    half, width = own.shape
    tiles = half // FEED_ROWS
    result = jax.ShapeDtypeStruct((2 * half, width), bf16)
    spec = pl.BlockSpec((FEED_ROWS, width), lambda i, head: (i, 0))
    return pl.pallas_call(
        first_kernel,
        out_shape=(result, result),
        grid_spec=pltpu.PrefetchScalarGridSpec(
            num_scalar_prefetch=1,
            grid=(2 * tiles,),
            in_specs=[
                pl.BlockSpec(
                    (FEED_ROWS, width),
                    lambda i, head: (jnp.clip(i - head[0] * tiles, 0, tiles - 1), 0),
                ),
                pl.BlockSpec(
                    (FEED_ROWS, width),
                    lambda i, head: (jnp.clip(i - (1 - head[0]) * tiles, 0, tiles - 1), 0),
                ),
                pl.BlockSpec((1, width), lambda i, head: (0, 0)),
            ],
            out_specs=[spec, spec],
        ),
        compiler_params=pltpu.CompilerParams(dimension_semantics=("arbitrary",)),
        name="first_norm",
    )(head, own, other, gain)


def gradient_kernel(back, normed, *refs):
    grads, total = refs[:-1], refs[-1]
    step = pl.program_id(0)

    @pl.when(step == 0)
    def _():
        total[...] = dot(back[...], normed[...], NN)

    @pl.when(step > 0)
    def _():
        total[...] += dot(back[...], normed[...], NN)

    @pl.when(step == pl.num_programs(0) - 1)
    def _():
        first = 0
        for grad in grads:
            grad[...] = total[:, first : first + grad.shape[1]].astype(bf16)
            first += grad.shape[1]


def joined_gradient(back, normed):
    lines, count = back.shape
    width = normed.shape[1]
    tile = 2 * FEED_ROWS
    half = width // 256 * 128
    parts = [half, width - half]
    return pl.pallas_call(
        gradient_kernel,
        grid=(count // tile,),
        in_specs=[
            pl.BlockSpec((lines, tile), lambda i: (0, i)),
            pl.BlockSpec((tile, width), lambda i: (i, 0)),
        ],
        out_specs=[pl.BlockSpec((lines, part), lambda i: (0, 0)) for part in parts],
        out_shape=[jax.ShapeDtypeStruct((lines, part), bf16) for part in parts],
        scratch_shapes=[pltpu.VMEM((lines, width), f32)],
        compiler_params=pltpu.CompilerParams(
            dimension_semantics=("arbitrary",), vmem_limit_bytes=32 << 20
        ),
        name="joined_gradient",
    )(back, normed)


def pull_kernel(head, back, weight, out):
    out[...] = dot(back[...].T, weight[...], NN).astype(bf16)


def pull_other(head, back, weight):
    lines, count = back.shape
    width = weight.shape[1]
    tiles = count // 2 // FEED_ROWS
    return pl.pallas_call(
        pull_kernel,
        out_shape=jax.ShapeDtypeStruct((count // 2, width), bf16),
        grid_spec=pltpu.PrefetchScalarGridSpec(
            num_scalar_prefetch=1,
            grid=(tiles,),
            in_specs=[
                pl.BlockSpec((lines, FEED_ROWS), lambda i, head: (0, (1 - head[0]) * tiles + i)),
                pl.BlockSpec((lines, width), lambda i, head: (0, 0)),
            ],
            out_specs=pl.BlockSpec((FEED_ROWS, width), lambda i, head: (i, 0)),
        ),
        compiler_params=pltpu.CompilerParams(
            dimension_semantics=("arbitrary",), vmem_limit_bytes=24 << 20
        ),
        name="pull_other",
    )(head, back, weight)


def input_kernel(head, back, weight, other, rows, middle_grad, gain, input_grad, gain_grad):
    @pl.when(pl.program_id(0) == 0)
    def _():
        gain_grad[...] = jnp.zeros(gain_grad.shape, f32)

    pulled = dot(back[...].T, weight[...], NN) + other[...].astype(f32)
    unused, normal, inverse = layer_norm(rows[...].astype(f32), gain[...])
    input_grad[...] = middle_grad[...] + norm_back(pulled, gain[...], normal, inverse)
    gain_grad[...] += jnp.sum(pulled * normal, axis=0, keepdims=True)


def input_backward(head, back, weight, other, rows, middle_grad, gain):
    lines, count = back.shape
    width = weight.shape[1]
    tiles = count // 2 // FEED_ROWS

    def down():
        return pl.BlockSpec((FEED_ROWS, width), lambda i, head: (i, 0))

    return pl.pallas_call(
        input_kernel,
        out_shape=(
            jax.ShapeDtypeStruct((count // 2, width), f32),
            jax.ShapeDtypeStruct((1, width), f32),
        ),
        grid_spec=pltpu.PrefetchScalarGridSpec(
            num_scalar_prefetch=1,
            grid=(tiles,),
            in_specs=[
                pl.BlockSpec((lines, FEED_ROWS), lambda i, head: (0, head[0] * tiles + i)),
                pl.BlockSpec((lines, width), lambda i, head: (0, 0)),
                down(),
                down(),
                pl.BlockSpec((FEED_ROWS, width), lambda i, head: (head[0] * tiles + i, 0)),
                pl.BlockSpec((1, width), lambda i, head: (0, 0)),
            ],
            out_specs=[down(), pl.BlockSpec((1, width), lambda i, head: (0, 0))],
        ),
        compiler_params=pltpu.CompilerParams(
            dimension_semantics=("arbitrary",), vmem_limit_bytes=24 << 20
        ),
        name="input_backward",
    )(head, back, weight, other, rows, middle_grad, gain)


def feed_kernel(
    rows, attended, attended_other, upstream, gain, both, mixer_other, expand_left, expand_right,
    middle, hidden, second_part, shrink_grad, left_grad, right_grad, shrink,
    shrink_sum, expand_sum, expand
):
    step = pl.program_id(0)
    mixed, units = attended.shape[0], shrink.shape[0]
    chunk = units // FEED_CHUNKS

    @pl.when(step == 0)
    def _():
        expand[:, : expand_left.shape[1]] = expand_left[...]
        expand[:, expand_left.shape[1] :] = expand_right[...]
        shrink[...] = turn(both[:, mixed:])
        shrink_sum[...] = jnp.zeros(shrink_sum.shape, f32)
        expand_sum[...] = jnp.zeros(expand_sum.shape, f32)

    total = rows[...].astype(f32) + dot(attended[...].T, both[:, :mixed], NT)
    total = total + dot(attended_other[...].T, mixer_other[...], NT)
    middle[...] = total
    normed = layer_norm(total, gain[...])[0].astype(bf16)
    above = upstream[...]

    def project(c):
        first = slice(c * chunk, (c + 1) * chunk)
        second = slice(units + c * chunk, units + (c + 1) * chunk)
        return (
            dot(expand[first, :], normed, NT),
            dot(expand[second, :], normed, NT),
            dot(shrink[first, :], above, NT),
        )

    waiting = project(0)
    back = jnp.zeros(total.shape, f32)
    for c in range(FEED_CHUNKS):
        active, linear, grad = waiting
        if c + 1 < FEED_CHUNKS:
            waiting = project(c + 1)
        first = slice(c * chunk, (c + 1) * chunk)
        second = slice(units + c * chunk, units + (c + 1) * chunk)
        area = 0.5 * error_function(active * math.sqrt(0.5)) + 0.5
        gate = active * area
        density = jnp.exp(-0.5 * active * active) * (1.0 / math.sqrt(2.0 * math.pi))
        unit = (gate * linear).astype(bf16)
        active_back = (grad * linear * (area + active * density)).astype(bf16)
        linear_back = (grad * gate).astype(bf16)
        hidden[first, :] = unit
        shrink_sum[first, :] += dot(unit, above, NN)
        expand_sum[first, :] += dot(active_back, normed, NN)
        expand_sum[second, :] += dot(linear_back, normed, NN)
        back = back + dot(active_back, expand[first, :], TN) + dot(linear_back, expand[second, :], TN)
    second_part[...] = back.astype(bf16)

    @pl.when(step == pl.num_programs(0) - 1)
    def _():
        shrink_grad[...] = shrink_sum[...].astype(bf16)
        cut = left_grad.shape[1]
        left_grad[...] = expand_sum[:, :cut].astype(bf16)
        right_grad[...] = expand_sum[:, cut:].astype(bf16)


def feed_forward(rows, attended, attended_other, upstream, gain, both, mixer_other, expand):
    count, width = rows.shape
    mixed, units = attended.shape[0], expand[0].shape[0] // 2

    def full(*shape):
        return pl.BlockSpec(shape, lambda i: (0, 0))

    def down(columns):
        return pl.BlockSpec((FEED_TILE, columns), lambda i: (i, 0))

    def along(lines):
        return pl.BlockSpec((lines, FEED_TILE), lambda i: (0, i))

    return pl.pallas_call(
        feed_kernel,
        grid=(count // FEED_TILE,),
        in_specs=[
            down(width), along(mixed), along(mixed), down(width), full(1, width),
            full(*both.shape), full(width, mixed), full(*expand[0].shape), full(*expand[1].shape),
        ],
        out_specs=[
            down(width), along(units), down(width), full(units, width),
            full(*expand[0].shape), full(*expand[1].shape), full(units, width),
        ],
        out_shape=(
            jax.ShapeDtypeStruct((count, width), f32),
            jax.ShapeDtypeStruct((units, count), bf16),
            jax.ShapeDtypeStruct((count, width), bf16),
            jax.ShapeDtypeStruct((units, width), bf16),
            jax.ShapeDtypeStruct(expand[0].shape, bf16),
            jax.ShapeDtypeStruct(expand[1].shape, bf16),
            jax.ShapeDtypeStruct((units, width), bf16),
        ),
        scratch_shapes=[
            pltpu.VMEM((units, width), f32),
            pltpu.VMEM((2 * units, width), f32),
            pltpu.VMEM((2 * units, width), bf16),
        ],
        compiler_params=pltpu.CompilerParams(
            dimension_semantics=("arbitrary",), vmem_limit_bytes=48 << 20
        ),
        name="feed_forward",
    )(rows, attended, attended_other, upstream, gain, both, mixer_other, *expand)


def norm_kernel(
    middle, own, other, upstream, gain, both, attended, shrink_grad,
    middle_grad, attended_grad, both_grad, gain_grad, mixer_turned, mixer_sum
):
    step = pl.program_id(0)

    @pl.when(step == 0)
    def _():
        mixer_turned[...] = both[:, : attended.shape[0]].T
        mixer_sum[...] = jnp.zeros(mixer_sum.shape, f32)
        gain_grad[...] = jnp.zeros(gain_grad.shape, f32)

    unused, normal, inverse = layer_norm(middle[...], gain[...])
    back = own[...].astype(f32) + other[...].astype(f32)
    grad = upstream[...].astype(f32) + norm_back(back, gain[...], normal, inverse)
    middle_grad[...] = grad
    grad_low = grad.astype(bf16)
    attended_grad[...] = dot(mixer_turned[...], grad_low, NT).astype(bf16)
    mixer_sum[...] += dot(attended[...], grad_low, NN)
    gain_grad[...] += jnp.sum(back * normal, axis=0, keepdims=True)

    @pl.when(step == pl.num_programs(0) - 1)
    def _():
        mixed = attended.shape[0]
        both_grad[:, :mixed] = mixer_sum[...].T.astype(bf16)
        both_grad[:, mixed:] = turn_back(shrink_grad[...])


def norm_backward(middle, own, other, upstream, gain, both, attended, shrink_grad):
    count, width = middle.shape
    mixed = attended.shape[0]

    def full(*shape):
        return pl.BlockSpec(shape, lambda i: (0, 0))

    def down(columns):
        return pl.BlockSpec((FEED_TILE, columns), lambda i: (i, 0))

    def along(lines):
        return pl.BlockSpec((lines, FEED_TILE), lambda i: (0, i))

    return pl.pallas_call(
        norm_kernel,
        grid=(count // FEED_TILE,),
        in_specs=[
            down(width), down(width), down(width), down(width), full(1, width),
            full(*both.shape), along(mixed), full(*shrink_grad.shape),
        ],
        out_specs=[down(width), along(mixed), full(*both.shape), full(1, width)],
        out_shape=(
            jax.ShapeDtypeStruct((count, width), f32),
            jax.ShapeDtypeStruct((mixed, count), bf16),
            jax.ShapeDtypeStruct(both.shape, bf16),
            jax.ShapeDtypeStruct((1, width), f32),
        ),
        scratch_shapes=[pltpu.VMEM((mixed, width), bf16), pltpu.VMEM((mixed, width), f32)],
        compiler_params=pltpu.CompilerParams(
            dimension_semantics=("arbitrary",), vmem_limit_bytes=40 << 20
        ),
        name="norm_backward",
    )(middle, own, other, upstream, gain, both, attended, shrink_grad)


def swap(value, axis, bit):
    count = lax.axis_size(axis)
    return lax.ppermute(value, axis, [(i, i ^ bit) for i in range(count)])


def bit_order(lead):
    bits = lax.axis_size("dp").bit_length() - 1
    return [int(bit) for bit in lead] + list(range(len(lead), bits))


def steps_count():
    return lax.axis_size("dp").bit_length() - 1


def cut(held, bit):
    axis = steps_count() - 1 - bit
    side = (lax.axis_index("dp") >> bit) & 1
    kept = lax.dynamic_slice_in_dim(held, side, 1, axis)
    return kept, lax.dynamic_slice_in_dim(held, 1 - side, 1, axis)


def reduce_start(value, lead):
    bits = steps_count()
    rows = value.shape[0] >> bits
    return cut(value.reshape((2,) * bits + (rows, value.shape[1])), bit_order(lead)[0])


def reduce_step(held, step, lead):
    bits = steps_count()
    kept, sent = held if step == 0 else cut(held, bit_order(lead)[step])
    total = kept.astype(f32) + swap(sent, "dp", 1 << bit_order(lead)[step]).astype(f32)
    if step + 1 == bits:
        return total.reshape(kept.shape[-2:])
    return total.astype(bf16)


def gather_start(value):
    return value[(None,) * steps_count()]


def gather_step(held, step, lead):
    bits = steps_count()
    bit = bit_order(lead)[bits - 1 - step]
    return jnp.concatenate([held, swap(held, "dp", 1 << bit)], axis=bits - 1 - bit)


def ordered_step(held, step, lead):
    bits = steps_count()
    bit = bit_order(lead)[bits - 1 - step]
    got = swap(held, "dp", 1 << bit)
    low_side = ((lax.axis_index("dp") >> bit) & 1) == 0
    return jnp.concatenate(
        [jnp.where(low_side, held, got), jnp.where(low_side, got, held)], axis=bits - 1 - bit
    )


def gather_rows(held):
    return held.reshape(-1, held.shape[-1])


def halves_of(value):
    unit = value.shape[1] // 256 * 128
    return [value[:, :unit], value[:, unit:]]


def quarter(step, states, part, leads):
    bits = steps_count()
    for index in range(bits * part // QUARTERS, bits * (part + 1) // QUARTERS):
        states = [step(state, index, lead) for state, lead in zip(states, leads)]
    return states


def tie(*values):
    return lax.optimization_barrier(values)


def total_step(value, part):
    if part == 0:
        return value + swap(value, "head", 1)
    bits = steps_count()
    for bit in range(bits * (part - 1) // QUARTERS, bits * part // QUARTERS):
        value = value + swap(value, "dp", 1 << bit)
    return value


def schulz_start(held, own, gram, low):
    down = 0
    for left in held:
        along = 0
        for right in held:
            gram[down : down + left.shape[1], along : along + right.shape[1]] = dot(left, right, TN)
            along += right.shape[1]
        down += left.shape[1]
    shape = gram.shape
    diagonal = lax.broadcasted_iota(jnp.int32, shape, 0) == lax.broadcasted_iota(jnp.int32, shape, 1)
    trace = jnp.sum(jnp.where(diagonal, gram[...], 0.0), axis=0, keepdims=True)
    norm_value = jnp.sqrt(jnp.sum(trace, axis=1, keepdims=True)) + 1e-07
    gram[...] = gram[...] * (1.0 / (norm_value * norm_value))
    low[...] = gram[...].astype(bf16)
    return own[...] / norm_value


def schulz_steps(rows, gram, low, change, first, stop):
    columns = gram.shape[0]
    lines = 256 if columns % 256 == 0 else columns

    def per_block(body):
        def run(index, carry):
            body(pl.ds(pl.multiple_of(index * lines, lines), lines))
            return carry

        lax.fori_loop(0, columns // lines, run, 0, unroll=True)

    def form_change(block):
        squared = dot(low[block, :], low[...], NN)
        change[block, :] = (ns_second * gram[block, :] + ns_third * squared).astype(bf16)

    def next_gram(block):
        once = ns_first * gram[block, :] + dot(low[block, :], change[...], NN)
        twice = ns_first * once + dot(once.astype(bf16), change[...], NN)
        gram[block, :] = twice
        low[block, :] = twice.astype(bf16)

    for iteration in range(first, stop):
        per_block(form_change)
        rows = ns_first * rows + dot(rows.astype(bf16), change[...], NN)
        if iteration + 1 < NS_ITERS:
            per_block(next_gram)
    return rows


def whole_kernel(*refs, count, offset, scale):
    parts = refs[:count]
    own, weight, updated, gram, low, change = refs[count:]
    if offset is None:
        held = [part[...] for part in parts]
    else:
        held = [parts[0][:, offset : offset + gram.shape[0]]]
    rows = schulz_start(held, own, gram, low)
    updated[...] = weight[...] - scale * schulz_steps(rows, gram, low, change, 0, NS_ITERS)


def early_kernel(*refs, count):
    own, rows, gram_out, low_out, gram, low, change = refs[count:]
    start = schulz_start([part[...] for part in refs[:count]], own, gram, low)
    rows[...] = start
    gram_out[...] = gram[...]
    low_out[...] = low[...]


def late_kernel(rows, gram_in, low_in, weight, updated, gram, low, change, *, scale):
    gram[...] = gram_in[...]
    low[...] = low_in[...]
    done = schulz_steps(rows[...], gram, low, change, 0, NS_ITERS)
    updated[...] = weight[...] - scale * done


def square_scratch(columns):
    return [
        pltpu.VMEM((columns, columns), f32),
        pltpu.VMEM((columns, columns), bf16),
        pltpu.VMEM((columns, columns), bf16),
    ]


def shape_scale(rows, columns):
    return muon_rate * math.sqrt(rows / columns)


def schulz(parts, offset, own, weight, name):
    columns = own.shape[1]
    return pl.pallas_call(
        functools.partial(
            whole_kernel, count=len(parts), offset=offset, scale=shape_scale(parts[0].shape[0], columns)
        ),
        out_shape=jax.ShapeDtypeStruct(own.shape, f32),
        scratch_shapes=square_scratch(columns),
        compiler_params=pltpu.CompilerParams(vmem_limit_bytes=40 << 20),
        name=name,
    )(*parts, own, weight)


def schulz_early(parts, own):
    columns = own.shape[1]
    return pl.pallas_call(
        functools.partial(early_kernel, count=len(parts)),
        out_shape=(
            jax.ShapeDtypeStruct(own.shape, f32),
            jax.ShapeDtypeStruct((columns, columns), f32),
            jax.ShapeDtypeStruct((columns, columns), bf16),
        ),
        scratch_shapes=square_scratch(columns),
        compiler_params=pltpu.CompilerParams(vmem_limit_bytes=40 << 20),
        name="schulz_early",
    )(*parts, own)


def schulz_late(state, weight, rows):
    columns = weight.shape[1]
    return pl.pallas_call(
        functools.partial(late_kernel, scale=shape_scale(rows, columns)),
        out_shape=jax.ShapeDtypeStruct(weight.shape, f32),
        scratch_shapes=square_scratch(columns),
        compiler_params=pltpu.CompilerParams(vmem_limit_bytes=40 << 20),
        name="schulz_late",
    )(*state, weight)


def shards(
    tokens,
    lengths,
    norm_gains,
    joined_weight,
    mixer_weight,
    expand_weight,
    shrink_weight,
    joined_momentum,
    mixer_momentum,
    expand_momentum,
    shrink_momentum,
    gain_momentum,
    cotangent,
):
    row_count = cotangent.shape[0]
    local_rows = tokens.shape[0]
    head = lax.axis_index("head")
    mixer_width = mixer_weight.shape[2]

    def own_half(value):
        return lax.dynamic_slice_in_dim(value, head * local_rows, local_rows, 0)

    joined_parts = [gather_start(part) for part in halves_of(joined_weight[0].astype(bf16))]
    joined_parts = quarter(ordered_step, joined_parts, 0, JOINED_FIRST)
    others = [gather_start(part) for part in halves_of(expand_weight[0].astype(bf16))] + [
        gather_start(jnp.concatenate([mixer_weight[0], shrink_weight[0]], axis=1).astype(bf16))
    ]
    key_rows, query_rows, cosine, sine = doc_tables(lengths[0], row_count)
    low, high = key_bounds(lengths[0], row_count)
    head_place = head[None]
    tokens_other = swap(tokens, "head", 1)

    joined_parts, others, tokens_other = tie(joined_parts, others, tokens_other)
    joined_parts = quarter(ordered_step, joined_parts, 1, JOINED_FIRST)
    others = quarter(ordered_step, others, 0, OTHERS_FIRST)
    rows_low, first_low = first_norm(head_place, tokens, tokens_other, norm_gains[0:1])
    joined_parts, others, first_low = tie(joined_parts, others, first_low)
    joined_parts = quarter(ordered_step, joined_parts, 2, JOINED_FIRST)
    others = quarter(ordered_step, others, 1, OTHERS_FIRST)
    joined_parts, others = tie(joined_parts, others)
    joined_parts = quarter(ordered_step, joined_parts, 3, JOINED_FIRST)
    moved = quarter(ordered_step, others, 2, OTHERS_FIRST)

    joined_low = jnp.concatenate([gather_rows(part) for part in joined_parts], axis=1)
    joined = dot(joined_low, first_low, NT)
    width = joined.shape[0] // 3
    queries = (rotate(joined[:width], cosine, sine) * QUERY_SCALE).astype(bf16)
    keys = rotate(joined[width : 2 * width], cosine, sine).astype(bf16)
    values = joined[2 * width :].astype(bf16)
    others, queries, keys, values, low = tie(moved, queries, keys, values, low)
    moved = quarter(ordered_step, others, 3, OTHERS_FIRST)
    attended, logsum = attention_forward(low, high, queries, keys, values, key_rows, query_rows)
    others, attended, logsum = tie(moved, attended, logsum)
    attended_other = swap(attended, "head", 1)
    both_low = gather_rows(others[2])
    mixer_other = swap(both_low[:, :mixer_width], "head", 1)

    second_gain = norm_gains[1:2]
    middle, hidden, second_part, shrink_grad, left_grad, right_grad, shrink_turned = feed_forward(
        rows_low, attended, attended_other, cotangent, second_gain,
        both_low, mixer_other, [gather_rows(part) for part in others[:2]],
    )
    second_other = swap(second_part, "head", 1)

    sums = [reduce_start(part, lead) for part, lead in zip((left_grad, right_grad), PAIR)]
    sums, second_other = tie(sums, second_other)
    moved = quarter(reduce_step, sums, 0, PAIR)
    middle_grad, attended_grad, both_grad, second_gain_grad = norm_backward(
        middle, second_part, second_other, cotangent, second_gain, both_low, attended, shrink_grad
    )
    both_sum = [reduce_start(both_grad, ONE[0])]

    sums, attended_grad, shrink_now = tie(moved, attended_grad, shrink_turned)
    moved = quarter(reduce_step, sums, 1, PAIR)

    def fed(columns):
        units = lax.dynamic_slice_in_dim(hidden, columns, local_rows, 1)
        return dot(units, shrink_now, TN)

    fed_other = fed((1 - head) * local_rows).astype(bf16)
    fed_own = fed(head * local_rows)

    sums, both_sum, fed_other, fed_own, low = tie(moved, both_sum, fed_other, fed_own, low)
    moved = quarter(reduce_step, sums, 2, PAIR)
    both_moved = quarter(reduce_step, both_sum, 0, ONE)
    fed_other = swap(fed_other, "head", 1)
    joined_back = attention_backward(
        low, high, queries, keys, values, attended_grad, attended, logsum, key_rows, query_rows,
        cosine, sine,
    )
    sums, both_sum, joined_back, fed_other = tie(moved, both_moved, joined_back, fed_other)
    moved = quarter(reduce_step, sums, 3, PAIR)
    both_moved = quarter(reduce_step, both_sum, 1, ONE)
    joined_grad = joined_gradient(joined_back, first_low)

    sums, both_sum, joined_grad, joined_now = tie(moved, both_moved, joined_grad, joined_low)
    expand_next = 0.5 * expand_momentum[0] + jnp.concatenate(sums, axis=1)
    gathers = [gather_start(part) for part in halves_of(expand_next.astype(bf16))]
    sums = [reduce_start(part, lead) for part, lead in zip(joined_grad, PAIR)]
    sums = quarter(reduce_step, sums, 0, PAIR)
    moved = quarter(gather_step, gathers, 0, PAIR)
    both_moved = quarter(reduce_step, both_sum, 2, ONE)
    first_other = pull_other(head_place, joined_back, joined_now)

    sums, gathers, both_sum, first_other, fed_own = tie(sums, moved, both_moved, first_other, fed_own)
    first_other = swap(first_other, "head", 1)
    moved = quarter(reduce_step, sums, 1, PAIR)
    gathers_moved = quarter(gather_step, gathers, 1, PAIR)
    both_moved = quarter(reduce_step, both_sum, 3, ONE)

    sums, gathers, both_sum, first_other, fed_own = tie(
        moved, gathers_moved, both_moved, first_other, fed_own
    )
    mixer_next = 0.5 * mixer_momentum[0] + both_sum[0][:, :mixer_width]
    shrink_next = 0.5 * shrink_momentum[0] + both_sum[0][:, mixer_width:]
    both_gather = [gather_start(jnp.concatenate([mixer_next, shrink_next], axis=1).astype(bf16))]
    moved = quarter(reduce_step, sums, 2, PAIR)
    gathers_moved = quarter(gather_step, gathers, 2, PAIR)
    both_moved = quarter(gather_step, both_gather, 0, ONE)
    layer_output = (own_half(middle) + fed_own + fed_other.astype(f32)).astype(bf16)

    sums, gathers, both_gather, first_other, layer_output = tie(
        moved, gathers_moved, both_moved, first_other, layer_output
    )
    moved = quarter(reduce_step, sums, 3, PAIR)
    gathers_moved = quarter(gather_step, gathers, 3, PAIR)
    both_moved = quarter(gather_step, both_gather, 1, ONE)
    input_gradient, first_gain_grad = input_backward(
        head_place, joined_back, joined_now, first_other, tokens, middle_grad, norm_gains[0:1]
    )
    gain_totals = jnp.concatenate([first_gain_grad, 0.5 * second_gain_grad], axis=0)

    sums, gathers, both_gather, gain_totals = tie(moved, gathers_moved, both_moved, gain_totals)
    joined_next = 0.5 * joined_momentum[0] + jnp.concatenate(sums, axis=1)
    joined_gather = [gather_start(part) for part in halves_of(joined_next.astype(bf16))]
    moved = quarter(gather_step, joined_gather, 0, PAIR)
    both_moved = quarter(gather_step, both_gather, 2, ONE)
    gain_moved = total_step(gain_totals, 0)
    expand_state = schulz_early([gather_rows(part) for part in gathers], expand_next)
    joined_gather, both_gather, gain_totals, expand_state = tie(
        moved, both_moved, gain_moved, expand_state
    )
    moved = quarter(gather_step, joined_gather, 1, PAIR)
    both_moved = quarter(gather_step, both_gather, 3, ONE)
    gain_moved = total_step(gain_totals, 1)
    updated_expand = schulz_late(expand_state, expand_weight[0], left_grad.shape[0])
    joined_gather, both_gather, gain_totals, updated_expand = tie(
        moved, both_moved, gain_moved, updated_expand
    )
    both_full = [gather_rows(both_gather[0])]
    moved = quarter(gather_step, joined_gather, 2, PAIR)
    gain_moved = total_step(gain_totals, 2)
    updated_shrink = schulz(
        both_full, mixer_width, shrink_next, shrink_weight[0], "schulz_shrink"
    )
    joined_gather, both_full, gain_totals, updated_shrink = tie(
        moved, both_full, gain_moved, updated_shrink
    )
    moved = quarter(gather_step, joined_gather, 3, PAIR)
    gain_moved = total_step(gain_totals, 3)
    updated_mixer = schulz(both_full, 0, mixer_next, mixer_weight[0], "schulz_mixer")
    joined_gather, gain_totals, updated_mixer = tie(moved, gain_moved, updated_mixer)
    gain_totals = total_step(gain_totals, 4)
    updated_joined = schulz(
        [gather_rows(part) for part in joined_gather],
        None, joined_next, joined_weight[0], "schulz_joined",
    )

    momentum_gains = 0.5 * gain_momentum + gain_totals
    updated_gains = norm_gains - gain_rate * momentum_gains * lax.rsqrt(
        jnp.mean(momentum_gains * momentum_gains, axis=-1, keepdims=True) + 1e-06
    )
    return (
        layer_output,
        input_gradient,
        joined_next[None],
        mixer_next[None],
        expand_next[None],
        shrink_next[None],
        updated_joined[None],
        updated_mixer[None],
        updated_expand[None],
        updated_shrink[None],
        momentum_gains,
        updated_gains,
    )


def solution(mesh):
    rows = P(("dp", "head"), None)
    weight = P("head", "dp", None)
    return jax.shard_map(
        shards,
        mesh=mesh,
        in_specs=(rows, P("dp", None), P()) + (weight,) * 8 + (P(), P("dp", None)),
        out_specs=(rows, rows) + (weight,) * 8 + (P(), P()),
        check_vma=False,
    )
```
